32 devices in a mesh: replica: 8 (over y, x, core), group: 4 (over z).
Axes of the slice: x: 2, y: 2, z: 4, core: 2. Of those that a mesh axis runs over, the one named last changes fastest.
Arguments:
- inputs: bfloat16 [8, 512, 2048], P('replica', 'group'), may hold values from -6 to 6
- seq_lengths: int32 [8], P('replica'), may hold values from 128 to 512, as said below
- bucket_ids: int32 [1023], replicated, may hold values from 0 to 31, as said below
- norm1_gain: bfloat16 [2048], P('group'), may hold values from 0.25 to 1.75
- w_query: bfloat16 [2048, 2048], P(None, 'group'), may hold values from -0.0625 to 0.0625
- w_key: bfloat16 [2048, 2048], P(None, 'group'), may hold values from -0.0625 to 0.0625
- w_value: bfloat16 [2048, 2048], P(None, 'group'), may hold values from -0.125 to 0.125
- w_attn_out: bfloat16 [2048, 2048], P('group'), may hold values from -0.5 to 0.5
- bias_table: bfloat16 [32, 32], P(None, 'group'), may hold values from -4 to 4
- norm2_gain: bfloat16 [2048], P('group'), may hold values from 0.25 to 1.75
- w_gate: bfloat16 [2048, 5120], P(None, 'group'), may hold values from -0.125 to 0.125
- w_up: bfloat16 [2048, 5120], P(None, 'group'), may hold values from -0.125 to 0.125
- w_ffn_out: bfloat16 [5120, 2048], P('group'), may hold values from -0.078125 to 0.078125
- cotangent: bfloat16 [8, 512, 2048], P('replica', 'group'), may hold values from -6 to 6
Outputs:
- result: bfloat16 [8, 512, 2048], P('replica', 'group')
- input_grad: bfloat16 [8, 512, 2048], P('replica', 'group')
- norm1_gain_grad: float32 [2048], P('group')
- query_grad: float32 [2048, 2048], P(None, 'group')
- key_grad: float32 [2048, 2048], P(None, 'group')
- value_grad: float32 [2048, 2048], P(None, 'group')
- attn_out_grad: float32 [2048, 2048], P('group')
- bias_table_grad: float32 [32, 32], P(None, 'group')
- norm2_gain_grad: float32 [2048], P('group')
- gate_grad: float32 [2048, 5120], P(None, 'group')
- up_grad: float32 [2048, 5120], P(None, 'group')
- ffn_out_grad: float32 [5120, 2048], P('group')
The draws below stay inside these ranges and needn't reach their ends.
Inputs may be any that keep to these rules, and one draw needn't show every extreme that they name: `seq_lengths`: one sequence has exactly 512 valid positions and another exactly 128. `bucket_ids`: entry 511 + o is the bucket of the offset o = key position - query position; every bucket occurs.
All inputs are finite; a program needn't handle non-finite values.
Results may differ from the reference program's by a relative error of at most 0.02.
Values may be sent and summed in bfloat16 or wider, within the bound.
A program may use at most 448 MiB of HBM per device.

```python
import jax
import jax.numpy as jnp
from jax import lax

D = 2048
HEADS = 32
HEAD_DIM = 64
FF = 5120
BUCKETS = 32
SEQ_LEN = 512
BATCH = 8


def draw_seq_lengths(key, part):
    key_vals, key_long, key_stride = jax.random.split(key, 3)
    lengths = jax.random.randint(key_vals, (BATCH,), SEQ_LEN // 4, SEQ_LEN + 1)
    longest = jax.random.randint(key_long, (), 0, BATCH)
    stride = jax.random.randint(key_stride, (), 1, BATCH)
    shortest = (longest + stride) % BATCH
    positions = jnp.arange(BATCH)
    lengths = jnp.where(positions == longest, SEQ_LEN, lengths)
    lengths = jnp.where(positions == shortest, SEQ_LEN // 4, lengths)
    return lengths.astype(jnp.int32)


def draw_bucket_ids(key, part):
    key_ids, key_order = jax.random.split(key)
    bucket_list = jax.random.randint(key_ids, (2 * SEQ_LEN - 1,), 0, BUCKETS)
    ordering = jax.random.permutation(key_order, BUCKETS)
    bucket_list = bucket_list.at[:BUCKETS].set(ordering)
    return bucket_list.astype(jnp.int32)


def block_scale(rng, shape, shards, least, top_value):
    def one(axis_at, blocks):
        draws = jax.random.uniform(jax.random.fold_in(jax.random.fold_in(rng, 6), axis_at), (blocks,), jnp.float32, least / len(shards), top_value / len(shards))
        return jnp.repeat(jnp.exp(draws), shape[axis_at] // blocks).reshape((-1,) + (1,) * (len(shape) - axis_at - 1))

    level = one(*shards[0])
    for cut in shards[1:]:
        level = level * one(*cut)
    return level


def centred(rng, shape, scale, most, shards=(), dtype=jnp.bfloat16):
    level = block_scale(rng, shape, shards, -0.22, 0.18) if shards else 1.0
    entries = jax.random.normal(rng, shape, jnp.float32) * scale * level
    return jnp.minimum(jnp.maximum(entries, -most), most).astype(dtype)


def setup_inputs(seed: int = 0) -> dict:
    streams_of = jax.random.split(jax.random.key(seed), 15)
    inputs = centred(streams_of[0], (BATCH, SEQ_LEN, D), 1.0, 6.0, ((0, 8), (1, 4)))
    seq_lengths = draw_seq_lengths(jax.random.fold_in(streams_of[14], 71), 0)
    bucket_ids = draw_bucket_ids(jax.random.fold_in(streams_of[14], 71), 0)
    norm1_gain = jnp.clip(1.0 + 0.15 * jax.random.normal(streams_of[3], (D,), jnp.float32), 0.25, 1.75).astype(jnp.bfloat16)
    w_query = centred(streams_of[4], (D, HEADS * HEAD_DIM), (4 * D) ** -0.5, 0.0625, ((1, 4),))
    w_key = centred(streams_of[5], (D, HEADS * HEAD_DIM), (4 * D) ** -0.5, 0.0625, ((1, 4),))
    w_value = centred(streams_of[6], (D, HEADS * HEAD_DIM), D ** -0.5, 0.125, ((1, 4),))
    w_attn_out = centred(streams_of[7], (HEADS * HEAD_DIM, D), (max(HEADS * HEAD_DIM // 16, 1)) ** -0.5, 0.5, ((0, 4),))
    bias_table = centred(streams_of[8], (BUCKETS, HEADS), 1.0, 4.0, ((1, 4),))
    norm2_gain = jnp.clip(1.0 + 0.15 * jax.random.normal(streams_of[9], (D,), jnp.float32), 0.25, 1.75).astype(jnp.bfloat16)
    w_gate = centred(streams_of[10], (D, FF), D ** -0.5, 0.125, ((1, 4),))
    w_up = centred(streams_of[11], (D, FF), D ** -0.5, 0.125, ((1, 4),))
    w_ffn_out = centred(streams_of[12], (FF, D), FF ** -0.5, 0.078125, ((0, 4),))
    cotangent = centred(streams_of[13], (BATCH, SEQ_LEN, D), 1.0, 6.0, ((0, 8), (1, 4)))
    return {"inputs": inputs, "seq_lengths": seq_lengths, "bucket_ids": bucket_ids, "norm1_gain": norm1_gain, "w_query": w_query, "w_key": w_key, "w_value": w_value, "w_attn_out": w_attn_out, "bias_table": bias_table, "norm2_gain": norm2_gain, "w_gate": w_gate, "w_up": w_up, "w_ffn_out": w_ffn_out, "cotangent": cotangent}


@jax.custom_vjp
def low(v):
    return lax.optimization_barrier(v.astype(jnp.bfloat16)).astype(jnp.float32)

@jax.custom_vjp
def low_back(v):
    return v

def low_keep(v):
    return (low(v), None)

def low_pass(kept, grad):
    return (grad,)

def back_keep(v):
    return (v, None)

def back_low(kept, grad):
    return (low(grad),)
low.defvjp(low_keep, low_pass)
low_back.defvjp(back_keep, back_low)
epsilon = 1e-06
negative = -1000000000.0
head_block = 8
highest = lax.Precision.HIGHEST

def rms_scale(values, gain):
    return values * lax.rsqrt(lax.optimization_barrier(jnp.mean(values * values, axis=-1, keepdims=True)) + epsilon) * gain

def encoder_layer(hidden_in, length, index_table, gain_one, query_w, key_w, value_w, attn_w, bias_tab, gain_two, gate_w, up_w, ffn_w):
    positions = hidden_in.shape[0]
    head_count = bias_tab.shape[1]
    groups = head_count // head_block
    key_valid = (jnp.arange(positions) < length)[None, None, :]
    normed_one = low(rms_scale(hidden_in, gain_one))
    queries = low_back(low(jnp.dot(normed_one, query_w, precision=highest)))
    key_rows = low_back(low(jnp.dot(normed_one, key_w, precision=highest)))
    value_rows = low_back(low(jnp.dot(normed_one, value_w, precision=highest)))

    def heads_split(matrix):
        return matrix.reshape(positions, groups, head_block, -1).transpose(1, 0, 2, 3)
    table_blocks = bias_tab.reshape(bias_tab.shape[0], groups, head_block).transpose(1, 0, 2)

    def head_group_raw(operands):
        query_blk, key_blk, value_blk, table_blk = operands
        bias_blk = jnp.take(table_blk, index_table, axis=0).transpose(2, 0, 1)
        scores = jnp.einsum('qhd,khd->hqk', query_blk, key_blk, precision=highest) + bias_blk
        scores = low_back(jnp.where(key_valid, scores, negative))
        probs_low = low(jax.nn.softmax(scores, axis=-1))
        return jnp.einsum('hqk,khd->qhd', probs_low, value_blk, precision=highest)
    head_group = jax.checkpoint(head_group_raw)
    attended = lax.map(head_group, (heads_split(queries), heads_split(key_rows), heads_split(value_rows), table_blocks))
    attended = low_back(low(attended.transpose(1, 0, 2, 3).reshape(positions, -1)))
    middle = hidden_in + low_back(jnp.dot(attended, attn_w, precision=highest))
    normed_two = low(rms_scale(middle, gain_two))
    gate_pre = low_back(jnp.dot(normed_two, gate_w, precision=highest))
    up_pre = low_back(jnp.dot(normed_two, up_w, precision=highest))
    hidden = low(jax.nn.gelu(gate_pre, approximate=True) * up_pre)
    return middle + low_back(jnp.dot(hidden, ffn_w, precision=highest))

def reference(inputs, seq_lengths, bucket_ids, norm1_gain, w_query, w_key, w_value, w_attn_out, bias_table, norm2_gain, w_gate, w_up, w_ffn_out, cotangent):
    positions = inputs.shape[1]
    params = tuple((weight.astype(jnp.float32) for weight in (norm1_gain, w_query, w_key, w_value, w_attn_out, bias_table, norm2_gain, w_gate, w_up, w_ffn_out)))
    offsets = (jnp.arange(positions)[None, :] - jnp.arange(positions)[:, None] + (positions - 1)).astype(jnp.int32)
    index_table = jnp.take(bucket_ids, offsets, axis=0)

    def one_sequence(totals, operands):
        tokens_in, length, grad_in = operands
        row_valid = (jnp.arange(positions) < length).astype(jnp.float32)

        def apply_layer(hidden_in, *weights):
            return encoder_layer(hidden_in, length, index_table, *weights)
        outputs, pull_back = jax.vjp(apply_layer, tokens_in.astype(jnp.float32), *params)
        gradients = pull_back(grad_in.astype(jnp.float32) * row_valid[:, None])
        totals = tuple((total + grad for total, grad in zip(totals, gradients[1:])))
        return (totals, (outputs.astype(jnp.bfloat16), gradients[0].astype(jnp.bfloat16)))
    zeros_init = tuple((jnp.zeros(weight.shape, jnp.float32) for weight in params))
    totals, (results, input_grads) = lax.scan(one_sequence, zeros_init, (inputs, seq_lengths, cotangent))
    return (results, input_grads, totals[0], totals[1], totals[2], totals[3], totals[4], totals[5], totals[6], totals[7], totals[8], totals[9])
```

```python
import jax
import jax.numpy as jnp
from jax import lax
from jax.sharding import PartitionSpec as P

epsilon = 1e-06
negative = -1000000000.0
highest = lax.Precision.HIGHEST
head_dim = 64


def rms_scale(values, gain):
    return values * lax.rsqrt(jnp.mean(values * values, axis=-1, keepdims=True) + epsilon) * gain


def gated_gelu(gate_pre, up_pre):
    return jax.nn.gelu(gate_pre, approximate=True) * up_pre


def rows_dot(left, right):
    return lax.dot_general(
        left, right, (((0,), (0,)), ((), ())), preferred_element_type=jnp.float32
    )


def cols_dot(left, right):
    return lax.dot_general(
        left, right, (((1,), (1,)), ((), ())), preferred_element_type=jnp.float32
    )


def plain_dot(left, right):
    return jnp.dot(left, right, preferred_element_type=jnp.float32)


def spread_offsets(vector, row_count, col_count):
    span_width = row_count + col_count + 1
    block_heads = vector.shape[0]
    tiled_rows = jnp.broadcast_to(vector[:, None, :], (block_heads, row_count, span_width))
    flattened = tiled_rows.reshape(block_heads, row_count * span_width)[
        :, : row_count * (span_width - 1)
    ]
    return flattened.reshape(block_heads, row_count, span_width - 1)[:, :, row_count:]


def fold_offsets(matrix):
    block_heads, row_count, col_count = matrix.shape
    padded = jnp.pad(matrix, ((0, 0), (0, 0), (row_count, 0)))
    flattened = jnp.pad(
        padded.reshape(block_heads, row_count * (row_count + col_count)), ((0, 0), (0, row_count))
    )
    sums_all = flattened.reshape(block_heads, row_count, row_count + col_count + 1).sum(axis=1)
    return sums_all[:, 1 : row_count + col_count]


def heads(matrix):
    return matrix.reshape(matrix.shape[0], -1, head_dim)


def local(
    inputs,
    seq_lengths,
    bucket_ids,
    norm1_gain,
    w_query,
    w_key,
    w_value,
    w_attn_out,
    bias_table,
    norm2_gain,
    w_gate,
    w_up,
    w_ffn_out,
    cotangent,
):
    group = lax.axis_index("group")
    rows = inputs.shape[1]
    length = seq_lengths[0]
    total = rows * lax.axis_size("group")
    start = group * rows
    valid = jnp.arange(total) < length

    def gather(values):
        return lax.all_gather(values, "group", axis=0, tiled=True)

    def scatter(values):
        return lax.psum_scatter(
            values.astype(jnp.bfloat16), "group", scatter_dimension=0, tiled=True
        ).astype(jnp.float32)

    x_all_low = gather(inputs[0])
    g_all = jnp.where(valid[:, None], gather(cotangent[0]), jnp.bfloat16(0))
    gains = lax.all_gather(jnp.stack([norm1_gain, norm2_gain]), "group", axis=1, tiled=True)
    gains = gains.astype(jnp.float32)
    gain_first, gain_second = gains[0], gains[1]
    x_local = inputs[0].astype(jnp.float32)
    normed_one = rms_scale(x_all_low.astype(jnp.float32), gain_first).astype(jnp.bfloat16)
    query = plain_dot(normed_one, w_query).astype(jnp.bfloat16)
    key = plain_dot(normed_one, w_key).astype(jnp.bfloat16)
    value = plain_dot(normed_one, w_value).astype(jnp.bfloat16)

    buckets = bias_table.shape[0]
    one_hot = (bucket_ids[:, None] == jnp.arange(buckets)[None, :]).astype(jnp.float32)
    per_offset = jnp.dot(one_hot, bias_table.astype(jnp.float32), precision=highest)
    bias = spread_offsets(jnp.pad(per_offset.T, ((0, 0), (1, 1))), total, total)
    scores = jnp.einsum(
        "qhd,khd->hqk", heads(query), heads(key), preferred_element_type=jnp.float32
    )
    scores = jnp.where(valid[None, None, :], scores + bias, negative)
    probs = jax.nn.softmax(scores, axis=-1)
    probs_low = probs.astype(jnp.bfloat16)
    attended = jnp.einsum(
        "hqk,khd->qhd", probs_low, heads(value), preferred_element_type=jnp.float32
    )
    attended = attended.reshape(total, -1).astype(jnp.bfloat16)
    middle = x_local + scatter(plain_dot(attended, w_attn_out))
    normed_two = gather(rms_scale(middle, gain_second).astype(jnp.bfloat16))

    gate_pre = plain_dot(normed_two, w_gate)
    up_pre = plain_dot(normed_two, w_up)
    hidden_low = gated_gelu(gate_pre, up_pre).astype(jnp.bfloat16)
    grad_hidden = cols_dot(g_all, w_ffn_out)
    _, pull_gelu = jax.vjp(gated_gelu, gate_pre, up_pre)
    grad_gate, grad_up = pull_gelu(grad_hidden)
    grad_gate = grad_gate.astype(jnp.bfloat16)
    grad_up = grad_up.astype(jnp.bfloat16)
    grad_normed_two = scatter(cols_dot(grad_gate, w_gate) + cols_dot(grad_up, w_up))
    ffn_out_grad = rows_dot(hidden_low, g_all)
    gate_grad = rows_dot(normed_two, grad_gate)
    up_grad = rows_dot(normed_two, grad_up)

    def total_sum(values):
        return lax.psum(values.astype(jnp.bfloat16), "replica").astype(jnp.float32)

    ffn_out_grad, gate_grad, up_grad = (
        total_sum(ffn_out_grad), total_sum(gate_grad), total_sum(up_grad)
    )
    result = (middle + scatter(plain_dot(hidden_low, w_ffn_out))).astype(jnp.bfloat16)

    row_valid = start + jnp.arange(rows) < length
    g_local = jnp.where(row_valid[:, None], cotangent[0], jnp.bfloat16(0)).astype(jnp.float32)
    _, pull_two = jax.vjp(rms_scale, middle, gain_second)
    grad_mid_norm, gain_two_grad = pull_two(grad_normed_two)
    grad_middle = g_local + grad_mid_norm
    grad_branch = gather(grad_middle.astype(jnp.bfloat16))

    attn_out_grad = rows_dot(attended, grad_branch)
    grad_attended = cols_dot(grad_branch, w_attn_out).astype(jnp.bfloat16)
    grad_probs = jnp.einsum(
        "qhd,khd->hqk", heads(grad_attended), heads(value), preferred_element_type=jnp.float32
    )
    inner_sum = jnp.sum(probs * grad_probs, axis=-1, keepdims=True)
    grad_scores = (probs * (grad_probs - inner_sum)).astype(jnp.bfloat16)

    def merge(values):
        return values.reshape(total, -1).astype(jnp.bfloat16)

    grad_query = merge(
        jnp.einsum("hqk,khd->qhd", grad_scores, heads(key), preferred_element_type=jnp.float32)
    )
    grad_key = merge(
        jnp.einsum("hqk,qhd->khd", grad_scores, heads(query), preferred_element_type=jnp.float32)
    )
    grad_value = merge(
        jnp.einsum(
            "hqk,qhd->khd", probs_low, heads(grad_attended), preferred_element_type=jnp.float32
        )
    )
    offset_sums = fold_offsets(grad_scores.astype(jnp.float32))
    table_grad = jnp.dot(offset_sums, one_hot, precision=highest).T
    query_grad = rows_dot(normed_one, grad_query)
    key_grad = rows_dot(normed_one, grad_key)
    value_grad = rows_dot(normed_one, grad_value)
    grad_normed_one = scatter(
        cols_dot(grad_query, w_query) + cols_dot(grad_key, w_key) + cols_dot(grad_value, w_value)
    )
    query_grad, key_grad, value_grad, attn_out_grad = (
        total_sum(query_grad), total_sum(key_grad), total_sum(value_grad), total_sum(attn_out_grad)
    )
    table_grad = lax.psum(table_grad, "replica")
    _, pull_one = jax.vjp(rms_scale, x_local, gain_first)
    grad_in_norm, gain_one_grad = pull_one(grad_normed_one)
    input_grad = (grad_middle + grad_in_norm).astype(jnp.bfloat16)
    gain_sums = lax.psum(jnp.stack([gain_one_grad, gain_two_grad]), ("replica", "group"))
    width = norm1_gain.shape[0]
    gain_sums = lax.dynamic_slice_in_dim(gain_sums, group * width, width, axis=1)
    return (
        result[None],
        input_grad[None],
        gain_sums[0],
        query_grad,
        key_grad,
        value_grad,
        attn_out_grad,
        table_grad,
        gain_sums[1],
        gate_grad,
        up_grad,
        ffn_out_grad,
    )

def solution(mesh):
    placed = (
        P("replica", "group", None),
        P("replica"),
        P(),
        P("group"),
        P(None, "group"),
        P(None, "group"),
        P(None, "group"),
        P("group", None),
        P(None, "group"),
        P("group"),
        P(None, "group"),
        P(None, "group"),
        P("group", None),
        P("replica", "group", None),
    )
    return jax.shard_map(
        local,
        mesh=mesh,
        in_specs=placed,
        out_specs=(
            P("replica", "group", None),
            P("replica", "group", None),
            P("group"),
            P(None, "group"),
            P(None, "group"),
            P(None, "group"),
            P("group", None),
            P(None, "group"),
            P("group"),
            P(None, "group"),
            P(None, "group"),
            P("group", None),
        ),
        check_vma=False,
    )
```

```python
import functools
import jax
import jax.numpy as jnp
from jax import lax
from jax.experimental import pallas as pl
from jax.experimental.pallas import tpu as pltpu
from jax.sharding import PartitionSpec as P

epsilon = 1e-06
negative = -1000000000.0
head_dim = 64
lanes = 128
MESH = pl.DeviceIdType.MESH
any_space = pl.BlockSpec(memory_space=pl.ANY)
vmem_space = pl.BlockSpec(memory_space=pltpu.VMEM)
smem_space = pl.BlockSpec(memory_space=pltpu.SMEM)


def nn_dot(left, right):
    return jnp.dot(left, right, preferred_element_type=jnp.float32)


def nt_dot(left, right):
    return lax.dot_general(
        left, right, (((1,), (1,)), ((), ())), preferred_element_type=jnp.float32
    )


def line_barrier(me, count):
    barrier = pltpu.get_barrier_semaphore()

    @pl.when(me > 0)
    def _():
        pl.semaphore_signal(barrier, inc=1, device_id={"group": me - 1}, device_id_type=MESH)

    @pl.when(me < count - 1)
    def _():
        pl.semaphore_signal(barrier, inc=1, device_id={"group": me + 1}, device_id_type=MESH)

    peers = jnp.where(me > 0, 1, 0) + jnp.where(me < count - 1, 1, 0)
    pl.semaphore_wait(barrier, peers)


class LineGather:
    def __init__(self, me, count, buffer, sems):
        self.me, self.count, self.buffer, self.sems = me, count, buffer, sems

    def copy(self, side, step):
        shift = 1 if side == 0 else -1
        block = self.me - step if side == 0 else self.me + step
        return pltpu.make_async_remote_copy(
            src_ref=self.buffer.at[block],
            dst_ref=self.buffer.at[block],
            send_sem=self.sems.at[side, 0, step],
            recv_sem=self.sems.at[side, 1, step],
            device_id={"group": self.me + shift},
            device_id_type=MESH,
        )

    def sends(self, side, step):
        if side == 0:
            return (self.me - step >= 0) & (self.me + 1 < self.count)
        return (self.me + step < self.count) & (self.me >= 1)

    def arrives(self, side, step):
        if side == 0:
            return self.me - 1 - step >= 0
        return self.me + 1 + step < self.count

    def arrived_block(self, side, step):
        return self.me - 1 - step if side == 0 else self.me + 1 + step

    def start(self, step):
        for side in range(2):
            @pl.when(self.sends(side, step))
            def _():
                self.copy(side, step).start()

    def wait_arrival(self, side, step):
        @pl.when(self.arrives(side, step))
        def _():
            block = self.arrived_block(side, step)
            pltpu.make_async_remote_copy(
                src_ref=self.buffer.at[block],
                dst_ref=self.buffer.at[block],
                send_sem=self.sems.at[side, 0, step],
                recv_sem=self.sems.at[side, 1, step],
                device_id={"group": self.me},
                device_id_type=MESH,
            ).wait_recv()

    def wait_sends(self):
        for step in range(self.count - 1):
            for side in range(2):
                @pl.when(self.sends(side, step))
                def _():
                    self.copy(side, step).wait_send()


class LineScatter:
    def __init__(self, me, count, parts, inbox, sems):
        self.me, self.count, self.parts, self.inbox, self.sems = me, count, parts, inbox, sems

    def target(self, side, step):
        return step if side == 0 else self.count - 1 - step

    def passes(self, side, step):
        if side == 0:
            return step < self.me
        return self.count - 1 - step > self.me

    def receives(self, side, step):
        if side == 0:
            return (step <= self.me) & (self.me + 1 < self.count)
        return (self.count - 1 - step >= self.me) & (self.me >= 1)

    def copy(self, side, step):
        shift = -1 if side == 0 else 1
        return pltpu.make_async_remote_copy(
            src_ref=self.parts.at[self.target(side, step)],
            dst_ref=self.inbox.at[side, step],
            send_sem=self.sems.at[side, 0, step],
            recv_sem=self.sems.at[side, 1, step],
            device_id={"group": self.me + shift},
            device_id_type=MESH,
        )

    def forward(self, side, step):
        @pl.when(self.passes(side, step))
        def _():
            @pl.when(self.receives(side, step))
            def _():
                self.copy(side, step).wait_recv()
                target = self.target(side, step)
                self.parts[target] = (
                    self.parts[target].astype(jnp.float32)
                    + self.inbox[side, step].astype(jnp.float32)
                ).astype(jnp.bfloat16)

            self.copy(side, step).start()

    def finish(self, total_ref):
        for side in range(2):
            has = self.me + 1 < self.count if side == 0 else self.me >= 1

            @pl.when(has)
            def _():
                step = self.me if side == 0 else self.count - 1 - self.me
                self.copy(side, step).wait_recv()
                total_ref[...] += self.inbox[side, step].astype(jnp.float32)

    def wait_sends(self):
        for step in range(self.count - 1):
            for side in range(2):
                @pl.when(self.passes(side, step))
                def _():
                    self.copy(side, step).wait_send()


def head_masks():
    lane = lax.broadcasted_iota(jnp.int32, (1, lanes), 1)
    first = (lane < head_dim).astype(jnp.float32)
    return first.astype(jnp.bfloat16), (1.0 - first).astype(jnp.bfloat16)


def offset_bias(bias_ref, head, row_start, rows, total):
    width = bias_ref.shape[1]
    shift = lax.rem(row_start + (width - (total - 1)), width)
    vector = pltpu.roll(jnp.broadcast_to(bias_ref[pl.ds(head, 1), :], (8, width)), shift, 1)
    vector = jnp.broadcast_to(vector[0:1, :], (rows, width))
    return pltpu.roll(vector, 0, 1, stride=1, stride_axis=0)[:, :total]


def rms_rows(values):
    return lax.rsqrt(jnp.mean(values * values, axis=-1, keepdims=True) + epsilon)


def attention_forward_kernel(
    count,
    length_ref,
    x_hbm, cot_hbm, gains_hbm, wq_hbm, wk_hbm, wv_hbm, wo_hbm, ids_ref, table_ref,
    n1_out, q_out, k_out, v_out, att_out, lse_out, cot_out, middle_out, n2_out, gains_out, bias_out,
    x_all, gains_all, wq, wk, wv, wo, parts, inbox, n1_buf, q_buf, k_buf, v_buf, att_buf, lse_buf, total_buf, n2_buf,
    local_sems, x_sems, g_sems, c_sems, s_sems, out_sems,
):
    me = lax.axis_index("group")
    rows, width = x_hbm.shape
    total = rows * count
    columns = wq.shape[1]
    local_heads = columns // head_dim
    loads = [
        pltpu.make_async_copy(source, target, local_sems.at[index])
        for index, (source, target) in enumerate(
            [
                (x_hbm, x_all.at[me]),
                (gains_hbm, gains_all.at[me]),
                (wq_hbm, wq),
                (wk_hbm, wk),
                (wv_hbm, wv),
                (wo_hbm, wo),
                (cot_hbm, cot_out.at[me]),
            ]
        )
    ]
    for load in loads:
        load.start()
    line_barrier(me, count)
    x_line = LineGather(me, count, x_all, x_sems)
    g_line = LineGather(me, count, gains_all, g_sems)
    c_line = LineGather(me, count, cot_out, c_sems)
    loads[1].wait()
    g_line.start(0)
    loads[0].wait()
    x_line.start(0)

    bucket = lax.broadcasted_iota(jnp.int32, (table_ref.shape[1], ids_ref.shape[1]), 0)
    one_hot = (bucket == ids_ref[...]).astype(jnp.float32).astype(jnp.bfloat16)
    bias_out[...] = nn_dot(table_ref[...], one_hot)

    for step in range(count - 1):
        for side in range(2):
            g_line.wait_arrival(side, step)
        if step + 1 < count - 1:
            g_line.start(step + 1)
    for owner in range(count):
        gains_out[:, owner * (width // count) : (owner + 1) * (width // count)] = gains_all[owner]
    for load in loads[2:5]:
        load.wait()

    def project(block):
        values = x_all[block].astype(jnp.float32)
        normed = (values * rms_rows(values) * gains_out[0:1, :]).astype(jnp.bfloat16)
        n1_buf[block] = normed
        q_buf[block] = nn_dot(normed, wq[...]).astype(jnp.bfloat16)
        k_buf[block] = nn_dot(normed, wk[...]).astype(jnp.bfloat16)
        v_buf[block] = nn_dot(normed, wv[...]).astype(jnp.bfloat16)

    project(me)
    for step in range(count - 1):
        for side in range(2):
            x_line.wait_arrival(side, step)
        if step + 1 < count - 1:
            x_line.start(step + 1)

        @pl.loop(0, 2)
        def _(side):
            arrives = jnp.where(side == 0, me - 1 - step >= 0, me + 1 + step < count)

            @pl.when(arrives)
            def _():
                project(jnp.where(side == 0, me - 1 - step, me + 1 + step))

    loads[6].wait()
    c_line.start(0)
    loads[5].wait()
    mask_first, mask_second = head_masks()
    key_valid = lax.broadcasted_iota(jnp.int32, (1, total), 1) < length_ref[0]
    lane = lax.broadcasted_iota(jnp.int32, (1, lanes), 1)

    def attend(block):
        lse_buf[block] = jnp.zeros((rows, lanes), jnp.float32)

        @pl.loop(0, local_heads // 2)
        def _(pair):
            cols = pl.ds(pl.multiple_of(pair * lanes, lanes), lanes)
            query = q_buf[block, :, cols]
            key = k_buf[:, :, cols].reshape(total, lanes)
            value = v_buf[:, :, cols].reshape(total, lanes)
            outs = []
            for half, mask in enumerate((mask_first, mask_second)):
                head = pair * 2 + half
                scores = nt_dot(query * mask, key)
                scores = scores + offset_bias(bias_out, head, block * rows, rows, total)
                scores = jnp.where(key_valid, scores, negative)
                top = jnp.max(scores, axis=-1, keepdims=True)
                expd = jnp.exp(scores - top)
                summed = jnp.sum(expd, axis=-1, keepdims=True)
                probs = (expd * (1.0 / summed)).astype(jnp.bfloat16)
                outs.append(nn_dot(probs, value))
                lse_buf[block] = jnp.where(lane == head, top + jnp.log(summed), lse_buf[block])
            att_buf[block, :, cols] = jnp.where(lane < head_dim, outs[0], outs[1]).astype(
                jnp.bfloat16
            )

    def attend_and_project(block):
        attend(block)
        parts[block] = nn_dot(att_buf[block], wo[...]).astype(jnp.bfloat16)

    scatter = LineScatter(me, count, parts, inbox, s_sems)
    for step in range(count - 1):
        @pl.loop(0, 2)
        def _(side):
            passes = jnp.where(side == 0, step < me, count - 1 - step > me)

            @pl.when(passes)
            def _():
                attend_and_project(jnp.where(side == 0, step, count - 1 - step))

        for side in range(2):
            scatter.forward(side, step)
        if step < count - 2:
            for side in range(2):
                c_line.wait_arrival(side, step)
            c_line.start(step + 1)
    attend(me)
    outs = [
        pltpu.make_async_copy(source, target, out_sems.at[index])
        for index, (source, target) in enumerate(
            [(n1_buf, n1_out), (q_buf, q_out), (k_buf, k_out), (v_buf, v_out), (att_buf, att_out), (lse_buf, lse_out)]
        )
    ]
    for copy in outs:
        copy.start()
    total_buf[...] = x_all[me].astype(jnp.float32) + nn_dot(att_buf[me], wo[...])
    scatter.finish(total_buf)
    middle = total_buf[...]
    n2_buf[...] = (middle * rms_rows(middle) * gains_out[1:2, :]).astype(jnp.bfloat16)
    tail = [
        pltpu.make_async_copy(total_buf, middle_out, out_sems.at[len(outs)]),
        pltpu.make_async_copy(n2_buf, n2_out, out_sems.at[len(outs) + 1]),
    ]
    for copy in tail:
        copy.start()
    for side in range(2):
        c_line.wait_arrival(side, count - 2)
    for line in (g_line, x_line, c_line, scatter):
        line.wait_sends()
    for copy in outs + tail:
        copy.wait()


def attention_forward(count, length, x, cot, gains, wq, wk, wv, wo, ids, table):
    rows, width = x.shape
    columns = wq.shape[1]
    local_heads = columns // head_dim
    bf, f32 = jnp.bfloat16, jnp.float32
    shape = jax.ShapeDtypeStruct
    steps = count - 1
    dma = pltpu.SemaphoreType.DMA
    return pl.pallas_call(
        functools.partial(attention_forward_kernel, count),
        name="attention_forward",
        out_shape=(
            shape((count, rows, width), bf),
            shape((count, rows, columns), bf),
            shape((count, rows, columns), bf),
            shape((count, rows, columns), bf),
            shape((count, rows, columns), bf),
            shape((count, rows, lanes), f32),
            shape((count, rows, width), bf),
            shape((rows, width), f32),
            shape((rows, width), bf),
            shape((8, width), f32),
            shape((local_heads, ids.shape[1]), f32),
        ),
        in_specs=[smem_space] + [any_space] * 7 + [vmem_space] * 2,
        out_specs=[any_space] * 9 + [vmem_space] * 2,
        scratch_shapes=[
            pltpu.VMEM((count, rows, width), bf),
            pltpu.VMEM((count,) + gains.shape, f32),
            pltpu.VMEM(wq.shape, bf),
            pltpu.VMEM(wk.shape, bf),
            pltpu.VMEM(wv.shape, bf),
            pltpu.VMEM(wo.shape, bf),
            pltpu.VMEM((count, rows, width), bf),
            pltpu.VMEM((2, steps, rows, width), bf),
            pltpu.VMEM((count, rows, width), bf),
            pltpu.VMEM((count, rows, columns), bf),
            pltpu.VMEM((count, rows, columns), bf),
            pltpu.VMEM((count, rows, columns), bf),
            pltpu.VMEM((count, rows, columns), bf),
            pltpu.VMEM((count, rows, lanes), f32),
            pltpu.VMEM((rows, width), f32),
            pltpu.VMEM((rows, width), bf),
            dma((7,)),
            dma((2, 2, steps)),
            dma((2, 2, steps)),
            dma((2, 2, steps)),
            dma((2, 2, steps)),
            dma((8,)),
        ],
        compiler_params=pltpu.CompilerParams(
            collective_id=0, has_side_effects=True, vmem_limit_bytes=56 * 2**20
        ),
    )(length, x, cot, gains, wq, wk, wv, wo, ids, table)


highest = lax.Precision.HIGHEST


def rms_scale(values, gain):
    return values * lax.rsqrt(jnp.mean(values * values, axis=-1, keepdims=True) + epsilon) * gain


def gated_gelu(gate_pre, up_pre):
    return jax.nn.gelu(gate_pre, approximate=True) * up_pre


def rows_dot(left, right):
    return lax.dot_general(
        left, right, (((0,), (0,)), ((), ())), preferred_element_type=jnp.float32
    )


def cols_dot(left, right):
    return lax.dot_general(
        left, right, (((1,), (1,)), ((), ())), preferred_element_type=jnp.float32
    )


def plain_dot(left, right):
    return jnp.dot(left, right, preferred_element_type=jnp.float32)


def spread_offsets(vector, row_count, col_count):
    span_width = row_count + col_count + 1
    block_heads = vector.shape[0]
    tiled_rows = jnp.broadcast_to(vector[:, None, :], (block_heads, row_count, span_width))
    flattened = tiled_rows.reshape(block_heads, row_count * span_width)[
        :, : row_count * (span_width - 1)
    ]
    return flattened.reshape(block_heads, row_count, span_width - 1)[:, :, row_count:]


def fold_offsets(matrix):
    block_heads, row_count, col_count = matrix.shape
    padded = jnp.pad(matrix, ((0, 0), (0, 0), (row_count, 0)))
    flattened = jnp.pad(
        padded.reshape(block_heads, row_count * (row_count + col_count)), ((0, 0), (0, row_count))
    )
    sums_all = flattened.reshape(block_heads, row_count, row_count + col_count + 1).sum(axis=1)
    return sums_all[:, 1 : row_count + col_count]


def heads(matrix):
    return matrix.reshape(matrix.shape[0], -1, head_dim)


def local(
    inputs,
    seq_lengths,
    bucket_ids,
    norm1_gain,
    w_query,
    w_key,
    w_value,
    w_attn_out,
    bias_table,
    norm2_gain,
    w_gate,
    w_up,
    w_ffn_out,
    cotangent,
):
    group = lax.axis_index("group")
    rows = inputs.shape[1]
    length = seq_lengths[0]
    total = rows * lax.axis_size("group")
    start = group * rows
    valid = jnp.arange(total) < length

    def gather(values):
        return lax.all_gather(values, "group", axis=0, tiled=True)

    def scatter(values):
        return lax.psum_scatter(
            values.astype(jnp.bfloat16), "group", scatter_dimension=0, tiled=True
        ).astype(jnp.float32)

    count = lax.axis_size("group")
    gains_local = jnp.pad(
        jnp.stack([norm1_gain, norm2_gain]).astype(jnp.float32), ((0, 6), (0, 0))
    )
    ids = jnp.pad(bucket_ids, (0, 1))[None, :]
    (
        normed_one, query, key, value, attended, log_totals, g_all, middle, normed_two, gains, bias_rows,
    ) = attention_forward(
        count, seq_lengths, inputs[0], cotangent[0], gains_local,
        w_query, w_key, w_value, w_attn_out, ids, bias_table.T,
    )
    normed_one, query, key, value, attended, g_all = (
        array.reshape(total, -1) for array in (normed_one, query, key, value, attended, g_all)
    )
    g_all = jnp.where(valid[:, None], g_all, jnp.bfloat16(0))
    gain_first, gain_second = gains[0], gains[1]
    x_local = inputs[0].astype(jnp.float32)
    buckets = bias_table.shape[0]
    one_hot = (bucket_ids[:, None] == jnp.arange(buckets)[None, :]).astype(jnp.float32)
    bias = spread_offsets(jnp.pad(bias_rows[:, :-1], ((0, 0), (1, 1))), total, total)
    scores = jnp.einsum(
        "qhd,khd->hqk", heads(query), heads(key), preferred_element_type=jnp.float32
    )
    scores = jnp.where(valid[None, None, :], scores + bias, negative)
    log_rows = log_totals.reshape(total, -1)[:, : bias.shape[0]].T
    probs = jnp.exp(scores - log_rows[:, :, None])
    probs_low = probs.astype(jnp.bfloat16)
    normed_two = gather(normed_two)

    gate_pre = plain_dot(normed_two, w_gate)
    up_pre = plain_dot(normed_two, w_up)
    hidden_low = gated_gelu(gate_pre, up_pre).astype(jnp.bfloat16)
    grad_hidden = cols_dot(g_all, w_ffn_out)
    _, pull_gelu = jax.vjp(gated_gelu, gate_pre, up_pre)
    grad_gate, grad_up = pull_gelu(grad_hidden)
    grad_gate = grad_gate.astype(jnp.bfloat16)
    grad_up = grad_up.astype(jnp.bfloat16)
    grad_normed_two = scatter(cols_dot(grad_gate, w_gate) + cols_dot(grad_up, w_up))
    ffn_out_grad = rows_dot(hidden_low, g_all)
    gate_grad = rows_dot(normed_two, grad_gate)
    up_grad = rows_dot(normed_two, grad_up)

    def total_sum(values):
        return lax.psum(values.astype(jnp.bfloat16), "replica").astype(jnp.float32)

    ffn_out_grad, gate_grad, up_grad = (
        total_sum(ffn_out_grad), total_sum(gate_grad), total_sum(up_grad)
    )
    result = (middle + scatter(plain_dot(hidden_low, w_ffn_out))).astype(jnp.bfloat16)

    row_valid = start + jnp.arange(rows) < length
    g_local = jnp.where(row_valid[:, None], cotangent[0], jnp.bfloat16(0)).astype(jnp.float32)
    _, pull_two = jax.vjp(rms_scale, middle, gain_second)
    grad_mid_norm, gain_two_grad = pull_two(grad_normed_two)
    grad_middle = g_local + grad_mid_norm
    grad_branch = gather(grad_middle.astype(jnp.bfloat16))

    attn_out_grad = rows_dot(attended, grad_branch)
    grad_attended = cols_dot(grad_branch, w_attn_out).astype(jnp.bfloat16)
    grad_probs = jnp.einsum(
        "qhd,khd->hqk", heads(grad_attended), heads(value), preferred_element_type=jnp.float32
    )
    inner_sum = jnp.sum(probs * grad_probs, axis=-1, keepdims=True)
    grad_scores = (probs * (grad_probs - inner_sum)).astype(jnp.bfloat16)

    def merge(values):
        return values.reshape(total, -1).astype(jnp.bfloat16)

    grad_query = merge(
        jnp.einsum("hqk,khd->qhd", grad_scores, heads(key), preferred_element_type=jnp.float32)
    )
    grad_key = merge(
        jnp.einsum("hqk,qhd->khd", grad_scores, heads(query), preferred_element_type=jnp.float32)
    )
    grad_value = merge(
        jnp.einsum(
            "hqk,qhd->khd", probs_low, heads(grad_attended), preferred_element_type=jnp.float32
        )
    )
    offset_sums = fold_offsets(grad_scores.astype(jnp.float32))
    table_grad = jnp.dot(offset_sums, one_hot, precision=highest).T
    query_grad = rows_dot(normed_one, grad_query)
    key_grad = rows_dot(normed_one, grad_key)
    value_grad = rows_dot(normed_one, grad_value)
    grad_normed_one = scatter(
        cols_dot(grad_query, w_query) + cols_dot(grad_key, w_key) + cols_dot(grad_value, w_value)
    )
    query_grad, key_grad, value_grad, attn_out_grad = (
        total_sum(query_grad), total_sum(key_grad), total_sum(value_grad), total_sum(attn_out_grad)
    )
    table_grad = lax.psum(table_grad, "replica")
    _, pull_one = jax.vjp(rms_scale, x_local, gain_first)
    grad_in_norm, gain_one_grad = pull_one(grad_normed_one)
    input_grad = (grad_middle + grad_in_norm).astype(jnp.bfloat16)
    gain_sums = lax.psum(jnp.stack([gain_one_grad, gain_two_grad]), ("replica", "group"))
    width = norm1_gain.shape[0]
    gain_sums = lax.dynamic_slice_in_dim(gain_sums, group * width, width, axis=1)
    return (
        result[None],
        input_grad[None],
        gain_sums[0],
        query_grad,
        key_grad,
        value_grad,
        attn_out_grad,
        table_grad,
        gain_sums[1],
        gate_grad,
        up_grad,
        ffn_out_grad,
    )


def solution(mesh):
    placed = (
        P("replica", "group", None),
        P("replica"),
        P(),
        P("group"),
        P(None, "group"),
        P(None, "group"),
        P(None, "group"),
        P("group", None),
        P(None, "group"),
        P("group"),
        P(None, "group"),
        P(None, "group"),
        P("group", None),
        P("replica", "group", None),
    )
    return jax.shard_map(
        local,
        mesh=mesh,
        in_specs=placed,
        out_specs=(
            P("replica", "group", None),
            P("replica", "group", None),
            P("group"),
            P(None, "group"),
            P(None, "group"),
            P(None, "group"),
            P("group", None),
            P(None, "group"),
            P("group"),
            P(None, "group"),
            P(None, "group"),
            P("group", None),
        ),
        check_vma=False,
    )
```

```python
import functools
import jax
import jax.numpy as jnp
from jax import lax
from jax.experimental import pallas as pl
from jax.experimental.pallas import tpu as pltpu
from jax.sharding import PartitionSpec as P

epsilon = 1e-06
negative = -1000000000.0
head_dim = 64
lanes = 128
MESH = pl.DeviceIdType.MESH
any_space = pl.BlockSpec(memory_space=pl.ANY)
vmem_space = pl.BlockSpec(memory_space=pltpu.VMEM)
smem_space = pl.BlockSpec(memory_space=pltpu.SMEM)


def nn_dot(left, right):
    return jnp.dot(left, right, preferred_element_type=jnp.float32)


def nt_dot(left, right):
    return lax.dot_general(
        left, right, (((1,), (1,)), ((), ())), preferred_element_type=jnp.float32
    )


def line_barrier(me, count):
    barrier = pltpu.get_barrier_semaphore()

    @pl.when(me > 0)
    def _():
        pl.semaphore_signal(barrier, inc=1, device_id={"group": me - 1}, device_id_type=MESH)

    @pl.when(me < count - 1)
    def _():
        pl.semaphore_signal(barrier, inc=1, device_id={"group": me + 1}, device_id_type=MESH)

    peers = jnp.where(me > 0, 1, 0) + jnp.where(me < count - 1, 1, 0)
    pl.semaphore_wait(barrier, peers)


class LineGather:
    def __init__(self, me, count, buffer, sems):
        self.me, self.count, self.buffer, self.sems = me, count, buffer, sems

    def copy(self, side, step):
        shift = 1 if side == 0 else -1
        block = self.me - step if side == 0 else self.me + step
        return pltpu.make_async_remote_copy(
            src_ref=self.buffer.at[block],
            dst_ref=self.buffer.at[block],
            send_sem=self.sems.at[side, 0, step],
            recv_sem=self.sems.at[side, 1, step],
            device_id={"group": self.me + shift},
            device_id_type=MESH,
        )

    def sends(self, side, step):
        if side == 0:
            return (self.me - step >= 0) & (self.me + 1 < self.count)
        return (self.me + step < self.count) & (self.me >= 1)

    def arrives(self, side, step):
        if side == 0:
            return self.me - 1 - step >= 0
        return self.me + 1 + step < self.count

    def arrived_block(self, side, step):
        return self.me - 1 - step if side == 0 else self.me + 1 + step

    def start(self, step):
        for side in range(2):
            @pl.when(self.sends(side, step))
            def _():
                self.copy(side, step).start()

    def wait_arrival(self, side, step):
        @pl.when(self.arrives(side, step))
        def _():
            block = self.arrived_block(side, step)
            pltpu.make_async_remote_copy(
                src_ref=self.buffer.at[block],
                dst_ref=self.buffer.at[block],
                send_sem=self.sems.at[side, 0, step],
                recv_sem=self.sems.at[side, 1, step],
                device_id={"group": self.me},
                device_id_type=MESH,
            ).wait_recv()

    def wait_sends(self):
        for step in range(self.count - 1):
            for side in range(2):
                @pl.when(self.sends(side, step))
                def _():
                    self.copy(side, step).wait_send()


class LineScatter:
    def __init__(self, me, count, parts, inbox, sems):
        self.me, self.count, self.parts, self.inbox, self.sems = me, count, parts, inbox, sems

    def target(self, side, step):
        return step if side == 0 else self.count - 1 - step

    def passes(self, side, step):
        if side == 0:
            return step < self.me
        return self.count - 1 - step > self.me

    def receives(self, side, step):
        if side == 0:
            return (step <= self.me) & (self.me + 1 < self.count)
        return (self.count - 1 - step >= self.me) & (self.me >= 1)

    def copy(self, side, step):
        shift = -1 if side == 0 else 1
        return pltpu.make_async_remote_copy(
            src_ref=self.parts.at[self.target(side, step)],
            dst_ref=self.inbox.at[side, step],
            send_sem=self.sems.at[side, 0, step],
            recv_sem=self.sems.at[side, 1, step],
            device_id={"group": self.me + shift},
            device_id_type=MESH,
        )

    def forward(self, side, step):
        @pl.when(self.passes(side, step))
        def _():
            @pl.when(self.receives(side, step))
            def _():
                self.copy(side, step).wait_recv()
                target = self.target(side, step)
                self.parts[target] = (
                    self.parts[target].astype(jnp.float32)
                    + self.inbox[side, step].astype(jnp.float32)
                ).astype(jnp.bfloat16)

            self.copy(side, step).start()

    def finish(self, total_ref):
        for side in range(2):
            has = self.me + 1 < self.count if side == 0 else self.me >= 1

            @pl.when(has)
            def _():
                step = self.me if side == 0 else self.count - 1 - self.me
                self.copy(side, step).wait_recv()
                total_ref[...] += self.inbox[side, step].astype(jnp.float32)

    def wait_sends(self):
        for step in range(self.count - 1):
            for side in range(2):
                @pl.when(self.passes(side, step))
                def _():
                    self.copy(side, step).wait_send()


def head_masks():
    lane = lax.broadcasted_iota(jnp.int32, (1, lanes), 1)
    first = (lane < head_dim).astype(jnp.float32)
    return first.astype(jnp.bfloat16), (1.0 - first).astype(jnp.bfloat16)


def offset_bias(bias_ref, head, row_start, rows, total):
    width = bias_ref.shape[1]
    shift = lax.rem(row_start + (width - (total - 1)), width)
    vector = pltpu.roll(jnp.broadcast_to(bias_ref[pl.ds(head, 1), :], (8, width)), shift, 1)
    vector = jnp.broadcast_to(vector[0:1, :], (rows, width))
    return pltpu.roll(vector, 0, 1, stride=1, stride_axis=0)[:, :total]


def rms_rows(values):
    return lax.rsqrt(jnp.mean(values * values, axis=-1, keepdims=True) + epsilon)


def attention_forward_kernel(
    count,
    length_ref,
    x_hbm, cot_hbm, gains_hbm, wq_hbm, wk_hbm, wv_hbm, wo_hbm, ids_ref, table_ref,
    n1_out, q_out, k_out, v_out, att_out, lse_out, cot_out, middle_out, n2_out, gains_out, bias_out,
    x_all, gains_all, wq, wk, wv, wo, parts, inbox, n1_buf, q_buf, k_buf, v_buf, att_buf, lse_buf, total_buf, n2_buf,
    local_sems, x_sems, g_sems, c_sems, s_sems, out_sems,
):
    me = lax.axis_index("group")
    rows, width = x_hbm.shape
    total = rows * count
    columns = wq.shape[1]
    local_heads = columns // head_dim
    loads = [
        pltpu.make_async_copy(source, target, local_sems.at[index])
        for index, (source, target) in enumerate(
            [
                (x_hbm, x_all.at[me]),
                (gains_hbm, gains_all.at[me]),
                (wq_hbm, wq),
                (wk_hbm, wk),
                (wv_hbm, wv),
                (wo_hbm, wo),
                (cot_hbm, cot_out.at[me]),
            ]
        )
    ]
    for load in loads:
        load.start()
    line_barrier(me, count)
    x_line = LineGather(me, count, x_all, x_sems)
    g_line = LineGather(me, count, gains_all, g_sems)
    c_line = LineGather(me, count, cot_out, c_sems)
    loads[1].wait()
    g_line.start(0)
    loads[0].wait()
    x_line.start(0)

    bucket = lax.broadcasted_iota(jnp.int32, (table_ref.shape[1], ids_ref.shape[1]), 0)
    one_hot = (bucket == ids_ref[...]).astype(jnp.float32).astype(jnp.bfloat16)
    bias_out[...] = nn_dot(table_ref[...], one_hot)

    for step in range(count - 1):
        for side in range(2):
            g_line.wait_arrival(side, step)
        if step + 1 < count - 1:
            g_line.start(step + 1)
    for owner in range(count):
        gains_out[:, owner * (width // count) : (owner + 1) * (width // count)] = gains_all[owner]
    for load in loads[2:5]:
        load.wait()

    def project(block):
        values = x_all[block].astype(jnp.float32)
        normed = (values * rms_rows(values) * gains_out[0:1, :]).astype(jnp.bfloat16)
        n1_buf[block] = normed
        q_buf[block] = nn_dot(normed, wq[...]).astype(jnp.bfloat16)
        k_buf[block] = nn_dot(normed, wk[...]).astype(jnp.bfloat16)
        v_buf[block] = nn_dot(normed, wv[...]).astype(jnp.bfloat16)

    project(me)
    for step in range(count - 1):
        for side in range(2):
            x_line.wait_arrival(side, step)
        if step + 1 < count - 1:
            x_line.start(step + 1)

        @pl.loop(0, 2)
        def _(side):
            arrives = jnp.where(side == 0, me - 1 - step >= 0, me + 1 + step < count)

            @pl.when(arrives)
            def _():
                project(jnp.where(side == 0, me - 1 - step, me + 1 + step))

    loads[6].wait()
    c_line.start(0)
    loads[5].wait()
    mask_first, mask_second = head_masks()
    key_valid = lax.broadcasted_iota(jnp.int32, (1, total), 1) < length_ref[0]
    lane = lax.broadcasted_iota(jnp.int32, (1, lanes), 1)

    def attend(block):
        lse_buf[block] = jnp.zeros((rows, lanes), jnp.float32)

        @pl.loop(0, local_heads // 2)
        def _(pair):
            cols = pl.ds(pl.multiple_of(pair * lanes, lanes), lanes)
            query = q_buf[block, :, cols]
            key = k_buf[:, :, cols].reshape(total, lanes)
            value = v_buf[:, :, cols].reshape(total, lanes)
            outs = []
            for half, mask in enumerate((mask_first, mask_second)):
                head = pair * 2 + half
                scores = nt_dot(query * mask, key)
                scores = scores + offset_bias(bias_out, head, block * rows, rows, total)
                scores = jnp.where(key_valid, scores, negative)
                top = jnp.max(scores, axis=-1, keepdims=True)
                expd = jnp.exp(scores - top)
                summed = jnp.sum(expd, axis=-1, keepdims=True)
                probs = (expd * (1.0 / summed)).astype(jnp.bfloat16)
                outs.append(nn_dot(probs, value))
                lse_buf[block] = jnp.where(lane == head, top + jnp.log(summed), lse_buf[block])
            att_buf[block, :, cols] = jnp.where(lane < head_dim, outs[0], outs[1]).astype(
                jnp.bfloat16
            )

    def attend_and_project(block):
        attend(block)
        parts[block] = nn_dot(att_buf[block], wo[...]).astype(jnp.bfloat16)

    scatter = LineScatter(me, count, parts, inbox, s_sems)
    for step in range(count - 1):
        @pl.loop(0, 2)
        def _(side):
            passes = jnp.where(side == 0, step < me, count - 1 - step > me)

            @pl.when(passes)
            def _():
                attend_and_project(jnp.where(side == 0, step, count - 1 - step))

        for side in range(2):
            scatter.forward(side, step)
        if step < count - 2:
            for side in range(2):
                c_line.wait_arrival(side, step)
            c_line.start(step + 1)
    attend(me)
    outs = [
        pltpu.make_async_copy(source, target, out_sems.at[index])
        for index, (source, target) in enumerate(
            [(n1_buf, n1_out), (q_buf, q_out), (k_buf, k_out), (v_buf, v_out), (att_buf, att_out), (lse_buf, lse_out)]
        )
    ]
    for copy in outs:
        copy.start()
    total_buf[...] = x_all[me].astype(jnp.float32) + nn_dot(att_buf[me], wo[...])
    scatter.finish(total_buf)
    middle = total_buf[...]
    n2_buf[...] = (middle * rms_rows(middle) * gains_out[1:2, :]).astype(jnp.bfloat16)
    tail = [
        pltpu.make_async_copy(total_buf, middle_out, out_sems.at[len(outs)]),
        pltpu.make_async_copy(n2_buf, n2_out, out_sems.at[len(outs) + 1]),
    ]
    for copy in tail:
        copy.start()
    for side in range(2):
        c_line.wait_arrival(side, count - 2)
    for line in (g_line, x_line, c_line, scatter):
        line.wait_sends()
    for copy in outs + tail:
        copy.wait()


def attention_forward(count, length, x, cot, gains, wq, wk, wv, wo, ids, table):
    rows, width = x.shape
    columns = wq.shape[1]
    local_heads = columns // head_dim
    bf, f32 = jnp.bfloat16, jnp.float32
    shape = jax.ShapeDtypeStruct
    steps = count - 1
    dma = pltpu.SemaphoreType.DMA
    return pl.pallas_call(
        functools.partial(attention_forward_kernel, count),
        name="attention_forward",
        out_shape=(
            shape((count, rows, width), bf),
            shape((count, rows, columns), bf),
            shape((count, rows, columns), bf),
            shape((count, rows, columns), bf),
            shape((count, rows, columns), bf),
            shape((count, rows, lanes), f32),
            shape((count, rows, width), bf),
            shape((rows, width), f32),
            shape((rows, width), bf),
            shape((8, width), f32),
            shape((local_heads, ids.shape[1]), f32),
        ),
        in_specs=[smem_space] + [any_space] * 7 + [vmem_space] * 2,
        out_specs=[any_space] * 9 + [vmem_space] * 2,
        scratch_shapes=[
            pltpu.VMEM((count, rows, width), bf),
            pltpu.VMEM((count,) + gains.shape, f32),
            pltpu.VMEM(wq.shape, bf),
            pltpu.VMEM(wk.shape, bf),
            pltpu.VMEM(wv.shape, bf),
            pltpu.VMEM(wo.shape, bf),
            pltpu.VMEM((count, rows, width), bf),
            pltpu.VMEM((2, steps, rows, width), bf),
            pltpu.VMEM((count, rows, width), bf),
            pltpu.VMEM((count, rows, columns), bf),
            pltpu.VMEM((count, rows, columns), bf),
            pltpu.VMEM((count, rows, columns), bf),
            pltpu.VMEM((count, rows, columns), bf),
            pltpu.VMEM((count, rows, lanes), f32),
            pltpu.VMEM((rows, width), f32),
            pltpu.VMEM((rows, width), bf),
            dma((7,)),
            dma((2, 2, steps)),
            dma((2, 2, steps)),
            dma((2, 2, steps)),
            dma((2, 2, steps)),
            dma((8,)),
        ],
        compiler_params=pltpu.CompilerParams(
            collective_id=0, has_side_effects=True, vmem_limit_bytes=56 * 2**20
        ),
    )(length, x, cot, gains, wq, wk, wv, wo, ids, table)


def gelu_parts(gate):
    root = 0.7978845608028654
    inner = root * (gate + 0.044715 * gate * gate * gate)
    tanh = jnp.tanh(inner)
    half = 0.5 * (1.0 + tanh)
    slope = half + 0.5 * gate * (1.0 - tanh * tanh) * root * (1.0 + 3 * 0.044715 * gate * gate)
    return gate * half, slope


def feed_forward_kernel(
    count, tile,
    length_ref,
    n2_hbm, cot_hbm, wg_hbm, wu_hbm, wf_hbm,
    gate_out, up_out, ffn_out, back_out, res_out,
    n2_all, g_all, wg, wu, wf, hid, grad_gate, grad_up, back_buf, res_buf, turned, stage,
    local_sems, n_sems, out_sems, stage_sems,
):
    me = lax.axis_index("group")
    rows, width = n2_hbm.shape
    total = rows * count
    units = wg.shape[1]
    loads = [
        pltpu.make_async_copy(source, target, local_sems.at[index])
        for index, (source, target) in enumerate(
            [(n2_hbm, n2_all.at[me]), (wg_hbm, wg), (wu_hbm, wu), (wf_hbm, wf), (cot_hbm, g_all)]
        )
    ]
    for load in loads:
        load.start()
    line_barrier(me, count)
    line = LineGather(me, count, n2_all, n_sems)
    loads[0].wait()
    line.start(0)
    for load in loads[1:]:
        load.wait()

    def mask_rows(block):
        position = block * rows + lax.broadcasted_iota(jnp.int32, (rows, 1), 0)
        valid = (position < length_ref[0]).astype(jnp.float32).astype(jnp.bfloat16)
        g_all[block] = g_all[block] * valid

    def block_pass(block):
        mask_rows(block)
        normed = n2_all[block]
        grads = g_all[block]

        @pl.loop(0, units // tile)
        def _(index):
            cols = pl.ds(pl.multiple_of(index * tile, tile), tile)
            gate = nn_dot(normed, wg[:, cols])
            up = nn_dot(normed, wu[:, cols])
            grad_hidden = nt_dot(grads, wf[cols, :])
            act, slope = gelu_parts(gate)
            hid[block, :, cols] = (act * up).astype(jnp.bfloat16)
            grad_gate[block, :, cols] = (grad_hidden * up * slope).astype(jnp.bfloat16)
            grad_up[block, :, cols] = (grad_hidden * act).astype(jnp.bfloat16)

        chunk = 2 * tile

        @pl.loop(0, width // chunk)
        def _(index):
            cols = pl.ds(pl.multiple_of(index * chunk, chunk), chunk)
            back_buf[block, :, cols] = (
                nt_dot(grad_gate[block], wg[cols, :]) + nt_dot(grad_up[block], wu[cols, :])
            ).astype(jnp.bfloat16)
            res_buf[block, :, cols] = nn_dot(hid[block], wf[:, cols]).astype(jnp.bfloat16)

    block_pass(me)
    for step in range(count - 1):
        for side in range(2):
            line.wait_arrival(side, step)
        if step + 1 < count - 1:
            line.start(step + 1)

        @pl.loop(0, 2)
        def _(side):
            arrives = jnp.where(side == 0, me - 1 - step >= 0, me + 1 + step < count)

            @pl.when(arrives)
            def _():
                block_pass(jnp.where(side == 0, me - 1 - step, me + 1 + step))

    outs = [
        pltpu.make_async_copy(back_buf, back_out, out_sems.at[0]),
        pltpu.make_async_copy(res_buf, res_out, out_sems.at[1]),
    ]
    for copy in outs:
        copy.start()

    def weight_grad(left, right, target, first):
        height = target.shape[0]
        depth = right.shape[2]
        factor = right[...].reshape(total, depth)

        @pl.loop(0, height // tile)
        def _(index):
            slot = lax.rem(index, 2)
            here = pl.ds(pl.multiple_of(index * tile, tile), tile)
            turned[...] = left[:, :, here].reshape(total, tile).T

            @pl.when(index >= 2)
            def _():
                pltpu.make_async_copy(
                    stage.at[slot, :, pl.ds(0, depth)], target.at[here], stage_sems.at[slot]
                ).wait()

            stage[slot, :, pl.ds(0, depth)] = nn_dot(turned[...], factor).astype(jnp.bfloat16)
            pltpu.make_async_copy(
                stage.at[slot, :, pl.ds(0, depth)], target.at[here], stage_sems.at[slot]
            ).start()

        for slot in range(2):
            pltpu.make_async_copy(
                stage.at[slot, :, pl.ds(0, depth)], target.at[pl.ds(0, tile)], stage_sems.at[slot]
            ).wait()

    weight_grad(hid, g_all, ffn_out, 0)
    weight_grad(n2_all, grad_gate, gate_out, 0)
    weight_grad(n2_all, grad_up, up_out, 0)
    line.wait_sends()
    for copy in outs:
        copy.wait()


def feed_forward(count, length, n2, cot, wg, wu, wf):
    rows, width = n2.shape
    units = wg.shape[1]
    tile = 128 if units % 256 else 256
    bf = jnp.bfloat16
    shape = jax.ShapeDtypeStruct
    steps = count - 1
    dma = pltpu.SemaphoreType.DMA
    return pl.pallas_call(
        functools.partial(feed_forward_kernel, count, tile),
        name="feed_forward",
        out_shape=(
            shape(wg.shape, bf),
            shape(wu.shape, bf),
            shape(wf.shape, bf),
            shape((count, rows, width), bf),
            shape((count, rows, width), bf),
        ),
        in_specs=[smem_space] + [any_space] * 5,
        out_specs=[any_space] * 5,
        scratch_shapes=[
            pltpu.VMEM((count, rows, width), bf),
            pltpu.VMEM((count, rows, width), bf),
            pltpu.VMEM(wg.shape, bf),
            pltpu.VMEM(wu.shape, bf),
            pltpu.VMEM(wf.shape, bf),
            pltpu.VMEM((count, rows, units), bf),
            pltpu.VMEM((count, rows, units), bf),
            pltpu.VMEM((count, rows, units), bf),
            pltpu.VMEM((count, rows, width), bf),
            pltpu.VMEM((count, rows, width), bf),
            pltpu.VMEM((tile, count * rows), bf),
            pltpu.VMEM((2, tile, max(width, units)), bf),
            dma((5,)),
            dma((2, 2, steps)),
            dma((2,)),
            dma((2,)),
        ],
        compiler_params=pltpu.CompilerParams(
            collective_id=1, has_side_effects=True, vmem_limit_bytes=56 * 2**20
        ),
    )(length, n2, cot, wg, wu, wf)


highest = lax.Precision.HIGHEST


def rms_scale(values, gain):
    return values * lax.rsqrt(jnp.mean(values * values, axis=-1, keepdims=True) + epsilon) * gain


def gated_gelu(gate_pre, up_pre):
    return jax.nn.gelu(gate_pre, approximate=True) * up_pre


def rows_dot(left, right):
    return lax.dot_general(
        left, right, (((0,), (0,)), ((), ())), preferred_element_type=jnp.float32
    )


def cols_dot(left, right):
    return lax.dot_general(
        left, right, (((1,), (1,)), ((), ())), preferred_element_type=jnp.float32
    )


def plain_dot(left, right):
    return jnp.dot(left, right, preferred_element_type=jnp.float32)


def spread_offsets(vector, row_count, col_count):
    span_width = row_count + col_count + 1
    block_heads = vector.shape[0]
    tiled_rows = jnp.broadcast_to(vector[:, None, :], (block_heads, row_count, span_width))
    flattened = tiled_rows.reshape(block_heads, row_count * span_width)[
        :, : row_count * (span_width - 1)
    ]
    return flattened.reshape(block_heads, row_count, span_width - 1)[:, :, row_count:]


def fold_offsets(matrix):
    block_heads, row_count, col_count = matrix.shape
    padded = jnp.pad(matrix, ((0, 0), (0, 0), (row_count, 0)))
    flattened = jnp.pad(
        padded.reshape(block_heads, row_count * (row_count + col_count)), ((0, 0), (0, row_count))
    )
    sums_all = flattened.reshape(block_heads, row_count, row_count + col_count + 1).sum(axis=1)
    return sums_all[:, 1 : row_count + col_count]


def heads(matrix):
    return matrix.reshape(matrix.shape[0], -1, head_dim)


def local(
    inputs,
    seq_lengths,
    bucket_ids,
    norm1_gain,
    w_query,
    w_key,
    w_value,
    w_attn_out,
    bias_table,
    norm2_gain,
    w_gate,
    w_up,
    w_ffn_out,
    cotangent,
):
    group = lax.axis_index("group")
    rows = inputs.shape[1]
    length = seq_lengths[0]
    total = rows * lax.axis_size("group")
    start = group * rows
    valid = jnp.arange(total) < length

    def gather(values):
        return lax.all_gather(values, "group", axis=0, tiled=True)

    def scatter(values):
        return lax.psum_scatter(
            values.astype(jnp.bfloat16), "group", scatter_dimension=0, tiled=True
        ).astype(jnp.float32)

    count = lax.axis_size("group")
    gains_local = jnp.pad(
        jnp.stack([norm1_gain, norm2_gain]).astype(jnp.float32), ((0, 6), (0, 0))
    )
    ids = jnp.pad(bucket_ids, (0, 1))[None, :]
    (
        normed_one, query, key, value, attended, log_totals, g_all, middle, normed_two, gains, bias_rows,
    ) = attention_forward(
        count, seq_lengths, inputs[0], cotangent[0], gains_local,
        w_query, w_key, w_value, w_attn_out, ids, bias_table.T,
    )
    gate_part, up_part, ffn_part, back_part, result_part = feed_forward(
        count, seq_lengths, normed_two, g_all, w_gate, w_up, w_ffn_out
    )

    def total_sum(values):
        return lax.psum(values.astype(jnp.bfloat16), "replica").astype(jnp.float32)

    ffn_out_grad, gate_grad, up_grad = total_sum(ffn_part), total_sum(gate_part), total_sum(up_part)
    grad_normed_two = scatter(back_part.reshape(total, -1))
    result = (middle + scatter(result_part.reshape(total, -1))).astype(jnp.bfloat16)
    normed_one, query, key, value, attended = (
        array.reshape(total, -1) for array in (normed_one, query, key, value, attended)
    )
    gain_first, gain_second = gains[0], gains[1]
    x_local = inputs[0].astype(jnp.float32)
    buckets = bias_table.shape[0]
    one_hot = (bucket_ids[:, None] == jnp.arange(buckets)[None, :]).astype(jnp.float32)
    bias = spread_offsets(jnp.pad(bias_rows[:, :-1], ((0, 0), (1, 1))), total, total)
    scores = jnp.einsum(
        "qhd,khd->hqk", heads(query), heads(key), preferred_element_type=jnp.float32
    )
    scores = jnp.where(valid[None, None, :], scores + bias, negative)
    log_rows = log_totals.reshape(total, -1)[:, : bias.shape[0]].T
    probs = jnp.exp(scores - log_rows[:, :, None])
    probs_low = probs.astype(jnp.bfloat16)

    row_valid = start + jnp.arange(rows) < length
    g_local = jnp.where(row_valid[:, None], cotangent[0], jnp.bfloat16(0)).astype(jnp.float32)
    _, pull_two = jax.vjp(rms_scale, middle, gain_second)
    grad_mid_norm, gain_two_grad = pull_two(grad_normed_two)
    grad_middle = g_local + grad_mid_norm
    grad_branch = gather(grad_middle.astype(jnp.bfloat16))

    attn_out_grad = rows_dot(attended, grad_branch)
    grad_attended = cols_dot(grad_branch, w_attn_out).astype(jnp.bfloat16)
    grad_probs = jnp.einsum(
        "qhd,khd->hqk", heads(grad_attended), heads(value), preferred_element_type=jnp.float32
    )
    inner_sum = jnp.sum(probs * grad_probs, axis=-1, keepdims=True)
    grad_scores = (probs * (grad_probs - inner_sum)).astype(jnp.bfloat16)

    def merge(values):
        return values.reshape(total, -1).astype(jnp.bfloat16)

    grad_query = merge(
        jnp.einsum("hqk,khd->qhd", grad_scores, heads(key), preferred_element_type=jnp.float32)
    )
    grad_key = merge(
        jnp.einsum("hqk,qhd->khd", grad_scores, heads(query), preferred_element_type=jnp.float32)
    )
    grad_value = merge(
        jnp.einsum(
            "hqk,qhd->khd", probs_low, heads(grad_attended), preferred_element_type=jnp.float32
        )
    )
    offset_sums = fold_offsets(grad_scores.astype(jnp.float32))
    table_grad = jnp.dot(offset_sums, one_hot, precision=highest).T
    query_grad = rows_dot(normed_one, grad_query)
    key_grad = rows_dot(normed_one, grad_key)
    value_grad = rows_dot(normed_one, grad_value)
    grad_normed_one = scatter(
        cols_dot(grad_query, w_query) + cols_dot(grad_key, w_key) + cols_dot(grad_value, w_value)
    )
    query_grad, key_grad, value_grad, attn_out_grad = (
        total_sum(query_grad), total_sum(key_grad), total_sum(value_grad), total_sum(attn_out_grad)
    )
    table_grad = lax.psum(table_grad, "replica")
    _, pull_one = jax.vjp(rms_scale, x_local, gain_first)
    grad_in_norm, gain_one_grad = pull_one(grad_normed_one)
    input_grad = (grad_middle + grad_in_norm).astype(jnp.bfloat16)
    gain_sums = lax.psum(jnp.stack([gain_one_grad, gain_two_grad]), ("replica", "group"))
    width = norm1_gain.shape[0]
    gain_sums = lax.dynamic_slice_in_dim(gain_sums, group * width, width, axis=1)
    return (
        result[None],
        input_grad[None],
        gain_sums[0],
        query_grad,
        key_grad,
        value_grad,
        attn_out_grad,
        table_grad,
        gain_sums[1],
        gate_grad,
        up_grad,
        ffn_out_grad,
    )


def solution(mesh):
    placed = (
        P("replica", "group", None),
        P("replica"),
        P(),
        P("group"),
        P(None, "group"),
        P(None, "group"),
        P(None, "group"),
        P("group", None),
        P(None, "group"),
        P("group"),
        P(None, "group"),
        P(None, "group"),
        P("group", None),
        P("replica", "group", None),
    )
    return jax.shard_map(
        local,
        mesh=mesh,
        in_specs=placed,
        out_specs=(
            P("replica", "group", None),
            P("replica", "group", None),
            P("group"),
            P(None, "group"),
            P(None, "group"),
            P(None, "group"),
            P("group", None),
            P(None, "group"),
            P("group"),
            P(None, "group"),
            P(None, "group"),
            P("group", None),
        ),
        check_vma=False,
    )
```

```python
import functools
import jax
import jax.numpy as jnp
from jax import lax
from jax.experimental import pallas as pl
from jax.experimental.pallas import tpu as pltpu
from jax.sharding import PartitionSpec as P

epsilon = 1e-06
negative = -1000000000.0
head_dim = 64
lanes = 128
MESH = pl.DeviceIdType.MESH
any_space = pl.BlockSpec(memory_space=pl.ANY)
vmem_space = pl.BlockSpec(memory_space=pltpu.VMEM)
smem_space = pl.BlockSpec(memory_space=pltpu.SMEM)


def nn_dot(left, right):
    return jnp.dot(left, right, preferred_element_type=jnp.float32)


def nt_dot(left, right):
    return lax.dot_general(
        left, right, (((1,), (1,)), ((), ())), preferred_element_type=jnp.float32
    )


def line_barrier(me, count):
    barrier = pltpu.get_barrier_semaphore()

    @pl.when(me > 0)
    def _():
        pl.semaphore_signal(barrier, inc=1, device_id={"group": me - 1}, device_id_type=MESH)

    @pl.when(me < count - 1)
    def _():
        pl.semaphore_signal(barrier, inc=1, device_id={"group": me + 1}, device_id_type=MESH)

    peers = jnp.where(me > 0, 1, 0) + jnp.where(me < count - 1, 1, 0)
    pl.semaphore_wait(barrier, peers)


class LineGather:
    def __init__(self, me, count, buffer, sems):
        self.me, self.count, self.buffer, self.sems = me, count, buffer, sems

    def copy(self, side, step):
        shift = 1 if side == 0 else -1
        block = self.me - step if side == 0 else self.me + step
        return pltpu.make_async_remote_copy(
            src_ref=self.buffer.at[block],
            dst_ref=self.buffer.at[block],
            send_sem=self.sems.at[side, 0, step],
            recv_sem=self.sems.at[side, 1, step],
            device_id={"group": self.me + shift},
            device_id_type=MESH,
        )

    def sends(self, side, step):
        if side == 0:
            return (self.me - step >= 0) & (self.me + 1 < self.count)
        return (self.me + step < self.count) & (self.me >= 1)

    def arrives(self, side, step):
        if side == 0:
            return self.me - 1 - step >= 0
        return self.me + 1 + step < self.count

    def arrived_block(self, side, step):
        return self.me - 1 - step if side == 0 else self.me + 1 + step

    def start(self, step):
        for side in range(2):
            @pl.when(self.sends(side, step))
            def _():
                self.copy(side, step).start()

    def wait_arrival(self, side, step):
        @pl.when(self.arrives(side, step))
        def _():
            block = self.arrived_block(side, step)
            pltpu.make_async_remote_copy(
                src_ref=self.buffer.at[block],
                dst_ref=self.buffer.at[block],
                send_sem=self.sems.at[side, 0, step],
                recv_sem=self.sems.at[side, 1, step],
                device_id={"group": self.me},
                device_id_type=MESH,
            ).wait_recv()

    def wait_sends(self):
        for step in range(self.count - 1):
            for side in range(2):
                @pl.when(self.sends(side, step))
                def _():
                    self.copy(side, step).wait_send()


class LineScatter:
    def __init__(self, me, count, parts, inbox, sems):
        self.me, self.count, self.parts, self.inbox, self.sems = me, count, parts, inbox, sems

    def target(self, side, step):
        return step if side == 0 else self.count - 1 - step

    def passes(self, side, step):
        if side == 0:
            return step < self.me
        return self.count - 1 - step > self.me

    def receives(self, side, step):
        if side == 0:
            return (step <= self.me) & (self.me + 1 < self.count)
        return (self.count - 1 - step >= self.me) & (self.me >= 1)

    def copy(self, side, step):
        shift = -1 if side == 0 else 1
        return pltpu.make_async_remote_copy(
            src_ref=self.parts.at[self.target(side, step)],
            dst_ref=self.inbox.at[side, step],
            send_sem=self.sems.at[side, 0, step],
            recv_sem=self.sems.at[side, 1, step],
            device_id={"group": self.me + shift},
            device_id_type=MESH,
        )

    def forward(self, side, step):
        @pl.when(self.passes(side, step))
        def _():
            @pl.when(self.receives(side, step))
            def _():
                self.copy(side, step).wait_recv()
                target = self.target(side, step)
                self.parts[target] = (
                    self.parts[target].astype(jnp.float32)
                    + self.inbox[side, step].astype(jnp.float32)
                ).astype(self.parts.dtype)

            self.copy(side, step).start()

    def finish(self, total_ref):
        for side in range(2):
            has = self.me + 1 < self.count if side == 0 else self.me >= 1

            @pl.when(has)
            def _():
                step = self.me if side == 0 else self.count - 1 - self.me
                self.copy(side, step).wait_recv()
                total_ref[...] += self.inbox[side, step].astype(jnp.float32)

    def wait_sends(self):
        for step in range(self.count - 1):
            for side in range(2):
                @pl.when(self.passes(side, step))
                def _():
                    self.copy(side, step).wait_send()


def head_masks():
    lane = lax.broadcasted_iota(jnp.int32, (1, lanes), 1)
    first = (lane < head_dim).astype(jnp.float32)
    return first.astype(jnp.bfloat16), (1.0 - first).astype(jnp.bfloat16)


def offset_bias(bias_ref, head, row_start, rows, total):
    width = bias_ref.shape[1]
    shift = lax.rem(row_start + (width - (total - 1)), width)
    vector = pltpu.roll(jnp.broadcast_to(bias_ref[pl.ds(head, 1), :], (8, width)), shift, 1)
    vector = jnp.broadcast_to(vector[0:1, :], (rows, width))
    return pltpu.roll(vector, 0, 1, stride=1, stride_axis=0)[:, :total]


def rms_rows(values):
    return lax.rsqrt(jnp.mean(values * values, axis=-1, keepdims=True) + epsilon)


def attention_forward_kernel(
    count,
    length_ref,
    x_hbm, cot_hbm, gains_hbm, wq_hbm, wk_hbm, wv_hbm, wo_hbm, ids_ref, table_ref,
    n1_out, q_out, k_out, v_out, att_out, lse_out, cot_out, middle_out, n2_out, gains_out, bias_out,
    x_all, gains_all, wq, wk, wv, wo, parts, inbox, n1_buf, q_buf, k_buf, v_buf, att_buf, lse_buf, total_buf, n2_buf,
    local_sems, x_sems, g_sems, c_sems, s_sems, out_sems,
):
    me = lax.axis_index("group")
    rows, width = x_hbm.shape
    total = rows * count
    columns = wq.shape[1]
    local_heads = columns // head_dim
    loads = [
        pltpu.make_async_copy(source, target, local_sems.at[index])
        for index, (source, target) in enumerate(
            [
                (x_hbm, x_all.at[me]),
                (gains_hbm, gains_all.at[me]),
                (wq_hbm, wq),
                (wk_hbm, wk),
                (wv_hbm, wv),
                (wo_hbm, wo),
                (cot_hbm, cot_out.at[me]),
            ]
        )
    ]
    for load in loads:
        load.start()
    line_barrier(me, count)
    x_line = LineGather(me, count, x_all, x_sems)
    g_line = LineGather(me, count, gains_all, g_sems)
    c_line = LineGather(me, count, cot_out, c_sems)
    loads[1].wait()
    g_line.start(0)
    loads[0].wait()
    x_line.start(0)

    bucket = lax.broadcasted_iota(jnp.int32, (table_ref.shape[1], ids_ref.shape[1]), 0)
    one_hot = (bucket == ids_ref[...]).astype(jnp.float32).astype(jnp.bfloat16)
    bias_out[...] = nn_dot(table_ref[...], one_hot)

    for step in range(count - 1):
        for side in range(2):
            g_line.wait_arrival(side, step)
        if step + 1 < count - 1:
            g_line.start(step + 1)
    for owner in range(count):
        gains_out[:, owner * (width // count) : (owner + 1) * (width // count)] = gains_all[owner]
    for load in loads[2:5]:
        load.wait()

    def project(block):
        values = x_all[block].astype(jnp.float32)
        normed = (values * rms_rows(values) * gains_out[0:1, :]).astype(jnp.bfloat16)
        n1_buf[block] = normed
        q_buf[block] = nn_dot(normed, wq[...]).astype(jnp.bfloat16)
        k_buf[block] = nn_dot(normed, wk[...]).astype(jnp.bfloat16)
        v_buf[block] = nn_dot(normed, wv[...]).astype(jnp.bfloat16)

    project(me)
    for step in range(count - 1):
        for side in range(2):
            x_line.wait_arrival(side, step)
        if step + 1 < count - 1:
            x_line.start(step + 1)

        @pl.loop(0, 2)
        def _(side):
            arrives = jnp.where(side == 0, me - 1 - step >= 0, me + 1 + step < count)

            @pl.when(arrives)
            def _():
                project(jnp.where(side == 0, me - 1 - step, me + 1 + step))

    loads[6].wait()
    c_line.start(0)
    loads[5].wait()
    mask_first, mask_second = head_masks()
    key_valid = lax.broadcasted_iota(jnp.int32, (1, total), 1) < length_ref[0]
    lane = lax.broadcasted_iota(jnp.int32, (1, lanes), 1)

    def attend(block):
        lse_buf[block] = jnp.zeros((rows, lanes), jnp.float32)

        @pl.loop(0, local_heads // 2)
        def _(pair):
            cols = pl.ds(pl.multiple_of(pair * lanes, lanes), lanes)
            query = q_buf[block, :, cols]
            key = k_buf[:, :, cols].reshape(total, lanes)
            value = v_buf[:, :, cols].reshape(total, lanes)
            outs = []
            for half, mask in enumerate((mask_first, mask_second)):
                head = pair * 2 + half
                scores = nt_dot(query * mask, key)
                scores = scores + offset_bias(bias_out, head, block * rows, rows, total)
                scores = jnp.where(key_valid, scores, negative)
                top = jnp.max(scores, axis=-1, keepdims=True)
                expd = jnp.exp(scores - top)
                summed = jnp.sum(expd, axis=-1, keepdims=True)
                probs = (expd * (1.0 / summed)).astype(jnp.bfloat16)
                outs.append(nn_dot(probs, value))
                lse_buf[block] = jnp.where(lane == head, top + jnp.log(summed), lse_buf[block])
            att_buf[block, :, cols] = jnp.where(lane < head_dim, outs[0], outs[1]).astype(
                jnp.bfloat16
            )

    def attend_and_project(block):
        attend(block)
        parts[block] = nn_dot(att_buf[block], wo[...]).astype(jnp.bfloat16)

    scatter = LineScatter(me, count, parts, inbox, s_sems)
    for step in range(count - 1):
        @pl.loop(0, 2)
        def _(side):
            passes = jnp.where(side == 0, step < me, count - 1 - step > me)

            @pl.when(passes)
            def _():
                attend_and_project(jnp.where(side == 0, step, count - 1 - step))

        for side in range(2):
            scatter.forward(side, step)
        if step < count - 2:
            for side in range(2):
                c_line.wait_arrival(side, step)
            c_line.start(step + 1)
    attend(me)
    outs = [
        pltpu.make_async_copy(source, target, out_sems.at[index])
        for index, (source, target) in enumerate(
            [(n1_buf, n1_out), (q_buf, q_out), (k_buf, k_out), (v_buf, v_out), (att_buf, att_out), (lse_buf, lse_out)]
        )
    ]
    for copy in outs:
        copy.start()
    total_buf[...] = x_all[me].astype(jnp.float32) + nn_dot(att_buf[me], wo[...])
    scatter.finish(total_buf)
    middle = total_buf[...]
    n2_buf[...] = (middle * rms_rows(middle) * gains_out[1:2, :]).astype(jnp.bfloat16)
    tail = [
        pltpu.make_async_copy(total_buf, middle_out, out_sems.at[len(outs)]),
        pltpu.make_async_copy(n2_buf, n2_out, out_sems.at[len(outs) + 1]),
    ]
    for copy in tail:
        copy.start()
    for side in range(2):
        c_line.wait_arrival(side, count - 2)
    for line in (g_line, x_line, c_line, scatter):
        line.wait_sends()
    for copy in outs + tail:
        copy.wait()


def attention_forward(count, length, x, cot, gains, wq, wk, wv, wo, ids, table):
    rows, width = x.shape
    columns = wq.shape[1]
    local_heads = columns // head_dim
    bf, f32 = jnp.bfloat16, jnp.float32
    shape = jax.ShapeDtypeStruct
    steps = count - 1
    dma = pltpu.SemaphoreType.DMA
    return pl.pallas_call(
        functools.partial(attention_forward_kernel, count),
        name="attention_forward",
        out_shape=(
            shape((count, rows, width), bf),
            shape((count, rows, columns), bf),
            shape((count, rows, columns), bf),
            shape((count, rows, columns), bf),
            shape((count, rows, columns), bf),
            shape((count, rows, lanes), f32),
            shape((count, rows, width), bf),
            shape((rows, width), f32),
            shape((rows, width), bf),
            shape((8, width), f32),
            shape((local_heads, ids.shape[1]), f32),
        ),
        in_specs=[smem_space] + [any_space] * 7 + [vmem_space] * 2,
        out_specs=[any_space] * 9 + [vmem_space] * 2,
        scratch_shapes=[
            pltpu.VMEM((count, rows, width), bf),
            pltpu.VMEM((count,) + gains.shape, f32),
            pltpu.VMEM(wq.shape, bf),
            pltpu.VMEM(wk.shape, bf),
            pltpu.VMEM(wv.shape, bf),
            pltpu.VMEM(wo.shape, bf),
            pltpu.VMEM((count, rows, width), bf),
            pltpu.VMEM((2, steps, rows, width), bf),
            pltpu.VMEM((count, rows, width), bf),
            pltpu.VMEM((count, rows, columns), bf),
            pltpu.VMEM((count, rows, columns), bf),
            pltpu.VMEM((count, rows, columns), bf),
            pltpu.VMEM((count, rows, columns), bf),
            pltpu.VMEM((count, rows, lanes), f32),
            pltpu.VMEM((rows, width), f32),
            pltpu.VMEM((rows, width), bf),
            dma((7,)),
            dma((2, 2, steps)),
            dma((2, 2, steps)),
            dma((2, 2, steps)),
            dma((2, 2, steps)),
            dma((8,)),
        ],
        compiler_params=pltpu.CompilerParams(
            collective_id=0, has_side_effects=True, vmem_limit_bytes=56 * 2**20
        ),
    )(length, x, cot, gains, wq, wk, wv, wo, ids, table)


def gelu_parts(gate):
    root = 0.7978845608028654
    inner = root * (gate + 0.044715 * gate * gate * gate)
    tanh = jnp.tanh(inner)
    half = 0.5 * (1.0 + tanh)
    slope = half + 0.5 * gate * (1.0 - tanh * tanh) * root * (1.0 + 3 * 0.044715 * gate * gate)
    return gate * half, slope


def feed_forward_kernel(
    count, tile,
    length_ref,
    n2_hbm, cot_hbm, wg_hbm, wu_hbm, wf_hbm,
    flat_out, back_out, res_out,
    n2_all, g_all, wg, wu, wf, hid, grad_gate, grad_up, back_buf, res_buf, turned, stage,
    local_sems, n_sems, out_sems, stage_sems,
):
    me = lax.axis_index("group")
    rows, width = n2_hbm.shape
    total = rows * count
    units = wg.shape[1]
    loads = [
        pltpu.make_async_copy(source, target, local_sems.at[index])
        for index, (source, target) in enumerate(
            [(n2_hbm, n2_all.at[me]), (wg_hbm, wg), (wu_hbm, wu), (wf_hbm, wf), (cot_hbm, g_all)]
        )
    ]
    for load in loads:
        load.start()
    line_barrier(me, count)
    line = LineGather(me, count, n2_all, n_sems)
    loads[0].wait()
    line.start(0)
    for load in loads[1:]:
        load.wait()

    def mask_rows(block):
        position = block * rows + lax.broadcasted_iota(jnp.int32, (rows, 1), 0)
        valid = (position < length_ref[0]).astype(jnp.float32).astype(jnp.bfloat16)
        g_all[block] = g_all[block] * valid

    def block_pass(block):
        mask_rows(block)
        normed = n2_all[block]
        grads = g_all[block]

        @pl.loop(0, units // tile)
        def _(index):
            cols = pl.ds(pl.multiple_of(index * tile, tile), tile)
            gate = nn_dot(normed, wg[:, cols])
            up = nn_dot(normed, wu[:, cols])
            grad_hidden = nt_dot(grads, wf[cols, :])
            act, slope = gelu_parts(gate)
            hid[block, :, cols] = (act * up).astype(jnp.bfloat16)
            grad_gate[block, :, cols] = (grad_hidden * up * slope).astype(jnp.bfloat16)
            grad_up[block, :, cols] = (grad_hidden * act).astype(jnp.bfloat16)

        chunk = 2 * tile

        @pl.loop(0, width // chunk)
        def _(index):
            cols = pl.ds(pl.multiple_of(index * chunk, chunk), chunk)
            back_buf[block, :, cols] = (
                nt_dot(grad_gate[block], wg[cols, :]) + nt_dot(grad_up[block], wu[cols, :])
            ).astype(jnp.bfloat16)
            res_buf[block, :, cols] = nn_dot(hid[block], wf[:, cols]).astype(jnp.bfloat16)

    block_pass(me)
    for step in range(count - 1):
        for side in range(2):
            line.wait_arrival(side, step)
        if step + 1 < count - 1:
            line.start(step + 1)

        @pl.loop(0, 2)
        def _(side):
            arrives = jnp.where(side == 0, me - 1 - step >= 0, me + 1 + step < count)

            @pl.when(arrives)
            def _():
                block_pass(jnp.where(side == 0, me - 1 - step, me + 1 + step))

    outs = [
        pltpu.make_async_copy(back_buf, back_out, out_sems.at[0]),
        pltpu.make_async_copy(res_buf, res_out, out_sems.at[1]),
    ]
    for copy in outs:
        copy.start()

    def weight_grad(left, right, base, height):
        depth = right.shape[2]
        panels = depth // lanes
        factor = right[...].reshape(total, depth)

        def store(slot, panel, row):
            return pltpu.make_async_copy(
                stage.at[slot, panel],
                flat_out.at[pl.ds(base + panel * height + row, tile)],
                stage_sems.at[slot, panel],
            )

        @pl.loop(0, height // tile)
        def _(index):
            slot = lax.rem(index, 2)
            row = pl.multiple_of(index * tile, tile)
            turned[...] = left[:, :, pl.ds(row, tile)].reshape(total, tile).T
            product = nn_dot(turned[...], factor).astype(jnp.bfloat16)

            @pl.when(index >= 2)
            def _():
                for panel in range(panels):
                    store(slot, panel, row).wait()

            for panel in range(panels):
                stage[slot, panel] = product[:, panel * lanes : (panel + 1) * lanes]
                store(slot, panel, row).start()

        for slot in range(2):
            for panel in range(panels):
                store(slot, panel, 0).wait()

    weight_grad(hid, g_all, 0, units)
    weight_grad(n2_all, grad_gate, units * width // lanes, width)
    weight_grad(n2_all, grad_up, 2 * units * width // lanes, width)
    line.wait_sends()
    for copy in outs:
        copy.wait()


def feed_forward(count, length, n2, cot, wg, wu, wf):
    rows, width = n2.shape
    units = wg.shape[1]
    tile = 128 if units % 256 else 256
    bf = jnp.bfloat16
    shape = jax.ShapeDtypeStruct
    steps = count - 1
    dma = pltpu.SemaphoreType.DMA
    return pl.pallas_call(
        functools.partial(feed_forward_kernel, count, tile),
        name="feed_forward",
        out_shape=(
            shape((3 * units * width // lanes, lanes), bf),
            shape((count, rows, width), bf),
            shape((count, rows, width), bf),
        ),
        in_specs=[smem_space] + [any_space] * 5,
        out_specs=[any_space] * 3,
        scratch_shapes=[
            pltpu.VMEM((count, rows, width), bf),
            pltpu.VMEM((count, rows, width), bf),
            pltpu.VMEM(wg.shape, bf),
            pltpu.VMEM(wu.shape, bf),
            pltpu.VMEM(wf.shape, bf),
            pltpu.VMEM((count, rows, units), bf),
            pltpu.VMEM((count, rows, units), bf),
            pltpu.VMEM((count, rows, units), bf),
            pltpu.VMEM((count, rows, width), bf),
            pltpu.VMEM((count, rows, width), bf),
            pltpu.VMEM((tile, count * rows), bf),
            pltpu.VMEM((2, max(width, units) // lanes, tile, lanes), bf),
            dma((5,)),
            dma((2, 2, steps)),
            dma((2,)),
            dma((2, max(width, units) // lanes)),
        ],
        compiler_params=pltpu.CompilerParams(
            collective_id=1, has_side_effects=True, vmem_limit_bytes=56 * 2**20
        ),
    )(length, n2, cot, wg, wu, wf)


def when(condition, body):
    if isinstance(condition, bool):
        if condition:
            body()
    else:
        pl.when(condition)(body)


class ReplicaSum:
    slots = 4

    def __init__(self, replicas, chunk, chunks, source, target, work, core_box, path_box, sems):
        self.mine = lax.axis_index("replica")
        self.chunk, self.chunks, self.source, self.target = chunk, chunks, source, target
        self.work, self.core_box, self.path_box, self.sems = work, core_box, path_box, sems
        self.depth = work.shape[0]
        bits = [1 << index for index in range(1, replicas.bit_length() - 1)]
        self.orders = (bits, bits[::-1])
        self.levels = len(bits)
        self.last_phase = 2 * self.levels + 2
        self.ticks = chunks + 2 * self.last_phase
        self.half = chunk // 2

    def bit(self, mask):
        return jnp.where((self.mine & mask) != 0, 1, 0)

    def region(self, path, level):
        size = self.half // 2
        offset = path * size
        for mask in self.orders[path][:level]:
            size //= 2
            offset = offset + self.bit(mask) * size
        return offset, size

    def out_rows(self, chunk, offset, size):
        start = chunk * self.chunk + self.bit(1) * self.half + offset
        return self.target.at[pl.ds(pl.multiple_of(start, 16), size)]

    def sem(self, kind, phase, path, chunk):
        return self.sems.at[kind, phase, path, chunk % self.slots]

    def remote(self, source, target, phase, path, chunk, mask):
        return pltpu.make_async_remote_copy(
            src_ref=source,
            dst_ref=target,
            send_sem=self.sem(0, phase, path, chunk),
            recv_sem=self.sem(1, phase, path, chunk),
            device_id={"replica": self.mine ^ mask},
            device_id_type=MESH,
        )

    def core_copy(self, chunk):
        start = chunk * self.chunk + (1 - self.bit(1)) * self.half
        return self.remote(
            self.source(start, self.half), self.core_box.at[chunk % self.slots], 0, 0, chunk, 1
        )

    def load_copy(self, chunk):
        start = chunk * self.chunk + self.bit(1) * self.half
        return pltpu.make_async_copy(
            self.source(start, self.half), self.work.at[chunk % self.depth], self.sem(0, 0, 1, chunk)
        )

    def reduce_copy(self, chunk, path, level):
        mask = self.orders[path][level - 1]
        offset, size = self.region(path, level - 1)
        size //= 2
        start = pl.multiple_of(offset + (1 - self.bit(mask)) * size, 16)
        return self.remote(
            self.work.at[chunk % self.depth, pl.ds(start, size)],
            self.box(chunk, path, level),
            level, path, chunk, mask,
        )

    def box(self, chunk, path, level):
        size = self.half // 2 >> level
        start = sum(self.half // 2 >> step for step in range(1, level))
        return self.path_box.at[chunk % self.slots, path, pl.ds(start, size)]

    def add_box(self, chunk, path, level):
        offset, size = self.region(path, level)
        here = pl.ds(pl.multiple_of(offset, 16), size)
        slot = chunk % self.depth
        self.work[slot, here, :] = self.work[slot, here, :] + self.box(chunk, path, level)[...]

    def own_copy(self, chunk, path):
        offset, size = self.region(path, self.levels)
        return pltpu.make_async_copy(
            self.work.at[chunk % self.depth, pl.ds(pl.multiple_of(offset, 16), size)],
            self.out_rows(chunk, offset, size),
            self.sems.at[1, 0, 1 + path, chunk % self.slots],
        )

    def spread_copy(self, chunk, path, level):
        offset, size = self.region(path, level)
        if level == self.levels:
            source = self.work.at[chunk % self.depth, pl.ds(pl.multiple_of(offset, 16), size)]
        else:
            source = self.out_rows(chunk, offset, size)
        return self.remote(
            source, self.out_rows(chunk, offset, size),
            2 * self.levels + 1 - level, path, chunk, self.orders[path][level - 1],
        )

    def share_copy(self, chunk):
        rows = self.out_rows(chunk, 0, self.half)
        return self.remote(rows, rows, self.last_phase - 1, 0, chunk, 1)

    def advance(self, phase, chunk):
        levels = self.levels
        if phase == 0:
            self.core_copy(chunk).start()
            self.load_copy(chunk).start()
        elif phase <= levels + 1:
            if phase == 1:
                self.load_copy(chunk).wait()
                self.core_copy(chunk).wait()
                slot = chunk % self.depth
                self.work[slot] = self.work[slot] + self.core_box[chunk % self.slots]
            for path in range(2):
                if phase > 1:
                    self.reduce_copy(chunk, path, phase - 1).wait()
                    self.add_box(chunk, path, phase - 1)
                if phase <= levels:
                    self.reduce_copy(chunk, path, phase).start()
                else:
                    self.own_copy(chunk, path).start()
                    self.spread_copy(chunk, path, levels).start()
        else:
            level = 2 * levels + 1 - phase
            if level >= 0:
                for path in range(2):
                    self.spread_copy(chunk, path, level + 1).wait()
                    if level + 1 == levels:
                        self.own_copy(chunk, path).wait()
                    if level >= 1:
                        self.spread_copy(chunk, path, level).start()
                if level == 0:
                    self.share_copy(chunk).start()


def rms_backward(values, grads, gain):
    scale = rms_rows(values)
    unit = values * scale
    scaled = grads * gain
    inner = jnp.mean(scaled * unit, axis=-1, keepdims=True)
    return scale * (scaled - unit * inner), jnp.sum(grads * unit, axis=0, keepdims=True)


def backward_kernel(
    count, replicas, chunk, chunks,
    length_ref,
    flat_hbm, back_hbm, res_hbm, middle_hbm, cot_hbm, x_hbm, q_hbm, k_hbm, v_hbm, att_hbm, lse_hbm, n1_hbm,
    wq_hbm, wk_hbm, wv_hbm, wo_hbm, gains_ref, bias_ref, ids_ref,
    sums_out, flat_out, result_out, input_out, small_out,
    back, res, middle, cot, x_own, q_buf, k_buf, v_buf, att_buf, lse_buf, n1_buf, wq, wk, wv, wo,
    back_box, res_box, total_buf, middle_grad, branch, grad_att, key_acc, value_acc, grad_qkv,
    reverse, offsets, turned, stage, out_buf, small, small_parts, small_box, pair_box,
    work, core_box, path_box,
    load_sems, b_sems, r_sems, f_sems, a_sems, p_sems, pair_sems, stage_sems, out_sems, sum_sems,
):
    me = lax.axis_index("group")
    mine = lax.axis_index("replica")
    rows, width = middle.shape
    total = rows * count
    columns = wq.shape[1]
    local_heads = columns // head_dim
    sources = [
        back_hbm, res_hbm, middle_hbm, cot_hbm, x_hbm, wo_hbm, att_hbm, q_hbm, k_hbm, v_hbm, lse_hbm, n1_hbm,
        wq_hbm, wk_hbm, wv_hbm,
    ]
    targets = [
        back, res, middle, cot, x_own, wo, att_buf, q_buf, k_buf, v_buf, lse_buf, n1_buf, wq, wk, wv
    ]
    loads = [
        pltpu.make_async_copy(source, target, load_sems.at[index])
        for index, (source, target) in enumerate(zip(sources, targets))
    ]
    masks = [1 << index for index in range(replicas.bit_length() - 1)]
    barrier = pltpu.get_barrier_semaphore()

    @pl.when(me > 0)
    def _():
        pl.semaphore_signal(barrier, inc=1, device_id={"group": me - 1}, device_id_type=MESH)

    @pl.when(me < count - 1)
    def _():
        pl.semaphore_signal(barrier, inc=1, device_id={"group": me + 1}, device_id_type=MESH)

    for mask in masks:
        pl.semaphore_signal(barrier, inc=1, device_id={"replica": mine ^ mask}, device_id_type=MESH)
    peers = jnp.where(me > 0, 1, 0) + jnp.where(me < count - 1, 1, 0) + len(masks)
    for load in loads[:5]:
        load.start()
    pl.semaphore_wait(barrier, peers)

    ffn_rows = flat_hbm.shape[0]
    from_ffn = ffn_rows // chunk

    def make_sum(source_ref, base):
        return lambda start, size: source_ref.at[pl.ds(pl.multiple_of(start - base, 16), size)]

    parts = ReplicaSum(
        replicas, chunk, chunks, None, sums_out, work, core_box, path_box, sum_sems
    )
    from_first, from_second = make_sum(flat_hbm, 0), make_sum(flat_out, ffn_rows)

    def tick(time):
        for phase in range(parts.last_phase, -1, -1):
            piece = time - 2 * phase
            if isinstance(piece, int):
                inside = 0 <= piece < chunks
            else:
                inside = (piece >= 0) & (piece < chunks)

            def body(phase=phase, piece=piece):
                if phase > 1:
                    if phase == parts.last_phase:
                        parts.share_copy(piece).wait()
                    else:
                        parts.advance(phase, piece)
                    return
                for source, here in (
                    (from_first, piece < from_ffn),
                    (from_second, piece >= from_ffn),
                ):
                    def start(source=source):
                        parts.source = source
                        parts.core_copy(piece).start()
                        parts.load_copy(piece).start()

                    if phase == 0:
                        when(here, start)
                if phase == 1:
                    parts.source = lambda start, size: flat_hbm.at[pl.ds(0, size)]
                    parts.advance(1, piece)

            when(inside, body)

    back_line = LineScatter(me, count, back, back_box, b_sems)
    res_line = LineScatter(me, count, res, res_box, r_sems)
    first_line = LineScatter(me, count, back, back_box, f_sems)
    branch_line = LineGather(me, count, branch, a_sems)
    small_line = LineScatter(me, count, small_parts, small_box, p_sems)

    tick(0)
    for load in loads[5:]:
        load.start()
    anti = lax.broadcasted_iota(jnp.int32, (total, total), 0) + lax.broadcasted_iota(
        jnp.int32, (total, total), 1
    )
    reverse[...] = (anti == total - 1).astype(jnp.float32).astype(jnp.bfloat16)
    loads[0].wait()
    time = 1
    for step in range(count - 1):
        for side in range(2):
            back_line.forward(side, step)
        tick(time)
        time += 1
    for load in loads[2:5]:
        load.wait()
    total_buf[...] = back[me].astype(jnp.float32)
    back_line.finish(total_buf)
    position = me * rows + lax.broadcasted_iota(jnp.int32, (rows, 1), 0)
    valid = (position < length_ref[0]).astype(jnp.float32)
    grad_mid, gain_grad = rms_backward(middle[...], total_buf[...], gains_ref[1:2, :])
    middle_grad[...] = cot[...].astype(jnp.float32) * valid + grad_mid
    branch[me] = middle_grad[...].astype(jnp.bfloat16)
    small_parts[...] = jnp.zeros_like(small_parts)
    part_width = width // count
    for owner in range(count):
        small_parts[owner, 1:2, :] = gain_grad[:, owner * part_width : (owner + 1) * part_width]
    branch_line.start(0)
    for load in loads[5:]:
        load.wait()

    def attended_grad(block):
        grad_att[block] = nt_dot(branch[block], wo[...]).astype(jnp.bfloat16)

    attended_grad(me)
    tick(time)
    time += 1
    for step in range(count - 1):
        for side in range(2):
            branch_line.wait_arrival(side, step)
        if step + 1 < count - 1:
            branch_line.start(step + 1)

        @pl.loop(0, 2)
        def _(side):
            arrives = jnp.where(side == 0, me - 1 - step >= 0, me + 1 + step < count)

            @pl.when(arrives)
            def _():
                attended_grad(jnp.where(side == 0, me - 1 - step, me + 1 + step))

        if step + 1 < count - 1:
            tick(time)
            time += 1

    tile = 256

    def weight_grad(left, factor, base, height, per_output):
        panels = factor.shape[1] // lanes
        per_panel = per_output // lanes

        def store(slot, panel, row):
            return pltpu.make_async_copy(
                stage.at[slot, panel],
                flat_out.at[pl.ds(base + panel * height + row, tile)],
                stage_sems.at[slot, panel],
            )

        @pl.loop(0, height // tile)
        def _(index):
            slot = lax.rem(index, 2)
            row = pl.multiple_of(index * tile, tile)
            turned[...] = left[:, :, pl.ds(row, tile)].reshape(total, tile).T
            product = nn_dot(turned[...], factor).astype(jnp.bfloat16)

            @pl.when(index >= 2)
            def _():
                for panel in range(panels):
                    store(slot, panel, row).wait()

            for panel in range(panels):
                stage[slot, panel] = product[:, panel * lanes : (panel + 1) * lanes]
                store(slot, panel, row).start()

        for slot in range(min(2, height // tile)):
            for panel in range(panels):
                store(slot, panel, 0).wait()

    weight_grad(att_buf, branch[...].reshape(total, width), 0, columns, width)
    loads[1].wait()

    mask_first, mask_second = head_masks()
    key_valid = lax.broadcasted_iota(jnp.int32, (1, total), 1) < length_ref[0]
    lane = lax.broadcasted_iota(jnp.int32, (1, lanes), 1)
    offsets[...] = jnp.zeros_like(offsets)

    def head_pair(pair):
        cols = pl.ds(pl.multiple_of(pair * lanes, lanes), lanes)
        key = k_buf[:, :, cols].reshape(total, lanes)
        value = v_buf[:, :, cols].reshape(total, lanes)
        key_acc[...] = jnp.zeros_like(key_acc)
        value_acc[...] = jnp.zeros_like(value_acc)

        @pl.loop(0, count)
        def _(block):
            query = q_buf[block, :, cols]
            grads = grad_att[block, :, cols]
            logs = lse_buf[block]
            query_parts = []
            for half, mask in enumerate((mask_first, mask_second)):
                head = pair * 2 + half
                query_half, grads_half = query * mask, grads * mask
                scores = nt_dot(query_half, key)
                scores = scores + offset_bias(bias_ref, head, block * rows, rows, total)
                scores = jnp.where(key_valid, scores, negative)
                log_total = jnp.sum(jnp.where(lane == head, logs, 0.0), axis=-1, keepdims=True)
                probs = jnp.exp(scores - log_total)
                grad_probs = nt_dot(grads_half, value)
                inner = jnp.sum(probs * grad_probs, axis=-1, keepdims=True)
                grad_scores = (probs * (grad_probs - inner)).astype(jnp.bfloat16)
                query_parts.append(nn_dot(grad_scores, key))
                key_acc[...] += nn_dot(query_half.astype(jnp.float32).T.astype(jnp.bfloat16), grad_scores)
                value_acc[...] += nn_dot(
                    grads_half.astype(jnp.float32).T.astype(jnp.bfloat16), probs.astype(jnp.bfloat16)
                )
                turned_scores = nn_dot(grad_scores, reverse[...])
                padded = jnp.concatenate([turned_scores, jnp.zeros_like(turned_scores)], axis=1)
                sheared = pltpu.roll(padded, 0, 1, stride=1, stride_axis=0)
                sums = jnp.broadcast_to(jnp.sum(sheared, axis=0, keepdims=True), (8, 2 * total))
                sums = pltpu.roll(sums, block * rows, 1)
                offsets[pl.ds(head, 1), :] += sums[0:1, :]
            grad_qkv[pl.ds(pl.multiple_of(block * rows, rows), rows), cols] = jnp.where(
                lane < head_dim, query_parts[0], query_parts[1]
            ).astype(jnp.bfloat16)

        grad_qkv[:, pl.ds(pl.multiple_of(columns + pair * lanes, lanes), lanes)] = key_acc[
            ...
        ].T.astype(jnp.bfloat16)
        grad_qkv[:, pl.ds(pl.multiple_of(2 * columns + pair * lanes, lanes), lanes)] = value_acc[
            ...
        ].T.astype(jnp.bfloat16)

    pairs = local_heads // 2
    for step in range(count - 1):
        for side in range(2):
            res_line.forward(side, step)
        tick(time)
        time += 1
        if step < pairs:
            head_pair(step)
    for pair in range(count - 1, pairs):
        head_pair(pair)
    total_buf[...] = middle[...] + res[me].astype(jnp.float32)
    res_line.finish(total_buf)
    out_buf[0] = total_buf[...].astype(jnp.bfloat16)
    result_copy = pltpu.make_async_copy(out_buf.at[0], result_out, out_sems.at[0])
    result_copy.start()
    tick(time)
    time += 1
    weight_grad(n1_buf, grad_qkv[...], columns * width // lanes, width, columns)
    tick(time)
    time += 1

    back_line.wait_sends()

    def first_part(block):
        here = pl.ds(pl.multiple_of(block * rows, rows), rows)
        back[block] = (
            nt_dot(grad_qkv[here, 0:columns], wq[...])
            + nt_dot(grad_qkv[here, columns : 2 * columns], wk[...])
            + nt_dot(grad_qkv[here, 2 * columns :], wv[...])
        ).astype(jnp.bfloat16)

    @pl.loop(0, count)
    def _(block):
        first_part(block)

    for step in range(count - 1):
        for side in range(2):
            first_line.forward(side, step)
        tick(time)
        time += 1
    total_buf[...] = back[me].astype(jnp.float32)
    first_line.finish(total_buf)
    grad_in, gain_grad = rms_backward(
        x_own[...].astype(jnp.float32), total_buf[...], gains_ref[0:1, :]
    )
    out_buf[1] = (middle_grad[...] + grad_in).astype(jnp.bfloat16)
    input_copy = pltpu.make_async_copy(out_buf.at[1], input_out, out_sems.at[1])
    input_copy.start()
    for owner in range(count):
        small_parts[owner, 0:1, :] = gain_grad[:, owner * part_width : (owner + 1) * part_width]
    for step in range(count - 1):
        for side in range(2):
            small_line.forward(side, step)
        tick(time)
        time += 1
    small[0:8, :] = small_parts[me]
    small_line.finish(small.at[pl.ds(0, 8)])
    bucket = lax.broadcasted_iota(jnp.int32, (lanes, ids_ref.shape[1]), 0)
    one_hot = (bucket == ids_ref[...]).astype(jnp.float32).astype(jnp.bfloat16)
    high = offsets[...].astype(jnp.bfloat16)
    rest = offsets[...] - high.astype(jnp.float32)
    middle_part = rest.astype(jnp.bfloat16)
    low_part = (rest - middle_part.astype(jnp.float32)).astype(jnp.bfloat16)
    small[8:16, 0:lanes] = nt_dot(high, one_hot) + nt_dot(middle_part, one_hot) + nt_dot(low_part, one_hot)
    small[8:16, lanes:] = jnp.zeros((8, part_width - lanes), jnp.float32)
    for index, mask in enumerate(masks):
        copy = pltpu.make_async_remote_copy(
            src_ref=small,
            dst_ref=pair_box.at[index],
            send_sem=pair_sems.at[0, index],
            recv_sem=pair_sems.at[1, index],
            device_id={"replica": mine ^ mask},
            device_id_type=MESH,
        )
        copy.start()
        tick(time)
        time += 1
        copy.wait()
        small[...] += pair_box[index]
    small_out[...] = small[...]

    @pl.loop(time, parts.ticks)
    def _(now):
        tick(now)

    for line in (res_line, first_line, branch_line, small_line):
        line.wait_sends()
    result_copy.wait()
    input_copy.wait()


def backward(count, replicas, length, flat, back, res, middle, cot, x, q, k, v, att, lse, n1, wq, wk, wv, wo, gains, bias, ids):
    rows, width = middle.shape
    total = count * rows
    columns = wq.shape[1]
    bf, f32 = jnp.bfloat16, jnp.float32
    shape = jax.ShapeDtypeStruct
    steps = count - 1
    dma = pltpu.SemaphoreType.DMA
    chunk = flat.shape[0] // 15
    attn_rows = 4 * columns * width // lanes
    chunks = 15 + attn_rows // chunk
    levels = replicas.bit_length() - 2
    masks = levels + 1
    depth = 2 * (levels + 2) + 2
    part_width = width // count
    vmem = pltpu.VMEM
    blocks = lambda kind: vmem((count, rows, width), kind)
    narrow = lambda: vmem((count, rows, columns), bf)
    boxes = lambda: vmem((2, steps, rows, width), bf)
    return pl.pallas_call(
        functools.partial(backward_kernel, count, replicas, chunk, chunks),
        name="backward",
        out_shape=(
            shape((flat.shape[0] + attn_rows, lanes), bf),
            shape((attn_rows, lanes), bf),
            shape((rows, width), bf),
            shape((rows, width), bf),
            shape((16, part_width), f32),
        ),
        in_specs=[smem_space] + [any_space] * 16 + [vmem_space] * 3,
        out_specs=[any_space] * 4 + [vmem_space],
        scratch_shapes=[
            blocks(bf), blocks(bf), vmem((rows, width), f32), vmem((rows, width), bf), vmem((rows, width), bf),
            narrow(), narrow(), narrow(), narrow(), vmem((count, rows, lanes), f32), blocks(bf),
            vmem(wq.shape, bf), vmem(wk.shape, bf), vmem(wv.shape, bf), vmem(wo.shape, bf),
            boxes(), boxes(), vmem((rows, width), f32), vmem((rows, width), f32), blocks(bf), narrow(),
            vmem((lanes, total), f32), vmem((lanes, total), f32), vmem((total, 3 * columns), bf),
            vmem((total, total), bf), vmem((8, 2 * total), f32), vmem((256, total), bf),
            vmem((2, width // lanes, 256, lanes), bf), vmem((2, rows, width), bf),
            vmem((16, part_width), f32), vmem((count, 8, part_width), f32), vmem((2, steps, 8, part_width), f32),
            vmem((masks, 16, part_width), f32),
            vmem((depth, chunk // 2, lanes), bf), vmem((4, chunk // 2, lanes), bf), vmem((4, 2, chunk // 4, lanes), bf),
            dma((15,)), dma((2, 2, steps)), dma((2, 2, steps)), dma((2, 2, steps)), dma((2, 2, steps)),
            dma((2, 2, steps)), dma((2, masks)), dma((2, width // lanes)), dma((2,)),
            dma((2, 2 * levels + 3, 3, 4)),
        ],
        compiler_params=pltpu.CompilerParams(
            collective_id=2, has_side_effects=True, vmem_limit_bytes=60 * 2**20
        ),
    )(length, flat, back, res, middle, cot, x, q, k, v, att, lse, n1, wq, wk, wv, wo, gains, bias, ids)


def local(
    inputs,
    seq_lengths,
    bucket_ids,
    norm1_gain,
    w_query,
    w_key,
    w_value,
    w_attn_out,
    bias_table,
    norm2_gain,
    w_gate,
    w_up,
    w_ffn_out,
    cotangent,
):
    count = lax.axis_size("group")
    replicas = lax.axis_size("replica")
    gains_local = jnp.pad(
        jnp.stack([norm1_gain, norm2_gain]).astype(jnp.float32), ((0, 6), (0, 0))
    )
    ids = jnp.pad(bucket_ids, (0, 1))[None, :]
    ids_back = jnp.pad(bucket_ids[::-1], (0, 1), constant_values=-1)[None, :]
    normed_one, query, key, value, attended, log_totals, g_all, middle, normed_two, gains, bias = (
        attention_forward(
            count, seq_lengths, inputs[0], cotangent[0], gains_local,
            w_query, w_key, w_value, w_attn_out, ids, bias_table.T,
        )
    )
    flat, back_part, result_part = feed_forward(
        count, seq_lengths, normed_two, g_all, w_gate, w_up, w_ffn_out
    )
    sums, _, result, input_grad, small = backward(
        count, replicas, seq_lengths, flat, back_part, result_part, middle, cotangent[0], inputs[0],
        query, key, value, attended, log_totals, normed_one,
        w_query, w_key, w_value, w_attn_out, gains, bias, ids_back,
    )
    start = 0
    grads = []
    for weight in (w_ffn_out, w_gate, w_up, w_attn_out, w_query, w_key, w_value):
        height, depth = weight.shape
        panels = depth // lanes
        part = sums[start : start + panels * height].reshape(panels, height, lanes)
        grads.append(part.transpose(1, 0, 2).reshape(height, depth).astype(jnp.float32))
        start += panels * height
    ffn_out_grad, gate_grad, up_grad, attn_out_grad, query_grad, key_grad, value_grad = grads
    buckets, local_heads = bias_table.shape
    table_grad = small[8 : 8 + local_heads, :buckets].T
    return (
        result[None],
        input_grad[None],
        small[0],
        query_grad,
        key_grad,
        value_grad,
        attn_out_grad,
        table_grad,
        small[1],
        gate_grad,
        up_grad,
        ffn_out_grad,
    )


def solution(mesh):
    placed = (
        P("replica", "group", None),
        P("replica"),
        P(),
        P("group"),
        P(None, "group"),
        P(None, "group"),
        P(None, "group"),
        P("group", None),
        P(None, "group"),
        P("group"),
        P(None, "group"),
        P(None, "group"),
        P("group", None),
        P("replica", "group", None),
    )
    return jax.shard_map(
        local,
        mesh=mesh,
        in_specs=placed,
        out_specs=(
            P("replica", "group", None),
            P("replica", "group", None),
            P("group"),
            P(None, "group"),
            P(None, "group"),
            P(None, "group"),
            P("group", None),
            P(None, "group"),
            P("group"),
            P(None, "group"),
            P(None, "group"),
            P("group", None),
        ),
        check_vma=False,
    )
```

```python
import functools
import jax
import jax.numpy as jnp
from jax import lax
from jax.experimental import pallas as pl
from jax.experimental.pallas import tpu as pltpu
from jax.sharding import PartitionSpec as P

epsilon = 1e-06
negative = -1000000000.0
head_dim = 64
lanes = 128
MESH = pl.DeviceIdType.MESH
any_space = pl.BlockSpec(memory_space=pl.ANY)
vmem_space = pl.BlockSpec(memory_space=pltpu.VMEM)
smem_space = pl.BlockSpec(memory_space=pltpu.SMEM)


def nn_dot(left, right):
    return jnp.dot(left, right, preferred_element_type=jnp.float32)


def nt_dot(left, right):
    return lax.dot_general(
        left, right, (((1,), (1,)), ((), ())), preferred_element_type=jnp.float32
    )


def line_barrier(me, count):
    barrier = pltpu.get_barrier_semaphore()

    @pl.when(me > 0)
    def _():
        pl.semaphore_signal(barrier, inc=1, device_id={"group": me - 1}, device_id_type=MESH)

    @pl.when(me < count - 1)
    def _():
        pl.semaphore_signal(barrier, inc=1, device_id={"group": me + 1}, device_id_type=MESH)

    peers = jnp.where(me > 0, 1, 0) + jnp.where(me < count - 1, 1, 0)
    pl.semaphore_wait(barrier, peers)


class LineGather:
    def __init__(self, me, count, buffer, sems, subs=1):
        self.me, self.count, self.buffer, self.sems, self.subs = me, count, buffer, sems, subs
        self.pieces = (count - 1) * subs
        self.size = buffer.shape[1] // subs

    def copy(self, side, piece, hops):
        block = self.me - hops if side == 0 else self.me + hops
        here = self.buffer.at[block, pl.ds(piece % self.subs * self.size, self.size)]
        return pltpu.make_async_remote_copy(
            src_ref=here,
            dst_ref=here,
            send_sem=self.sems.at[side, 0, piece],
            recv_sem=self.sems.at[side, 1, piece],
            device_id={"group": self.me + (1 if side == 0 else -1)},
            device_id_type=MESH,
        )

    def sends(self, side, piece):
        hops = piece // self.subs
        if side == 0:
            return (self.me - hops >= 0) & (self.me + 1 < self.count)
        return (self.me + hops < self.count) & (self.me >= 1)

    def arrives(self, side, piece):
        hops = piece // self.subs
        if side == 0:
            return self.me - 1 - hops >= 0
        return self.me + 1 + hops < self.count

    def send(self, piece):
        for side in range(2):
            @pl.when(self.sends(side, piece))
            def _():
                self.copy(side, piece, piece // self.subs).start()

    def begin(self):
        for piece in range(self.subs):
            self.send(piece)

    def arrive(self, piece):
        for side in range(2):
            @pl.when(self.arrives(side, piece))
            def _():
                self.copy(side, piece, piece // self.subs + 1).wait_recv()

        if piece + self.subs < self.pieces:
            self.send(piece + self.subs)

    def arrive_block(self, hops, body):
        for piece in range(hops * self.subs, (hops + 1) * self.subs):
            self.arrive(piece)
        self.each_block(hops, body)

    def each_block(self, hops, body):
        @pl.loop(0, 2)
        def _(side):
            block = jnp.where(side == 0, self.me - 1 - hops, self.me + 1 + hops)

            @pl.when((block >= 0) & (block < self.count))
            def _():
                body(block)

    def wait_sends(self):
        for piece in range(self.pieces):
            for side in range(2):
                @pl.when(self.sends(side, piece))
                def _():
                    self.copy(side, piece, piece // self.subs).wait_send()


class LineScatter:
    def __init__(self, me, count, parts, inbox, total, sems, subs=1):
        self.me, self.count, self.parts, self.inbox = me, count, parts, inbox
        self.total, self.sems, self.subs = total, sems, subs
        self.times = (count - 1) * subs + 1
        self.size = parts.shape[1] // subs

    def order(self, index):
        picked = 0
        for device in range(self.count):
            due = [(step * self.subs + self.count - 1 - device, step) for step in range(device)]
            due += [
                (step * self.subs + device, self.count - 1 - step)
                for step in range(self.count - 1 - device)
            ]
            blocks = [block for _, block in sorted(due)] + [device]
            picked = picked + jnp.where(self.me == device, blocks[index], 0)
        return picked

    def copy(self, side, piece):
        step = piece // self.subs
        here = pl.ds(pl.multiple_of(piece % self.subs * self.size, self.size), self.size)
        owner = step if side == 0 else self.count - 1 - step
        return pltpu.make_async_remote_copy(
            src_ref=self.parts.at[owner, here],
            dst_ref=self.inbox.at[self.slot(side, step), here],
            send_sem=self.sems.at[side, 0, piece],
            recv_sem=self.sems.at[side, 1, piece],
            device_id={"group": self.me + (-1 if side == 0 else 1)},
            device_id_type=MESH,
        )

    def slot(self, side, step):
        return step if side == 0 else self.count - step

    def at_time(self, time):
        for side in range(2):
            before = self.count - 1 - self.me if side == 0 else self.me
            after = self.count - 1 - before
            piece = time - before
            step = piece // self.subs

            @pl.when((piece >= 0) & (step < after))
            def _():
                owner = step if side == 0 else self.count - 1 - step
                here = pl.ds(pl.multiple_of(piece % self.subs * self.size, self.size), self.size)

                @pl.when(before > 0)
                def _():
                    self.copy(side, piece).wait_recv()
                    self.parts[owner, here, :] = (
                        self.parts[owner, here, :].astype(jnp.float32)
                        + self.inbox[self.slot(side, step), here, :].astype(jnp.float32)
                    ).astype(self.parts.dtype)

                self.copy(side, piece).start()

            @pl.when((piece >= 0) & (step == after) & (before > 0))
            def _():
                here = pl.ds(pl.multiple_of(piece % self.subs * self.size, self.size), self.size)
                self.copy(side, piece).wait_recv()
                self.total[here, :] += self.inbox[self.slot(side, step), here, :].astype(jnp.float32)

    def wait_sends(self):
        for piece in range((self.count - 1) * self.subs):
            step = piece // self.subs
            for side in range(2):
                after = self.me if side == 0 else self.count - 1 - self.me

                @pl.when(step < after)
                def _():
                    self.copy(side, piece).wait_send()


def head_masks():
    lane = lax.broadcasted_iota(jnp.int32, (1, lanes), 1)
    first = (lane < head_dim).astype(jnp.float32)
    return first.astype(jnp.bfloat16), (1.0 - first).astype(jnp.bfloat16)


def offset_bias(bias_ref, head, row_start, rows, total):
    width = bias_ref.shape[1]
    shift = lax.rem(row_start + (width - (total - 1)), width)
    vector = pltpu.roll(jnp.broadcast_to(bias_ref[pl.ds(head, 1), :], (8, width)), shift, 1)
    vector = jnp.broadcast_to(vector[0:1, :], (rows, width))
    return pltpu.roll(vector, 0, 1, stride=1, stride_axis=0)[:, :total]


def rms_rows(values):
    return lax.rsqrt(jnp.mean(values * values, axis=-1, keepdims=True) + epsilon)


def attention_forward_kernel(
    count, subs,
    length_ref,
    x_hbm, cot_hbm, gains_hbm, wq_hbm, wk_hbm, wv_hbm, wo_hbm, ids_ref, table_ref,
    n1_out, q_out, k_out, v_out, att_out, lse_out, cot_out, middle_out, n2_out, gains_out, bias_out,
    x_all, gains_all, wq, wk, wv, wo, parts, inbox, n1_buf, q_buf, k_buf, v_buf, att_buf, lse_buf, total_buf, n2_buf,
    local_sems, x_sems, g_sems, c_sems, s_sems, out_sems,
):
    me = lax.axis_index("group")
    rows, width = x_hbm.shape
    total = rows * count
    columns = wq.shape[1]
    local_heads = columns // head_dim
    loads = [
        pltpu.make_async_copy(source, target, local_sems.at[index])
        for index, (source, target) in enumerate(
            [
                (x_hbm, x_all.at[me]),
                (gains_hbm, gains_all.at[me]),
                (wq_hbm, wq),
                (wk_hbm, wk),
                (wv_hbm, wv),
                (wo_hbm, wo),
                (cot_hbm, cot_out.at[me]),
            ]
        )
    ]
    for load in loads:
        load.start()
    line_barrier(me, count)
    x_line = LineGather(me, count, x_all, x_sems, subs)
    g_line = LineGather(me, count, gains_all, g_sems)
    c_line = LineGather(me, count, cot_out, c_sems, subs)
    loads[1].wait()
    g_line.begin()
    loads[0].wait()
    x_line.begin()

    bucket = lax.broadcasted_iota(jnp.int32, (table_ref.shape[1], ids_ref.shape[1]), 0)
    one_hot = (bucket == ids_ref[...]).astype(jnp.float32).astype(jnp.bfloat16)
    bias_out[...] = nn_dot(table_ref[...], one_hot)

    for piece in range(g_line.pieces):
        g_line.arrive(piece)
    for owner in range(count):
        gains_out[:, owner * (width // count) : (owner + 1) * (width // count)] = gains_all[owner]
    for load in loads[2:5]:
        load.wait()

    def project(block):
        values = x_all[block].astype(jnp.float32)
        normed = (values * rms_rows(values) * gains_out[0:1, :]).astype(jnp.bfloat16)
        n1_buf[block] = normed
        q_buf[block] = nn_dot(normed, wq[...]).astype(jnp.bfloat16)
        k_buf[block] = nn_dot(normed, wk[...]).astype(jnp.bfloat16)
        v_buf[block] = nn_dot(normed, wv[...]).astype(jnp.bfloat16)

    for piece in range(subs):
        x_line.arrive(piece)
    project(me)
    x_line.each_block(0, project)
    for hops in range(1, count - 1):
        x_line.arrive_block(hops, project)

    loads[6].wait()
    c_line.begin()
    loads[5].wait()
    mask_first, mask_second = head_masks()
    key_valid = lax.broadcasted_iota(jnp.int32, (1, total), 1) < length_ref[0]
    lane = lax.broadcasted_iota(jnp.int32, (1, lanes), 1)

    def attend(block):
        lse_buf[block] = jnp.zeros((rows, lanes), jnp.float32)

        @pl.loop(0, local_heads // 2)
        def _(pair):
            cols = pl.ds(pl.multiple_of(pair * lanes, lanes), lanes)
            query = q_buf[block, :, cols]
            key = k_buf[:, :, cols].reshape(total, lanes)
            value = v_buf[:, :, cols].reshape(total, lanes)
            outs = []
            for half, mask in enumerate((mask_first, mask_second)):
                head = pair * 2 + half
                scores = nt_dot(query * mask, key)
                scores = scores + offset_bias(bias_out, head, block * rows, rows, total)
                scores = jnp.where(key_valid, scores, negative)
                top = jnp.max(scores, axis=-1, keepdims=True)
                expd = jnp.exp(scores - top)
                summed = jnp.sum(expd, axis=-1, keepdims=True)
                probs = (expd * (1.0 / summed)).astype(jnp.bfloat16)
                outs.append(nn_dot(probs, value))
                lse_buf[block] = jnp.where(lane == head, top + jnp.log(summed), lse_buf[block])
            att_buf[block, :, cols] = jnp.where(lane < head_dim, outs[0], outs[1]).astype(
                jnp.bfloat16
            )

    scatter = LineScatter(me, count, parts, inbox, total_buf, s_sems, subs)
    arrived = 0
    for index in range(count - 1):
        block = scatter.order(index)
        attend(block)
        parts[block] = nn_dot(att_buf[block], wo[...]).astype(jnp.bfloat16)
        scatter.at_time(index)
    attend(me)
    total_buf[...] = x_all[me].astype(jnp.float32) + nn_dot(att_buf[me], wo[...])
    outs = [
        pltpu.make_async_copy(source, target, out_sems.at[index])
        for index, (source, target) in enumerate(
            [(n1_buf, n1_out), (q_buf, q_out), (k_buf, k_out), (v_buf, v_out), (att_buf, att_out), (lse_buf, lse_out)]
        )
    ]
    for copy in outs:
        copy.start()
    for time in range(count - 1, scatter.times):
        scatter.at_time(time)
        if arrived < c_line.pieces:
            c_line.arrive(arrived)
            arrived += 1
    middle = total_buf[...]
    n2_buf[...] = (middle * rms_rows(middle) * gains_out[1:2, :]).astype(jnp.bfloat16)
    tail = [
        pltpu.make_async_copy(total_buf, middle_out, out_sems.at[len(outs)]),
        pltpu.make_async_copy(n2_buf, n2_out, out_sems.at[len(outs) + 1]),
    ]
    for copy in tail:
        copy.start()
    for piece in range(arrived, c_line.pieces):
        c_line.arrive(piece)
    for line in (g_line, x_line, c_line, scatter):
        line.wait_sends()
    for copy in outs + tail:
        copy.wait()


def attention_forward(count, length, x, cot, gains, wq, wk, wv, wo, ids, table):
    rows, width = x.shape
    columns = wq.shape[1]
    local_heads = columns // head_dim
    bf, f32 = jnp.bfloat16, jnp.float32
    shape = jax.ShapeDtypeStruct
    steps = count - 1
    subs = 2
    dma = pltpu.SemaphoreType.DMA
    return pl.pallas_call(
        functools.partial(attention_forward_kernel, count, subs),
        name="attention_forward",
        out_shape=(
            shape((count, rows, width), bf),
            shape((count, rows, columns), bf),
            shape((count, rows, columns), bf),
            shape((count, rows, columns), bf),
            shape((count, rows, columns), bf),
            shape((count, rows, lanes), f32),
            shape((count, rows, width), bf),
            shape((rows, width), f32),
            shape((rows, width), bf),
            shape((8, width), f32),
            shape((local_heads, ids.shape[1]), f32),
        ),
        in_specs=[smem_space] + [any_space] * 7 + [vmem_space] * 2,
        out_specs=[any_space] * 9 + [vmem_space] * 2,
        scratch_shapes=[
            pltpu.VMEM((count, rows, width), bf),
            pltpu.VMEM((count,) + gains.shape, f32),
            pltpu.VMEM(wq.shape, bf),
            pltpu.VMEM(wk.shape, bf),
            pltpu.VMEM(wv.shape, bf),
            pltpu.VMEM(wo.shape, bf),
            pltpu.VMEM((count, rows, width), bf),
            pltpu.VMEM((count + 1, rows, width), bf),
            pltpu.VMEM((count, rows, width), bf),
            pltpu.VMEM((count, rows, columns), bf),
            pltpu.VMEM((count, rows, columns), bf),
            pltpu.VMEM((count, rows, columns), bf),
            pltpu.VMEM((count, rows, columns), bf),
            pltpu.VMEM((count, rows, lanes), f32),
            pltpu.VMEM((rows, width), f32),
            pltpu.VMEM((rows, width), bf),
            dma((7,)),
            dma((2, 2, steps * subs)),
            dma((2, 2, steps)),
            dma((2, 2, steps * subs)),
            dma((2, 2, steps * subs)),
            dma((8,)),
        ],
        compiler_params=pltpu.CompilerParams(
            collective_id=0, has_side_effects=True, vmem_limit_bytes=56 * 2**20
        ),
    )(length, x, cot, gains, wq, wk, wv, wo, ids, table)


def gelu_parts(gate):
    root = 0.7978845608028654
    inner = root * (gate + 0.044715 * gate * gate * gate)
    tanh = jnp.tanh(inner)
    half = 0.5 * (1.0 + tanh)
    slope = half + 0.5 * gate * (1.0 - tanh * tanh) * root * (1.0 + 3 * 0.044715 * gate * gate)
    return gate * half, slope


def feed_forward_kernel(
    count, tile, subs,
    length_ref,
    n2_hbm, cot_hbm, wg_hbm, wu_hbm, wf_hbm,
    flat_out, back_out, res_out,
    n2_all, g_all, wg, wu, wf, hid, grad_gate, grad_up, back_buf, res_buf, turned, stage,
    local_sems, n_sems, out_sems, stage_sems,
):
    me = lax.axis_index("group")
    rows, width = n2_hbm.shape
    total = rows * count
    units = wg.shape[1]
    loads = [
        pltpu.make_async_copy(source, target, local_sems.at[index])
        for index, (source, target) in enumerate(
            [(n2_hbm, n2_all.at[me]), (wg_hbm, wg), (wu_hbm, wu), (wf_hbm, wf), (cot_hbm, g_all)]
        )
    ]
    for load in loads:
        load.start()
    line_barrier(me, count)
    line = LineGather(me, count, n2_all, n_sems, subs)
    loads[0].wait()
    line.begin()
    for load in loads[1:]:
        load.wait()

    def mask_rows(block):
        position = block * rows + lax.broadcasted_iota(jnp.int32, (rows, 1), 0)
        valid = (position < length_ref[0]).astype(jnp.float32).astype(jnp.bfloat16)
        g_all[block] = g_all[block] * valid

    def block_pass(block):
        mask_rows(block)
        normed = n2_all[block]
        grads = g_all[block]

        @pl.loop(0, units // tile)
        def _(index):
            cols = pl.ds(pl.multiple_of(index * tile, tile), tile)
            gate = nn_dot(normed, wg[:, cols])
            up = nn_dot(normed, wu[:, cols])
            grad_hidden = nt_dot(grads, wf[cols, :])
            act, slope = gelu_parts(gate)
            hid[block, :, cols] = (act * up).astype(jnp.bfloat16)
            grad_gate[block, :, cols] = (grad_hidden * up * slope).astype(jnp.bfloat16)
            grad_up[block, :, cols] = (grad_hidden * act).astype(jnp.bfloat16)

        chunk = 2 * tile

        @pl.loop(0, width // chunk)
        def _(index):
            cols = pl.ds(pl.multiple_of(index * chunk, chunk), chunk)
            back_buf[block, :, cols] = (
                nt_dot(grad_gate[block], wg[cols, :]) + nt_dot(grad_up[block], wu[cols, :])
            ).astype(jnp.bfloat16)
            res_buf[block, :, cols] = nn_dot(hid[block], wf[:, cols]).astype(jnp.bfloat16)

    block_pass(me)
    for hops in range(count - 1):
        line.arrive_block(hops, block_pass)
    outs = [
        pltpu.make_async_copy(back_buf, back_out, out_sems.at[0]),
        pltpu.make_async_copy(res_buf, res_out, out_sems.at[1]),
    ]
    for copy in outs:
        copy.start()

    def weight_grad(left, right, base, height):
        depth = right.shape[2]
        panels = depth // lanes
        factor = right[...].reshape(total, depth)

        def store(slot, panel, row):
            return pltpu.make_async_copy(
                stage.at[slot, panel],
                flat_out.at[pl.ds(base + panel * height + row, tile)],
                stage_sems.at[slot, panel],
            )

        @pl.loop(0, height // tile)
        def _(index):
            slot = lax.rem(index, 2)
            row = pl.multiple_of(index * tile, tile)
            turned[...] = left[:, :, pl.ds(row, tile)].reshape(total, tile).T
            product = nn_dot(turned[...], factor).astype(jnp.bfloat16)

            @pl.when(index >= 2)
            def _():
                for panel in range(panels):
                    store(slot, panel, row).wait()

            for panel in range(panels):
                stage[slot, panel] = product[:, panel * lanes : (panel + 1) * lanes]
                store(slot, panel, row).start()

        for slot in range(2):
            for panel in range(panels):
                store(slot, panel, 0).wait()

    weight_grad(hid, g_all, 0, units)
    weight_grad(n2_all, grad_gate, units * width // lanes, width)
    weight_grad(n2_all, grad_up, 2 * units * width // lanes, width)
    line.wait_sends()
    for copy in outs:
        copy.wait()


def feed_forward(count, length, n2, cot, wg, wu, wf):
    rows, width = n2.shape
    units = wg.shape[1]
    tile = 128 if units % 256 else 256
    bf = jnp.bfloat16
    shape = jax.ShapeDtypeStruct
    steps = count - 1
    subs = 2
    dma = pltpu.SemaphoreType.DMA
    return pl.pallas_call(
        functools.partial(feed_forward_kernel, count, tile, subs),
        name="feed_forward",
        out_shape=(
            shape((3 * units * width // lanes, lanes), bf),
            shape((count, rows, width), bf),
            shape((count, rows, width), bf),
        ),
        in_specs=[smem_space] + [any_space] * 5,
        out_specs=[any_space] * 3,
        scratch_shapes=[
            pltpu.VMEM((count, rows, width), bf),
            pltpu.VMEM((count, rows, width), bf),
            pltpu.VMEM(wg.shape, bf),
            pltpu.VMEM(wu.shape, bf),
            pltpu.VMEM(wf.shape, bf),
            pltpu.VMEM((count, rows, units), bf),
            pltpu.VMEM((count, rows, units), bf),
            pltpu.VMEM((count, rows, units), bf),
            pltpu.VMEM((count, rows, width), bf),
            pltpu.VMEM((count, rows, width), bf),
            pltpu.VMEM((tile, count * rows), bf),
            pltpu.VMEM((2, max(width, units) // lanes, tile, lanes), bf),
            dma((5,)),
            dma((2, 2, steps * subs)),
            dma((2,)),
            dma((2, max(width, units) // lanes)),
        ],
        compiler_params=pltpu.CompilerParams(
            collective_id=1, has_side_effects=True, vmem_limit_bytes=56 * 2**20
        ),
    )(length, n2, cot, wg, wu, wf)


def when(condition, body):
    if isinstance(condition, bool):
        if condition:
            body()
    else:
        pl.when(condition)(body)


class ReplicaSum:
    def __init__(self, replicas, chunk, source, target, work, core_box, path_box, sems):
        self.mine = lax.axis_index("replica")
        self.chunk, self.source, self.target = chunk, source, target
        self.work, self.core_box, self.path_box, self.sems = work, core_box, path_box, sems
        self.depth, self.slots = work.shape[0], core_box.shape[0]
        bits = [1 << index for index in range(1, replicas.bit_length() - 1)]
        self.orders = (bits, bits[::-1])
        self.levels = len(bits)
        self.last_phase = 2 * self.levels + 2
        self.half = chunk // 2

    def bit(self, mask):
        return jnp.where((self.mine & mask) != 0, 1, 0)

    def region(self, path, level):
        size = self.half // 2
        offset = path * size
        for mask in self.orders[path][:level]:
            size //= 2
            offset = offset + self.bit(mask) * size
        return offset, size

    def out_rows(self, chunk, offset, size):
        start = chunk * self.chunk + self.bit(1) * self.half + offset
        return self.target.at[pl.ds(pl.multiple_of(start, 16), size)]

    def sem(self, kind, phase, path, chunk):
        return self.sems.at[kind, phase, path, chunk % self.slots]

    def remote(self, source, target, phase, path, chunk, mask):
        return pltpu.make_async_remote_copy(
            src_ref=source,
            dst_ref=target,
            send_sem=self.sem(0, phase, path, chunk),
            recv_sem=self.sem(1, phase, path, chunk),
            device_id={"replica": self.mine ^ mask},
            device_id_type=MESH,
        )

    def core_copy(self, chunk):
        start = chunk * self.chunk + (1 - self.bit(1)) * self.half
        return self.remote(
            self.source(start, self.half), self.core_box.at[chunk % self.slots], 0, 0, chunk, 1
        )

    def load_copy(self, chunk):
        start = chunk * self.chunk + self.bit(1) * self.half
        return pltpu.make_async_copy(
            self.source(start, self.half), self.work.at[chunk % self.depth], self.sem(0, 0, 1, chunk)
        )

    def reduce_copy(self, chunk, path, level):
        mask = self.orders[path][level - 1]
        offset, size = self.region(path, level - 1)
        size //= 2
        start = pl.multiple_of(offset + (1 - self.bit(mask)) * size, 16)
        return self.remote(
            self.work.at[chunk % self.depth, pl.ds(start, size)],
            self.box(chunk, path, level),
            level, path, chunk, mask,
        )

    def box(self, chunk, path, level):
        size = self.half // 2 >> level
        start = sum(self.half // 2 >> step for step in range(1, level))
        return self.path_box.at[chunk % self.slots, path, pl.ds(start, size)]

    def add_box(self, chunk, path, level):
        offset, size = self.region(path, level)
        here = pl.ds(pl.multiple_of(offset, 16), size)
        slot = chunk % self.depth
        self.work[slot, here, :] = self.work[slot, here, :] + self.box(chunk, path, level)[...]

    def own_copy(self, chunk, path):
        offset, size = self.region(path, self.levels)
        return pltpu.make_async_copy(
            self.work.at[chunk % self.depth, pl.ds(pl.multiple_of(offset, 16), size)],
            self.out_rows(chunk, offset, size),
            self.sems.at[1, 0, 1 + path, chunk % self.slots],
        )

    def spread_copy(self, chunk, path, level):
        offset, size = self.region(path, level)
        if level == self.levels:
            source = self.work.at[chunk % self.depth, pl.ds(pl.multiple_of(offset, 16), size)]
        else:
            source = self.out_rows(chunk, offset, size)
        return self.remote(
            source, self.out_rows(chunk, offset, size),
            2 * self.levels + 1 - level, path, chunk, self.orders[path][level - 1],
        )

    def share_copy(self, chunk):
        rows = self.out_rows(chunk, 0, self.half)
        return self.remote(rows, rows, self.last_phase - 1, 0, chunk, 1)

    def advance(self, phase, chunk):
        levels = self.levels
        if phase == 0:
            self.core_copy(chunk).start()
            self.load_copy(chunk).start()
        elif phase <= levels + 1:
            if phase == 1:
                self.load_copy(chunk).wait()
                self.core_copy(chunk).wait()
                slot = chunk % self.depth
                self.work[slot] = self.work[slot] + self.core_box[chunk % self.slots]
            for path in range(2):
                if phase > 1:
                    self.reduce_copy(chunk, path, phase - 1).wait()
                    self.add_box(chunk, path, phase - 1)
                if phase <= levels:
                    self.reduce_copy(chunk, path, phase).start()
                else:
                    self.own_copy(chunk, path).start()
                    self.spread_copy(chunk, path, levels).start()
        else:
            level = 2 * levels + 1 - phase
            if level >= 0:
                for path in range(2):
                    self.spread_copy(chunk, path, level + 1).wait()
                    if level + 1 == levels:
                        self.own_copy(chunk, path).wait()
                    if level >= 1:
                        self.spread_copy(chunk, path, level).start()
                if level == 0:
                    self.share_copy(chunk).start()


scatter_pace, both_pace, pair_pace = 0.7, 0.9, 0.34


def rms_backward(values, grads, gain):
    scale = rms_rows(values)
    unit = values * scale
    scaled = grads * gain
    inner = jnp.mean(scaled * unit, axis=-1, keepdims=True)
    return scale * (scaled - unit * inner), jnp.sum(grads * unit, axis=0, keepdims=True)


def backward_kernel(
    count, replicas, chunk, attn_chunks, skew, subs,
    length_ref,
    flat_hbm, back_hbm, res_hbm, middle_hbm, cot_hbm, x_hbm, q_hbm, k_hbm, v_hbm, att_hbm, lse_hbm, n1_hbm,
    wq_hbm, wk_hbm, wv_hbm, wo_hbm, gains_ref, bias_ref, ids_ref,
    sums_out, flat_out, result_out, input_out, small_out,
    back, res, middle, cot, x_own, q_buf, k_buf, v_buf, att_buf, lse_buf, n1_buf, wq, wk, wv, wo,
    back_box, res_box, total_buf, res_total, middle_grad, branch, grad_att, key_acc, value_acc, grad_qkv,
    reverse, offsets, turned, stage, out_buf, small, small_parts, small_box, pair_box,
    work, core_box, path_box,
    load_sems, b_sems, r_sems, f_sems, a_sems, p_sems, pair_sems, stage_sems, out_sems, sum_sems,
):
    me = lax.axis_index("group")
    mine = lax.axis_index("replica")
    rows, width = middle.shape
    total = rows * count
    columns = wq.shape[1]
    local_heads = columns // head_dim
    sources = [
        back_hbm, res_hbm, middle_hbm, cot_hbm, x_hbm, wo_hbm, att_hbm, q_hbm, k_hbm, v_hbm, lse_hbm, n1_hbm,
        wq_hbm, wk_hbm, wv_hbm,
    ]
    targets = [
        back, res, middle, cot, x_own, wo, att_buf, q_buf, k_buf, v_buf, lse_buf, n1_buf, wq, wk, wv
    ]
    loads = [
        pltpu.make_async_copy(source, target, load_sems.at[index])
        for index, (source, target) in enumerate(zip(sources, targets))
    ]
    masks = [1 << index for index in range(replicas.bit_length() - 1)]
    barrier = pltpu.get_barrier_semaphore()

    @pl.when(me > 0)
    def _():
        pl.semaphore_signal(barrier, inc=1, device_id={"group": me - 1}, device_id_type=MESH)

    @pl.when(me < count - 1)
    def _():
        pl.semaphore_signal(barrier, inc=1, device_id={"group": me + 1}, device_id_type=MESH)

    for mask in masks:
        pl.semaphore_signal(barrier, inc=1, device_id={"replica": mine ^ mask}, device_id_type=MESH)
    peers = jnp.where(me > 0, 1, 0) + jnp.where(me < count - 1, 1, 0) + len(masks)
    for load in loads[:5]:
        load.start()
    pl.semaphore_wait(barrier, peers)

    ffn_rows = flat_hbm.shape[0]
    from_ffn = ffn_rows // chunk
    chunks = from_ffn + attn_chunks

    def make_source(source_ref, base):
        return lambda start, size: source_ref.at[pl.ds(pl.multiple_of(start - base, 16), size)]

    parts = ReplicaSum(replicas, chunk, None, sums_out, work, core_box, path_box, sum_sems)
    from_first, from_second = make_source(flat_hbm, 0), make_source(flat_out, ffn_rows)
    clock = {"time": 0, "gap": None, "credit": 0.0}

    def start_piece(source, piece):
        parts.source = source
        parts.core_copy(piece).start()
        parts.load_copy(piece).start()

    def tick(time):
        gap = clock["gap"]
        for phase in range(parts.last_phase, -1, -1):
            entry = time - skew * phase
            if isinstance(entry, int):
                early = 0 <= entry < from_ffn
                late = gap is not None and from_ffn + gap <= entry < chunks + gap
                piece = entry if early else entry - (gap or 0)
                inside = early or late
            else:
                early = (entry >= 0) & (entry < from_ffn)
                late = (entry >= from_ffn + gap) & (entry < chunks + gap)
                piece = jnp.where(entry < from_ffn, entry, entry - gap)
                inside = early | late

            def body(phase=phase, piece=piece):
                if phase == parts.last_phase:
                    parts.share_copy(piece).wait()
                elif phase:
                    parts.source = lambda start, size: flat_hbm.at[pl.ds(0, size)]
                    parts.advance(phase, piece)

            if phase:
                when(inside, body)
            else:
                when(early, functools.partial(start_piece, from_first, piece))
                when(late, functools.partial(start_piece, from_second, piece))

    def pace(amount):
        clock["credit"] += amount
        while clock["credit"] >= 1:
            tick(clock["time"])
            clock["time"] += 1
            clock["credit"] -= 1

    back_line = LineScatter(me, count, back, back_box, total_buf, b_sems, subs)
    res_line = LineScatter(me, count, res, res_box, res_total, r_sems, subs)
    first_line = LineScatter(me, count, back, back_box, total_buf, f_sems, subs)
    branch_line = LineGather(me, count, branch, a_sems, subs)
    small_line = LineScatter(me, count, small_parts, small_box, small.at[pl.ds(0, 8)], p_sems)

    tick(0)
    for load in loads[5:]:
        load.start()
    loads[0].wait()
    total_buf[...] = back[me].astype(jnp.float32)
    back_line.at_time(0)
    clock["time"] = 1
    pace(2 * skew - 1)
    anti = lax.broadcasted_iota(jnp.int32, (total, total), 0) + lax.broadcasted_iota(
        jnp.int32, (total, total), 1
    )
    reverse[...] = (anti == total - 1).astype(jnp.float32).astype(jnp.bfloat16)
    for now in range(1, back_line.times):
        back_line.at_time(now)
        pace(scatter_pace)
    for load in loads[1:5]:
        load.wait()
    position = me * rows + lax.broadcasted_iota(jnp.int32, (rows, 1), 0)
    valid = (position < length_ref[0]).astype(jnp.float32)
    grad_mid, gain_grad = rms_backward(middle[...], total_buf[...], gains_ref[1:2, :])
    middle_grad[...] = cot[...].astype(jnp.float32) * valid + grad_mid
    branch[me] = middle_grad[...].astype(jnp.bfloat16)
    branch_line.begin()
    res_total[...] = middle[...] + res[me].astype(jnp.float32)
    res_line.at_time(0)
    small_parts[...] = jnp.zeros_like(small_parts)
    part_width = width // count
    for owner in range(count):
        small_parts[owner, 1:2, :] = gain_grad[:, owner * part_width : (owner + 1) * part_width]
    for load in loads[5:]:
        load.wait()

    def attended_grad(block):
        grad_att[block] = nt_dot(branch[block], wo[...]).astype(jnp.bfloat16)

    attended_grad(me)
    pace(both_pace)
    for now in range(1, res_line.times):
        branch_line.arrive(now - 1)
        res_line.at_time(now)
        pace(both_pace)
        if now % subs == 0:
            branch_line.each_block(now // subs - 1, attended_grad)
    out_buf[0] = res_total[...].astype(jnp.bfloat16)
    result_copy = pltpu.make_async_copy(out_buf.at[0], result_out, out_sems.at[0])
    result_copy.start()

    tile = 256

    def weight_grad(left, factor, base, height, per_output):
        panels = factor.shape[1] // lanes
        per_panel = per_output // lanes

        def store(slot, panel, row):
            return pltpu.make_async_copy(
                stage.at[slot, panel],
                flat_out.at[pl.ds(base + panel * height + row, tile)],
                stage_sems.at[slot, panel],
            )

        @pl.loop(0, height // tile)
        def _(index):
            slot = lax.rem(index, 2)
            row = pl.multiple_of(index * tile, tile)
            turned[...] = left[:, :, pl.ds(row, tile)].reshape(total, tile).T
            product = nn_dot(turned[...], factor).astype(jnp.bfloat16)

            @pl.when(index >= 2)
            def _():
                for panel in range(panels):
                    store(slot, panel, row).wait()

            for panel in range(panels):
                stage[slot, panel] = product[:, panel * lanes : (panel + 1) * lanes]
                store(slot, panel, row).start()

        for slot in range(min(2, height // tile)):
            for panel in range(panels):
                store(slot, panel, 0).wait()

    mask_first, mask_second = head_masks()
    key_valid = lax.broadcasted_iota(jnp.int32, (1, total), 1) < length_ref[0]
    lane = lax.broadcasted_iota(jnp.int32, (1, lanes), 1)
    offsets[...] = jnp.zeros_like(offsets)

    def head_pair(pair):
        cols = pl.ds(pl.multiple_of(pair * lanes, lanes), lanes)
        key = k_buf[:, :, cols].reshape(total, lanes)
        value = v_buf[:, :, cols].reshape(total, lanes)
        key_acc[...] = jnp.zeros_like(key_acc)
        value_acc[...] = jnp.zeros_like(value_acc)

        @pl.loop(0, count)
        def _(block):
            query = q_buf[block, :, cols]
            grads = grad_att[block, :, cols]
            logs = lse_buf[block]
            query_parts = []
            for half, mask in enumerate((mask_first, mask_second)):
                head = pair * 2 + half
                query_half, grads_half = query * mask, grads * mask
                scores = nt_dot(query_half, key)
                scores = scores + offset_bias(bias_ref, head, block * rows, rows, total)
                scores = jnp.where(key_valid, scores, negative)
                log_total = jnp.sum(jnp.where(lane == head, logs, 0.0), axis=-1, keepdims=True)
                probs = jnp.exp(scores - log_total)
                grad_probs = nt_dot(grads_half, value)
                inner = jnp.sum(probs * grad_probs, axis=-1, keepdims=True)
                grad_scores = (probs * (grad_probs - inner)).astype(jnp.bfloat16)
                query_parts.append(nn_dot(grad_scores, key))
                key_acc[...] += nn_dot(query_half.astype(jnp.float32).T.astype(jnp.bfloat16), grad_scores)
                value_acc[...] += nn_dot(
                    grads_half.astype(jnp.float32).T.astype(jnp.bfloat16), probs.astype(jnp.bfloat16)
                )
                turned_scores = nn_dot(grad_scores, reverse[...])
                padded = jnp.concatenate([turned_scores, jnp.zeros_like(turned_scores)], axis=1)
                sheared = pltpu.roll(padded, 0, 1, stride=1, stride_axis=0)
                sums = jnp.broadcast_to(jnp.sum(sheared, axis=0, keepdims=True), (8, 2 * total))
                sums = pltpu.roll(sums, block * rows, 1)
                offsets[pl.ds(head, 1), :] += sums[0:1, :]
            grad_qkv[pl.ds(pl.multiple_of(block * rows, rows), rows), cols] = jnp.where(
                lane < head_dim, query_parts[0], query_parts[1]
            ).astype(jnp.bfloat16)

        grad_qkv[:, pl.ds(pl.multiple_of(columns + pair * lanes, lanes), lanes)] = key_acc[
            ...
        ].T.astype(jnp.bfloat16)
        grad_qkv[:, pl.ds(pl.multiple_of(2 * columns + pair * lanes, lanes), lanes)] = value_acc[
            ...
        ].T.astype(jnp.bfloat16)

    for pair in range(local_heads // 2):
        head_pair(pair)
        pace(pair_pace)

    back_line.wait_sends()

    def first_part(block):
        here = pl.ds(pl.multiple_of(block * rows, rows), rows)
        back[block] = (
            nt_dot(grad_qkv[here, 0:columns], wq[...])
            + nt_dot(grad_qkv[here, columns : 2 * columns], wk[...])
            + nt_dot(grad_qkv[here, 2 * columns :], wv[...])
        ).astype(jnp.bfloat16)

    for index in range(count):
        first_part(first_line.order(index))
        if index < count - 1:
            first_line.at_time(index)
        if index == count // 2 - 1:
            pace(1)
    total_buf[...] = back[me].astype(jnp.float32)
    weight_grad(att_buf, branch[...].reshape(total, width), 0, columns, width)
    weight_grad(n1_buf, grad_qkv[...], columns * width // lanes, width, columns)
    clock["gap"] = max(clock["time"] - from_ffn, 0)
    pace(1)
    for now in range(count - 1, first_line.times):
        first_line.at_time(now)
        pace(1)
    grad_in, gain_grad = rms_backward(
        x_own[...].astype(jnp.float32), total_buf[...], gains_ref[0:1, :]
    )
    out_buf[1] = (middle_grad[...] + grad_in).astype(jnp.bfloat16)
    input_copy = pltpu.make_async_copy(out_buf.at[1], input_out, out_sems.at[1])
    input_copy.start()
    for owner in range(count):
        small_parts[owner, 0:1, :] = gain_grad[:, owner * part_width : (owner + 1) * part_width]
    small[0:8, :] = small_parts[me]
    for now in range(small_line.times):
        small_line.at_time(now)
        pace(1)
    bucket = lax.broadcasted_iota(jnp.int32, (lanes, ids_ref.shape[1]), 0)
    one_hot = (bucket == ids_ref[...]).astype(jnp.float32).astype(jnp.bfloat16)
    high = offsets[...].astype(jnp.bfloat16)
    rest = offsets[...] - high.astype(jnp.float32)
    middle_part = rest.astype(jnp.bfloat16)
    low_part = (rest - middle_part.astype(jnp.float32)).astype(jnp.bfloat16)
    small[8:16, 0:lanes] = nt_dot(high, one_hot) + nt_dot(middle_part, one_hot) + nt_dot(low_part, one_hot)
    small[8:16, lanes:] = jnp.zeros((8, part_width - lanes), jnp.float32)
    for index, mask in enumerate(masks):
        copy = pltpu.make_async_remote_copy(
            src_ref=small,
            dst_ref=pair_box.at[index],
            send_sem=pair_sems.at[0, index],
            recv_sem=pair_sems.at[1, index],
            device_id={"replica": mine ^ mask},
            device_id_type=MESH,
        )
        copy.start()
        pace(1)
        copy.wait()
        small[...] += pair_box[index]
    small_out[...] = small[...]

    @pl.loop(clock["time"], chunks + clock["gap"] + skew * parts.last_phase)
    def _(now):
        tick(now)

    for line in (res_line, first_line, branch_line, small_line):
        line.wait_sends()
    result_copy.wait()
    input_copy.wait()


def backward(count, replicas, length, flat, back, res, middle, cot, x, q, k, v, att, lse, n1, wq, wk, wv, wo, gains, bias, ids):
    rows, width = middle.shape
    total = count * rows
    columns = wq.shape[1]
    bf, f32 = jnp.bfloat16, jnp.float32
    shape = jax.ShapeDtypeStruct
    steps = count - 1
    dma = pltpu.SemaphoreType.DMA
    chunk = flat.shape[0] // 15
    attn_rows = 4 * columns * width // lanes
    skew, subs = 3, 2
    levels = replicas.bit_length() - 2
    masks = levels + 1
    depth = skew * (levels + 2)
    part_width = width // count
    vmem = pltpu.VMEM
    blocks = lambda kind: vmem((count, rows, width), kind)
    narrow = lambda: vmem((count, rows, columns), bf)
    boxes = lambda: vmem((count + 1, rows, width), bf)
    return pl.pallas_call(
        functools.partial(
            backward_kernel, count, replicas, chunk, attn_rows // chunk, skew, subs
        ),
        name="backward",
        out_shape=(
            shape((flat.shape[0] + attn_rows, lanes), bf),
            shape((attn_rows, lanes), bf),
            shape((rows, width), bf),
            shape((rows, width), bf),
            shape((16, part_width), f32),
        ),
        in_specs=[smem_space] + [any_space] * 16 + [vmem_space] * 3,
        out_specs=[any_space] * 4 + [vmem_space],
        scratch_shapes=[
            blocks(bf), blocks(bf), vmem((rows, width), f32), vmem((rows, width), bf), vmem((rows, width), bf),
            narrow(), narrow(), narrow(), narrow(), vmem((count, rows, lanes), f32), blocks(bf),
            vmem(wq.shape, bf), vmem(wk.shape, bf), vmem(wv.shape, bf), vmem(wo.shape, bf),
            boxes(), boxes(), vmem((rows, width), f32), vmem((rows, width), f32), vmem((rows, width), f32), blocks(bf),
            narrow(),
            vmem((lanes, total), f32), vmem((lanes, total), f32), vmem((total, 3 * columns), bf),
            vmem((total, total), bf), vmem((8, 2 * total), f32), vmem((256, total), bf),
            vmem((2, width // lanes, 256, lanes), bf), vmem((2, rows, width), bf),
            vmem((16, part_width), f32), vmem((count, 8, part_width), f32), vmem((count + 1, 8, part_width), f32),
            vmem((masks, 16, part_width), f32),
            vmem((depth, chunk // 2, lanes), bf), vmem((2 * skew, chunk // 2, lanes), bf),
            vmem((2 * skew, 2, chunk // 4, lanes), bf),
            dma((15,)), dma((2, 2, steps * subs)), dma((2, 2, steps * subs)), dma((2, 2, steps * subs)),
            dma((2, 2, steps * subs)),
            dma((2, 2, steps)), dma((2, masks)), dma((2, width // lanes)), dma((2,)),
            dma((2, 2 * levels + 3, 3, 2 * skew)),
        ],
        compiler_params=pltpu.CompilerParams(
            collective_id=2, has_side_effects=True, vmem_limit_bytes=61 * 2**20
        ),
    )(length, flat, back, res, middle, cot, x, q, k, v, att, lse, n1, wq, wk, wv, wo, gains, bias, ids)


def widen_kernel(source, target):
    target[...] = source[...].astype(jnp.float32)


def widen(sums, start, shape):
    height, depth = shape
    return pl.pallas_call(
        widen_kernel,
        name="widen",
        out_shape=jax.ShapeDtypeStruct(shape, jnp.float32),
        grid=(depth // lanes,),
        in_specs=[pl.BlockSpec((height, lanes), lambda index: (start // height + index, 0))],
        out_specs=pl.BlockSpec((height, lanes), lambda index: (0, index)),
        compiler_params=pltpu.CompilerParams(vmem_limit_bytes=32 * 2**20),
    )(sums)


def widen_tall_kernel(bounds, source, *targets):
    index = pl.program_id(0)
    for target, (first, last) in zip(targets, bounds):
        @pl.when((index >= first) & (index < last))
        def _():
            target[...] = source[...].astype(jnp.float32)


def widen_tall(sums, start, weights, skipped):
    height = weights[0].shape[0]
    bounds, first = [], 0
    for weight in weights:
        panels = weight.shape[1] // lanes
        bounds.append((first, first + panels))
        first += panels
    split, jump, base = bounds[2][0], skipped // height, start // height

    def out_spec(low, high):
        return pl.BlockSpec(
            (height, lanes), lambda index: (0, jnp.clip(index - low, 0, high - low - 1))
        )

    return pl.pallas_call(
        functools.partial(widen_tall_kernel, bounds),
        name="widen_tall",
        out_shape=[jax.ShapeDtypeStruct(weight.shape, jnp.float32) for weight in weights],
        grid=(first,),
        in_specs=[
            pl.BlockSpec(
                (height, lanes),
                lambda index: (base + index + jnp.where(index >= split, jump, 0), 0),
            )
        ],
        out_specs=[out_spec(low, high) for low, high in bounds],
        compiler_params=pltpu.CompilerParams(vmem_limit_bytes=48 * 2**20),
    )(sums)


def local(
    inputs,
    seq_lengths,
    bucket_ids,
    norm1_gain,
    w_query,
    w_key,
    w_value,
    w_attn_out,
    bias_table,
    norm2_gain,
    w_gate,
    w_up,
    w_ffn_out,
    cotangent,
):
    count = lax.axis_size("group")
    replicas = lax.axis_size("replica")
    gains_local = jnp.pad(
        jnp.stack([norm1_gain, norm2_gain]).astype(jnp.float32), ((0, 6), (0, 0))
    )
    ids = jnp.pad(bucket_ids, (0, 1))[None, :]
    ids_back = jnp.pad(bucket_ids[::-1], (0, 1), constant_values=-1)[None, :]
    normed_one, query, key, value, attended, log_totals, g_all, middle, normed_two, gains, bias = (
        attention_forward(
            count, seq_lengths, inputs[0], cotangent[0], gains_local,
            w_query, w_key, w_value, w_attn_out, ids, bias_table.T,
        )
    )
    flat, back_part, result_part = feed_forward(
        count, seq_lengths, normed_two, g_all, w_gate, w_up, w_ffn_out
    )
    sums, _, result, input_grad, small = backward(
        count, replicas, seq_lengths, flat, back_part, result_part, middle, cotangent[0], inputs[0],
        query, key, value, attended, log_totals, normed_one,
        w_query, w_key, w_value, w_attn_out, gains, bias, ids_back,
    )
    gate_grad, up_grad, query_grad, key_grad, value_grad = widen_tall(
        sums, w_ffn_out.size // lanes, (w_gate, w_up, w_query, w_key, w_value), w_attn_out.size // lanes
    )
    ffn_out_grad = widen(sums, 0, w_ffn_out.shape)
    attn_out_grad = widen(sums, (3 * w_gate.size) // lanes, w_attn_out.shape)
    buckets, local_heads = bias_table.shape
    table_grad = small[8 : 8 + local_heads, :buckets].T
    return (
        result[None],
        input_grad[None],
        small[0],
        query_grad,
        key_grad,
        value_grad,
        attn_out_grad,
        table_grad,
        small[1],
        gate_grad,
        up_grad,
        ffn_out_grad,
    )


def solution(mesh):
    placed = (
        P("replica", "group", None),
        P("replica"),
        P(),
        P("group"),
        P(None, "group"),
        P(None, "group"),
        P(None, "group"),
        P("group", None),
        P(None, "group"),
        P("group"),
        P(None, "group"),
        P(None, "group"),
        P("group", None),
        P("replica", "group", None),
    )
    return jax.shard_map(
        local,
        mesh=mesh,
        in_specs=placed,
        out_specs=(
            P("replica", "group", None),
            P("replica", "group", None),
            P("group"),
            P(None, "group"),
            P(None, "group"),
            P(None, "group"),
            P("group", None),
            P(None, "group"),
            P("group"),
            P(None, "group"),
            P(None, "group"),
            P("group", None),
        ),
        check_vma=False,
    )
```

```python
import functools
import jax
import jax.numpy as jnp
from jax import lax
from jax.experimental import pallas as pl
from jax.experimental.pallas import tpu as pltpu
from jax.sharding import PartitionSpec as P

epsilon = 1e-06
negative = -1000000000.0
head_dim = 64
lanes = 128
MESH = pl.DeviceIdType.MESH
any_space = pl.BlockSpec(memory_space=pl.ANY)
vmem_space = pl.BlockSpec(memory_space=pltpu.VMEM)
smem_space = pl.BlockSpec(memory_space=pltpu.SMEM)


def nn_dot(left, right):
    return jnp.dot(left, right, preferred_element_type=jnp.float32)


def nt_dot(left, right):
    return lax.dot_general(
        left, right, (((1,), (1,)), ((), ())), preferred_element_type=jnp.float32
    )


def line_barrier(me, count):
    barrier = pltpu.get_barrier_semaphore()

    @pl.when(me > 0)
    def _():
        pl.semaphore_signal(barrier, inc=1, device_id={"group": me - 1}, device_id_type=MESH)

    @pl.when(me < count - 1)
    def _():
        pl.semaphore_signal(barrier, inc=1, device_id={"group": me + 1}, device_id_type=MESH)

    peers = jnp.where(me > 0, 1, 0) + jnp.where(me < count - 1, 1, 0)
    pl.semaphore_wait(barrier, peers)


class LineGather:
    def __init__(self, me, count, buffer, sems, subs=1):
        self.me, self.count, self.buffer, self.sems, self.subs = me, count, buffer, sems, subs
        self.pieces = (count - 1) * subs
        self.size = buffer.shape[1] // subs

    def copy(self, side, piece, hops):
        block = self.me - hops if side == 0 else self.me + hops
        here = self.buffer.at[block, pl.ds(piece % self.subs * self.size, self.size)]
        return pltpu.make_async_remote_copy(
            src_ref=here,
            dst_ref=here,
            send_sem=self.sems.at[side, 0, piece],
            recv_sem=self.sems.at[side, 1, piece],
            device_id={"group": self.me + (1 if side == 0 else -1)},
            device_id_type=MESH,
        )

    def sends(self, side, piece):
        hops = piece // self.subs
        if side == 0:
            return (self.me - hops >= 0) & (self.me + 1 < self.count)
        return (self.me + hops < self.count) & (self.me >= 1)

    def arrives(self, side, piece):
        hops = piece // self.subs
        if side == 0:
            return self.me - 1 - hops >= 0
        return self.me + 1 + hops < self.count

    def send_side(self, side, piece):
        @pl.when(self.sends(side, piece))
        def _():
            self.copy(side, piece, piece // self.subs).start()

    def send(self, piece):
        for side in range(2):
            self.send_side(side, piece)

    def begin(self):
        for piece in range(self.subs):
            self.send(piece)

    def arrive(self, piece):
        for side in range(2):
            @pl.when(self.arrives(side, piece))
            def _():
                self.copy(side, piece, piece // self.subs + 1).wait_recv()

        if piece + self.subs < self.pieces:
            self.send(piece + self.subs)

    def arrive_block(self, hops, body):
        for piece in range(hops * self.subs, (hops + 1) * self.subs):
            self.arrive(piece)
        self.each_block(hops, body)

    def each_block(self, hops, body):
        @pl.loop(0, 2)
        def _(side):
            block = jnp.where(side == 0, self.me - 1 - hops, self.me + 1 + hops)

            @pl.when((block >= 0) & (block < self.count))
            def _():
                body(block)

    def wait_sends(self):
        for piece in range(self.pieces):
            for side in range(2):
                @pl.when(self.sends(side, piece))
                def _():
                    self.copy(side, piece, piece // self.subs).wait_send()


class LineScatter:
    def __init__(self, me, count, parts, inbox, total, sems, subs=1):
        self.me, self.count, self.parts, self.inbox = me, count, parts, inbox
        self.total, self.sems, self.subs = total, sems, subs
        self.times = (count - 1) * subs + 1
        self.size = parts.shape[1] // subs

    def order(self, index):
        picked = 0
        for device in range(self.count):
            due = [(step * self.subs + self.count - 1 - device, step) for step in range(device)]
            due += [
                (step * self.subs + device, self.count - 1 - step)
                for step in range(self.count - 1 - device)
            ]
            blocks = [block for _, block in sorted(due)] + [device]
            picked = picked + jnp.where(self.me == device, blocks[index], 0)
        return picked

    def copy(self, side, piece):
        step = piece // self.subs
        here = pl.ds(pl.multiple_of(piece % self.subs * self.size, self.size), self.size)
        owner = step if side == 0 else self.count - 1 - step
        return pltpu.make_async_remote_copy(
            src_ref=self.parts.at[owner, here],
            dst_ref=self.inbox.at[self.slot(side, step), here],
            send_sem=self.sems.at[side, 0, piece],
            recv_sem=self.sems.at[side, 1, piece],
            device_id={"group": self.me + (-1 if side == 0 else 1)},
            device_id_type=MESH,
        )

    def slot(self, side, step):
        return step if side == 0 else self.count - step

    def at_time(self, time):
        for side in range(2):
            before = self.count - 1 - self.me if side == 0 else self.me
            after = self.count - 1 - before
            piece = time - before
            step = piece // self.subs

            @pl.when((piece >= 0) & (step < after))
            def _():
                owner = step if side == 0 else self.count - 1 - step
                here = pl.ds(pl.multiple_of(piece % self.subs * self.size, self.size), self.size)

                @pl.when(before > 0)
                def _():
                    self.copy(side, piece).wait_recv()
                    self.parts[owner, here, :] = (
                        self.parts[owner, here, :].astype(jnp.float32)
                        + self.inbox[self.slot(side, step), here, :].astype(jnp.float32)
                    ).astype(self.parts.dtype)

                self.copy(side, piece).start()

            @pl.when((piece >= 0) & (step == after) & (before > 0))
            def _():
                here = pl.ds(pl.multiple_of(piece % self.subs * self.size, self.size), self.size)
                self.copy(side, piece).wait_recv()
                self.total[here, :] += self.inbox[self.slot(side, step), here, :].astype(jnp.float32)

    def wait_sends(self):
        for piece in range((self.count - 1) * self.subs):
            step = piece // self.subs
            for side in range(2):
                after = self.me if side == 0 else self.count - 1 - self.me

                @pl.when(step < after)
                def _():
                    self.copy(side, piece).wait_send()


def head_masks():
    lane = lax.broadcasted_iota(jnp.int32, (1, lanes), 1)
    first = (lane < head_dim).astype(jnp.float32)
    return first.astype(jnp.bfloat16), (1.0 - first).astype(jnp.bfloat16)


def offset_bias(bias_ref, head, row_start, rows, total):
    width = bias_ref.shape[1]
    shift = lax.rem(row_start + (width - (total - 1)), width)
    vector = pltpu.roll(jnp.broadcast_to(bias_ref[pl.ds(head, 1), :], (8, width)), shift, 1)
    vector = jnp.broadcast_to(vector[0:1, :], (rows, width))
    return pltpu.roll(vector, 0, 1, stride=1, stride_axis=0)[:, :total]


def rms_rows(values):
    return lax.rsqrt(jnp.mean(values * values, axis=-1, keepdims=True) + epsilon)


def attention_forward_kernel(
    count, subs,
    length_ref,
    x_hbm, cot_hbm, gains_hbm, wq_hbm, wk_hbm, wv_hbm, wo_hbm, ids_ref, table_ref,
    n1_out, q_out, k_out, v_out, att_out, lse_out, cot_out, middle_out, n2_out, gains_out, bias_out,
    x_all, gains_all, wq, wk, wv, wo, parts, inbox, n1_buf, q_buf, k_buf, v_buf, att_buf, lse_buf, total_buf, n2_buf,
    local_sems, x_sems, g_sems, c_sems, s_sems, out_sems,
):
    me = lax.axis_index("group")
    rows, width = x_hbm.shape
    total = rows * count
    columns = wq.shape[1]
    local_heads = columns // head_dim
    loads = [
        pltpu.make_async_copy(source, target, local_sems.at[index])
        for index, (source, target) in enumerate(
            [
                (x_hbm, x_all.at[me]),
                (gains_hbm, gains_all.at[me]),
                (wq_hbm, wq),
                (wk_hbm, wk),
                (wv_hbm, wv),
                (wo_hbm, wo),
                (cot_hbm, cot_out.at[me]),
            ]
        )
    ]
    for load in loads:
        load.start()
    line_barrier(me, count)
    x_line = LineGather(me, count, x_all, x_sems, subs)
    g_line = LineGather(me, count, gains_all, g_sems)
    c_line = LineGather(me, count, cot_out, c_sems, subs)
    loads[1].wait()
    g_line.begin()
    loads[0].wait()
    x_line.begin()

    bucket = lax.broadcasted_iota(jnp.int32, (table_ref.shape[1], ids_ref.shape[1]), 0)
    one_hot = (bucket == ids_ref[...]).astype(jnp.float32).astype(jnp.bfloat16)
    bias_out[...] = nn_dot(table_ref[...], one_hot)

    for piece in range(g_line.pieces):
        g_line.arrive(piece)
    for owner in range(count):
        gains_out[:, owner * (width // count) : (owner + 1) * (width // count)] = gains_all[owner]
    for load in loads[2:5]:
        load.wait()

    def project(block):
        values = x_all[block].astype(jnp.float32)
        normed = (values * rms_rows(values) * gains_out[0:1, :]).astype(jnp.bfloat16)
        n1_buf[block] = normed
        q_buf[block] = nn_dot(normed, wq[...]).astype(jnp.bfloat16)
        k_buf[block] = nn_dot(normed, wk[...]).astype(jnp.bfloat16)
        v_buf[block] = nn_dot(normed, wv[...]).astype(jnp.bfloat16)

    def begin_cotangent(sent):
        for side in range(2):
            last = me if side == 0 else count - 1 - me

            @pl.when(last == sent)
            def _():
                for piece in range(subs):
                    c_line.send_side(side, piece)

    loads[6].wait()
    begin_cotangent(0)
    for piece in range(subs):
        x_line.arrive(piece)
    begin_cotangent(1)
    project(me)
    x_line.each_block(0, project)
    for hops in range(1, count - 1):
        for piece in range(hops * subs, (hops + 1) * subs):
            x_line.arrive(piece)
        begin_cotangent(hops + 1)
        x_line.each_block(hops, project)

    loads[5].wait()
    mask_first, mask_second = head_masks()
    key_valid = lax.broadcasted_iota(jnp.int32, (1, total), 1) < length_ref[0]
    lane = lax.broadcasted_iota(jnp.int32, (1, lanes), 1)

    def attend(block):
        lse_buf[block] = jnp.zeros((rows, lanes), jnp.float32)

        @pl.loop(0, local_heads // 2)
        def _(pair):
            cols = pl.ds(pl.multiple_of(pair * lanes, lanes), lanes)
            query = q_buf[block, :, cols]
            key = k_buf[:, :, cols].reshape(total, lanes)
            value = v_buf[:, :, cols].reshape(total, lanes)
            outs = []
            for half, mask in enumerate((mask_first, mask_second)):
                head = pair * 2 + half
                scores = nt_dot(query * mask, key)
                scores = scores + offset_bias(bias_out, head, block * rows, rows, total)
                scores = jnp.where(key_valid, scores, negative)
                top = jnp.max(scores, axis=-1, keepdims=True)
                expd = jnp.exp(scores - top)
                summed = jnp.sum(expd, axis=-1, keepdims=True)
                probs = (expd * (1.0 / summed)).astype(jnp.bfloat16)
                outs.append(nn_dot(probs, value))
                lse_buf[block] = jnp.where(lane == head, top + jnp.log(summed), lse_buf[block])
            att_buf[block, :, cols] = jnp.where(lane < head_dim, outs[0], outs[1]).astype(
                jnp.bfloat16
            )

    scatter = LineScatter(me, count, parts, inbox, total_buf, s_sems, subs)
    arrived = 0
    for index in range(count - 1):
        block = scatter.order(index)
        attend(block)
        parts[block] = nn_dot(att_buf[block], wo[...]).astype(jnp.bfloat16)
        scatter.at_time(index)
        if index:
            c_line.arrive(arrived)
            arrived += 1
    attend(me)
    total_buf[...] = x_all[me].astype(jnp.float32) + nn_dot(att_buf[me], wo[...])
    outs = [
        pltpu.make_async_copy(source, target, out_sems.at[index])
        for index, (source, target) in enumerate(
            [(n1_buf, n1_out), (q_buf, q_out), (k_buf, k_out), (v_buf, v_out), (att_buf, att_out), (lse_buf, lse_out)]
        )
    ]
    for copy in outs:
        copy.start()
    for time in range(count - 1, scatter.times):
        scatter.at_time(time)
        if arrived < c_line.pieces:
            c_line.arrive(arrived)
            arrived += 1
    middle = total_buf[...]
    n2_buf[...] = (middle * rms_rows(middle) * gains_out[1:2, :]).astype(jnp.bfloat16)
    tail = [
        pltpu.make_async_copy(total_buf, middle_out, out_sems.at[len(outs)]),
        pltpu.make_async_copy(n2_buf, n2_out, out_sems.at[len(outs) + 1]),
    ]
    for copy in tail:
        copy.start()
    for piece in range(arrived, c_line.pieces):
        c_line.arrive(piece)
    for line in (g_line, x_line, c_line, scatter):
        line.wait_sends()
    for copy in outs + tail:
        copy.wait()


def attention_forward(count, length, x, cot, gains, wq, wk, wv, wo, ids, table):
    rows, width = x.shape
    columns = wq.shape[1]
    local_heads = columns // head_dim
    bf, f32 = jnp.bfloat16, jnp.float32
    shape = jax.ShapeDtypeStruct
    steps = count - 1
    subs = 2
    dma = pltpu.SemaphoreType.DMA
    return pl.pallas_call(
        functools.partial(attention_forward_kernel, count, subs),
        name="attention_forward",
        out_shape=(
            shape((count, rows, width), bf),
            shape((count, rows, columns), bf),
            shape((count, rows, columns), bf),
            shape((count, rows, columns), bf),
            shape((count, rows, columns), bf),
            shape((count, rows, lanes), f32),
            shape((count, rows, width), bf),
            shape((rows, width), f32),
            shape((rows, width), bf),
            shape((8, width), f32),
            shape((local_heads, ids.shape[1]), f32),
        ),
        in_specs=[smem_space] + [any_space] * 7 + [vmem_space] * 2,
        out_specs=[any_space] * 9 + [vmem_space] * 2,
        scratch_shapes=[
            pltpu.VMEM((count, rows, width), bf),
            pltpu.VMEM((count,) + gains.shape, f32),
            pltpu.VMEM(wq.shape, bf),
            pltpu.VMEM(wk.shape, bf),
            pltpu.VMEM(wv.shape, bf),
            pltpu.VMEM(wo.shape, bf),
            pltpu.VMEM((count, rows, width), bf),
            pltpu.VMEM((count + 1, rows, width), bf),
            pltpu.VMEM((count, rows, width), bf),
            pltpu.VMEM((count, rows, columns), bf),
            pltpu.VMEM((count, rows, columns), bf),
            pltpu.VMEM((count, rows, columns), bf),
            pltpu.VMEM((count, rows, columns), bf),
            pltpu.VMEM((count, rows, lanes), f32),
            pltpu.VMEM((rows, width), f32),
            pltpu.VMEM((rows, width), bf),
            dma((7,)),
            dma((2, 2, steps * subs)),
            dma((2, 2, steps)),
            dma((2, 2, steps * subs)),
            dma((2, 2, steps * subs)),
            dma((8,)),
        ],
        compiler_params=pltpu.CompilerParams(
            collective_id=0, has_side_effects=True, vmem_limit_bytes=56 * 2**20
        ),
    )(length, x, cot, gains, wq, wk, wv, wo, ids, table)


def gelu_parts(gate):
    root = 0.7978845608028654
    inner = root * (gate + 0.044715 * gate * gate * gate)
    tanh = jnp.tanh(inner)
    half = 0.5 * (1.0 + tanh)
    slope = half + 0.5 * gate * (1.0 - tanh * tanh) * root * (1.0 + 3 * 0.044715 * gate * gate)
    return gate * half, slope


def feed_forward_kernel(
    count, tile, subs,
    length_ref,
    n2_hbm, cot_hbm, wg_hbm, wu_hbm, wf_hbm,
    flat_out, back_out, res_out,
    n2_all, g_all, wg, wu, wf, hid, grad_gate, grad_up, back_buf, res_buf, turned, stage,
    local_sems, n_sems, out_sems, stage_sems,
):
    me = lax.axis_index("group")
    rows, width = n2_hbm.shape
    total = rows * count
    units = wg.shape[1]
    loads = [
        pltpu.make_async_copy(source, target, local_sems.at[index])
        for index, (source, target) in enumerate(
            [(n2_hbm, n2_all.at[me]), (wg_hbm, wg), (wu_hbm, wu), (wf_hbm, wf), (cot_hbm, g_all)]
        )
    ]
    for load in loads:
        load.start()
    line_barrier(me, count)
    line = LineGather(me, count, n2_all, n_sems, subs)
    loads[0].wait()
    line.begin()
    for load in loads[1:]:
        load.wait()

    def mask_rows(block):
        position = block * rows + lax.broadcasted_iota(jnp.int32, (rows, 1), 0)
        valid = (position < length_ref[0]).astype(jnp.float32).astype(jnp.bfloat16)
        g_all[block] = g_all[block] * valid

    def block_pass(block):
        mask_rows(block)
        normed = n2_all[block]
        grads = g_all[block]

        @pl.loop(0, units // tile)
        def _(index):
            cols = pl.ds(pl.multiple_of(index * tile, tile), tile)
            gate = nn_dot(normed, wg[:, cols])
            up = nn_dot(normed, wu[:, cols])
            grad_hidden = nt_dot(grads, wf[cols, :])
            act, slope = gelu_parts(gate)
            hid[block, :, cols] = (act * up).astype(jnp.bfloat16)
            grad_gate[block, :, cols] = (grad_hidden * up * slope).astype(jnp.bfloat16)
            grad_up[block, :, cols] = (grad_hidden * act).astype(jnp.bfloat16)

        chunk = 2 * tile

        @pl.loop(0, width // chunk)
        def _(index):
            cols = pl.ds(pl.multiple_of(index * chunk, chunk), chunk)
            back_buf[block, :, cols] = (
                nt_dot(grad_gate[block], wg[cols, :]) + nt_dot(grad_up[block], wu[cols, :])
            ).astype(jnp.bfloat16)
            res_buf[block, :, cols] = nn_dot(hid[block], wf[:, cols]).astype(jnp.bfloat16)

    block_pass(me)
    for hops in range(count - 1):
        line.arrive_block(hops, block_pass)
    outs = [
        pltpu.make_async_copy(back_buf, back_out, out_sems.at[0]),
        pltpu.make_async_copy(res_buf, res_out, out_sems.at[1]),
    ]
    for copy in outs:
        copy.start()

    def weight_grad(left, right, base, height):
        depth = right.shape[2]
        panels = depth // lanes
        factor = right[...].reshape(total, depth)

        def store(slot, panel, row):
            return pltpu.make_async_copy(
                stage.at[slot, panel],
                flat_out.at[pl.ds(base + panel * height + row, tile)],
                stage_sems.at[slot, panel],
            )

        @pl.loop(0, height // tile)
        def _(index):
            slot = lax.rem(index, 2)
            row = pl.multiple_of(index * tile, tile)
            turned[...] = left[:, :, pl.ds(row, tile)].reshape(total, tile).T
            product = nn_dot(turned[...], factor).astype(jnp.bfloat16)

            @pl.when(index >= 2)
            def _():
                for panel in range(panels):
                    store(slot, panel, row).wait()

            for panel in range(panels):
                stage[slot, panel] = product[:, panel * lanes : (panel + 1) * lanes]
                store(slot, panel, row).start()

        for slot in range(2):
            for panel in range(panels):
                store(slot, panel, 0).wait()

    weight_grad(hid, g_all, 0, units)
    weight_grad(n2_all, grad_gate, units * width // lanes, width)
    weight_grad(n2_all, grad_up, 2 * units * width // lanes, width)
    line.wait_sends()
    for copy in outs:
        copy.wait()


def feed_forward(count, length, n2, cot, wg, wu, wf):
    rows, width = n2.shape
    units = wg.shape[1]
    tile = 128 if units % 256 else 256
    bf = jnp.bfloat16
    shape = jax.ShapeDtypeStruct
    steps = count - 1
    subs = 2
    dma = pltpu.SemaphoreType.DMA
    return pl.pallas_call(
        functools.partial(feed_forward_kernel, count, tile, subs),
        name="feed_forward",
        out_shape=(
            shape((3 * units * width // lanes, lanes), bf),
            shape((count, rows, width), bf),
            shape((count, rows, width), bf),
        ),
        in_specs=[smem_space] + [any_space] * 5,
        out_specs=[any_space] * 3,
        scratch_shapes=[
            pltpu.VMEM((count, rows, width), bf),
            pltpu.VMEM((count, rows, width), bf),
            pltpu.VMEM(wg.shape, bf),
            pltpu.VMEM(wu.shape, bf),
            pltpu.VMEM(wf.shape, bf),
            pltpu.VMEM((count, rows, units), bf),
            pltpu.VMEM((count, rows, units), bf),
            pltpu.VMEM((count, rows, units), bf),
            pltpu.VMEM((count, rows, width), bf),
            pltpu.VMEM((count, rows, width), bf),
            pltpu.VMEM((tile, count * rows), bf),
            pltpu.VMEM((2, max(width, units) // lanes, tile, lanes), bf),
            dma((5,)),
            dma((2, 2, steps * subs)),
            dma((2,)),
            dma((2, max(width, units) // lanes)),
        ],
        compiler_params=pltpu.CompilerParams(
            collective_id=1, has_side_effects=True, vmem_limit_bytes=56 * 2**20
        ),
    )(length, n2, cot, wg, wu, wf)


def when(condition, body):
    if isinstance(condition, bool):
        if condition:
            body()
    else:
        pl.when(condition)(body)


class ReplicaSum:
    def __init__(self, replicas, chunk, source, target, work, core_box, path_box, sems):
        self.mine = lax.axis_index("replica")
        self.chunk, self.source, self.target = chunk, source, target
        self.work, self.core_box, self.path_box, self.sems = work, core_box, path_box, sems
        self.depth, self.slots = work.shape[0], core_box.shape[0]
        bits = [1 << index for index in range(1, replicas.bit_length() - 1)]
        self.orders = (bits, bits[::-1])
        self.levels = len(bits)
        self.last_phase = 2 * self.levels + 2
        self.half = chunk // 2

    def bit(self, mask):
        return jnp.where((self.mine & mask) != 0, 1, 0)

    def region(self, path, level):
        size = self.half // 2
        offset = path * size
        for mask in self.orders[path][:level]:
            size //= 2
            offset = offset + self.bit(mask) * size
        return offset, size

    def out_rows(self, chunk, offset, size):
        start = chunk * self.chunk + self.bit(1) * self.half + offset
        return self.target.at[pl.ds(pl.multiple_of(start, 16), size)]

    def sem(self, kind, phase, path, chunk):
        return self.sems.at[kind, phase, path, chunk % self.slots]

    def remote(self, source, target, phase, path, chunk, mask):
        return pltpu.make_async_remote_copy(
            src_ref=source,
            dst_ref=target,
            send_sem=self.sem(0, phase, path, chunk),
            recv_sem=self.sem(1, phase, path, chunk),
            device_id={"replica": self.mine ^ mask},
            device_id_type=MESH,
        )

    def core_copy(self, chunk):
        start = chunk * self.chunk + (1 - self.bit(1)) * self.half
        return self.remote(
            self.source(start, self.half), self.core_box.at[chunk % self.slots], 0, 0, chunk, 1
        )

    def load_copy(self, chunk):
        start = chunk * self.chunk + self.bit(1) * self.half
        return pltpu.make_async_copy(
            self.source(start, self.half), self.work.at[chunk % self.depth], self.sem(0, 0, 1, chunk)
        )

    def reduce_copy(self, chunk, path, level):
        mask = self.orders[path][level - 1]
        offset, size = self.region(path, level - 1)
        size //= 2
        start = pl.multiple_of(offset + (1 - self.bit(mask)) * size, 16)
        return self.remote(
            self.work.at[chunk % self.depth, pl.ds(start, size)],
            self.box(chunk, path, level),
            level, path, chunk, mask,
        )

    def box(self, chunk, path, level):
        size = self.half // 2 >> level
        start = sum(self.half // 2 >> step for step in range(1, level))
        return self.path_box.at[chunk % self.slots, path, pl.ds(start, size)]

    def add_box(self, chunk, path, level):
        offset, size = self.region(path, level)
        here = pl.ds(pl.multiple_of(offset, 16), size)
        slot = chunk % self.depth
        self.work[slot, here, :] = self.work[slot, here, :] + self.box(chunk, path, level)[...]

    def own_copy(self, chunk, path):
        offset, size = self.region(path, self.levels)
        return pltpu.make_async_copy(
            self.work.at[chunk % self.depth, pl.ds(pl.multiple_of(offset, 16), size)],
            self.out_rows(chunk, offset, size),
            self.sems.at[1, 0, 1 + path, chunk % self.slots],
        )

    def spread_copy(self, chunk, path, level):
        offset, size = self.region(path, level)
        if level == self.levels:
            source = self.work.at[chunk % self.depth, pl.ds(pl.multiple_of(offset, 16), size)]
        else:
            source = self.out_rows(chunk, offset, size)
        return self.remote(
            source, self.out_rows(chunk, offset, size),
            2 * self.levels + 1 - level, path, chunk, self.orders[path][level - 1],
        )

    def share_copy(self, chunk):
        rows = self.out_rows(chunk, 0, self.half)
        return self.remote(rows, rows, self.last_phase - 1, 0, chunk, 1)

    def advance(self, phase, chunk):
        levels = self.levels
        if phase == 0:
            self.core_copy(chunk).start()
            self.load_copy(chunk).start()
        elif phase <= levels + 1:
            if phase == 1:
                self.load_copy(chunk).wait()
                self.core_copy(chunk).wait()
                slot = chunk % self.depth
                self.work[slot] = self.work[slot] + self.core_box[chunk % self.slots]
            for path in range(2):
                if phase > 1:
                    self.reduce_copy(chunk, path, phase - 1).wait()
                    self.add_box(chunk, path, phase - 1)
                if phase <= levels:
                    self.reduce_copy(chunk, path, phase).start()
                else:
                    self.own_copy(chunk, path).start()
                    self.spread_copy(chunk, path, levels).start()
        else:
            level = 2 * levels + 1 - phase
            if level >= 0:
                for path in range(2):
                    self.spread_copy(chunk, path, level + 1).wait()
                    if level + 1 == levels:
                        self.own_copy(chunk, path).wait()
                    if level >= 1:
                        self.spread_copy(chunk, path, level).start()
                if level == 0:
                    self.share_copy(chunk).start()


scatter_pace, both_pace, pair_pace = 1.0, 1.0, 0.5


def rms_backward(values, grads, gain):
    scale = rms_rows(values)
    unit = values * scale
    scaled = grads * gain
    inner = jnp.mean(scaled * unit, axis=-1, keepdims=True)
    return scale * (scaled - unit * inner), jnp.sum(grads * unit, axis=0, keepdims=True)


def backward_kernel(
    count, replicas, chunk, attn_chunks, skew, subs,
    length_ref,
    flat_hbm, back_hbm, res_hbm, middle_hbm, cot_hbm, x_hbm, q_hbm, k_hbm, v_hbm, att_hbm, lse_hbm, n1_hbm,
    wq_hbm, wk_hbm, wv_hbm, wo_hbm, gains_ref, bias_ref, ids_ref,
    sums_out, flat_out, result_out, input_out, small_out,
    back, res, middle, cot, x_own, q_buf, k_buf, v_buf, att_buf, lse_buf, n1_buf, wq, wk, wv, wo,
    back_box, res_box, total_buf, res_total, middle_grad, branch, grad_att, key_acc, value_acc, grad_qkv,
    reverse, offsets, turned, stage, out_buf, small, small_parts, small_box, pair_box,
    work, core_box, path_box,
    load_sems, b_sems, r_sems, f_sems, a_sems, p_sems, pair_sems, stage_sems, out_sems, sum_sems,
):
    me = lax.axis_index("group")
    mine = lax.axis_index("replica")
    rows, width = middle.shape
    total = rows * count
    columns = wq.shape[1]
    local_heads = columns // head_dim
    sources = [
        back_hbm, res_hbm, middle_hbm, cot_hbm, x_hbm, wo_hbm, att_hbm, q_hbm, k_hbm, v_hbm, lse_hbm, n1_hbm,
        wq_hbm, wk_hbm, wv_hbm,
    ]
    targets = [
        back, res, middle, cot, x_own, wo, att_buf, q_buf, k_buf, v_buf, lse_buf, n1_buf, wq, wk, wv
    ]
    loads = [
        pltpu.make_async_copy(source, target, load_sems.at[index])
        for index, (source, target) in enumerate(zip(sources, targets))
    ]
    masks = [1 << index for index in range(replicas.bit_length() - 1)]
    barrier = pltpu.get_barrier_semaphore()

    @pl.when(me > 0)
    def _():
        pl.semaphore_signal(barrier, inc=1, device_id={"group": me - 1}, device_id_type=MESH)

    @pl.when(me < count - 1)
    def _():
        pl.semaphore_signal(barrier, inc=1, device_id={"group": me + 1}, device_id_type=MESH)

    for mask in masks:
        pl.semaphore_signal(barrier, inc=1, device_id={"replica": mine ^ mask}, device_id_type=MESH)
    peers = jnp.where(me > 0, 1, 0) + jnp.where(me < count - 1, 1, 0) + len(masks)
    for load in loads[:5]:
        load.start()
    pl.semaphore_wait(barrier, peers)

    ffn_rows = flat_hbm.shape[0]
    from_ffn = ffn_rows // chunk
    chunks = from_ffn + attn_chunks

    def make_source(source_ref, base):
        return lambda start, size: source_ref.at[pl.ds(pl.multiple_of(start - base, 16), size)]

    parts = ReplicaSum(replicas, chunk, None, sums_out, work, core_box, path_box, sum_sems)
    from_first, from_second = make_source(flat_hbm, 0), make_source(flat_out, ffn_rows)
    clock = {"time": 0, "gap": None, "credit": 0.0}

    def start_piece(source, piece):
        parts.source = source
        parts.core_copy(piece).start()
        parts.load_copy(piece).start()

    def tick(time):
        gap = clock["gap"]
        for phase in range(parts.last_phase, -1, -1):
            entry = time - skew * phase
            if isinstance(entry, int):
                early = 0 <= entry < from_ffn
                late = gap is not None and from_ffn + gap <= entry < chunks + gap
                piece = entry if early else entry - (gap or 0)
                inside = early or late
            else:
                early = (entry >= 0) & (entry < from_ffn)
                late = (entry >= from_ffn + gap) & (entry < chunks + gap)
                piece = jnp.where(entry < from_ffn, entry, entry - gap)
                inside = early | late

            def body(phase=phase, piece=piece):
                if phase == parts.last_phase:
                    parts.share_copy(piece).wait()
                elif phase:
                    parts.source = lambda start, size: flat_hbm.at[pl.ds(0, size)]
                    parts.advance(phase, piece)

            if phase:
                when(inside, body)
            else:
                when(early, functools.partial(start_piece, from_first, piece))
                when(late, functools.partial(start_piece, from_second, piece))

    def pace(amount):
        clock["credit"] += amount
        while clock["credit"] >= 1:
            tick(clock["time"])
            clock["time"] += 1
            clock["credit"] -= 1

    back_line = LineScatter(me, count, back, back_box, total_buf, b_sems, subs)
    res_line = LineScatter(me, count, res, res_box, res_total, r_sems, subs)
    first_line = LineScatter(me, count, back, back_box, total_buf, f_sems, subs)
    branch_line = LineGather(me, count, branch, a_sems, subs)
    small_line = LineScatter(me, count, small_parts, small_box, small.at[pl.ds(0, 8)], p_sems)

    tick(0)
    for load in loads[5:]:
        load.start()
    loads[0].wait()
    total_buf[...] = back[me].astype(jnp.float32)
    back_line.at_time(0)
    clock["time"] = 1
    pace(2 * skew - 1)
    anti = lax.broadcasted_iota(jnp.int32, (total, total), 0) + lax.broadcasted_iota(
        jnp.int32, (total, total), 1
    )
    reverse[...] = (anti == total - 1).astype(jnp.float32).astype(jnp.bfloat16)
    for now in range(1, back_line.times):
        back_line.at_time(now)
        pace(scatter_pace)
    for load in loads[1:5]:
        load.wait()
    position = me * rows + lax.broadcasted_iota(jnp.int32, (rows, 1), 0)
    valid = (position < length_ref[0]).astype(jnp.float32)
    grad_mid, gain_grad = rms_backward(middle[...], total_buf[...], gains_ref[1:2, :])
    middle_grad[...] = cot[...].astype(jnp.float32) * valid + grad_mid
    branch[me] = middle_grad[...].astype(jnp.bfloat16)
    branch_line.begin()
    res_total[...] = middle[...] + res[me].astype(jnp.float32)
    res_line.at_time(0)
    small_parts[...] = jnp.zeros_like(small_parts)
    part_width = width // count
    for owner in range(count):
        small_parts[owner, 1:2, :] = gain_grad[:, owner * part_width : (owner + 1) * part_width]
    for load in loads[5:]:
        load.wait()

    def attended_grad(block):
        grad_att[block] = nt_dot(branch[block], wo[...]).astype(jnp.bfloat16)

    attended_grad(me)
    pace(both_pace)
    for now in range(1, res_line.times):
        branch_line.arrive(now - 1)
        res_line.at_time(now)
        pace(both_pace)
        if now % subs == 0:
            branch_line.each_block(now // subs - 1, attended_grad)
    out_buf[0] = res_total[...].astype(jnp.bfloat16)
    result_copy = pltpu.make_async_copy(out_buf.at[0], result_out, out_sems.at[0])
    result_copy.start()

    tile = 256

    def weight_grad(left, factor, base, height, per_output):
        panels = factor.shape[1] // lanes
        per_panel = per_output // lanes

        def store(slot, panel, row):
            return pltpu.make_async_copy(
                stage.at[slot, panel],
                flat_out.at[pl.ds(base + panel * height + row, tile)],
                stage_sems.at[slot, panel],
            )

        @pl.loop(0, height // tile)
        def _(index):
            slot = lax.rem(index, 2)
            row = pl.multiple_of(index * tile, tile)
            turned[...] = left[:, :, pl.ds(row, tile)].reshape(total, tile).T
            product = nn_dot(turned[...], factor).astype(jnp.bfloat16)

            @pl.when(index >= 2)
            def _():
                for panel in range(panels):
                    store(slot, panel, row).wait()

            for panel in range(panels):
                stage[slot, panel] = product[:, panel * lanes : (panel + 1) * lanes]
                store(slot, panel, row).start()

        for slot in range(min(2, height // tile)):
            for panel in range(panels):
                store(slot, panel, 0).wait()

    mask_first, mask_second = head_masks()
    key_valid = lax.broadcasted_iota(jnp.int32, (1, total), 1) < length_ref[0]
    lane = lax.broadcasted_iota(jnp.int32, (1, lanes), 1)
    offsets[...] = jnp.zeros_like(offsets)

    def head_pair(pair):
        cols = pl.ds(pl.multiple_of(pair * lanes, lanes), lanes)
        key = k_buf[:, :, cols].reshape(total, lanes)
        value = v_buf[:, :, cols].reshape(total, lanes)
        key_acc[...] = jnp.zeros_like(key_acc)
        value_acc[...] = jnp.zeros_like(value_acc)

        @pl.loop(0, count)
        def _(block):
            query = q_buf[block, :, cols]
            grads = grad_att[block, :, cols]
            logs = lse_buf[block]
            query_parts = []
            for half, mask in enumerate((mask_first, mask_second)):
                head = pair * 2 + half
                query_half, grads_half = query * mask, grads * mask
                scores = nt_dot(query_half, key)
                scores = scores + offset_bias(bias_ref, head, block * rows, rows, total)
                scores = jnp.where(key_valid, scores, negative)
                log_total = jnp.sum(jnp.where(lane == head, logs, 0.0), axis=-1, keepdims=True)
                probs = jnp.exp(scores - log_total)
                grad_probs = nt_dot(grads_half, value)
                inner = jnp.sum(probs * grad_probs, axis=-1, keepdims=True)
                grad_scores = (probs * (grad_probs - inner)).astype(jnp.bfloat16)
                query_parts.append(nn_dot(grad_scores, key))
                key_acc[...] += nn_dot(query_half.astype(jnp.float32).T.astype(jnp.bfloat16), grad_scores)
                value_acc[...] += nn_dot(
                    grads_half.astype(jnp.float32).T.astype(jnp.bfloat16), probs.astype(jnp.bfloat16)
                )
                turned_scores = nn_dot(grad_scores, reverse[...])
                padded = jnp.concatenate([turned_scores, jnp.zeros_like(turned_scores)], axis=1)
                sheared = pltpu.roll(padded, 0, 1, stride=1, stride_axis=0)
                sums = jnp.broadcast_to(jnp.sum(sheared, axis=0, keepdims=True), (8, 2 * total))
                sums = pltpu.roll(sums, block * rows, 1)
                offsets[pl.ds(head, 1), :] += sums[0:1, :]
            grad_qkv[pl.ds(pl.multiple_of(block * rows, rows), rows), cols] = jnp.where(
                lane < head_dim, query_parts[0], query_parts[1]
            ).astype(jnp.bfloat16)

        grad_qkv[:, pl.ds(pl.multiple_of(columns + pair * lanes, lanes), lanes)] = key_acc[
            ...
        ].T.astype(jnp.bfloat16)
        grad_qkv[:, pl.ds(pl.multiple_of(2 * columns + pair * lanes, lanes), lanes)] = value_acc[
            ...
        ].T.astype(jnp.bfloat16)

    for pair in range(local_heads // 2):
        head_pair(pair)
        pace(pair_pace)

    back_line.wait_sends()

    def first_part(block):
        here = pl.ds(pl.multiple_of(block * rows, rows), rows)
        back[block] = (
            nt_dot(grad_qkv[here, 0:columns], wq[...])
            + nt_dot(grad_qkv[here, columns : 2 * columns], wk[...])
            + nt_dot(grad_qkv[here, 2 * columns :], wv[...])
        ).astype(jnp.bfloat16)

    for index in range(count):
        first_part(first_line.order(index))
        if index < count - 1:
            first_line.at_time(index)
        if index == count // 2 - 1:
            pace(1)
    total_buf[...] = back[me].astype(jnp.float32)
    weight_grad(att_buf, branch[...].reshape(total, width), 0, columns, width)
    weight_grad(n1_buf, grad_qkv[...], columns * width // lanes, width, columns)
    clock["gap"] = max(clock["time"] - from_ffn, 0)
    pace(1)
    for now in range(count - 1, first_line.times):
        first_line.at_time(now)
        pace(1)
    grad_in, gain_grad = rms_backward(
        x_own[...].astype(jnp.float32), total_buf[...], gains_ref[0:1, :]
    )
    out_buf[1] = (middle_grad[...] + grad_in).astype(jnp.bfloat16)
    input_copy = pltpu.make_async_copy(out_buf.at[1], input_out, out_sems.at[1])
    input_copy.start()
    for owner in range(count):
        small_parts[owner, 0:1, :] = gain_grad[:, owner * part_width : (owner + 1) * part_width]
    small[0:8, :] = small_parts[me]
    for now in range(small_line.times):
        small_line.at_time(now)
        pace(1)
    bucket = lax.broadcasted_iota(jnp.int32, (lanes, ids_ref.shape[1]), 0)
    one_hot = (bucket == ids_ref[...]).astype(jnp.float32).astype(jnp.bfloat16)
    high = offsets[...].astype(jnp.bfloat16)
    rest = offsets[...] - high.astype(jnp.float32)
    middle_part = rest.astype(jnp.bfloat16)
    low_part = (rest - middle_part.astype(jnp.float32)).astype(jnp.bfloat16)
    small[8:16, 0:lanes] = nt_dot(high, one_hot) + nt_dot(middle_part, one_hot) + nt_dot(low_part, one_hot)
    small[8:16, lanes:] = jnp.zeros((8, part_width - lanes), jnp.float32)
    for index, mask in enumerate(masks):
        copy = pltpu.make_async_remote_copy(
            src_ref=small,
            dst_ref=pair_box.at[index],
            send_sem=pair_sems.at[0, index],
            recv_sem=pair_sems.at[1, index],
            device_id={"replica": mine ^ mask},
            device_id_type=MESH,
        )
        copy.start()
        pace(1)
        copy.wait()
        small[...] += pair_box[index]
    small_out[...] = small[...]

    @pl.loop(clock["time"], chunks + clock["gap"] + skew * parts.last_phase)
    def _(now):
        tick(now)

    for line in (res_line, first_line, branch_line, small_line):
        line.wait_sends()
    result_copy.wait()
    input_copy.wait()


def backward(count, replicas, length, flat, back, res, middle, cot, x, q, k, v, att, lse, n1, wq, wk, wv, wo, gains, bias, ids):
    rows, width = middle.shape
    total = count * rows
    columns = wq.shape[1]
    bf, f32 = jnp.bfloat16, jnp.float32
    shape = jax.ShapeDtypeStruct
    steps = count - 1
    dma = pltpu.SemaphoreType.DMA
    chunk = flat.shape[0] // 15
    attn_rows = 4 * columns * width // lanes
    skew, subs = 3, 2
    levels = replicas.bit_length() - 2
    masks = levels + 1
    depth = skew * (levels + 2)
    part_width = width // count
    vmem = pltpu.VMEM
    blocks = lambda kind: vmem((count, rows, width), kind)
    narrow = lambda: vmem((count, rows, columns), bf)
    boxes = lambda: vmem((count + 1, rows, width), bf)
    return pl.pallas_call(
        functools.partial(
            backward_kernel, count, replicas, chunk, attn_rows // chunk, skew, subs
        ),
        name="backward",
        out_shape=(
            shape((flat.shape[0] + attn_rows, lanes), bf),
            shape((attn_rows, lanes), bf),
            shape((rows, width), bf),
            shape((rows, width), bf),
            shape((16, part_width), f32),
        ),
        in_specs=[smem_space] + [any_space] * 16 + [vmem_space] * 3,
        out_specs=[any_space] * 4 + [vmem_space],
        scratch_shapes=[
            blocks(bf), blocks(bf), vmem((rows, width), f32), vmem((rows, width), bf), vmem((rows, width), bf),
            narrow(), narrow(), narrow(), narrow(), vmem((count, rows, lanes), f32), blocks(bf),
            vmem(wq.shape, bf), vmem(wk.shape, bf), vmem(wv.shape, bf), vmem(wo.shape, bf),
            boxes(), boxes(), vmem((rows, width), f32), vmem((rows, width), f32), vmem((rows, width), f32), blocks(bf),
            narrow(),
            vmem((lanes, total), f32), vmem((lanes, total), f32), vmem((total, 3 * columns), bf),
            vmem((total, total), bf), vmem((8, 2 * total), f32), vmem((256, total), bf),
            vmem((2, width // lanes, 256, lanes), bf), vmem((2, rows, width), bf),
            vmem((16, part_width), f32), vmem((count, 8, part_width), f32), vmem((count + 1, 8, part_width), f32),
            vmem((masks, 16, part_width), f32),
            vmem((depth, chunk // 2, lanes), bf), vmem((2 * skew, chunk // 2, lanes), bf),
            vmem((2 * skew, 2, chunk // 4, lanes), bf),
            dma((15,)), dma((2, 2, steps * subs)), dma((2, 2, steps * subs)), dma((2, 2, steps * subs)),
            dma((2, 2, steps * subs)),
            dma((2, 2, steps)), dma((2, masks)), dma((2, width // lanes)), dma((2,)),
            dma((2, 2 * levels + 3, 3, 2 * skew)),
        ],
        compiler_params=pltpu.CompilerParams(
            collective_id=2, has_side_effects=True, vmem_limit_bytes=61 * 2**20
        ),
    )(length, flat, back, res, middle, cot, x, q, k, v, att, lse, n1, wq, wk, wv, wo, gains, bias, ids)


def widen_kernel(plan, slots, sums, *refs):
    targets, (inbox, outbox, in_sems, out_sems) = refs[:-4], refs[-4:]
    tiles = [
        (target, start, height, depth // lanes, size, row)
        for target, (start, height, depth, size) in zip(targets, plan)
        for row in range(0, height, size)
    ]

    def load(number):
        _, start, height, panels, size, row = tiles[number]
        slot = number % slots

        @pl.loop(0, panels)
        def _(panel):
            pltpu.make_async_copy(
                sums.at[pl.ds(start + row + panel * height, size)],
                inbox.at[slot, pl.ds(pl.multiple_of(panel * size, size), size)],
                in_sems.at[slot],
            ).start()

    def store(number):
        target, _, _, panels, size, row = tiles[number]
        return pltpu.make_async_copy(
            outbox.at[number % slots, pl.ds(0, size), pl.ds(0, panels * lanes)],
            target.at[pl.ds(row, size)],
            out_sems.at[number % slots],
        )

    for number in range(min(slots - 1, len(tiles))):
        load(number)
    for number in range(len(tiles)):
        _, _, _, panels, size, _ = tiles[number]
        slot = number % slots
        if number + slots - 1 < len(tiles):
            load(number + slots - 1)
        whole = inbox.at[slot, pl.ds(0, panels * size)]
        pltpu.make_async_copy(whole, whole, in_sems.at[slot]).wait()
        if number >= slots:
            store(number - slots).wait()

        @pl.loop(0, panels)
        def _(panel):
            outbox[slot, pl.ds(0, size), pl.ds(pl.multiple_of(panel * lanes, lanes), lanes)] = inbox[
                slot, pl.ds(pl.multiple_of(panel * size, size), size)
            ].astype(jnp.float32)

        store(number).start()
    for number in range(max(len(tiles) - slots, 0), len(tiles)):
        store(number).wait()


def widen(sums, shapes):
    slots = 4
    plan, start = [], 0
    for height, depth in shapes:
        size = 512 if depth <= 1024 else 256
        while height % size:
            size //= 2
        plan.append((start, height, depth, size))
        start += height * depth // lanes
    most_in = max(size * depth // lanes for _, _, depth, size in plan)
    most_rows = max(size for _, _, _, size in plan)
    return pl.pallas_call(
        functools.partial(widen_kernel, plan, slots),
        name="widen",
        out_shape=[jax.ShapeDtypeStruct(shape, jnp.float32) for shape in shapes],
        in_specs=[any_space],
        out_specs=[any_space] * len(shapes),
        scratch_shapes=[
            pltpu.VMEM((slots, most_in, lanes), jnp.bfloat16),
            pltpu.VMEM((slots, most_rows, max(depth for _, depth in shapes)), jnp.float32),
            pltpu.SemaphoreType.DMA((slots,)),
            pltpu.SemaphoreType.DMA((slots,)),
        ],
        compiler_params=pltpu.CompilerParams(vmem_limit_bytes=40 * 2**20),
    )(sums)


def local(
    inputs,
    seq_lengths,
    bucket_ids,
    norm1_gain,
    w_query,
    w_key,
    w_value,
    w_attn_out,
    bias_table,
    norm2_gain,
    w_gate,
    w_up,
    w_ffn_out,
    cotangent,
):
    count = lax.axis_size("group")
    replicas = lax.axis_size("replica")
    gains_local = jnp.pad(
        jnp.stack([norm1_gain, norm2_gain]).astype(jnp.float32), ((0, 6), (0, 0))
    )
    ids = jnp.pad(bucket_ids, (0, 1))[None, :]
    ids_back = jnp.pad(bucket_ids[::-1], (0, 1), constant_values=-1)[None, :]
    normed_one, query, key, value, attended, log_totals, g_all, middle, normed_two, gains, bias = (
        attention_forward(
            count, seq_lengths, inputs[0], cotangent[0], gains_local,
            w_query, w_key, w_value, w_attn_out, ids, bias_table.T,
        )
    )
    flat, back_part, result_part = feed_forward(
        count, seq_lengths, normed_two, g_all, w_gate, w_up, w_ffn_out
    )
    sums, _, result, input_grad, small = backward(
        count, replicas, seq_lengths, flat, back_part, result_part, middle, cotangent[0], inputs[0],
        query, key, value, attended, log_totals, normed_one,
        w_query, w_key, w_value, w_attn_out, gains, bias, ids_back,
    )
    weights = (w_ffn_out, w_gate, w_up, w_attn_out, w_query, w_key, w_value)
    ffn_out_grad, gate_grad, up_grad, attn_out_grad, query_grad, key_grad, value_grad = widen(
        sums, [weight.shape for weight in weights]
    )
    buckets, local_heads = bias_table.shape
    table_grad = small[8 : 8 + local_heads, :buckets].T
    return (
        result[None],
        input_grad[None],
        small[0],
        query_grad,
        key_grad,
        value_grad,
        attn_out_grad,
        table_grad,
        small[1],
        gate_grad,
        up_grad,
        ffn_out_grad,
    )


def solution(mesh):
    placed = (
        P("replica", "group", None),
        P("replica"),
        P(),
        P("group"),
        P(None, "group"),
        P(None, "group"),
        P(None, "group"),
        P("group", None),
        P(None, "group"),
        P("group"),
        P(None, "group"),
        P(None, "group"),
        P("group", None),
        P("replica", "group", None),
    )
    return jax.shard_map(
        local,
        mesh=mesh,
        in_specs=placed,
        out_specs=(
            P("replica", "group", None),
            P("replica", "group", None),
            P("group"),
            P(None, "group"),
            P(None, "group"),
            P(None, "group"),
            P("group", None),
            P(None, "group"),
            P("group"),
            P(None, "group"),
            P(None, "group"),
            P("group", None),
        ),
        check_vma=False,
    )
```

```python
import functools
import jax
import jax.numpy as jnp
from jax import lax
from jax.experimental import pallas as pl
from jax.experimental.pallas import tpu as pltpu
from jax.sharding import PartitionSpec as P

epsilon = 1e-06
negative = -1000000000.0
head_dim = 64
lanes = 128
MESH = pl.DeviceIdType.MESH
any_space = pl.BlockSpec(memory_space=pl.ANY)
vmem_space = pl.BlockSpec(memory_space=pltpu.VMEM)
smem_space = pl.BlockSpec(memory_space=pltpu.SMEM)


def nn_dot(left, right):
    return jnp.dot(left, right, preferred_element_type=jnp.float32)


def nt_dot(left, right):
    return lax.dot_general(
        left, right, (((1,), (1,)), ((), ())), preferred_element_type=jnp.float32
    )


def line_barrier(me, count):
    barrier = pltpu.get_barrier_semaphore()

    @pl.when(me > 0)
    def _():
        pl.semaphore_signal(barrier, inc=1, device_id={"group": me - 1}, device_id_type=MESH)

    @pl.when(me < count - 1)
    def _():
        pl.semaphore_signal(barrier, inc=1, device_id={"group": me + 1}, device_id_type=MESH)

    peers = jnp.where(me > 0, 1, 0) + jnp.where(me < count - 1, 1, 0)
    pl.semaphore_wait(barrier, peers)


class LineGather:
    def __init__(self, me, count, buffer, sems, subs=1):
        self.me, self.count, self.buffer, self.sems, self.subs = me, count, buffer, sems, subs
        self.pieces = (count - 1) * subs
        self.size = buffer.shape[1] // subs

    def copy(self, side, piece, hops):
        block = self.me - hops if side == 0 else self.me + hops
        here = self.buffer.at[block, pl.ds(piece % self.subs * self.size, self.size)]
        return pltpu.make_async_remote_copy(
            src_ref=here,
            dst_ref=here,
            send_sem=self.sems.at[side, 0, piece],
            recv_sem=self.sems.at[side, 1, piece],
            device_id={"group": self.me + (1 if side == 0 else -1)},
            device_id_type=MESH,
        )

    def sends(self, side, piece):
        hops = piece // self.subs
        if side == 0:
            return (self.me - hops >= 0) & (self.me + 1 < self.count)
        return (self.me + hops < self.count) & (self.me >= 1)

    def arrives(self, side, piece):
        hops = piece // self.subs
        if side == 0:
            return self.me - 1 - hops >= 0
        return self.me + 1 + hops < self.count

    def send_side(self, side, piece):
        @pl.when(self.sends(side, piece))
        def _():
            self.copy(side, piece, piece // self.subs).start()

    def send(self, piece):
        for side in range(2):
            self.send_side(side, piece)

    def begin(self):
        for piece in range(self.subs):
            self.send(piece)

    def arrive(self, piece):
        for side in range(2):
            @pl.when(self.arrives(side, piece))
            def _():
                self.copy(side, piece, piece // self.subs + 1).wait_recv()

        if piece + self.subs < self.pieces:
            self.send(piece + self.subs)

    def arrive_block(self, hops, body):
        for piece in range(hops * self.subs, (hops + 1) * self.subs):
            self.arrive(piece)
        self.each_block(hops, body)

    def each_block(self, hops, body):
        @pl.loop(0, 2)
        def _(side):
            block = jnp.where(side == 0, self.me - 1 - hops, self.me + 1 + hops)

            @pl.when((block >= 0) & (block < self.count))
            def _():
                body(block)

    def wait_sends(self):
        for piece in range(self.pieces):
            for side in range(2):
                @pl.when(self.sends(side, piece))
                def _():
                    self.copy(side, piece, piece // self.subs).wait_send()


class LineScatter:
    def __init__(self, me, count, parts, inbox, total, sems, subs=1):
        self.me, self.count, self.parts, self.inbox = me, count, parts, inbox
        self.total, self.sems, self.subs = total, sems, subs
        self.times = (count - 1) * subs + 1
        self.size = parts.shape[1] // subs

    def order(self, index):
        picked = 0
        for device in range(self.count):
            due = [(step * self.subs + self.count - 1 - device, step) for step in range(device)]
            due += [
                (step * self.subs + device, self.count - 1 - step)
                for step in range(self.count - 1 - device)
            ]
            blocks = [block for _, block in sorted(due)] + [device]
            picked = picked + jnp.where(self.me == device, blocks[index], 0)
        return picked

    def copy(self, side, piece):
        step = piece // self.subs
        here = pl.ds(pl.multiple_of(piece % self.subs * self.size, self.size), self.size)
        owner = step if side == 0 else self.count - 1 - step
        return pltpu.make_async_remote_copy(
            src_ref=self.parts.at[owner, here],
            dst_ref=self.inbox.at[self.slot(side, step), here],
            send_sem=self.sems.at[side, 0, piece],
            recv_sem=self.sems.at[side, 1, piece],
            device_id={"group": self.me + (-1 if side == 0 else 1)},
            device_id_type=MESH,
        )

    def slot(self, side, step):
        return step if side == 0 else self.count - step

    def at_time(self, time):
        for side in range(2):
            before = self.count - 1 - self.me if side == 0 else self.me
            after = self.count - 1 - before
            piece = time - before
            step = piece // self.subs

            @pl.when((piece >= 0) & (step < after))
            def _():
                owner = step if side == 0 else self.count - 1 - step
                here = pl.ds(pl.multiple_of(piece % self.subs * self.size, self.size), self.size)

                @pl.when(before > 0)
                def _():
                    self.copy(side, piece).wait_recv()
                    self.parts[owner, here, :] = (
                        self.parts[owner, here, :].astype(jnp.float32)
                        + self.inbox[self.slot(side, step), here, :].astype(jnp.float32)
                    ).astype(self.parts.dtype)

                self.copy(side, piece).start()

            @pl.when((piece >= 0) & (step == after) & (before > 0))
            def _():
                here = pl.ds(pl.multiple_of(piece % self.subs * self.size, self.size), self.size)
                self.copy(side, piece).wait_recv()
                self.total[here, :] += self.inbox[self.slot(side, step), here, :].astype(jnp.float32)

    def wait_sends(self):
        for piece in range((self.count - 1) * self.subs):
            step = piece // self.subs
            for side in range(2):
                after = self.me if side == 0 else self.count - 1 - self.me

                @pl.when(step < after)
                def _():
                    self.copy(side, piece).wait_send()


def head_masks():
    lane = lax.broadcasted_iota(jnp.int32, (1, lanes), 1)
    first = (lane < head_dim).astype(jnp.float32)
    return first.astype(jnp.bfloat16), (1.0 - first).astype(jnp.bfloat16)


def offset_bias(bias_ref, head, row_start, rows, total):
    width = bias_ref.shape[1]
    shift = lax.rem(row_start + (width - (total - 1)), width)
    vector = pltpu.roll(jnp.broadcast_to(bias_ref[pl.ds(head, 1), :], (8, width)), shift, 1)
    vector = jnp.broadcast_to(vector[0:1, :], (rows, width))
    return pltpu.roll(vector, 0, 1, stride=1, stride_axis=0)[:, :total]


def rms_rows(values):
    return lax.rsqrt(jnp.mean(values * values, axis=-1, keepdims=True) + epsilon)


def attention_forward_kernel(
    count, subs,
    length_ref,
    x_hbm, cot_hbm, gains_hbm, wq_hbm, wk_hbm, wv_hbm, wo_hbm, ids_ref, table_ref,
    n1_out, q_out, k_out, v_out, att_out, lse_out, cot_out, middle_out, n2_out, gains_out, bias_out,
    x_all, gains_all, wq, wk, wv, wo, parts, inbox, n1_buf, q_buf, k_buf, v_buf, att_buf, lse_buf, total_buf, n2_buf,
    local_sems, x_sems, g_sems, c_sems, s_sems, out_sems,
):
    me = lax.axis_index("group")
    rows, width = x_hbm.shape
    total = rows * count
    columns = wq.shape[1]
    local_heads = columns // head_dim
    loads = [
        pltpu.make_async_copy(source, target, local_sems.at[index])
        for index, (source, target) in enumerate(
            [
                (x_hbm, x_all.at[me]),
                (gains_hbm, gains_all.at[me]),
                (wq_hbm, wq),
                (wk_hbm, wk),
                (wv_hbm, wv),
                (wo_hbm, wo),
                (cot_hbm, cot_out.at[me]),
            ]
        )
    ]
    for load in loads:
        load.start()
    line_barrier(me, count)
    x_line = LineGather(me, count, x_all, x_sems, subs)
    g_line = LineGather(me, count, gains_all, g_sems)
    c_line = LineGather(me, count, cot_out, c_sems, subs)
    loads[1].wait()
    g_line.begin()
    loads[0].wait()
    x_line.begin()

    bucket = lax.broadcasted_iota(jnp.int32, (table_ref.shape[1], ids_ref.shape[1]), 0)
    one_hot = (bucket == ids_ref[...]).astype(jnp.float32).astype(jnp.bfloat16)
    bias_out[...] = nn_dot(table_ref[...], one_hot)

    for piece in range(g_line.pieces):
        g_line.arrive(piece)
    for owner in range(count):
        gains_out[:, owner * (width // count) : (owner + 1) * (width // count)] = gains_all[owner]
    for load in loads[2:5]:
        load.wait()

    def project(block):
        values = x_all[block].astype(jnp.float32)
        normed = (values * rms_rows(values) * gains_out[0:1, :]).astype(jnp.bfloat16)
        n1_buf[block] = normed
        q_buf[block] = nn_dot(normed, wq[...]).astype(jnp.bfloat16)
        k_buf[block] = nn_dot(normed, wk[...]).astype(jnp.bfloat16)
        v_buf[block] = nn_dot(normed, wv[...]).astype(jnp.bfloat16)

    def begin_cotangent(sent):
        for side in range(2):
            last = me if side == 0 else count - 1 - me

            @pl.when(last == sent)
            def _():
                for piece in range(subs):
                    c_line.send_side(side, piece)

    loads[6].wait()
    begin_cotangent(0)
    for piece in range(subs):
        x_line.arrive(piece)
    begin_cotangent(1)
    project(me)
    x_line.each_block(0, project)
    for hops in range(1, count - 1):
        for piece in range(hops * subs, (hops + 1) * subs):
            x_line.arrive(piece)
        begin_cotangent(hops + 1)
        x_line.each_block(hops, project)

    loads[5].wait()
    mask_first, mask_second = head_masks()
    key_valid = lax.broadcasted_iota(jnp.int32, (1, total), 1) < length_ref[0]
    lane = lax.broadcasted_iota(jnp.int32, (1, lanes), 1)

    def attend(block):
        lse_buf[block] = jnp.zeros((rows, lanes), jnp.float32)

        @pl.loop(0, local_heads // 2)
        def _(pair):
            cols = pl.ds(pl.multiple_of(pair * lanes, lanes), lanes)
            query = q_buf[block, :, cols]
            key = k_buf[:, :, cols].reshape(total, lanes)
            value = v_buf[:, :, cols].reshape(total, lanes)
            outs = []
            for half, mask in enumerate((mask_first, mask_second)):
                head = pair * 2 + half
                scores = nt_dot(query * mask, key)
                scores = scores + offset_bias(bias_out, head, block * rows, rows, total)
                scores = jnp.where(key_valid, scores, negative)
                top = jnp.max(scores, axis=-1, keepdims=True)
                expd = jnp.exp(scores - top)
                summed = jnp.sum(expd, axis=-1, keepdims=True)
                probs = (expd * (1.0 / summed)).astype(jnp.bfloat16)
                outs.append(nn_dot(probs, value))
                lse_buf[block] = jnp.where(lane == head, top + jnp.log(summed), lse_buf[block])
            att_buf[block, :, cols] = jnp.where(lane < head_dim, outs[0], outs[1]).astype(
                jnp.bfloat16
            )

    scatter = LineScatter(me, count, parts, inbox, total_buf, s_sems, subs)
    arrived = 0
    for index in range(count - 1):
        block = scatter.order(index)
        attend(block)
        parts[block] = nn_dot(att_buf[block], wo[...]).astype(jnp.bfloat16)
        scatter.at_time(index)
        if index:
            c_line.arrive(arrived)
            arrived += 1
    attend(me)
    total_buf[...] = x_all[me].astype(jnp.float32) + nn_dot(att_buf[me], wo[...])
    outs = [
        pltpu.make_async_copy(source, target, out_sems.at[index])
        for index, (source, target) in enumerate(
            [(n1_buf, n1_out), (q_buf, q_out), (k_buf, k_out), (v_buf, v_out), (att_buf, att_out), (lse_buf, lse_out)]
        )
    ]
    for copy in outs:
        copy.start()
    for time in range(count - 1, scatter.times):
        scatter.at_time(time)
        if arrived < c_line.pieces:
            c_line.arrive(arrived)
            arrived += 1
    middle = total_buf[...]
    n2_buf[...] = (middle * rms_rows(middle) * gains_out[1:2, :]).astype(jnp.bfloat16)
    tail = [
        pltpu.make_async_copy(total_buf, middle_out, out_sems.at[len(outs)]),
        pltpu.make_async_copy(n2_buf, n2_out, out_sems.at[len(outs) + 1]),
    ]
    for copy in tail:
        copy.start()
    for piece in range(arrived, c_line.pieces):
        c_line.arrive(piece)
    for line in (g_line, x_line, c_line, scatter):
        line.wait_sends()
    for copy in outs + tail:
        copy.wait()


def attention_forward(count, length, x, cot, gains, wq, wk, wv, wo, ids, table):
    rows, width = x.shape
    columns = wq.shape[1]
    local_heads = columns // head_dim
    bf, f32 = jnp.bfloat16, jnp.float32
    shape = jax.ShapeDtypeStruct
    steps = count - 1
    subs = 2
    dma = pltpu.SemaphoreType.DMA
    return pl.pallas_call(
        functools.partial(attention_forward_kernel, count, subs),
        name="attention_forward",
        out_shape=(
            shape((count, rows, width), bf),
            shape((count, rows, columns), bf),
            shape((count, rows, columns), bf),
            shape((count, rows, columns), bf),
            shape((count, rows, columns), bf),
            shape((count, rows, lanes), f32),
            shape((count, rows, width), bf),
            shape((rows, width), f32),
            shape((rows, width), bf),
            shape((8, width), f32),
            shape((local_heads, ids.shape[1]), f32),
        ),
        in_specs=[smem_space] + [any_space] * 7 + [vmem_space] * 2,
        out_specs=[any_space] * 9 + [vmem_space] * 2,
        scratch_shapes=[
            pltpu.VMEM((count, rows, width), bf),
            pltpu.VMEM((count,) + gains.shape, f32),
            pltpu.VMEM(wq.shape, bf),
            pltpu.VMEM(wk.shape, bf),
            pltpu.VMEM(wv.shape, bf),
            pltpu.VMEM(wo.shape, bf),
            pltpu.VMEM((count, rows, width), bf),
            pltpu.VMEM((count + 1, rows, width), bf),
            pltpu.VMEM((count, rows, width), bf),
            pltpu.VMEM((count, rows, columns), bf),
            pltpu.VMEM((count, rows, columns), bf),
            pltpu.VMEM((count, rows, columns), bf),
            pltpu.VMEM((count, rows, columns), bf),
            pltpu.VMEM((count, rows, lanes), f32),
            pltpu.VMEM((rows, width), f32),
            pltpu.VMEM((rows, width), bf),
            dma((7,)),
            dma((2, 2, steps * subs)),
            dma((2, 2, steps)),
            dma((2, 2, steps * subs)),
            dma((2, 2, steps * subs)),
            dma((8,)),
        ],
        compiler_params=pltpu.CompilerParams(
            collective_id=0, has_side_effects=True, vmem_limit_bytes=56 * 2**20
        ),
    )(length, x, cot, gains, wq, wk, wv, wo, ids, table)


def gelu_parts(gate):
    root = 0.7978845608028654
    inner = root * (gate + 0.044715 * gate * gate * gate)
    tanh = jnp.tanh(inner)
    half = 0.5 * (1.0 + tanh)
    slope = half + 0.5 * gate * (1.0 - tanh * tanh) * root * (1.0 + 3 * 0.044715 * gate * gate)
    return gate * half, slope


def feed_forward_kernel(
    count, tile, subs,
    length_ref,
    n2_hbm, cot_hbm, wg_hbm, wu_hbm, wf_hbm,
    flat_out, back_out, res_out, n2_out, gate_out, up_out,
    n2_all, g_all, wg, wu, wf, hid, grad_gate, grad_up, grad_hidden, back_buf, res_buf, turned, stage,
    local_sems, n_sems, out_sems, stage_sems,
):
    me = lax.axis_index("group")
    rows, width = n2_hbm.shape
    total = rows * count
    units = wg.shape[1]
    loads = [
        pltpu.make_async_copy(source, target, local_sems.at[index])
        for index, (source, target) in enumerate(
            [(n2_hbm, n2_all.at[me]), (cot_hbm, g_all), (wf_hbm, wf), (wg_hbm, wg), (wu_hbm, wu)]
        )
    ]
    for load in loads:
        load.start()
    line_barrier(me, count)
    line = LineGather(me, count, n2_all, n_sems, subs)
    loads[0].wait()
    line.begin()

    loads[1].wait()

    @pl.loop(0, count)
    def _(block):
        position = block * rows + lax.broadcasted_iota(jnp.int32, (rows, 1), 0)
        valid = (position < length_ref[0]).astype(jnp.float32).astype(jnp.bfloat16)
        g_all[block] = g_all[block] * valid

    loads[2].wait()

    @pl.loop(0, units // tile)
    def _(index):
        here = pl.ds(pl.multiple_of(index * tile, tile), tile)
        grad_hidden[:, here] = nt_dot(g_all[...].reshape(total, width), wf[here, :])

    for load in loads[3:]:
        load.wait()

    def block_pass(block):
        normed = n2_all[block]
        here = pl.ds(pl.multiple_of(block * rows, rows), rows)
        gate = nn_dot(normed, wg[...])
        up = nn_dot(normed, wu[...])
        act, slope = gelu_parts(gate)
        hid[block] = (act * up).astype(jnp.bfloat16)
        grads = grad_hidden[here, :]
        grad_gate[here, :] = (grads * up * slope).astype(jnp.bfloat16)
        grad_up[here, :] = (grads * act).astype(jnp.bfloat16)
        res_buf[block] = nn_dot(hid[block], wf[...]).astype(jnp.bfloat16)
        half = width // 2
        for cols in (pl.ds(0, half), pl.ds(half, half)):
            back_buf[block, :, cols] = (
                nt_dot(grad_gate[here, :], wg[cols, :]) + nt_dot(grad_up[here, :], wu[cols, :])
            ).astype(jnp.bfloat16)

    block_pass(me)
    for hops in range(count - 1):
        line.arrive_block(hops, block_pass)
    outs = [
        pltpu.make_async_copy(source, target, out_sems.at[index])
        for index, (source, target) in enumerate(
            [(back_buf, back_out), (res_buf, res_out), (n2_all, n2_out), (grad_gate, gate_out), (grad_up, up_out)]
        )
    ]
    for copy in outs:
        copy.start()

    def weight_grad(left, right, base, height):
        depth = right.shape[2]
        panels = depth // lanes
        factor = right[...].reshape(total, depth)

        def store(slot, panel, row):
            return pltpu.make_async_copy(
                stage.at[slot, panel],
                flat_out.at[pl.ds(base + panel * height + row, tile)],
                stage_sems.at[slot, panel],
            )

        @pl.loop(0, height // tile)
        def _(index):
            slot = lax.rem(index, 2)
            row = pl.multiple_of(index * tile, tile)
            turned[...] = left[:, :, pl.ds(row, tile)].reshape(total, tile).T
            product = nn_dot(turned[...], factor).astype(jnp.bfloat16)

            @pl.when(index >= 2)
            def _():
                for panel in range(panels):
                    store(slot, panel, row).wait()

            for panel in range(panels):
                stage[slot, panel] = product[:, panel * lanes : (panel + 1) * lanes]
                store(slot, panel, row).start()

        for slot in range(2):
            for panel in range(panels):
                store(slot, panel, 0).wait()

    weight_grad(hid, g_all, 0, units)
    line.wait_sends()
    for copy in outs:
        copy.wait()


def feed_forward(count, length, n2, cot, wg, wu, wf):
    rows, width = n2.shape
    units = wg.shape[1]
    tile = 128 if units % 256 else 256
    bf = jnp.bfloat16
    shape = jax.ShapeDtypeStruct
    steps = count - 1
    subs = 2
    dma = pltpu.SemaphoreType.DMA
    return pl.pallas_call(
        functools.partial(feed_forward_kernel, count, tile, subs),
        name="feed_forward",
        out_shape=(
            shape((units * width // lanes, lanes), bf),
            shape((count, rows, width), bf),
            shape((count, rows, width), bf),
            shape((count, rows, width), bf),
            shape((count * rows, units), bf),
            shape((count * rows, units), bf),
        ),
        in_specs=[smem_space] + [any_space] * 5,
        out_specs=[any_space] * 6,
        scratch_shapes=[
            pltpu.VMEM((count, rows, width), bf),
            pltpu.VMEM((count, rows, width), bf),
            pltpu.VMEM(wg.shape, bf),
            pltpu.VMEM(wu.shape, bf),
            pltpu.VMEM(wf.shape, bf),
            pltpu.VMEM((count, rows, units), bf),
            pltpu.VMEM((count * rows, units), bf),
            pltpu.VMEM((count * rows, units), bf),
            pltpu.VMEM((count * rows, units), jnp.float32),
            pltpu.VMEM((count, rows, width), bf),
            pltpu.VMEM((count, rows, width), bf),
            pltpu.VMEM((tile, count * rows), bf),
            pltpu.VMEM((2, width // lanes, tile, lanes), bf),
            dma((5,)),
            dma((2, 2, steps * subs)),
            dma((5,)),
            dma((2, width // lanes)),
        ],
        compiler_params=pltpu.CompilerParams(
            collective_id=1, has_side_effects=True, vmem_limit_bytes=56 * 2**20
        ),
    )(length, n2, cot, wg, wu, wf)


def when(condition, body):
    if isinstance(condition, bool):
        if condition:
            body()
    else:
        pl.when(condition)(body)


class ReplicaSum:
    def __init__(self, replicas, chunk, source, target, work, core_box, path_box, sems):
        self.mine = lax.axis_index("replica")
        self.chunk, self.source, self.target = chunk, source, target
        self.work, self.core_box, self.path_box, self.sems = work, core_box, path_box, sems
        self.depth, self.slots = work.shape[0], core_box.shape[0]
        bits = [1 << index for index in range(1, replicas.bit_length() - 1)]
        self.orders = (bits, bits[::-1])
        self.levels = len(bits)
        self.last_phase = 2 * self.levels + 2
        self.half = chunk // 2

    def bit(self, mask):
        return jnp.where((self.mine & mask) != 0, 1, 0)

    def region(self, path, level):
        size = self.half // 2
        offset = path * size
        for mask in self.orders[path][:level]:
            size //= 2
            offset = offset + self.bit(mask) * size
        return offset, size

    def out_rows(self, chunk, offset, size):
        start = chunk * self.chunk + self.bit(1) * self.half + offset
        return self.target.at[pl.ds(pl.multiple_of(start, 16), size)]

    def sem(self, kind, phase, path, chunk):
        return self.sems.at[kind, phase, path, chunk % self.slots]

    def remote(self, source, target, phase, path, chunk, mask):
        return pltpu.make_async_remote_copy(
            src_ref=source,
            dst_ref=target,
            send_sem=self.sem(0, phase, path, chunk),
            recv_sem=self.sem(1, phase, path, chunk),
            device_id={"replica": self.mine ^ mask},
            device_id_type=MESH,
        )

    def core_copy(self, chunk):
        start = chunk * self.chunk + (1 - self.bit(1)) * self.half
        return self.remote(
            self.source(start, self.half), self.core_box.at[chunk % self.slots], 0, 0, chunk, 1
        )

    def load_copy(self, chunk):
        start = chunk * self.chunk + self.bit(1) * self.half
        return pltpu.make_async_copy(
            self.source(start, self.half), self.work.at[chunk % self.depth], self.sem(0, 0, 1, chunk)
        )

    def reduce_copy(self, chunk, path, level):
        mask = self.orders[path][level - 1]
        offset, size = self.region(path, level - 1)
        size //= 2
        start = pl.multiple_of(offset + (1 - self.bit(mask)) * size, 16)
        return self.remote(
            self.work.at[chunk % self.depth, pl.ds(start, size)],
            self.box(chunk, path, level),
            level, path, chunk, mask,
        )

    def box(self, chunk, path, level):
        size = self.half // 2 >> level
        start = sum(self.half // 2 >> step for step in range(1, level))
        return self.path_box.at[chunk % self.slots, path, pl.ds(start, size)]

    def add_box(self, chunk, path, level):
        offset, size = self.region(path, level)
        here = pl.ds(pl.multiple_of(offset, 16), size)
        slot = chunk % self.depth
        self.work[slot, here, :] = self.work[slot, here, :] + self.box(chunk, path, level)[...]

    def own_copy(self, chunk, path):
        offset, size = self.region(path, self.levels)
        return pltpu.make_async_copy(
            self.work.at[chunk % self.depth, pl.ds(pl.multiple_of(offset, 16), size)],
            self.out_rows(chunk, offset, size),
            self.sems.at[1, 0, 1 + path, chunk % self.slots],
        )

    def spread_copy(self, chunk, path, level):
        offset, size = self.region(path, level)
        if level == self.levels:
            source = self.work.at[chunk % self.depth, pl.ds(pl.multiple_of(offset, 16), size)]
        else:
            source = self.out_rows(chunk, offset, size)
        return self.remote(
            source, self.out_rows(chunk, offset, size),
            2 * self.levels + 1 - level, path, chunk, self.orders[path][level - 1],
        )

    def share_copy(self, chunk):
        rows = self.out_rows(chunk, 0, self.half)
        return self.remote(rows, rows, self.last_phase - 1, 0, chunk, 1)

    def advance(self, phase, chunk):
        levels = self.levels
        if phase == 0:
            self.core_copy(chunk).start()
            self.load_copy(chunk).start()
        elif phase <= levels + 1:
            if phase == 1:
                self.load_copy(chunk).wait()
                self.core_copy(chunk).wait()
                slot = chunk % self.depth
                self.work[slot] = self.work[slot] + self.core_box[chunk % self.slots]
            for path in range(2):
                if phase > 1:
                    self.reduce_copy(chunk, path, phase - 1).wait()
                    self.add_box(chunk, path, phase - 1)
                if phase <= levels:
                    self.reduce_copy(chunk, path, phase).start()
                else:
                    self.own_copy(chunk, path).start()
                    self.spread_copy(chunk, path, levels).start()
        else:
            level = 2 * levels + 1 - phase
            if level >= 0:
                for path in range(2):
                    self.spread_copy(chunk, path, level + 1).wait()
                    if level + 1 == levels:
                        self.own_copy(chunk, path).wait()
                    if level >= 1:
                        self.spread_copy(chunk, path, level).start()
                if level == 0:
                    self.share_copy(chunk).start()


scatter_pace, gather_pace, pair_pace = 1.0, 1.0, 0.5


def rms_backward(values, grads, gain):
    scale = rms_rows(values)
    unit = values * scale
    scaled = grads * gain
    inner = jnp.mean(scaled * unit, axis=-1, keepdims=True)
    return scale * (scaled - unit * inner), jnp.sum(grads * unit, axis=0, keepdims=True)


def backward_kernel(
    count, replicas, chunk, ffn_chunks, attn_chunks, skew, subs,
    length_ref,
    flat_hbm, n2_hbm, gate_hbm, up_hbm, back_hbm, res_hbm, middle_hbm, cot_hbm, x_hbm,
    q_hbm, k_hbm, v_hbm, att_hbm, lse_hbm, n1_hbm,
    wq_hbm, wk_hbm, wv_hbm, wo_hbm, gains_ref, bias_ref, ids_ref,
    sums_out, flat_out, result_out, input_out, small_out,
    back, res, middle, cot, x_own, q_buf, k_buf, v_buf, att_buf, lse_buf, n1_buf, wq, wk, wv, wo,
    back_box, res_box, total_buf, res_total, middle_grad, branch, grad_att, key_acc, value_acc, grad_qkv, grad_up,
    reverse, offsets, turned, stage, out_buf, small, small_parts, small_box, pair_box,
    work, core_box, path_box,
    load_sems, b_sems, r_sems, f_sems, a_sems, p_sems, pair_sems, stage_sems, out_sems, sum_sems,
):
    me = lax.axis_index("group")
    mine = lax.axis_index("replica")
    rows, width = middle.shape
    total = rows * count
    columns = wq.shape[1]
    local_heads = columns // head_dim
    units = grad_up.shape[1]
    sources = [
        back_hbm, n2_hbm, gate_hbm, up_hbm, middle_hbm, cot_hbm, x_hbm, wo_hbm, att_hbm, q_hbm, k_hbm, v_hbm,
        lse_hbm, wq_hbm, wk_hbm, wv_hbm, res_hbm, n1_hbm,
    ]
    targets = [
        back, n1_buf, grad_qkv.at[:, pl.ds(0, units)], grad_up, middle, cot, x_own, wo, att_buf, q_buf, k_buf, v_buf,
        lse_buf, wq, wk, wv, res, n1_buf,
    ]
    loads = [
        pltpu.make_async_copy(source, target, load_sems.at[index])
        for index, (source, target) in enumerate(zip(sources, targets))
    ]
    masks = [1 << index for index in range(replicas.bit_length() - 1)]
    barrier = pltpu.get_barrier_semaphore()

    @pl.when(me > 0)
    def _():
        pl.semaphore_signal(barrier, inc=1, device_id={"group": me - 1}, device_id_type=MESH)

    @pl.when(me < count - 1)
    def _():
        pl.semaphore_signal(barrier, inc=1, device_id={"group": me + 1}, device_id_type=MESH)

    for mask in masks:
        pl.semaphore_signal(barrier, inc=1, device_id={"replica": mine ^ mask}, device_id_type=MESH)
    peers = jnp.where(me > 0, 1, 0) + jnp.where(me < count - 1, 1, 0) + len(masks)
    for load in loads[:7]:
        load.start()
    pl.semaphore_wait(barrier, peers)

    first_rows = flat_hbm.shape[0]
    from_first_chunks = first_rows // chunk
    from_ffn = ffn_chunks
    chunks = from_ffn + attn_chunks

    def make_source(source_ref, base):
        return lambda start, size: source_ref.at[pl.ds(pl.multiple_of(start - base, 16), size)]

    parts = ReplicaSum(replicas, chunk, None, sums_out, work, core_box, path_box, sum_sems)
    from_first, from_second = make_source(flat_hbm, 0), make_source(flat_out, first_rows)
    clock = {"time": 0, "gap": None, "credit": 0.0}

    def start_piece(source, piece):
        parts.source = source
        parts.core_copy(piece).start()
        parts.load_copy(piece).start()

    def tick(time):
        gap = clock["gap"]
        for phase in range(parts.last_phase, -1, -1):
            entry = time - skew * phase
            if isinstance(entry, int):
                early = 0 <= entry < from_ffn
                late = gap is not None and from_ffn + gap <= entry < chunks + gap
                piece = entry if early else entry - (gap or 0)
                inside = early or late
            else:
                early = (entry >= 0) & (entry < from_ffn)
                late = (entry >= from_ffn + gap) & (entry < chunks + gap)
                piece = jnp.where(entry < from_ffn, entry, entry - gap)
                inside = early | late

            def body(phase=phase, piece=piece):
                if phase == parts.last_phase:
                    parts.share_copy(piece).wait()
                elif phase:
                    parts.source = lambda start, size: flat_hbm.at[pl.ds(0, size)]
                    parts.advance(phase, piece)

            if phase:
                when(inside, body)
            else:
                if isinstance(entry, int):
                    first = early and entry < from_first_chunks
                    second = late or (early and not first)
                else:
                    first = early & (entry < from_first_chunks)
                    second = late | (early & (entry >= from_first_chunks))
                when(first, functools.partial(start_piece, from_first, piece))
                when(second, functools.partial(start_piece, from_second, piece))

    def pace(amount):
        clock["credit"] += amount
        while clock["credit"] >= 1:
            tick(clock["time"])
            clock["time"] += 1
            clock["credit"] -= 1

    back_line = LineScatter(me, count, back, back_box, total_buf, b_sems, subs)
    res_line = LineScatter(me, count, res, res_box, res_total, r_sems, subs)
    first_line = LineScatter(me, count, back, back_box, total_buf, f_sems, subs)
    branch_line = LineGather(me, count, branch, a_sems, subs)
    small_line = LineScatter(me, count, small_parts, small_box, small.at[pl.ds(0, 8)], p_sems)

    tile = 256

    def weight_grad(left, factor, base, height, per_output):
        panels = factor.shape[1] // lanes
        per_panel = per_output // lanes

        def store(slot, panel, row):
            return pltpu.make_async_copy(
                stage.at[slot, panel],
                flat_out.at[pl.ds(base + panel * height + row, tile)],
                stage_sems.at[slot, panel],
            )

        @pl.loop(0, height // tile)
        def _(index):
            slot = lax.rem(index, 2)
            row = pl.multiple_of(index * tile, tile)
            turned[...] = left[:, :, pl.ds(row, tile)].reshape(total, tile).T
            product = nn_dot(turned[...], factor).astype(jnp.bfloat16)

            @pl.when(index >= 2)
            def _():
                for panel in range(panels):
                    store(slot, panel, row).wait()

            for panel in range(panels):
                stage[slot, panel] = product[:, panel * lanes : (panel + 1) * lanes]
                store(slot, panel, row).start()

        for slot in range(min(2, height // tile)):
            for panel in range(panels):
                store(slot, panel, 0).wait()

    tick(0)
    for load in loads[7:17]:
        load.start()
    loads[0].wait()
    total_buf[...] = back[me].astype(jnp.float32)
    back_line.at_time(0)
    clock["time"] = 1
    pace(from_first_chunks - 1)
    for load in loads[1:3]:
        load.wait()
    gate_base, attn_base = 0, 2 * units * width // lanes
    weight_grad(n1_buf, grad_qkv[:, 0:units], gate_base, width, units)
    back_line.at_time(1)
    pace(1)
    loads[3].wait()
    weight_grad(n1_buf, grad_up[...], gate_base + units * width // lanes, width, units)
    loads[17].start()
    anti = lax.broadcasted_iota(jnp.int32, (total, total), 0) + lax.broadcasted_iota(
        jnp.int32, (total, total), 1
    )
    reverse[...] = (anti == total - 1).astype(jnp.float32).astype(jnp.bfloat16)
    for now in range(2, back_line.times):
        back_line.at_time(now)
        pace(scatter_pace)
    for load in loads[4:7]:
        load.wait()
    position = me * rows + lax.broadcasted_iota(jnp.int32, (rows, 1), 0)
    valid = (position < length_ref[0]).astype(jnp.float32)
    grad_mid, gain_grad = rms_backward(middle[...], total_buf[...], gains_ref[1:2, :])
    middle_grad[...] = cot[...].astype(jnp.float32) * valid + grad_mid
    branch[me] = middle_grad[...].astype(jnp.bfloat16)
    branch_line.begin()
    small_parts[...] = jnp.zeros_like(small_parts)
    part_width = width // count
    for owner in range(count):
        small_parts[owner, 1:2, :] = gain_grad[:, owner * part_width : (owner + 1) * part_width]
    for load in loads[7:18]:
        load.wait()
    res_total[...] = middle[...] + res[me].astype(jnp.float32)

    def attended_grad(block):
        grad_att[block] = nt_dot(branch[block], wo[...]).astype(jnp.bfloat16)

    attended_grad(me)
    for piece in range(branch_line.pieces):
        branch_line.arrive(piece)
        pace(gather_pace)
        if piece % subs == subs - 1:
            branch_line.each_block(piece // subs, attended_grad)

    mask_first, mask_second = head_masks()
    key_valid = lax.broadcasted_iota(jnp.int32, (1, total), 1) < length_ref[0]
    lane = lax.broadcasted_iota(jnp.int32, (1, lanes), 1)
    offsets[...] = jnp.zeros_like(offsets)

    def head_pair(pair):
        cols = pl.ds(pl.multiple_of(pair * lanes, lanes), lanes)
        key = k_buf[:, :, cols].reshape(total, lanes)
        value = v_buf[:, :, cols].reshape(total, lanes)
        key_acc[...] = jnp.zeros_like(key_acc)
        value_acc[...] = jnp.zeros_like(value_acc)

        @pl.loop(0, count)
        def _(block):
            query = q_buf[block, :, cols]
            grads = grad_att[block, :, cols]
            logs = lse_buf[block]
            query_parts = []
            for half, mask in enumerate((mask_first, mask_second)):
                head = pair * 2 + half
                query_half, grads_half = query * mask, grads * mask
                scores = nt_dot(query_half, key)
                scores = scores + offset_bias(bias_ref, head, block * rows, rows, total)
                scores = jnp.where(key_valid, scores, negative)
                log_total = jnp.sum(jnp.where(lane == head, logs, 0.0), axis=-1, keepdims=True)
                probs = jnp.exp(scores - log_total)
                grad_probs = nt_dot(grads_half, value)
                inner = jnp.sum(probs * grad_probs, axis=-1, keepdims=True)
                grad_scores = (probs * (grad_probs - inner)).astype(jnp.bfloat16)
                query_parts.append(nn_dot(grad_scores, key))
                key_acc[...] += nn_dot(query_half.astype(jnp.float32).T.astype(jnp.bfloat16), grad_scores)
                value_acc[...] += nn_dot(
                    grads_half.astype(jnp.float32).T.astype(jnp.bfloat16), probs.astype(jnp.bfloat16)
                )
                turned_scores = nn_dot(grad_scores, reverse[...])
                padded = jnp.concatenate([turned_scores, jnp.zeros_like(turned_scores)], axis=1)
                sheared = pltpu.roll(padded, 0, 1, stride=1, stride_axis=0)
                sums = jnp.broadcast_to(jnp.sum(sheared, axis=0, keepdims=True), (8, 2 * total))
                sums = pltpu.roll(sums, block * rows, 1)
                offsets[pl.ds(head, 1), :] += sums[0:1, :]
            grad_qkv[pl.ds(pl.multiple_of(block * rows, rows), rows), cols] = jnp.where(
                lane < head_dim, query_parts[0], query_parts[1]
            ).astype(jnp.bfloat16)

        grad_qkv[:, pl.ds(pl.multiple_of(columns + pair * lanes, lanes), lanes)] = key_acc[
            ...
        ].T.astype(jnp.bfloat16)
        grad_qkv[:, pl.ds(pl.multiple_of(2 * columns + pair * lanes, lanes), lanes)] = value_acc[
            ...
        ].T.astype(jnp.bfloat16)

    res_time = 0
    for pair in range(local_heads // 2):
        if res_time < 3:
            res_line.at_time(res_time)
            res_time += 1
        head_pair(pair)
        pace(pair_pace)

    back_line.wait_sends()

    def first_part(block):
        here = pl.ds(pl.multiple_of(block * rows, rows), rows)
        back[block] = (
            nt_dot(grad_qkv[here, 0:columns], wq[...])
            + nt_dot(grad_qkv[here, columns : 2 * columns], wk[...])
            + nt_dot(grad_qkv[here, 2 * columns :], wv[...])
        ).astype(jnp.bfloat16)

    for index in range(count):
        first_part(first_line.order(index))
        if index < count - 1:
            first_line.at_time(index)
        if index == count // 2 - 1:
            pace(1)
    total_buf[...] = back[me].astype(jnp.float32)
    weight_grad(att_buf, branch[...].reshape(total, width), attn_base, columns, width)
    weight_grad(n1_buf, grad_qkv[...], attn_base + columns * width // lanes, width, columns)
    clock["gap"] = max(clock["time"] - from_ffn, 0)
    pace(1)
    for now in range(count - 1, first_line.times):
        first_line.at_time(now)
        pace(1)
    grad_in, gain_grad = rms_backward(
        x_own[...].astype(jnp.float32), total_buf[...], gains_ref[0:1, :]
    )
    out_buf[1] = (middle_grad[...] + grad_in).astype(jnp.bfloat16)
    input_copy = pltpu.make_async_copy(out_buf.at[1], input_out, out_sems.at[1])
    input_copy.start()
    for owner in range(count):
        small_parts[owner, 0:1, :] = gain_grad[:, owner * part_width : (owner + 1) * part_width]
    small[0:8, :] = small_parts[me]
    for now in range(max(small_line.times, res_line.times - res_time)):
        if now < small_line.times:
            small_line.at_time(now)
        if res_time < res_line.times:
            res_line.at_time(res_time)
            res_time += 1
        pace(1)
    out_buf[0] = res_total[...].astype(jnp.bfloat16)
    result_copy = pltpu.make_async_copy(out_buf.at[0], result_out, out_sems.at[0])
    result_copy.start()
    bucket = lax.broadcasted_iota(jnp.int32, (lanes, ids_ref.shape[1]), 0)
    one_hot = (bucket == ids_ref[...]).astype(jnp.float32).astype(jnp.bfloat16)
    high = offsets[...].astype(jnp.bfloat16)
    rest = offsets[...] - high.astype(jnp.float32)
    middle_part = rest.astype(jnp.bfloat16)
    low_part = (rest - middle_part.astype(jnp.float32)).astype(jnp.bfloat16)
    small[8:16, 0:lanes] = nt_dot(high, one_hot) + nt_dot(middle_part, one_hot) + nt_dot(low_part, one_hot)
    small[8:16, lanes:] = jnp.zeros((8, part_width - lanes), jnp.float32)
    for index, mask in enumerate(masks):
        copy = pltpu.make_async_remote_copy(
            src_ref=small,
            dst_ref=pair_box.at[index],
            send_sem=pair_sems.at[0, index],
            recv_sem=pair_sems.at[1, index],
            device_id={"replica": mine ^ mask},
            device_id_type=MESH,
        )
        copy.start()
        pace(1)
        copy.wait()
        small[...] += pair_box[index]
    small_out[...] = small[...]

    @pl.loop(clock["time"], chunks + clock["gap"] + skew * parts.last_phase)
    def _(now):
        tick(now)

    for line in (res_line, first_line, branch_line, small_line):
        line.wait_sends()
    result_copy.wait()
    input_copy.wait()


def backward(count, replicas, length, flat, n2, grad_gate, grad_up, back, res, middle, cot, x, q, k, v, att, lse, n1, wq, wk, wv, wo, gains, bias, ids):
    rows, width = middle.shape
    total = count * rows
    columns = wq.shape[1]
    bf, f32 = jnp.bfloat16, jnp.float32
    shape = jax.ShapeDtypeStruct
    steps = count - 1
    dma = pltpu.SemaphoreType.DMA
    units = grad_up.shape[1]
    chunk = flat.shape[0] // 5
    ffn_rows = 3 * flat.shape[0]
    attn_rows = 4 * columns * width // lanes
    skew, subs = 3, 2
    levels = replicas.bit_length() - 2
    masks = levels + 1
    depth = skew * (levels + 2)
    part_width = width // count
    vmem = pltpu.VMEM
    blocks = lambda kind: vmem((count, rows, width), kind)
    narrow = lambda: vmem((count, rows, columns), bf)
    boxes = lambda: vmem((count + 1, rows, width), bf)
    return pl.pallas_call(
        functools.partial(
            backward_kernel, count, replicas, chunk, ffn_rows // chunk, attn_rows // chunk, skew, subs
        ),
        name="backward",
        out_shape=(
            shape((ffn_rows + attn_rows, lanes), bf),
            shape((2 * flat.shape[0] + attn_rows, lanes), bf),
            shape((rows, width), bf),
            shape((rows, width), bf),
            shape((16, part_width), f32),
        ),
        in_specs=[smem_space] + [any_space] * 19 + [vmem_space] * 3,
        out_specs=[any_space] * 4 + [vmem_space],
        scratch_shapes=[
            blocks(bf), blocks(bf), vmem((rows, width), f32), vmem((rows, width), bf), vmem((rows, width), bf),
            narrow(), narrow(), narrow(), narrow(), vmem((count, rows, lanes), f32), blocks(bf),
            vmem(wq.shape, bf), vmem(wk.shape, bf), vmem(wv.shape, bf), vmem(wo.shape, bf),
            boxes(), boxes(), vmem((rows, width), f32), vmem((rows, width), f32), vmem((rows, width), f32), blocks(bf),
            narrow(),
            vmem((lanes, total), f32), vmem((lanes, total), f32), vmem((total, 3 * columns), bf), vmem((total, units), bf),
            vmem((total, total), bf), vmem((8, 2 * total), f32), vmem((256, total), bf),
            vmem((2, width // lanes, 256, lanes), bf), vmem((2, rows, width), bf),
            vmem((16, part_width), f32), vmem((count, 8, part_width), f32), vmem((count + 1, 8, part_width), f32),
            vmem((masks, 16, part_width), f32),
            vmem((depth, chunk // 2, lanes), bf), vmem((2 * skew, chunk // 2, lanes), bf),
            vmem((2 * skew, 2, chunk // 4, lanes), bf),
            dma((18,)), dma((2, 2, steps * subs)), dma((2, 2, steps * subs)), dma((2, 2, steps * subs)),
            dma((2, 2, steps * subs)),
            dma((2, 2, steps)), dma((2, masks)), dma((2, width // lanes)), dma((2,)),
            dma((2, 2 * levels + 3, 3, 2 * skew)),
        ],
        compiler_params=pltpu.CompilerParams(
            collective_id=2, has_side_effects=True, vmem_limit_bytes=61 * 2**20
        ),
    )(length, flat, n2, grad_gate, grad_up, back, res, middle, cot, x, q, k, v, att, lse, n1, wq, wk, wv, wo, gains, bias, ids)


def widen_kernel(plan, slots, sums, *refs):
    targets, (inbox, outbox, in_sems, out_sems) = refs[:-4], refs[-4:]
    tiles = [
        (target, start, height, depth // lanes, size, row)
        for target, (start, height, depth, size) in zip(targets, plan)
        for row in range(0, height, size)
    ]

    def load(number):
        _, start, height, panels, size, row = tiles[number]
        slot = number % slots

        @pl.loop(0, panels)
        def _(panel):
            pltpu.make_async_copy(
                sums.at[pl.ds(start + row + panel * height, size)],
                inbox.at[slot, pl.ds(pl.multiple_of(panel * size, size), size)],
                in_sems.at[slot],
            ).start()

    def store(number):
        target, _, _, panels, size, row = tiles[number]
        return pltpu.make_async_copy(
            outbox.at[number % slots, pl.ds(0, size), pl.ds(0, panels * lanes)],
            target.at[pl.ds(row, size)],
            out_sems.at[number % slots],
        )

    for number in range(min(slots - 1, len(tiles))):
        load(number)
    for number in range(len(tiles)):
        _, _, _, panels, size, _ = tiles[number]
        slot = number % slots
        if number + slots - 1 < len(tiles):
            load(number + slots - 1)
        whole = inbox.at[slot, pl.ds(0, panels * size)]
        pltpu.make_async_copy(whole, whole, in_sems.at[slot]).wait()
        if number >= slots:
            store(number - slots).wait()

        @pl.loop(0, panels)
        def _(panel):
            outbox[slot, pl.ds(0, size), pl.ds(pl.multiple_of(panel * lanes, lanes), lanes)] = inbox[
                slot, pl.ds(pl.multiple_of(panel * size, size), size)
            ].astype(jnp.float32)

        store(number).start()
    for number in range(max(len(tiles) - slots, 0), len(tiles)):
        store(number).wait()


def widen(sums, shapes):
    slots = 4
    plan, start = [], 0
    for height, depth in shapes:
        size = 512 if depth <= 1024 else 256
        while height % size:
            size //= 2
        plan.append((start, height, depth, size))
        start += height * depth // lanes
    most_in = max(size * depth // lanes for _, _, depth, size in plan)
    most_rows = max(size for _, _, _, size in plan)
    return pl.pallas_call(
        functools.partial(widen_kernel, plan, slots),
        name="widen",
        out_shape=[jax.ShapeDtypeStruct(shape, jnp.float32) for shape in shapes],
        in_specs=[any_space],
        out_specs=[any_space] * len(shapes),
        scratch_shapes=[
            pltpu.VMEM((slots, most_in, lanes), jnp.bfloat16),
            pltpu.VMEM((slots, most_rows, max(depth for _, depth in shapes)), jnp.float32),
            pltpu.SemaphoreType.DMA((slots,)),
            pltpu.SemaphoreType.DMA((slots,)),
        ],
        compiler_params=pltpu.CompilerParams(vmem_limit_bytes=40 * 2**20),
    )(sums)


def local(
    inputs,
    seq_lengths,
    bucket_ids,
    norm1_gain,
    w_query,
    w_key,
    w_value,
    w_attn_out,
    bias_table,
    norm2_gain,
    w_gate,
    w_up,
    w_ffn_out,
    cotangent,
):
    count = lax.axis_size("group")
    replicas = lax.axis_size("replica")
    gains_local = jnp.pad(
        jnp.stack([norm1_gain, norm2_gain]).astype(jnp.float32), ((0, 6), (0, 0))
    )
    ids = jnp.pad(bucket_ids, (0, 1))[None, :]
    ids_back = jnp.pad(bucket_ids[::-1], (0, 1), constant_values=-1)[None, :]
    normed_one, query, key, value, attended, log_totals, g_all, middle, normed_two, gains, bias = (
        attention_forward(
            count, seq_lengths, inputs[0], cotangent[0], gains_local,
            w_query, w_key, w_value, w_attn_out, ids, bias_table.T,
        )
    )
    flat, back_part, result_part, normed_all, grad_gate, grad_up = feed_forward(
        count, seq_lengths, normed_two, g_all, w_gate, w_up, w_ffn_out
    )
    sums, _, result, input_grad, small = backward(
        count, replicas, seq_lengths, flat, normed_all, grad_gate, grad_up, back_part, result_part, middle,
        cotangent[0], inputs[0],
        query, key, value, attended, log_totals, normed_one,
        w_query, w_key, w_value, w_attn_out, gains, bias, ids_back,
    )
    weights = (w_ffn_out, w_gate, w_up, w_attn_out, w_query, w_key, w_value)
    ffn_out_grad, gate_grad, up_grad, attn_out_grad, query_grad, key_grad, value_grad = widen(
        sums, [weight.shape for weight in weights]
    )
    buckets, local_heads = bias_table.shape
    table_grad = small[8 : 8 + local_heads, :buckets].T
    return (
        result[None],
        input_grad[None],
        small[0],
        query_grad,
        key_grad,
        value_grad,
        attn_out_grad,
        table_grad,
        small[1],
        gate_grad,
        up_grad,
        ffn_out_grad,
    )


def solution(mesh):
    placed = (
        P("replica", "group", None),
        P("replica"),
        P(),
        P("group"),
        P(None, "group"),
        P(None, "group"),
        P(None, "group"),
        P("group", None),
        P(None, "group"),
        P("group"),
        P(None, "group"),
        P(None, "group"),
        P("group", None),
        P("replica", "group", None),
    )
    return jax.shard_map(
        local,
        mesh=mesh,
        in_specs=placed,
        out_specs=(
            P("replica", "group", None),
            P("replica", "group", None),
            P("group"),
            P(None, "group"),
            P(None, "group"),
            P(None, "group"),
            P("group", None),
            P(None, "group"),
            P("group"),
            P(None, "group"),
            P(None, "group"),
            P("group", None),
        ),
        check_vma=False,
    )
```

```python
import functools
import jax
import jax.numpy as jnp
from jax import lax
from jax.experimental import pallas as pl
from jax.experimental.pallas import tpu as pltpu
from jax.sharding import PartitionSpec as P

epsilon = 1e-06
negative = -1000000000.0
head_dim = 64
lanes = 128
MESH = pl.DeviceIdType.MESH
any_space = pl.BlockSpec(memory_space=pl.ANY)
vmem_space = pl.BlockSpec(memory_space=pltpu.VMEM)
smem_space = pl.BlockSpec(memory_space=pltpu.SMEM)


def nn_dot(left, right):
    return jnp.dot(left, right, preferred_element_type=jnp.float32)


def nt_dot(left, right):
    return lax.dot_general(
        left, right, (((1,), (1,)), ((), ())), preferred_element_type=jnp.float32
    )


def line_barrier(me, count):
    barrier = pltpu.get_barrier_semaphore()

    @pl.when(me > 0)
    def _():
        pl.semaphore_signal(barrier, inc=1, device_id={"group": me - 1}, device_id_type=MESH)

    @pl.when(me < count - 1)
    def _():
        pl.semaphore_signal(barrier, inc=1, device_id={"group": me + 1}, device_id_type=MESH)

    peers = jnp.where(me > 0, 1, 0) + jnp.where(me < count - 1, 1, 0)
    pl.semaphore_wait(barrier, peers)


class LineGather:
    def __init__(self, me, count, buffer, sems, subs=1, own=None):
        self.me, self.count, self.buffer, self.sems, self.subs = me, count, buffer, sems, subs
        self.own = own
        self.pieces = (count - 1) * subs
        self.size = buffer.shape[1] // subs

    def copy(self, side, piece, hops):
        block = self.me - hops if side == 0 else self.me + hops
        part = pl.ds(piece % self.subs * self.size, self.size)
        here = self.buffer.at[block, part]
        return pltpu.make_async_remote_copy(
            src_ref=here if hops or self.own is None else self.own.at[part],
            dst_ref=here,
            send_sem=self.sems.at[side, 0, piece],
            recv_sem=self.sems.at[side, 1, piece],
            device_id={"group": self.me + (1 if side == 0 else -1)},
            device_id_type=MESH,
        )

    def sends(self, side, piece):
        hops = piece // self.subs
        if side == 0:
            return (self.me - hops >= 0) & (self.me + 1 < self.count)
        return (self.me + hops < self.count) & (self.me >= 1)

    def arrives(self, side, piece):
        hops = piece // self.subs
        if side == 0:
            return self.me - 1 - hops >= 0
        return self.me + 1 + hops < self.count

    def send_side(self, side, piece):
        @pl.when(self.sends(side, piece))
        def _():
            self.copy(side, piece, piece // self.subs).start()

    def send(self, piece):
        for side in range(2):
            self.send_side(side, piece)

    def begin(self):
        for piece in range(self.subs):
            self.send(piece)

    def arrive(self, piece):
        for side in range(2):
            @pl.when(self.arrives(side, piece))
            def _():
                self.copy(side, piece, piece // self.subs + 1).wait_recv()

        if piece + self.subs < self.pieces:
            self.send(piece + self.subs)

    def arrive_block(self, hops, body):
        for piece in range(hops * self.subs, (hops + 1) * self.subs):
            self.arrive(piece)
        self.each_block(hops, body)

    def each_block(self, hops, body):
        @pl.loop(0, 2)
        def _(side):
            block = jnp.where(side == 0, self.me - 1 - hops, self.me + 1 + hops)

            @pl.when((block >= 0) & (block < self.count))
            def _():
                body(block)

    def wait_sends(self):
        for piece in range(self.pieces):
            for side in range(2):
                @pl.when(self.sends(side, piece))
                def _():
                    self.copy(side, piece, piece // self.subs).wait_send()


class LineScatter:
    def __init__(self, me, count, parts, inbox, total, sems, subs=1):
        self.me, self.count, self.parts, self.inbox = me, count, parts, inbox
        self.total, self.sems, self.subs = total, sems, subs
        self.times = (count - 1) * subs + 1
        self.size = parts.shape[1] // subs

    def order(self, index):
        picked = 0
        for device in range(self.count):
            due = [(step * self.subs + self.count - 1 - device, step) for step in range(device)]
            due += [
                (step * self.subs + device, self.count - 1 - step)
                for step in range(self.count - 1 - device)
            ]
            blocks = [block for _, block in sorted(due)] + [device]
            picked = picked + jnp.where(self.me == device, blocks[index], 0)
        return picked

    def copy(self, side, piece):
        step = piece // self.subs
        here = pl.ds(pl.multiple_of(piece % self.subs * self.size, self.size), self.size)
        owner = step if side == 0 else self.count - 1 - step
        return pltpu.make_async_remote_copy(
            src_ref=self.parts.at[owner, here],
            dst_ref=self.inbox.at[self.slot(side, step), here],
            send_sem=self.sems.at[side, 0, piece],
            recv_sem=self.sems.at[side, 1, piece],
            device_id={"group": self.me + (-1 if side == 0 else 1)},
            device_id_type=MESH,
        )

    def slot(self, side, step):
        return step if side == 0 else self.count - step

    def at_time(self, time):
        for side in range(2):
            before = self.count - 1 - self.me if side == 0 else self.me
            after = self.count - 1 - before
            piece = time - before
            step = piece // self.subs

            @pl.when((piece >= 0) & (step < after))
            def _():
                owner = step if side == 0 else self.count - 1 - step
                here = pl.ds(pl.multiple_of(piece % self.subs * self.size, self.size), self.size)

                @pl.when(before > 0)
                def _():
                    self.copy(side, piece).wait_recv()
                    self.parts[owner, here, :] = (
                        self.parts[owner, here, :].astype(jnp.float32)
                        + self.inbox[self.slot(side, step), here, :].astype(jnp.float32)
                    ).astype(self.parts.dtype)

                self.copy(side, piece).start()

            @pl.when((piece >= 0) & (step == after) & (before > 0))
            def _():
                here = pl.ds(pl.multiple_of(piece % self.subs * self.size, self.size), self.size)
                self.copy(side, piece).wait_recv()
                self.total[here, :] += self.inbox[self.slot(side, step), here, :].astype(jnp.float32)

    def wait_sends(self):
        for piece in range((self.count - 1) * self.subs):
            step = piece // self.subs
            for side in range(2):
                after = self.me if side == 0 else self.count - 1 - self.me

                @pl.when(step < after)
                def _():
                    self.copy(side, piece).wait_send()


def head_masks():
    lane = lax.broadcasted_iota(jnp.int32, (1, lanes), 1)
    first = (lane < head_dim).astype(jnp.float32)
    return first.astype(jnp.bfloat16), (1.0 - first).astype(jnp.bfloat16)


def offset_bias(bias_ref, head, row_start, rows, total):
    width = bias_ref.shape[1]
    shift = lax.rem(row_start + (width - (total - 1)), width)
    vector = pltpu.roll(jnp.broadcast_to(bias_ref[pl.ds(head, 1), :], (8, width)), shift, 1)
    vector = jnp.broadcast_to(vector[0:1, :], (rows, width))
    return pltpu.roll(vector, 0, 1, stride=1, stride_axis=0)[:, :total]


def rms_rows(values):
    return lax.rsqrt(jnp.mean(values * values, axis=-1, keepdims=True) + epsilon)


def attention_forward_kernel(
    count, subs,
    length_ref,
    x_hbm, cot_hbm, wq_hbm, wk_hbm, wv_hbm, wo_hbm, ids_ref, table_ref, gain1_ref, gain2_ref,
    n1_out, q_out, k_out, v_out, att_out, lse_out, cot_out, middle_out, n2_out, gains_out, bias_out,
    x_all, gains_all, wq, wk, wv, wo, parts, inbox, n1_buf, q_buf, k_buf, v_buf, att_buf, lse_buf, total_buf, n2_buf,
    local_sems, x_sems, g_sems, c_sems, s_sems, out_sems,
):
    me = lax.axis_index("group")
    rows, width = x_hbm.shape
    total = rows * count
    columns = wq.shape[1]
    local_heads = columns // head_dim
    loads = [
        pltpu.make_async_copy(source, target, local_sems.at[index])
        for index, (source, target) in enumerate(
            [
                (x_hbm, x_all.at[me]),
                (wq_hbm, wq),
                (wk_hbm, wk),
                (wv_hbm, wv),
                (wo_hbm, wo),
                (cot_hbm, cot_out.at[me]),
            ]
        )
    ]
    for load in loads:
        load.start()
    line_barrier(me, count)
    x_line = LineGather(me, count, x_all, x_sems, subs, x_hbm)
    g_line = LineGather(me, count, gains_all, g_sems)
    c_line = LineGather(me, count, cot_out, c_sems, subs, cot_hbm)
    gains_all[me, 0:1, :] = gain1_ref[...].astype(jnp.float32)
    gains_all[me, 1:2, :] = gain2_ref[...].astype(jnp.float32)
    g_line.begin()
    x_line.begin()

    bucket = lax.broadcasted_iota(jnp.int32, (table_ref.shape[1], ids_ref.shape[1]), 0)
    one_hot = (bucket == ids_ref[...]).astype(jnp.float32).astype(jnp.bfloat16)
    bias_out[...] = nn_dot(table_ref[...], one_hot)

    for piece in range(g_line.pieces):
        g_line.arrive(piece)
    for owner in range(count):
        gains_out[:, owner * (width // count) : (owner + 1) * (width // count)] = gains_all[owner]
    for load in loads[0:4]:
        load.wait()

    def project(block):
        values = x_all[block].astype(jnp.float32)
        normed = (values * rms_rows(values) * gains_out[0:1, :]).astype(jnp.bfloat16)
        n1_buf[block] = normed
        q_buf[block] = nn_dot(normed, wq[...]).astype(jnp.bfloat16)
        k_buf[block] = nn_dot(normed, wk[...]).astype(jnp.bfloat16)
        v_buf[block] = nn_dot(normed, wv[...]).astype(jnp.bfloat16)

    def begin_cotangent(sent):
        for side in range(2):
            last = me if side == 0 else count - 1 - me

            @pl.when(last == sent)
            def _():
                for piece in range(subs):
                    c_line.send_side(side, piece)

    begin_cotangent(0)
    for piece in range(subs):
        x_line.arrive(piece)
    begin_cotangent(1)
    project(me)
    x_line.each_block(0, project)
    for hops in range(1, count - 1):
        for piece in range(hops * subs, (hops + 1) * subs):
            x_line.arrive(piece)
        begin_cotangent(hops + 1)
        x_line.each_block(hops, project)

    loads[4].wait()
    mask_first, mask_second = head_masks()
    key_valid = lax.broadcasted_iota(jnp.int32, (1, total), 1) < length_ref[0]
    lane = lax.broadcasted_iota(jnp.int32, (1, lanes), 1)

    def attend(block):
        lse_buf[block] = jnp.zeros((rows, lanes), jnp.float32)

        @pl.loop(0, local_heads // 2)
        def _(pair):
            cols = pl.ds(pl.multiple_of(pair * lanes, lanes), lanes)
            query = q_buf[block, :, cols]
            key = k_buf[:, :, cols].reshape(total, lanes)
            value = v_buf[:, :, cols].reshape(total, lanes)
            outs = []
            for half, mask in enumerate((mask_first, mask_second)):
                head = pair * 2 + half
                scores = nt_dot(query * mask, key)
                scores = scores + offset_bias(bias_out, head, block * rows, rows, total)
                scores = jnp.where(key_valid, scores, negative)
                top = jnp.max(scores, axis=-1, keepdims=True)
                expd = jnp.exp(scores - top)
                summed = jnp.sum(expd, axis=-1, keepdims=True)
                probs = (expd * (1.0 / summed)).astype(jnp.bfloat16)
                outs.append(nn_dot(probs, value))
                lse_buf[block] = jnp.where(lane == head, top + jnp.log(summed), lse_buf[block])
            att_buf[block, :, cols] = jnp.where(lane < head_dim, outs[0], outs[1]).astype(
                jnp.bfloat16
            )

    scatter = LineScatter(me, count, parts, inbox, total_buf, s_sems, subs)
    arrived = 0
    for index in range(count - 1):
        block = scatter.order(index)
        attend(block)
        parts[block] = nn_dot(att_buf[block], wo[...]).astype(jnp.bfloat16)
        scatter.at_time(index)
        if index:
            c_line.arrive(arrived)
            arrived += 1
    attend(me)
    total_buf[...] = x_all[me].astype(jnp.float32) + nn_dot(att_buf[me], wo[...])
    outs = [
        pltpu.make_async_copy(source, target, out_sems.at[index])
        for index, (source, target) in enumerate(
            [(n1_buf, n1_out), (q_buf, q_out), (k_buf, k_out), (v_buf, v_out), (att_buf, att_out), (lse_buf, lse_out)]
        )
    ]
    for copy in outs:
        copy.start()
    for time in range(count - 1, scatter.times):
        scatter.at_time(time)
        if arrived < c_line.pieces:
            c_line.arrive(arrived)
            arrived += 1
    middle = total_buf[...]
    n2_buf[...] = (middle * rms_rows(middle) * gains_out[1:2, :]).astype(jnp.bfloat16)
    tail = [
        pltpu.make_async_copy(total_buf, middle_out, out_sems.at[len(outs)]),
        pltpu.make_async_copy(n2_buf, n2_out, out_sems.at[len(outs) + 1]),
    ]
    for copy in tail:
        copy.start()
    for piece in range(arrived, c_line.pieces):
        c_line.arrive(piece)
    for line in (g_line, x_line, c_line, scatter):
        line.wait_sends()
    loads[5].wait()
    for copy in outs + tail:
        copy.wait()


def attention_forward(count, length, x, cot, wq, wk, wv, wo, ids, table, gain1, gain2):
    rows, width = x.shape
    columns = wq.shape[1]
    local_heads = columns // head_dim
    bf, f32 = jnp.bfloat16, jnp.float32
    shape = jax.ShapeDtypeStruct
    steps = count - 1
    subs = 2
    dma = pltpu.SemaphoreType.DMA
    return pl.pallas_call(
        functools.partial(attention_forward_kernel, count, subs),
        name="attention_forward",
        out_shape=(
            shape((count, rows, width), bf),
            shape((count, rows, columns), bf),
            shape((count, rows, columns), bf),
            shape((count, rows, columns), bf),
            shape((count, rows, columns), bf),
            shape((count, rows, lanes), f32),
            shape((count, rows, width), bf),
            shape((rows, width), f32),
            shape((rows, width), bf),
            shape((8, width), f32),
            shape((local_heads, ids.shape[1]), f32),
        ),
        in_specs=[smem_space] + [any_space] * 6 + [vmem_space] * 4,
        out_specs=[any_space] * 9 + [vmem_space] * 2,
        scratch_shapes=[
            pltpu.VMEM((count, rows, width), bf),
            pltpu.VMEM((count, 8, gain1.shape[1]), f32),
            pltpu.VMEM(wq.shape, bf),
            pltpu.VMEM(wk.shape, bf),
            pltpu.VMEM(wv.shape, bf),
            pltpu.VMEM(wo.shape, bf),
            pltpu.VMEM((count, rows, width), bf),
            pltpu.VMEM((count + 1, rows, width), bf),
            pltpu.VMEM((count, rows, width), bf),
            pltpu.VMEM((count, rows, columns), bf),
            pltpu.VMEM((count, rows, columns), bf),
            pltpu.VMEM((count, rows, columns), bf),
            pltpu.VMEM((count, rows, columns), bf),
            pltpu.VMEM((count, rows, lanes), f32),
            pltpu.VMEM((rows, width), f32),
            pltpu.VMEM((rows, width), bf),
            dma((6,)),
            dma((2, 2, steps * subs)),
            dma((2, 2, steps)),
            dma((2, 2, steps * subs)),
            dma((2, 2, steps * subs)),
            dma((8,)),
        ],
        compiler_params=pltpu.CompilerParams(
            collective_id=0, has_side_effects=True, vmem_limit_bytes=56 * 2**20
        ),
    )(length, x, cot, wq, wk, wv, wo, ids, table, gain1, gain2)


def gelu_parts(gate):
    root = 0.7978845608028654
    inner = root * (gate + 0.044715 * gate * gate * gate)
    tanh = jnp.tanh(inner)
    half = 0.5 * (1.0 + tanh)
    slope = half + 0.5 * gate * (1.0 - tanh * tanh) * root * (1.0 + 3 * 0.044715 * gate * gate)
    return gate * half, slope


def feed_forward_kernel(
    count, tile, subs,
    length_ref,
    n2_hbm, cot_hbm, wg_hbm, wu_hbm, wf_hbm,
    flat_out, back_out, res_out, n2_out, gate_out, up_out,
    n2_all, g_all, wg, wu, wf, hid, grad_gate, grad_up, grad_hidden, back_buf, res_buf, turned, stage,
    local_sems, n_sems, out_sems, stage_sems,
):
    me = lax.axis_index("group")
    rows, width = n2_hbm.shape
    total = rows * count
    units = wg.shape[1]
    loads = [
        pltpu.make_async_copy(source, target, local_sems.at[index])
        for index, (source, target) in enumerate(
            [(n2_hbm, n2_all.at[me]), (cot_hbm, g_all), (wf_hbm, wf), (wg_hbm, wg), (wu_hbm, wu)]
        )
    ]
    for load in loads:
        load.start()
    line_barrier(me, count)
    line = LineGather(me, count, n2_all, n_sems, subs, n2_hbm)
    line.begin()

    loads[1].wait()

    @pl.loop(0, count)
    def _(block):
        position = block * rows + lax.broadcasted_iota(jnp.int32, (rows, 1), 0)
        valid = (position < length_ref[0]).astype(jnp.float32).astype(jnp.bfloat16)
        g_all[block] = g_all[block] * valid

    loads[2].wait()

    @pl.loop(0, units // tile)
    def _(index):
        here = pl.ds(pl.multiple_of(index * tile, tile), tile)
        grad_hidden[:, here] = nt_dot(g_all[...].reshape(total, width), wf[here, :])

    loads[0].wait()
    for load in loads[3:]:
        load.wait()

    def block_pass(block):
        normed = n2_all[block]
        here = pl.ds(pl.multiple_of(block * rows, rows), rows)
        gate = nn_dot(normed, wg[...])
        up = nn_dot(normed, wu[...])
        act, slope = gelu_parts(gate)
        hid[block] = (act * up).astype(jnp.bfloat16)
        grads = grad_hidden[here, :]
        grad_gate[here, :] = (grads * up * slope).astype(jnp.bfloat16)
        grad_up[here, :] = (grads * act).astype(jnp.bfloat16)
        res_buf[block] = nn_dot(hid[block], wf[...]).astype(jnp.bfloat16)
        half = width // 2
        for cols in (pl.ds(0, half), pl.ds(half, half)):
            back_buf[block, :, cols] = (
                nt_dot(grad_gate[here, :], wg[cols, :]) + nt_dot(grad_up[here, :], wu[cols, :])
            ).astype(jnp.bfloat16)

    block_pass(me)
    for hops in range(count - 1):
        line.arrive_block(hops, block_pass)
    outs = [
        pltpu.make_async_copy(source, target, out_sems.at[index])
        for index, (source, target) in enumerate(
            [(back_buf, back_out), (res_buf, res_out), (n2_all, n2_out), (grad_gate, gate_out), (grad_up, up_out)]
        )
    ]
    for copy in outs:
        copy.start()

    def weight_grad(left, right, base, height):
        depth = right.shape[2]
        panels = depth // lanes
        factor = right[...].reshape(total, depth)

        def store(slot, panel, row):
            return pltpu.make_async_copy(
                stage.at[slot, panel],
                flat_out.at[pl.ds(base + panel * height + row, tile)],
                stage_sems.at[slot, panel],
            )

        @pl.loop(0, height // tile)
        def _(index):
            slot = lax.rem(index, 2)
            row = pl.multiple_of(index * tile, tile)
            turned[...] = left[:, :, pl.ds(row, tile)].reshape(total, tile).T
            product = nn_dot(turned[...], factor).astype(jnp.bfloat16)

            @pl.when(index >= 2)
            def _():
                for panel in range(panels):
                    store(slot, panel, row).wait()

            for panel in range(panels):
                stage[slot, panel] = product[:, panel * lanes : (panel + 1) * lanes]
                store(slot, panel, row).start()

        for slot in range(2):
            for panel in range(panels):
                store(slot, panel, 0).wait()

    weight_grad(hid, g_all, 0, units)
    line.wait_sends()
    for copy in outs:
        copy.wait()


def feed_forward(count, length, n2, cot, wg, wu, wf):
    rows, width = n2.shape
    units = wg.shape[1]
    tile = 128 if units % 256 else 256
    bf = jnp.bfloat16
    shape = jax.ShapeDtypeStruct
    steps = count - 1
    subs = 2
    dma = pltpu.SemaphoreType.DMA
    return pl.pallas_call(
        functools.partial(feed_forward_kernel, count, tile, subs),
        name="feed_forward",
        out_shape=(
            shape((units * width // lanes, lanes), bf),
            shape((count, rows, width), bf),
            shape((count, rows, width), bf),
            shape((count, rows, width), bf),
            shape((count * rows, units), bf),
            shape((count * rows, units), bf),
        ),
        in_specs=[smem_space] + [any_space] * 5,
        out_specs=[any_space] * 6,
        scratch_shapes=[
            pltpu.VMEM((count, rows, width), bf),
            pltpu.VMEM((count, rows, width), bf),
            pltpu.VMEM(wg.shape, bf),
            pltpu.VMEM(wu.shape, bf),
            pltpu.VMEM(wf.shape, bf),
            pltpu.VMEM((count, rows, units), bf),
            pltpu.VMEM((count * rows, units), bf),
            pltpu.VMEM((count * rows, units), bf),
            pltpu.VMEM((count * rows, units), jnp.float32),
            pltpu.VMEM((count, rows, width), bf),
            pltpu.VMEM((count, rows, width), bf),
            pltpu.VMEM((tile, count * rows), bf),
            pltpu.VMEM((2, width // lanes, tile, lanes), bf),
            dma((5,)),
            dma((2, 2, steps * subs)),
            dma((5,)),
            dma((2, width // lanes)),
        ],
        compiler_params=pltpu.CompilerParams(
            collective_id=1, has_side_effects=True, vmem_limit_bytes=56 * 2**20
        ),
    )(length, n2, cot, wg, wu, wf)


def when(condition, body):
    if isinstance(condition, bool):
        if condition:
            body()
    else:
        pl.when(condition)(body)


class ReplicaSum:
    def __init__(self, replicas, chunk, source, target, work, core_box, path_box, sems):
        self.mine = lax.axis_index("replica")
        self.chunk, self.source, self.target = chunk, source, target
        self.work, self.core_box, self.path_box, self.sems = work, core_box, path_box, sems
        self.depth, self.slots = work.shape[0], core_box.shape[0]
        bits = [1 << index for index in range(1, replicas.bit_length() - 1)]
        self.orders = (bits, bits[::-1])
        self.levels = len(bits)
        self.last_phase = 2 * self.levels + 2
        self.half = chunk // 2

    def bit(self, mask):
        return jnp.where((self.mine & mask) != 0, 1, 0)

    def region(self, path, level):
        size = self.half // 2
        offset = path * size
        for mask in self.orders[path][:level]:
            size //= 2
            offset = offset + self.bit(mask) * size
        return offset, size

    def out_rows(self, chunk, offset, size):
        start = chunk * self.chunk + self.bit(1) * self.half + offset
        return self.target.at[pl.ds(pl.multiple_of(start, 16), size)]

    def sem(self, kind, phase, path, chunk):
        return self.sems.at[kind, phase, path, chunk % self.slots]

    def remote(self, source, target, phase, path, chunk, mask):
        return pltpu.make_async_remote_copy(
            src_ref=source,
            dst_ref=target,
            send_sem=self.sem(0, phase, path, chunk),
            recv_sem=self.sem(1, phase, path, chunk),
            device_id={"replica": self.mine ^ mask},
            device_id_type=MESH,
        )

    def core_copy(self, chunk):
        start = chunk * self.chunk + (1 - self.bit(1)) * self.half
        return self.remote(
            self.source(start, self.half), self.core_box.at[chunk % self.slots], 0, 0, chunk, 1
        )

    def load_copy(self, chunk):
        start = chunk * self.chunk + self.bit(1) * self.half
        return pltpu.make_async_copy(
            self.source(start, self.half), self.work.at[chunk % self.depth], self.sem(0, 0, 1, chunk)
        )

    def reduce_copy(self, chunk, path, level):
        mask = self.orders[path][level - 1]
        offset, size = self.region(path, level - 1)
        size //= 2
        start = pl.multiple_of(offset + (1 - self.bit(mask)) * size, 16)
        return self.remote(
            self.work.at[chunk % self.depth, pl.ds(start, size)],
            self.box(chunk, path, level),
            level, path, chunk, mask,
        )

    def box(self, chunk, path, level):
        size = self.half // 2 >> level
        start = sum(self.half // 2 >> step for step in range(1, level))
        return self.path_box.at[chunk % self.slots, path, pl.ds(start, size)]

    def add_box(self, chunk, path, level):
        offset, size = self.region(path, level)
        here = pl.ds(pl.multiple_of(offset, 16), size)
        slot = chunk % self.depth
        self.work[slot, here, :] = self.work[slot, here, :] + self.box(chunk, path, level)[...]

    def own_copy(self, chunk, path):
        offset, size = self.region(path, self.levels)
        return pltpu.make_async_copy(
            self.work.at[chunk % self.depth, pl.ds(pl.multiple_of(offset, 16), size)],
            self.out_rows(chunk, offset, size),
            self.sems.at[1, 0, 1 + path, chunk % self.slots],
        )

    def spread_copy(self, chunk, path, level):
        offset, size = self.region(path, level)
        if level == self.levels:
            source = self.work.at[chunk % self.depth, pl.ds(pl.multiple_of(offset, 16), size)]
        else:
            source = self.out_rows(chunk, offset, size)
        return self.remote(
            source, self.out_rows(chunk, offset, size),
            2 * self.levels + 1 - level, path, chunk, self.orders[path][level - 1],
        )

    def share_copy(self, chunk):
        rows = self.out_rows(chunk, 0, self.half)
        return self.remote(rows, rows, self.last_phase - 1, 0, chunk, 1)

    def advance(self, phase, chunk):
        levels = self.levels
        if phase == 0:
            self.core_copy(chunk).start()
            self.load_copy(chunk).start()
        elif phase <= levels + 1:
            if phase == 1:
                self.load_copy(chunk).wait()
                self.core_copy(chunk).wait()
                slot = chunk % self.depth
                self.work[slot] = self.work[slot] + self.core_box[chunk % self.slots]
            for path in range(2):
                if phase > 1:
                    self.reduce_copy(chunk, path, phase - 1).wait()
                    self.add_box(chunk, path, phase - 1)
                if phase <= levels:
                    self.reduce_copy(chunk, path, phase).start()
                else:
                    self.own_copy(chunk, path).start()
                    self.spread_copy(chunk, path, levels).start()
        else:
            level = 2 * levels + 1 - phase
            if level >= 0:
                for path in range(2):
                    self.spread_copy(chunk, path, level + 1).wait()
                    if level + 1 == levels:
                        self.own_copy(chunk, path).wait()
                    if level >= 1:
                        self.spread_copy(chunk, path, level).start()
                if level == 0:
                    self.share_copy(chunk).start()


scatter_pace, gather_pace, pair_pace = 1.0, 1.0, 1.0


def rms_backward(values, grads, gain):
    scale = rms_rows(values)
    unit = values * scale
    scaled = grads * gain
    inner = jnp.mean(scaled * unit, axis=-1, keepdims=True)
    return scale * (scaled - unit * inner), jnp.sum(grads * unit, axis=0, keepdims=True)


def backward_kernel(
    count, replicas, chunk, ffn_chunks, out_chunks, attn_chunks, skew, subs,
    length_ref,
    flat_hbm, n2_hbm, gate_hbm, up_hbm, back_hbm, res_hbm, middle_hbm, cot_hbm, x_hbm,
    q_hbm, k_hbm, v_hbm, att_hbm, lse_hbm, n1_hbm,
    wq_hbm, wk_hbm, wv_hbm, wo_hbm, gains_ref, bias_ref, ids_ref,
    sums_out, flat_out, result_out, input_out, small_out,
    back, res, middle, cot, x_own, q_buf, k_buf, v_buf, att_buf, lse_buf, n1_buf, wq, wk, wv, wo,
    back_box, res_box, total_buf, res_total, middle_grad, branch, grad_att, key_acc, value_acc, grad_qkv, grad_up,
    reverse, offsets, turned, stage, out_buf, small, small_parts, small_box, pair_box,
    work, core_box, path_box,
    load_sems, b_sems, r_sems, f_sems, a_sems, p_sems, pair_sems, stage_sems, out_sems, sum_sems,
):
    me = lax.axis_index("group")
    mine = lax.axis_index("replica")
    rows, width = middle.shape
    total = rows * count
    columns = wq.shape[1]
    local_heads = columns // head_dim
    units = grad_up.shape[1]
    sources = [
        back_hbm, n2_hbm, gate_hbm, up_hbm, middle_hbm, cot_hbm, x_hbm, wo_hbm, att_hbm, q_hbm, k_hbm, v_hbm,
        lse_hbm, wq_hbm, wk_hbm, wv_hbm, res_hbm, n1_hbm,
    ]
    targets = [
        back, n1_buf, grad_qkv.at[:, pl.ds(0, units)], grad_up, middle, cot, x_own, wo, att_buf, q_buf, k_buf, v_buf,
        lse_buf, wq, wk, wv, res, n1_buf,
    ]
    loads = [
        pltpu.make_async_copy(source, target, load_sems.at[index])
        for index, (source, target) in enumerate(zip(sources, targets))
    ]
    masks = [1 << index for index in range(replicas.bit_length() - 1)]
    barrier = pltpu.get_barrier_semaphore()

    @pl.when(me > 0)
    def _():
        pl.semaphore_signal(barrier, inc=1, device_id={"group": me - 1}, device_id_type=MESH)

    @pl.when(me < count - 1)
    def _():
        pl.semaphore_signal(barrier, inc=1, device_id={"group": me + 1}, device_id_type=MESH)

    for mask in masks:
        pl.semaphore_signal(barrier, inc=1, device_id={"replica": mine ^ mask}, device_id_type=MESH)
    peers = jnp.where(me > 0, 1, 0) + jnp.where(me < count - 1, 1, 0) + len(masks)
    for load in loads[:7]:
        load.start()
    pl.semaphore_wait(barrier, peers)

    first_rows = flat_hbm.shape[0]
    from_first_chunks = first_rows // chunk
    from_ffn = ffn_chunks
    chunks = from_ffn + attn_chunks

    def make_source(source_ref, base):
        return lambda start, size: source_ref.at[pl.ds(pl.multiple_of(start - base, 16), size)]

    parts = ReplicaSum(replicas, chunk, None, sums_out, work, core_box, path_box, sum_sems)
    from_first, from_second = make_source(flat_hbm, 0), make_source(flat_out, first_rows)
    clock = {"time": 0, "gaps": [0] + [None] * 4, "credit": 0.0}
    each = from_first_chunks
    bounds = [0, each, 2 * each, 3 * each, from_ffn + out_chunks, chunks]

    def start_piece(source, piece):
        parts.source = source
        parts.core_copy(piece).start()
        parts.load_copy(piece).start()

    def tick(time):
        for phase in range(parts.last_phase, -1, -1):
            entry = time - skew * phase
            inside, piece = False, entry
            for gap, low, high in zip(clock["gaps"], bounds, bounds[1:]):
                if gap is None:
                    continue
                if isinstance(entry, int):
                    if low + gap <= entry < high + gap:
                        inside, piece = True, entry - gap
                else:
                    here = (entry >= low + gap) & (entry < high + gap)
                    inside = inside | here
                    piece = jnp.where(here, entry - gap, piece)

            def body(phase=phase, piece=piece):
                if phase == parts.last_phase:
                    parts.share_copy(piece).wait()
                elif phase:
                    parts.source = lambda start, size: flat_hbm.at[pl.ds(0, size)]
                    parts.advance(phase, piece)

            if phase:
                when(inside, body)
            else:
                first, second = piece < from_first_chunks, piece >= from_first_chunks
                if isinstance(entry, int):
                    first, second = first and inside, second and inside
                else:
                    first, second = first & inside, second & inside
                when(first, functools.partial(start_piece, from_first, piece))
                when(second, functools.partial(start_piece, from_second, piece))

    def pace(amount):
        clock["credit"] += amount
        while clock["credit"] >= 1:
            tick(clock["time"])
            clock["time"] += 1
            clock["credit"] -= 1

    back_line = LineScatter(me, count, back, back_box, total_buf, b_sems, subs)
    res_line = LineScatter(me, count, res, res_box, res_total, r_sems, subs)
    first_line = LineScatter(me, count, back, back_box, total_buf, f_sems, subs)
    branch_line = LineGather(me, count, branch, a_sems, subs)
    small_line = LineScatter(me, count, small_parts, small_box, small.at[pl.ds(0, 8)], p_sems)

    tile = 256

    def weight_grad(left, factor, base, height, per_output, splits=1):
        panels = factor.shape[1] // lanes
        tiles = height // tile

        def store(slot, panel, row):
            return pltpu.make_async_copy(
                stage.at[slot, panel],
                flat_out.at[pl.ds(base + panel * height + row, tile)],
                stage_sems.at[slot, panel],
            )

        def run(first, last):
            @pl.loop(first, last)
            def _(index):
                slot = lax.rem(index, 2)
                row = pl.multiple_of(index * tile, tile)
                turned[...] = left[:, :, pl.ds(row, tile)].reshape(total, tile).T
                product = nn_dot(turned[...], factor).astype(jnp.bfloat16)

                @pl.when(index >= 2)
                def _():
                    for panel in range(panels):
                        store(slot, panel, row).wait()

                for panel in range(panels):
                    stage[slot, panel] = product[:, panel * lanes : (panel + 1) * lanes]
                    store(slot, panel, row).start()

        for split in range(splits):
            if split:
                pace(1)
            run(tiles * split // splits, tiles * (split + 1) // splits)
        for slot in range(min(2, tiles)):
            for panel in range(panels):
                store(slot, panel, 0).wait()

    def enter(group):
        before = clock["gaps"][group - 1]
        clock["gaps"][group] = max(clock["time"] - bounds[group], before)

    tick(0)
    for load in loads[7:17]:
        load.start()
    loads[0].wait()
    total_buf[...] = back[me].astype(jnp.float32)
    back_line.at_time(0)
    clock["time"] = 1
    pace(2 * skew - 1)
    for load in loads[1:3]:
        load.wait()
    gate_base, attn_base = 0, 2 * units * width // lanes
    weight_grad(n1_buf, grad_qkv[:, 0:units], gate_base, width, units, 2)
    enter(1)
    pace(1)
    back_line.at_time(1)
    pace(1)
    back_line.at_time(2)
    pace(1)
    loads[3].wait()
    weight_grad(n1_buf, grad_up[...], gate_base + units * width // lanes, width, units, 2)
    enter(2)
    loads[17].start()
    anti = lax.broadcasted_iota(jnp.int32, (rows, rows), 0) + lax.broadcasted_iota(
        jnp.int32, (rows, rows), 1
    )
    reverse[...] = (anti == rows - 1).astype(jnp.float32).astype(jnp.bfloat16)
    for now in range(3, back_line.times):
        back_line.at_time(now)
        pace(scatter_pace)
    for load in loads[4:7]:
        load.wait()
    position = me * rows + lax.broadcasted_iota(jnp.int32, (rows, 1), 0)
    valid = (position < length_ref[0]).astype(jnp.float32)
    grad_mid, gain_grad = rms_backward(middle[...], total_buf[...], gains_ref[1:2, :])
    middle_grad[...] = cot[...].astype(jnp.float32) * valid + grad_mid
    branch[me] = middle_grad[...].astype(jnp.bfloat16)
    branch_line.begin()
    small_parts[...] = jnp.zeros_like(small_parts)
    part_width = width // count
    for owner in range(count):
        small_parts[owner, 1:2, :] = gain_grad[:, owner * part_width : (owner + 1) * part_width]
    for load in loads[7:18]:
        load.wait()
    res_total[...] = middle[...] + res[me].astype(jnp.float32)

    def attended_grad(block):
        grad_att[block] = nt_dot(branch[block], wo[...]).astype(jnp.bfloat16)

    attended_grad(me)
    for piece in range(branch_line.pieces):
        branch_line.arrive(piece)
        pace(gather_pace)
        if piece % subs == subs - 1:
            branch_line.each_block(piece // subs, attended_grad)

    weight_grad(att_buf, branch[...].reshape(total, width), attn_base, columns, width)
    enter(3)
    pace(1)
    mask_first, mask_second = head_masks()
    key_valid = lax.broadcasted_iota(jnp.int32, (1, total), 1) < length_ref[0]
    lane = lax.broadcasted_iota(jnp.int32, (1, lanes), 1)
    offsets[...] = jnp.zeros_like(offsets)

    def head_pair(pair):
        cols = pl.ds(pl.multiple_of(pair * lanes, lanes), lanes)
        key = k_buf[:, :, cols].reshape(total, lanes)
        value = v_buf[:, :, cols].reshape(total, lanes)
        key_acc[...] = jnp.zeros_like(key_acc)
        value_acc[...] = jnp.zeros_like(value_acc)

        @pl.loop(0, count)
        def _(block):
            query = q_buf[block, :, cols]
            grads = grad_att[block, :, cols]
            logs = lse_buf[block]
            query_parts = []
            for half, mask in enumerate((mask_first, mask_second)):
                head = pair * 2 + half
                query_half, grads_half = query * mask, grads * mask
                scores = nt_dot(query_half, key)
                scores = scores + offset_bias(bias_ref, head, block * rows, rows, total)
                scores = jnp.where(key_valid, scores, negative)
                log_total = jnp.sum(jnp.where(lane == head, logs, 0.0), axis=-1, keepdims=True)
                probs = jnp.exp(scores - log_total)
                grad_probs = nt_dot(grads_half, value)
                inner = jnp.sum(probs * grad_probs, axis=-1, keepdims=True)
                grad_scores = (probs * (grad_probs - inner)).astype(jnp.bfloat16)
                query_parts.append(nn_dot(grad_scores, key))
                key_acc[...] += nn_dot(query_half.astype(jnp.float32).T.astype(jnp.bfloat16), grad_scores)
                value_acc[...] += nn_dot(
                    grads_half.astype(jnp.float32).T.astype(jnp.bfloat16), probs.astype(jnp.bfloat16)
                )
                turned_scores = nn_dot(reverse[...], grad_scores)
                padded = jnp.concatenate([turned_scores, jnp.zeros_like(turned_scores)], axis=1)
                sheared = pltpu.roll(padded, 0, 1, stride=1, stride_axis=0)
                sums = jnp.broadcast_to(jnp.sum(sheared, axis=0, keepdims=True), (8, 2 * total))
                sums = pltpu.roll(sums, total - rows - block * rows, 1)
                offsets[pl.ds(head, 1), :] += sums[0:1, :]
            grad_qkv[pl.ds(pl.multiple_of(block * rows, rows), rows), cols] = jnp.where(
                lane < head_dim, query_parts[0], query_parts[1]
            ).astype(jnp.bfloat16)

        grad_qkv[:, pl.ds(pl.multiple_of(columns + pair * lanes, lanes), lanes)] = key_acc[
            ...
        ].T.astype(jnp.bfloat16)
        grad_qkv[:, pl.ds(pl.multiple_of(2 * columns + pair * lanes, lanes), lanes)] = value_acc[
            ...
        ].T.astype(jnp.bfloat16)

    res_time = 0
    for pair in range(local_heads // 2):
        if res_time < 3:
            res_line.at_time(res_time)
            res_time += 1
        head_pair(pair)
        pace(pair_pace)

    back_line.wait_sends()

    quarter = width // 4
    for start in range(0, width, quarter):
        cols = pl.ds(start, quarter)
        back[:, :, cols] = (
            (
                nt_dot(grad_qkv[:, 0:columns], wq[cols, :])
                + nt_dot(grad_qkv[:, columns : 2 * columns], wk[cols, :])
                + nt_dot(grad_qkv[:, 2 * columns : 3 * columns], wv[cols, :])
            )
            .astype(jnp.bfloat16)
            .reshape(count, rows, quarter)
        )
        if start == quarter:
            pace(1)
    for now in range(count - 1):
        first_line.at_time(now)
    pace(1)
    total_buf[...] = back[me].astype(jnp.float32)
    weight_grad(n1_buf, grad_qkv[...], attn_base + columns * width // lanes, width, columns, 2)
    enter(4)
    pace(skew)
    for now in range(count - 1, first_line.times):
        first_line.at_time(now)
        pace(1)
    grad_in, gain_grad = rms_backward(
        x_own[...].astype(jnp.float32), total_buf[...], gains_ref[0:1, :]
    )
    out_buf[1] = (middle_grad[...] + grad_in).astype(jnp.bfloat16)
    input_copy = pltpu.make_async_copy(out_buf.at[1], input_out, out_sems.at[1])
    input_copy.start()
    for owner in range(count):
        small_parts[owner, 0:1, :] = gain_grad[:, owner * part_width : (owner + 1) * part_width]
    small[0:8, :] = small_parts[me]
    for now in range(max(small_line.times, res_line.times - res_time)):
        if now < small_line.times:
            small_line.at_time(now)
        if res_time < res_line.times:
            res_line.at_time(res_time)
            res_time += 1
        pace(1)
    out_buf[0] = res_total[...].astype(jnp.bfloat16)
    result_copy = pltpu.make_async_copy(out_buf.at[0], result_out, out_sems.at[0])
    result_copy.start()
    bucket = lax.broadcasted_iota(jnp.int32, (lanes, ids_ref.shape[1]), 0)
    one_hot = (bucket == ids_ref[...]).astype(jnp.float32).astype(jnp.bfloat16)
    high = offsets[...].astype(jnp.bfloat16)
    rest = offsets[...] - high.astype(jnp.float32)
    middle_part = rest.astype(jnp.bfloat16)
    low_part = (rest - middle_part.astype(jnp.float32)).astype(jnp.bfloat16)
    small[8:16, 0:lanes] = nt_dot(high, one_hot) + nt_dot(middle_part, one_hot) + nt_dot(low_part, one_hot)
    small[8:16, lanes:] = jnp.zeros((8, part_width - lanes), jnp.float32)
    for index, mask in enumerate(masks):
        copy = pltpu.make_async_remote_copy(
            src_ref=small,
            dst_ref=pair_box.at[index],
            send_sem=pair_sems.at[0, index],
            recv_sem=pair_sems.at[1, index],
            device_id={"replica": mine ^ mask},
            device_id_type=MESH,
        )
        copy.start()
        pace(1)
        copy.wait()
        small[...] += pair_box[index]
    small_out[...] = small[...]

    @pl.loop(clock["time"], chunks + clock["gaps"][4] + skew * parts.last_phase)
    def _(now):
        tick(now)

    for line in (res_line, first_line, branch_line, small_line):
        line.wait_sends()
    result_copy.wait()
    input_copy.wait()


def backward(count, replicas, length, flat, n2, grad_gate, grad_up, back, res, middle, cot, x, q, k, v, att, lse, n1, wq, wk, wv, wo, gains, bias, ids):
    rows, width = middle.shape
    total = count * rows
    columns = wq.shape[1]
    bf, f32 = jnp.bfloat16, jnp.float32
    shape = jax.ShapeDtypeStruct
    steps = count - 1
    dma = pltpu.SemaphoreType.DMA
    units = grad_up.shape[1]
    chunk = flat.shape[0] // 5
    ffn_rows = 3 * flat.shape[0]
    attn_rows = 4 * columns * width // lanes
    skew, subs = 3, 2
    levels = replicas.bit_length() - 2
    masks = levels + 1
    depth = skew * (levels + 2)
    part_width = width // count
    vmem = pltpu.VMEM
    blocks = lambda kind: vmem((count, rows, width), kind)
    narrow = lambda: vmem((count, rows, columns), bf)
    boxes = lambda: vmem((count + 1, rows, width), bf)
    return pl.pallas_call(
        functools.partial(
            backward_kernel, count, replicas, chunk, ffn_rows // chunk, wo.size // lanes // chunk,
            attn_rows // chunk, skew, subs
        ),
        name="backward",
        out_shape=(
            shape((ffn_rows + attn_rows, lanes), bf),
            shape((2 * flat.shape[0] + attn_rows, lanes), bf),
            shape((rows, width), bf),
            shape((rows, width), bf),
            shape((16, part_width), f32),
        ),
        in_specs=[smem_space] + [any_space] * 19 + [vmem_space] * 3,
        out_specs=[any_space] * 4 + [vmem_space],
        scratch_shapes=[
            blocks(bf), blocks(bf), vmem((rows, width), f32), vmem((rows, width), bf), vmem((rows, width), bf),
            narrow(), narrow(), narrow(), narrow(), vmem((count, rows, lanes), f32), blocks(bf),
            vmem(wq.shape, bf), vmem(wk.shape, bf), vmem(wv.shape, bf), vmem(wo.shape, bf),
            boxes(), boxes(), vmem((rows, width), f32), vmem((rows, width), f32), vmem((rows, width), f32), blocks(bf),
            narrow(),
            vmem((lanes, total), f32), vmem((lanes, total), f32), vmem((total, 3 * columns), bf), vmem((total, units), bf),
            vmem((rows, rows), bf), vmem((8, 2 * total), f32), vmem((256, total), bf),
            vmem((2, width // lanes, 256, lanes), bf), vmem((2, rows, width), bf),
            vmem((16, part_width), f32), vmem((count, 8, part_width), f32), vmem((count + 1, 8, part_width), f32),
            vmem((masks, 16, part_width), f32),
            vmem((depth, chunk // 2, lanes), bf), vmem((2 * skew, chunk // 2, lanes), bf),
            vmem((2 * skew, 2, chunk // 4, lanes), bf),
            dma((18,)), dma((2, 2, steps * subs)), dma((2, 2, steps * subs)), dma((2, 2, steps * subs)),
            dma((2, 2, steps * subs)),
            dma((2, 2, steps)), dma((2, masks)), dma((2, width // lanes)), dma((2,)),
            dma((2, 2 * levels + 3, 3, 2 * skew)),
        ],
        compiler_params=pltpu.CompilerParams(
            collective_id=2, has_side_effects=True, vmem_limit_bytes=61 * 2**20
        ),
    )(length, flat, n2, grad_gate, grad_up, back, res, middle, cot, x, q, k, v, att, lse, n1, wq, wk, wv, wo, gains, bias, ids)


def widen_kernel(plan, slots, sums, result, input_grad, *refs):
    targets, (inbox, outbox, in_sems, out_sems, pass_sems) = refs[:-5], refs[-5:]
    passed = [
        pltpu.make_async_copy(source, target, pass_sems.at[index])
        for index, (source, target) in enumerate(zip((result, input_grad), targets))
    ]
    for copy in passed:
        copy.start()
    targets = targets[2:]
    tiles = [
        (target, start, height, depth // lanes, size, row)
        for target, (start, height, depth, size) in zip(targets, plan)
        for row in range(0, height, size)
    ]

    def load(number):
        _, start, height, panels, size, row = tiles[number]
        slot = number % slots

        @pl.loop(0, panels)
        def _(panel):
            pltpu.make_async_copy(
                sums.at[pl.ds(start + row + panel * height, size)],
                inbox.at[slot, pl.ds(pl.multiple_of(panel * size, size), size)],
                in_sems.at[slot],
            ).start()

    def store(number):
        target, _, _, panels, size, row = tiles[number]
        return pltpu.make_async_copy(
            outbox.at[number % slots, pl.ds(0, size), pl.ds(0, panels * lanes)],
            target.at[pl.ds(row, size)],
            out_sems.at[number % slots],
        )

    for number in range(min(slots - 1, len(tiles))):
        load(number)
    for number in range(len(tiles)):
        _, _, _, panels, size, _ = tiles[number]
        slot = number % slots
        if number + slots - 1 < len(tiles):
            load(number + slots - 1)
        whole = inbox.at[slot, pl.ds(0, panels * size)]
        pltpu.make_async_copy(whole, whole, in_sems.at[slot]).wait()
        if number >= slots:
            store(number - slots).wait()

        @pl.loop(0, panels)
        def _(panel):
            outbox[slot, pl.ds(0, size), pl.ds(pl.multiple_of(panel * lanes, lanes), lanes)] = inbox[
                slot, pl.ds(pl.multiple_of(panel * size, size), size)
            ].astype(jnp.float32)

        store(number).start()
    for number in range(max(len(tiles) - slots, 0), len(tiles)):
        store(number).wait()
    for copy in passed:
        copy.wait()


def widen(sums, result, input_grad, shapes):
    slots = 4
    plan, start = [], 0
    for height, depth in shapes:
        size = 512 if depth <= 1024 else 256
        while height % size:
            size //= 2
        plan.append((start, height, depth, size))
        start += height * depth // lanes
    most_in = max(size * depth // lanes for _, _, depth, size in plan)
    most_rows = max(size for _, _, _, size in plan)
    return pl.pallas_call(
        functools.partial(widen_kernel, plan, slots),
        name="widen",
        out_shape=[jax.ShapeDtypeStruct(result.shape, result.dtype)] * 2
        + [jax.ShapeDtypeStruct(shape, jnp.float32) for shape in shapes],
        in_specs=[any_space] * 3,
        out_specs=[any_space] * (2 + len(shapes)),
        scratch_shapes=[
            pltpu.VMEM((slots, most_in, lanes), jnp.bfloat16),
            pltpu.VMEM((slots, most_rows, max(depth for _, depth in shapes)), jnp.float32),
            pltpu.SemaphoreType.DMA((slots,)),
            pltpu.SemaphoreType.DMA((slots,)),
            pltpu.SemaphoreType.DMA((2,)),
        ],
        compiler_params=pltpu.CompilerParams(vmem_limit_bytes=40 * 2**20),
    )(sums, result, input_grad)


def local(
    inputs,
    seq_lengths,
    bucket_ids,
    norm1_gain,
    w_query,
    w_key,
    w_value,
    w_attn_out,
    bias_table,
    norm2_gain,
    w_gate,
    w_up,
    w_ffn_out,
    cotangent,
):
    count = lax.axis_size("group")
    replicas = lax.axis_size("replica")
    ids = jnp.pad(bucket_ids, (0, 1))[None, :]
    normed_one, query, key, value, attended, log_totals, g_all, middle, normed_two, gains, bias = (
        attention_forward(
            count, seq_lengths, inputs[0], cotangent[0], w_query, w_key, w_value, w_attn_out,
            ids, bias_table.T, norm1_gain[None], norm2_gain[None],
        )
    )
    flat, back_part, result_part, normed_all, grad_gate, grad_up = feed_forward(
        count, seq_lengths, normed_two, g_all, w_gate, w_up, w_ffn_out
    )
    sums, _, result, input_grad, small = backward(
        count, replicas, seq_lengths, flat, normed_all, grad_gate, grad_up, back_part, result_part, middle,
        cotangent[0], inputs[0],
        query, key, value, attended, log_totals, normed_one,
        w_query, w_key, w_value, w_attn_out, gains, bias, ids,
    )
    weights = (w_ffn_out, w_gate, w_up, w_attn_out, w_query, w_key, w_value)
    result, input_grad, ffn_out_grad, gate_grad, up_grad, attn_out_grad, query_grad, key_grad, value_grad = (
        widen(sums, result, input_grad, [weight.shape for weight in weights])
    )
    buckets, local_heads = bias_table.shape
    table_grad = small[8 : 8 + local_heads, :buckets].T
    return (
        result[None],
        input_grad[None],
        small[0],
        query_grad,
        key_grad,
        value_grad,
        attn_out_grad,
        table_grad,
        small[1],
        gate_grad,
        up_grad,
        ffn_out_grad,
    )


def solution(mesh):
    placed = (
        P("replica", "group", None),
        P("replica"),
        P(),
        P("group"),
        P(None, "group"),
        P(None, "group"),
        P(None, "group"),
        P("group", None),
        P(None, "group"),
        P("group"),
        P(None, "group"),
        P(None, "group"),
        P("group", None),
        P("replica", "group", None),
    )
    return jax.shard_map(
        local,
        mesh=mesh,
        in_specs=placed,
        out_specs=(
            P("replica", "group", None),
            P("replica", "group", None),
            P("group"),
            P(None, "group"),
            P(None, "group"),
            P(None, "group"),
            P("group", None),
            P(None, "group"),
            P("group"),
            P(None, "group"),
            P(None, "group"),
            P("group", None),
        ),
        check_vma=False,
    )
```

```python
import functools
import jax
import jax.numpy as jnp
from jax import lax
from jax.experimental import pallas as pl
from jax.experimental.pallas import tpu as pltpu
from jax.sharding import PartitionSpec as P

epsilon = 1e-06
negative = -1000000000.0
head_dim = 64
lanes = 128
MESH = pl.DeviceIdType.MESH
any_space = pl.BlockSpec(memory_space=pl.ANY)
vmem_space = pl.BlockSpec(memory_space=pltpu.VMEM)
smem_space = pl.BlockSpec(memory_space=pltpu.SMEM)


def nn_dot(left, right):
    return jnp.dot(left, right, preferred_element_type=jnp.float32)


def nt_dot(left, right):
    return lax.dot_general(
        left, right, (((1,), (1,)), ((), ())), preferred_element_type=jnp.float32
    )


def line_barrier(me, count):
    barrier = pltpu.get_barrier_semaphore()

    @pl.when(me > 0)
    def _():
        pl.semaphore_signal(barrier, inc=1, device_id={"group": me - 1}, device_id_type=MESH)

    @pl.when(me < count - 1)
    def _():
        pl.semaphore_signal(barrier, inc=1, device_id={"group": me + 1}, device_id_type=MESH)

    peers = jnp.where(me > 0, 1, 0) + jnp.where(me < count - 1, 1, 0)
    pl.semaphore_wait(barrier, peers)


class LineGather:
    def __init__(self, me, count, buffer, sems, subs=1, own=None):
        self.me, self.count, self.buffer, self.sems, self.subs = me, count, buffer, sems, subs
        self.own = own
        self.pieces = (count - 1) * subs
        self.size = buffer.shape[1] // subs

    def copy(self, side, piece, hops):
        block = self.me - hops if side == 0 else self.me + hops
        part = pl.ds(piece % self.subs * self.size, self.size)
        here = self.buffer.at[block, part]
        return pltpu.make_async_remote_copy(
            src_ref=here if hops or self.own is None else self.own.at[part],
            dst_ref=here,
            send_sem=self.sems.at[side, 0, piece],
            recv_sem=self.sems.at[side, 1, piece],
            device_id={"group": self.me + (1 if side == 0 else -1)},
            device_id_type=MESH,
        )

    def sends(self, side, piece):
        hops = piece // self.subs
        if side == 0:
            return (self.me - hops >= 0) & (self.me + 1 < self.count)
        return (self.me + hops < self.count) & (self.me >= 1)

    def arrives(self, side, piece):
        hops = piece // self.subs
        if side == 0:
            return self.me - 1 - hops >= 0
        return self.me + 1 + hops < self.count

    def send_side(self, side, piece):
        @pl.when(self.sends(side, piece))
        def _():
            self.copy(side, piece, piece // self.subs).start()

    def send(self, piece):
        for side in range(2):
            self.send_side(side, piece)

    def begin(self):
        for piece in range(self.subs):
            self.send(piece)

    def arrive(self, piece):
        for side in range(2):
            @pl.when(self.arrives(side, piece))
            def _():
                self.copy(side, piece, piece // self.subs + 1).wait_recv()

        if piece + self.subs < self.pieces:
            self.send(piece + self.subs)

    def arrive_block(self, hops, body):
        for piece in range(hops * self.subs, (hops + 1) * self.subs):
            self.arrive(piece)
        self.each_block(hops, body)

    def each_block(self, hops, body):
        @pl.loop(0, 2)
        def _(side):
            block = jnp.where(side == 0, self.me - 1 - hops, self.me + 1 + hops)

            @pl.when((block >= 0) & (block < self.count))
            def _():
                body(block)

    def wait_sends(self):
        for piece in range(self.pieces):
            for side in range(2):
                @pl.when(self.sends(side, piece))
                def _():
                    self.copy(side, piece, piece // self.subs).wait_send()


class LineScatter:
    def __init__(self, me, count, parts, inbox, total, sems, subs=1):
        self.me, self.count, self.parts, self.inbox = me, count, parts, inbox
        self.total, self.sems, self.subs = total, sems, subs
        self.times = (count - 1) * subs + 1
        self.size = parts.shape[1] // subs

    def order(self, index):
        picked = 0
        for device in range(self.count):
            due = [(step * self.subs + self.count - 1 - device, step) for step in range(device)]
            due += [
                (step * self.subs + device, self.count - 1 - step)
                for step in range(self.count - 1 - device)
            ]
            blocks = [block for _, block in sorted(due)] + [device]
            picked = picked + jnp.where(self.me == device, blocks[index], 0)
        return picked

    def copy(self, side, piece):
        step = piece // self.subs
        here = pl.ds(pl.multiple_of(piece % self.subs * self.size, self.size), self.size)
        owner = step if side == 0 else self.count - 1 - step
        return pltpu.make_async_remote_copy(
            src_ref=self.parts.at[owner, here],
            dst_ref=self.inbox.at[self.slot(side, step), here],
            send_sem=self.sems.at[side, 0, piece],
            recv_sem=self.sems.at[side, 1, piece],
            device_id={"group": self.me + (-1 if side == 0 else 1)},
            device_id_type=MESH,
        )

    def slot(self, side, step):
        return step if side == 0 else self.count - step

    def at_time(self, time):
        for side in range(2):
            before = self.count - 1 - self.me if side == 0 else self.me
            after = self.count - 1 - before
            piece = time - before
            step = piece // self.subs

            @pl.when((piece >= 0) & (step < after))
            def _():
                owner = step if side == 0 else self.count - 1 - step
                here = pl.ds(pl.multiple_of(piece % self.subs * self.size, self.size), self.size)

                @pl.when(before > 0)
                def _():
                    self.copy(side, piece).wait_recv()
                    self.parts[owner, here, :] = (
                        self.parts[owner, here, :].astype(jnp.float32)
                        + self.inbox[self.slot(side, step), here, :].astype(jnp.float32)
                    ).astype(self.parts.dtype)

                self.copy(side, piece).start()

            @pl.when((piece >= 0) & (step == after) & (before > 0))
            def _():
                here = pl.ds(pl.multiple_of(piece % self.subs * self.size, self.size), self.size)
                self.copy(side, piece).wait_recv()
                self.total[here, :] += self.inbox[self.slot(side, step), here, :].astype(jnp.float32)

    def wait_sends(self):
        for piece in range((self.count - 1) * self.subs):
            step = piece // self.subs
            for side in range(2):
                after = self.me if side == 0 else self.count - 1 - self.me

                @pl.when(step < after)
                def _():
                    self.copy(side, piece).wait_send()


def head_masks():
    lane = lax.broadcasted_iota(jnp.int32, (1, lanes), 1)
    first = (lane < head_dim).astype(jnp.float32)
    return first.astype(jnp.bfloat16), (1.0 - first).astype(jnp.bfloat16)


def offset_bias(bias_ref, head, row_start, rows, total):
    width = bias_ref.shape[1]
    shift = lax.rem(row_start + (width - (total - 1)), width)
    vector = pltpu.roll(jnp.broadcast_to(bias_ref[pl.ds(head, 1), :], (8, width)), shift, 1)
    vector = jnp.broadcast_to(vector[0:1, :], (rows, width))
    return pltpu.roll(vector, 0, 1, stride=1, stride_axis=0)[:, :total]


def rms_rows(values):
    return lax.rsqrt(jnp.mean(values * values, axis=-1, keepdims=True) + epsilon)


def gelu_parts(gate):
    root = 0.7978845608028654
    inner = root * (gate + 0.044715 * gate * gate * gate)
    tanh = jnp.tanh(inner)
    half = 0.5 * (1.0 + tanh)
    slope = half + 0.5 * gate * (1.0 - tanh * tanh) * root * (1.0 + 3 * 0.044715 * gate * gate)
    return gate * half, slope


def forward_kernel(
    count, tile, subs,
    length_ref,
    x_hbm, cot_hbm, wq_hbm, wk_hbm, wv_hbm, wo_hbm, wf_hbm, wg_hbm, wu_hbm, packed_ref, table_ref,
    n1_out, q_out, k_out, v_out, att_out, lse_out, middle_out, flat_out, back_out, res_out, n2_out, gate_out, up_out,
    gains_out, bias_out, ids_out,
    x_all, g_all, gains_all, wq, wk, wv, wo, wf, wg, wu, back_buf, inbox, n1_buf, q_buf, k_buf, v_buf, att_buf, lse_buf,
    total_buf, hid, grad_gate, grad_up, grad_hidden, res_buf, turned, stage,
    local_sems, x_sems, g_sems, c_sems, s_sems, n_sems, out_sems, stage_sems,
):
    me = lax.axis_index("group")
    rows, width = x_hbm.shape
    total = rows * count
    columns = wq.shape[1]
    units = wg.shape[1]
    local_heads = columns // head_dim
    n2_all, parts = x_all, back_buf
    loads = [
        pltpu.make_async_copy(source, target, local_sems.at[index])
        for index, (source, target) in enumerate(
            [
                (x_hbm, x_all.at[me]),
                (cot_hbm, g_all.at[me]),
                (wq_hbm, wq),
                (wk_hbm, wk),
                (wv_hbm, wv),
                (wo_hbm, wo),
                (wf_hbm, wf),
                (wg_hbm, wg),
                (wu_hbm, wu),
            ]
        )
    ]
    for load in loads:
        load.start()
    line_barrier(me, count)
    x_line = LineGather(me, count, x_all, x_sems, subs, x_hbm)
    g_line = LineGather(me, count, gains_all, g_sems)
    c_line = LineGather(me, count, g_all, c_sems, subs)
    n_line = LineGather(me, count, n2_all, n_sems, subs)

    def packed_row(index, length):
        first = index * (packed_ref.shape[0] // 3)
        return jnp.concatenate(
            [packed_ref[row : row + 1, :] for row in range(first, first + length // lanes)], axis=1
        )

    for index in range(2):
        gains_all[me, index : index + 1, :] = packed_row(index, width // count)
    g_line.begin()
    x_line.begin()
    loads[1].wait()
    position = me * rows + lax.broadcasted_iota(jnp.int32, (rows, 1), 0)
    g_all[me] = g_all[me] * (position < length_ref[0]).astype(jnp.float32).astype(jnp.bfloat16)

    ids = packed_row(2, 2 * total)
    ids_out[...] = jnp.broadcast_to(ids, ids_out.shape)
    bucket = lax.broadcasted_iota(jnp.int32, (table_ref.shape[1], 2 * total), 0).astype(jnp.float32)
    one_hot = (bucket == ids).astype(jnp.float32).astype(jnp.bfloat16)
    bias_out[...] = nn_dot(table_ref[...], one_hot)

    for piece in range(g_line.pieces):
        g_line.arrive(piece)
    for owner in range(count):
        gains_out[:, owner * (width // count) : (owner + 1) * (width // count)] = gains_all[owner]
    for index in (0, 2, 3, 4):
        loads[index].wait()

    def project(block):
        values = x_all[block].astype(jnp.float32)
        normed = (values * rms_rows(values) * gains_out[0:1, :]).astype(jnp.bfloat16)
        n1_buf[block] = normed
        q_buf[block] = nn_dot(normed, wq[...]).astype(jnp.bfloat16)
        k_buf[block] = nn_dot(normed, wk[...]).astype(jnp.bfloat16)
        v_buf[block] = nn_dot(normed, wv[...]).astype(jnp.bfloat16)

    def begin_cotangent(sent):
        for side in range(2):
            last = me if side == 0 else count - 1 - me

            @pl.when(last == sent)
            def _():
                for piece in range(subs):
                    c_line.send_side(side, piece)

    begin_cotangent(0)
    for piece in range(subs):
        x_line.arrive(piece)
    begin_cotangent(1)
    project(me)
    x_line.each_block(0, project)
    for hops in range(1, count - 1):
        for piece in range(hops * subs, (hops + 1) * subs):
            x_line.arrive(piece)
        begin_cotangent(hops + 1)
        x_line.each_block(hops, project)

    loads[5].wait()
    mask_first, mask_second = head_masks()
    key_valid = lax.broadcasted_iota(jnp.int32, (1, total), 1) < length_ref[0]
    lane = lax.broadcasted_iota(jnp.int32, (1, lanes), 1)

    def attend(block):
        lse_buf[block] = jnp.zeros((rows, lanes), jnp.float32)

        @pl.loop(0, local_heads // 2)
        def _(pair):
            cols = pl.ds(pl.multiple_of(pair * lanes, lanes), lanes)
            query = q_buf[block, :, cols]
            key = k_buf[:, :, cols].reshape(total, lanes)
            value = v_buf[:, :, cols].reshape(total, lanes)
            outs = []
            for half, mask in enumerate((mask_first, mask_second)):
                head = pair * 2 + half
                scores = nt_dot(query * mask, key)
                scores = scores + offset_bias(bias_out, head, block * rows, rows, total)
                scores = jnp.where(key_valid, scores, negative)
                top = jnp.max(scores, axis=-1, keepdims=True)
                expd = jnp.exp(scores - top)
                summed = jnp.sum(expd, axis=-1, keepdims=True)
                probs = (expd * (1.0 / summed)).astype(jnp.bfloat16)
                outs.append(nn_dot(probs, value))
                lse_buf[block] = jnp.where(lane == head, top + jnp.log(summed), lse_buf[block])
            att_buf[block, :, cols] = jnp.where(lane < head_dim, outs[0], outs[1]).astype(
                jnp.bfloat16
            )

    scatter = LineScatter(me, count, parts, inbox, total_buf, s_sems, subs)
    arrived = 0
    for index in range(count - 1):
        block = scatter.order(index)
        attend(block)
        parts[block] = nn_dot(att_buf[block], wo[...]).astype(jnp.bfloat16)
        if index == 0:
            x_line.wait_sends()
        scatter.at_time(index)
        if index:
            c_line.arrive(arrived)
            arrived += 1
    attend(me)
    total_buf[...] = x_all[me].astype(jnp.float32) + nn_dot(att_buf[me], wo[...])
    early = [(n1_buf, n1_out), (q_buf, q_out), (k_buf, k_out), (v_buf, v_out), (att_buf, att_out), (lse_buf, lse_out)]
    late = [
        (total_buf, middle_out), (back_buf, back_out), (res_buf, res_out), (n2_all, n2_out), (grad_gate, gate_out),
        (grad_up, up_out),
    ]
    outs = [
        pltpu.make_async_copy(source, target, out_sems.at[index])
        for index, (source, target) in enumerate(early + late)
    ]
    for copy in outs[: len(early)]:
        copy.start()
    for time in range(count - 1, scatter.times):
        scatter.at_time(time)
        if arrived < c_line.pieces:
            c_line.arrive(arrived)
            arrived += 1
    middle = total_buf[...]
    n2_all[me] = (middle * rms_rows(middle) * gains_out[1:2, :]).astype(jnp.bfloat16)
    n_line.begin()
    outs[len(early)].start()
    for piece in range(arrived, c_line.pieces):
        c_line.arrive(piece)

    for load in loads[6:]:
        load.wait()

    @pl.loop(0, units // tile)
    def _(index):
        here = pl.ds(pl.multiple_of(index * tile, tile), tile)
        grad_hidden[:, here] = nt_dot(g_all[...].reshape(total, width), wf[here, :])

    scatter.wait_sends()

    def block_pass(block):
        normed = n2_all[block]
        here = pl.ds(pl.multiple_of(block * rows, rows), rows)
        gate = nn_dot(normed, wg[...])
        up = nn_dot(normed, wu[...])
        act, slope = gelu_parts(gate)
        hid[block] = (act * up).astype(jnp.bfloat16)
        grads = grad_hidden[here, :]
        grad_gate[here, :] = (grads * up * slope).astype(jnp.bfloat16)
        grad_up[here, :] = (grads * act).astype(jnp.bfloat16)
        res_buf[block] = nn_dot(hid[block], wf[...]).astype(jnp.bfloat16)
        half = width // 2
        for cols in (pl.ds(0, half), pl.ds(half, half)):
            back_buf[block, :, cols] = (
                nt_dot(grad_gate[here, :], wg[cols, :]) + nt_dot(grad_up[here, :], wu[cols, :])
            ).astype(jnp.bfloat16)

    for piece in range(subs):
        n_line.arrive(piece)
    block_pass(me)
    n_line.each_block(0, block_pass)
    for hops in range(1, count - 1):
        n_line.arrive_block(hops, block_pass)
    for copy in outs[len(early) + 1 :]:
        copy.start()

    def weight_grad(left, right, base, height):
        depth = right.shape[2]
        panels = depth // lanes
        factor = right[...].reshape(total, depth)

        def store(slot, panel, row):
            return pltpu.make_async_copy(
                stage.at[slot, panel],
                flat_out.at[pl.ds(base + panel * height + row, tile)],
                stage_sems.at[slot, panel],
            )

        @pl.loop(0, height // tile)
        def _(index):
            slot = lax.rem(index, 2)
            row = pl.multiple_of(index * tile, tile)
            turned[...] = left[:, :, pl.ds(row, tile)].reshape(total, tile).T
            product = nn_dot(turned[...], factor).astype(jnp.bfloat16)

            @pl.when(index >= 2)
            def _():
                for panel in range(panels):
                    store(slot, panel, row).wait()

            for panel in range(panels):
                stage[slot, panel] = product[:, panel * lanes : (panel + 1) * lanes]
                store(slot, panel, row).start()

        for slot in range(2):
            for panel in range(panels):
                store(slot, panel, 0).wait()

    weight_grad(hid, g_all, 0, units)
    for line in (g_line, c_line, n_line):
        line.wait_sends()
    for copy in outs:
        copy.wait()


def forward(count, length, x, cot, wq, wk, wv, wo, wf, wg, wu, packed, table):
    rows, width = x.shape
    columns, units = wq.shape[1], wg.shape[1]
    total = count * rows
    tile = 128 if units % 256 else 256
    bf, f32 = jnp.bfloat16, jnp.float32
    shape = jax.ShapeDtypeStruct
    steps = count - 1
    subs = 2
    dma = pltpu.SemaphoreType.DMA
    vmem = pltpu.VMEM
    blocks = (count, rows, width)
    narrow = (count, rows, columns)
    return pl.pallas_call(
        functools.partial(forward_kernel, count, tile, subs),
        name="forward",
        out_shape=(
            shape(blocks, bf), shape(narrow, bf), shape(narrow, bf), shape(narrow, bf), shape(narrow, bf),
            shape((count, rows, lanes), f32), shape((rows, width), f32),
            shape((units * width // lanes, lanes), bf), shape(blocks, bf), shape(blocks, bf), shape(blocks, bf),
            shape((total, units), bf), shape((total, units), bf),
            shape((8, width), f32), shape((columns // head_dim, 2 * total), f32), shape((8, 2 * total), f32),
        ),
        in_specs=[smem_space] + [any_space] * 9 + [vmem_space] * 2,
        out_specs=[any_space] * 13 + [vmem_space] * 3,
        scratch_shapes=[
            vmem(blocks, bf), vmem(blocks, bf), vmem((count, 8, width // count), f32),
            vmem(wq.shape, bf), vmem(wk.shape, bf), vmem(wv.shape, bf), vmem(wo.shape, bf),
            vmem(wf.shape, bf), vmem(wg.shape, bf), vmem(wu.shape, bf),
            vmem(blocks, bf), vmem((count + 1, rows, width), bf), vmem(blocks, bf),
            vmem(narrow, bf), vmem(narrow, bf), vmem(narrow, bf), vmem(narrow, bf), vmem((count, rows, lanes), f32),
            vmem((rows, width), f32), vmem((count, rows, units), bf), vmem((total, units), bf), vmem((total, units), bf),
            vmem((total, units), f32), vmem(blocks, bf), vmem((tile, total), bf),
            vmem((2, width // lanes, tile, lanes), bf),
            dma((9,)), dma((2, 2, steps * subs)), dma((2, 2, steps)), dma((2, 2, steps * subs)),
            dma((2, 2, steps * subs)), dma((2, 2, steps * subs)), dma((12,)), dma((2, width // lanes)),
        ],
        compiler_params=pltpu.CompilerParams(
            collective_id=0, has_side_effects=True, vmem_limit_bytes=61 * 2**20
        ),
    )(length, x, cot, wq, wk, wv, wo, wf, wg, wu, packed, table)


def when(condition, body):
    if isinstance(condition, bool):
        if condition:
            body()
    else:
        pl.when(condition)(body)


class ReplicaSum:
    def __init__(self, replicas, chunk, source, target, work, core_box, path_box, sems):
        self.mine = lax.axis_index("replica")
        self.chunk, self.source, self.target = chunk, source, target
        self.work, self.core_box, self.path_box, self.sems = work, core_box, path_box, sems
        self.depth, self.slots = work.shape[0], core_box.shape[0]
        bits = [1 << index for index in range(1, replicas.bit_length() - 1)]
        self.orders = (bits, bits[::-1])
        self.levels = len(bits)
        self.last_phase = 2 * self.levels + 2
        self.half = chunk // 2

    def bit(self, mask):
        return jnp.where((self.mine & mask) != 0, 1, 0)

    def region(self, path, level):
        size = self.half // 2
        offset = path * size
        for mask in self.orders[path][:level]:
            size //= 2
            offset = offset + self.bit(mask) * size
        return offset, size

    def out_rows(self, chunk, offset, size):
        start = chunk * self.chunk + self.bit(1) * self.half + offset
        return self.target.at[pl.ds(pl.multiple_of(start, 16), size)]

    def sem(self, kind, phase, path, chunk):
        return self.sems.at[kind, phase, path, chunk % self.slots]

    def remote(self, source, target, phase, path, chunk, mask):
        return pltpu.make_async_remote_copy(
            src_ref=source,
            dst_ref=target,
            send_sem=self.sem(0, phase, path, chunk),
            recv_sem=self.sem(1, phase, path, chunk),
            device_id={"replica": self.mine ^ mask},
            device_id_type=MESH,
        )

    def core_copy(self, chunk):
        start = chunk * self.chunk + (1 - self.bit(1)) * self.half
        return self.remote(
            self.source(start, self.half), self.core_box.at[chunk % self.slots], 0, 0, chunk, 1
        )

    def load_copy(self, chunk):
        start = chunk * self.chunk + self.bit(1) * self.half
        return pltpu.make_async_copy(
            self.source(start, self.half), self.work.at[chunk % self.depth], self.sem(0, 0, 1, chunk)
        )

    def reduce_copy(self, chunk, path, level):
        mask = self.orders[path][level - 1]
        offset, size = self.region(path, level - 1)
        size //= 2
        start = pl.multiple_of(offset + (1 - self.bit(mask)) * size, 16)
        return self.remote(
            self.work.at[chunk % self.depth, pl.ds(start, size)],
            self.box(chunk, path, level),
            level, path, chunk, mask,
        )

    def box(self, chunk, path, level):
        size = self.half // 2 >> level
        start = sum(self.half // 2 >> step for step in range(1, level))
        return self.path_box.at[chunk % self.slots, path, pl.ds(start, size)]

    def add_box(self, chunk, path, level):
        offset, size = self.region(path, level)
        here = pl.ds(pl.multiple_of(offset, 16), size)
        slot = chunk % self.depth
        self.work[slot, here, :] = self.work[slot, here, :] + self.box(chunk, path, level)[...]

    def own_copy(self, chunk, path):
        offset, size = self.region(path, self.levels)
        return pltpu.make_async_copy(
            self.work.at[chunk % self.depth, pl.ds(pl.multiple_of(offset, 16), size)],
            self.out_rows(chunk, offset, size),
            self.sems.at[1, 0, 1 + path, chunk % self.slots],
        )

    def spread_copy(self, chunk, path, level):
        offset, size = self.region(path, level)
        if level == self.levels:
            source = self.work.at[chunk % self.depth, pl.ds(pl.multiple_of(offset, 16), size)]
        else:
            source = self.out_rows(chunk, offset, size)
        return self.remote(
            source, self.out_rows(chunk, offset, size),
            2 * self.levels + 1 - level, path, chunk, self.orders[path][level - 1],
        )

    def share_copy(self, chunk):
        rows = self.out_rows(chunk, 0, self.half)
        return self.remote(rows, rows, self.last_phase - 1, 0, chunk, 1)

    def advance(self, phase, chunk):
        levels = self.levels
        if phase == 0:
            self.core_copy(chunk).start()
            self.load_copy(chunk).start()
        elif phase <= levels + 1:
            if phase == 1:
                self.load_copy(chunk).wait()
                self.core_copy(chunk).wait()
                slot = chunk % self.depth
                self.work[slot] = self.work[slot] + self.core_box[chunk % self.slots]
            for path in range(2):
                if phase > 1:
                    self.reduce_copy(chunk, path, phase - 1).wait()
                    self.add_box(chunk, path, phase - 1)
                if phase <= levels:
                    self.reduce_copy(chunk, path, phase).start()
                else:
                    self.own_copy(chunk, path).start()
                    self.spread_copy(chunk, path, levels).start()
        else:
            level = 2 * levels + 1 - phase
            if level >= 0:
                for path in range(2):
                    self.spread_copy(chunk, path, level + 1).wait()
                    if level + 1 == levels:
                        self.own_copy(chunk, path).wait()
                    if level >= 1:
                        self.spread_copy(chunk, path, level).start()
                if level == 0:
                    self.share_copy(chunk).start()


scatter_pace, gather_pace, pair_pace = 1.0, 1.0, 1.0


def rms_backward(values, grads, gain):
    scale = rms_rows(values)
    unit = values * scale
    scaled = grads * gain
    inner = jnp.mean(scaled * unit, axis=-1, keepdims=True)
    return scale * (scaled - unit * inner), jnp.sum(grads * unit, axis=0, keepdims=True)


def backward_kernel(
    count, replicas, chunk, ffn_chunks, out_chunks, attn_chunks, skew, subs,
    length_ref,
    flat_hbm, n2_hbm, gate_hbm, up_hbm, back_hbm, res_hbm, middle_hbm, cot_hbm, x_hbm,
    q_hbm, k_hbm, v_hbm, att_hbm, lse_hbm, n1_hbm,
    wq_hbm, wk_hbm, wv_hbm, wo_hbm, gains_ref, bias_ref, ids_ref,
    sums_out, flat_out, result_out, input_out, small_out,
    back, res, middle, cot, x_own, q_buf, k_buf, v_buf, att_buf, lse_buf, n1_buf, wq, wk, wv, wo,
    back_box, res_box, total_buf, res_total, middle_grad, branch, grad_att, key_acc, value_acc, grad_qkv, grad_up,
    reverse, offsets, turned, stage, out_buf, small, small_parts, small_box, pair_box,
    work, core_box, path_box,
    load_sems, b_sems, r_sems, f_sems, a_sems, p_sems, pair_sems, stage_sems, out_sems, sum_sems,
):
    me = lax.axis_index("group")
    mine = lax.axis_index("replica")
    rows, width = middle.shape
    total = rows * count
    columns = wq.shape[1]
    local_heads = columns // head_dim
    units = grad_up.shape[1]
    sources = [
        back_hbm, n2_hbm, gate_hbm, up_hbm, middle_hbm, cot_hbm, x_hbm, wo_hbm, att_hbm, q_hbm, k_hbm, v_hbm,
        lse_hbm, wq_hbm, wk_hbm, wv_hbm, res_hbm, n1_hbm,
    ]
    targets = [
        back, n1_buf, grad_qkv.at[:, pl.ds(0, units)], grad_up, middle, cot, x_own, wo, att_buf, q_buf, k_buf, v_buf,
        lse_buf, wq, wk, wv, res, n1_buf,
    ]
    loads = [
        pltpu.make_async_copy(source, target, load_sems.at[index])
        for index, (source, target) in enumerate(zip(sources, targets))
    ]
    masks = [1 << index for index in range(replicas.bit_length() - 1)]
    barrier = pltpu.get_barrier_semaphore()

    @pl.when(me > 0)
    def _():
        pl.semaphore_signal(barrier, inc=1, device_id={"group": me - 1}, device_id_type=MESH)

    @pl.when(me < count - 1)
    def _():
        pl.semaphore_signal(barrier, inc=1, device_id={"group": me + 1}, device_id_type=MESH)

    for mask in masks:
        pl.semaphore_signal(barrier, inc=1, device_id={"replica": mine ^ mask}, device_id_type=MESH)
    peers = jnp.where(me > 0, 1, 0) + jnp.where(me < count - 1, 1, 0) + len(masks)
    for load in loads[:7]:
        load.start()
    pl.semaphore_wait(barrier, peers)

    first_rows = flat_hbm.shape[0]
    from_first_chunks = first_rows // chunk
    from_ffn = ffn_chunks
    chunks = from_ffn + attn_chunks

    def make_source(source_ref, base):
        return lambda start, size: source_ref.at[pl.ds(pl.multiple_of(start - base, 16), size)]

    parts = ReplicaSum(replicas, chunk, None, sums_out, work, core_box, path_box, sum_sems)
    from_first, from_second = make_source(flat_hbm, 0), make_source(flat_out, first_rows)
    clock = {"time": 0, "gaps": [0] + [None] * 4, "credit": 0.0}
    each = from_first_chunks
    bounds = [0, each, 2 * each, 3 * each, from_ffn + out_chunks, chunks]

    def start_piece(source, piece):
        parts.source = source
        parts.core_copy(piece).start()
        parts.load_copy(piece).start()

    def tick(time):
        for phase in range(parts.last_phase, -1, -1):
            entry = time - skew * phase
            inside, piece = False, entry
            for gap, low, high in zip(clock["gaps"], bounds, bounds[1:]):
                if gap is None:
                    continue
                if isinstance(entry, int):
                    if low + gap <= entry < high + gap:
                        inside, piece = True, entry - gap
                else:
                    here = (entry >= low + gap) & (entry < high + gap)
                    inside = inside | here
                    piece = jnp.where(here, entry - gap, piece)

            def body(phase=phase, piece=piece):
                if phase == parts.last_phase:
                    parts.share_copy(piece).wait()
                elif phase:
                    parts.source = lambda start, size: flat_hbm.at[pl.ds(0, size)]
                    parts.advance(phase, piece)

            if phase:
                when(inside, body)
            else:
                first, second = piece < from_first_chunks, piece >= from_first_chunks
                if isinstance(entry, int):
                    first, second = first and inside, second and inside
                else:
                    first, second = first & inside, second & inside
                when(first, functools.partial(start_piece, from_first, piece))
                when(second, functools.partial(start_piece, from_second, piece))

    def pace(amount):
        clock["credit"] += amount
        while clock["credit"] >= 1:
            tick(clock["time"])
            clock["time"] += 1
            clock["credit"] -= 1

    back_line = LineScatter(me, count, back, back_box, total_buf, b_sems, subs)
    res_line = LineScatter(me, count, res, res_box, res_total, r_sems, subs)
    first_line = LineScatter(me, count, back, back_box, total_buf, f_sems, subs)
    branch_line = LineGather(me, count, branch, a_sems, subs)
    small_line = LineScatter(me, count, small_parts, small_box, small.at[pl.ds(0, 8)], p_sems)

    tile = 256

    def weight_grad(left, factor, base, height, per_output, splits=1):
        panels = factor.shape[1] // lanes
        tiles = height // tile

        def store(slot, panel, row):
            return pltpu.make_async_copy(
                stage.at[slot, panel],
                flat_out.at[pl.ds(base + panel * height + row, tile)],
                stage_sems.at[slot, panel],
            )

        def run(first, last):
            @pl.loop(first, last)
            def _(index):
                slot = lax.rem(index, 2)
                row = pl.multiple_of(index * tile, tile)
                turned[...] = left[:, :, pl.ds(row, tile)].reshape(total, tile).T
                product = nn_dot(turned[...], factor).astype(jnp.bfloat16)

                @pl.when(index >= 2)
                def _():
                    for panel in range(panels):
                        store(slot, panel, row).wait()

                for panel in range(panels):
                    stage[slot, panel] = product[:, panel * lanes : (panel + 1) * lanes]
                    store(slot, panel, row).start()

        for split in range(splits):
            if split:
                pace(1)
            run(tiles * split // splits, tiles * (split + 1) // splits)
        for slot in range(min(2, tiles)):
            for panel in range(panels):
                store(slot, panel, 0).wait()

    def enter(group):
        before = clock["gaps"][group - 1]
        clock["gaps"][group] = max(clock["time"] - bounds[group], before)

    tick(0)
    for load in loads[7:17]:
        load.start()
    loads[0].wait()
    total_buf[...] = back[me].astype(jnp.float32)
    back_line.at_time(0)
    clock["time"] = 1
    pace(2 * skew - 1)
    for load in loads[1:3]:
        load.wait()
    gate_base, attn_base = 0, 2 * units * width // lanes
    weight_grad(n1_buf, grad_qkv[:, 0:units], gate_base, width, units, 2)
    enter(1)
    pace(1)
    back_line.at_time(1)
    pace(1)
    back_line.at_time(2)
    pace(1)
    loads[3].wait()
    weight_grad(n1_buf, grad_up[...], gate_base + units * width // lanes, width, units, 2)
    enter(2)
    loads[17].start()
    anti = lax.broadcasted_iota(jnp.int32, (rows, rows), 0) + lax.broadcasted_iota(
        jnp.int32, (rows, rows), 1
    )
    reverse[...] = (anti == rows - 1).astype(jnp.float32).astype(jnp.bfloat16)
    for now in range(3, back_line.times):
        back_line.at_time(now)
        pace(scatter_pace)
    for load in loads[4:7]:
        load.wait()
    position = me * rows + lax.broadcasted_iota(jnp.int32, (rows, 1), 0)
    valid = (position < length_ref[0]).astype(jnp.float32)
    grad_mid, gain_grad = rms_backward(middle[...], total_buf[...], gains_ref[1:2, :])
    middle_grad[...] = cot[...].astype(jnp.float32) * valid + grad_mid
    branch[me] = middle_grad[...].astype(jnp.bfloat16)
    branch_line.begin()
    small_parts[...] = jnp.zeros_like(small_parts)
    part_width = width // count
    for owner in range(count):
        small_parts[owner, 1:2, :] = gain_grad[:, owner * part_width : (owner + 1) * part_width]
    for load in loads[7:18]:
        load.wait()
    res_total[...] = middle[...] + res[me].astype(jnp.float32)

    def attended_grad(block):
        grad_att[block] = nt_dot(branch[block], wo[...]).astype(jnp.bfloat16)

    attended_grad(me)
    for piece in range(branch_line.pieces):
        branch_line.arrive(piece)
        pace(gather_pace)
        if piece % subs == subs - 1:
            branch_line.each_block(piece // subs, attended_grad)

    weight_grad(att_buf, branch[...].reshape(total, width), attn_base, columns, width)
    enter(3)
    pace(1)
    mask_first, mask_second = head_masks()
    key_valid = lax.broadcasted_iota(jnp.int32, (1, total), 1) < length_ref[0]
    lane = lax.broadcasted_iota(jnp.int32, (1, lanes), 1)
    offsets[...] = jnp.zeros_like(offsets)

    def head_pair(pair):
        cols = pl.ds(pl.multiple_of(pair * lanes, lanes), lanes)
        key = k_buf[:, :, cols].reshape(total, lanes)
        value = v_buf[:, :, cols].reshape(total, lanes)
        key_acc[...] = jnp.zeros_like(key_acc)
        value_acc[...] = jnp.zeros_like(value_acc)

        @pl.loop(0, count)
        def _(block):
            query = q_buf[block, :, cols]
            grads = grad_att[block, :, cols]
            logs = lse_buf[block]
            query_parts = []
            for half, mask in enumerate((mask_first, mask_second)):
                head = pair * 2 + half
                query_half, grads_half = query * mask, grads * mask
                scores = nt_dot(query_half, key)
                scores = scores + offset_bias(bias_ref, head, block * rows, rows, total)
                scores = jnp.where(key_valid, scores, negative)
                log_total = jnp.sum(jnp.where(lane == head, logs, 0.0), axis=-1, keepdims=True)
                probs = jnp.exp(scores - log_total)
                grad_probs = nt_dot(grads_half, value)
                inner = jnp.sum(probs * grad_probs, axis=-1, keepdims=True)
                grad_scores = (probs * (grad_probs - inner)).astype(jnp.bfloat16)
                query_parts.append(nn_dot(grad_scores, key))
                key_acc[...] += nn_dot(query_half.astype(jnp.float32).T.astype(jnp.bfloat16), grad_scores)
                value_acc[...] += nn_dot(
                    grads_half.astype(jnp.float32).T.astype(jnp.bfloat16), probs.astype(jnp.bfloat16)
                )
                turned_scores = nn_dot(reverse[...], grad_scores)
                padded = jnp.concatenate([turned_scores, jnp.zeros_like(turned_scores)], axis=1)
                sheared = pltpu.roll(padded, 0, 1, stride=1, stride_axis=0)
                sums = jnp.broadcast_to(jnp.sum(sheared, axis=0, keepdims=True), (8, 2 * total))
                sums = pltpu.roll(sums, total - rows - block * rows, 1)
                offsets[pl.ds(head, 1), :] += sums[0:1, :]
            grad_qkv[pl.ds(pl.multiple_of(block * rows, rows), rows), cols] = jnp.where(
                lane < head_dim, query_parts[0], query_parts[1]
            ).astype(jnp.bfloat16)

        grad_qkv[:, pl.ds(pl.multiple_of(columns + pair * lanes, lanes), lanes)] = key_acc[
            ...
        ].T.astype(jnp.bfloat16)
        grad_qkv[:, pl.ds(pl.multiple_of(2 * columns + pair * lanes, lanes), lanes)] = value_acc[
            ...
        ].T.astype(jnp.bfloat16)

    res_time = 0
    for pair in range(local_heads // 2):
        if res_time < 3:
            res_line.at_time(res_time)
            res_time += 1
        head_pair(pair)
        pace(pair_pace)

    back_line.wait_sends()

    quarter = width // 4
    for start in range(0, width, quarter):
        cols = pl.ds(start, quarter)
        back[:, :, cols] = (
            (
                nt_dot(grad_qkv[:, 0:columns], wq[cols, :])
                + nt_dot(grad_qkv[:, columns : 2 * columns], wk[cols, :])
                + nt_dot(grad_qkv[:, 2 * columns : 3 * columns], wv[cols, :])
            )
            .astype(jnp.bfloat16)
            .reshape(count, rows, quarter)
        )
        if start == quarter:
            pace(1)
    for now in range(count - 1):
        first_line.at_time(now)
    pace(1)
    total_buf[...] = back[me].astype(jnp.float32)
    weight_grad(n1_buf, grad_qkv[...], attn_base + columns * width // lanes, width, columns, 2)
    enter(4)
    pace(skew)
    for now in range(count - 1, first_line.times):
        first_line.at_time(now)
        pace(1)
    grad_in, gain_grad = rms_backward(
        x_own[...].astype(jnp.float32), total_buf[...], gains_ref[0:1, :]
    )
    out_buf[1] = (middle_grad[...] + grad_in).astype(jnp.bfloat16)
    input_copy = pltpu.make_async_copy(out_buf.at[1], input_out, out_sems.at[1])
    input_copy.start()
    for owner in range(count):
        small_parts[owner, 0:1, :] = gain_grad[:, owner * part_width : (owner + 1) * part_width]
    small[0:8, :] = small_parts[me]
    for now in range(max(small_line.times, res_line.times - res_time)):
        if now < small_line.times:
            small_line.at_time(now)
        if res_time < res_line.times:
            res_line.at_time(res_time)
            res_time += 1
        pace(1)
    out_buf[0] = res_total[...].astype(jnp.bfloat16)
    result_copy = pltpu.make_async_copy(out_buf.at[0], result_out, out_sems.at[0])
    result_copy.start()
    bucket = lax.broadcasted_iota(jnp.int32, (lanes, ids_ref.shape[1]), 0).astype(jnp.float32)
    one_hot = (bucket == ids_ref[0:1, :]).astype(jnp.float32).astype(jnp.bfloat16)
    high = offsets[...].astype(jnp.bfloat16)
    rest = offsets[...] - high.astype(jnp.float32)
    middle_part = rest.astype(jnp.bfloat16)
    low_part = (rest - middle_part.astype(jnp.float32)).astype(jnp.bfloat16)
    small[8:16, 0:lanes] = nt_dot(high, one_hot) + nt_dot(middle_part, one_hot) + nt_dot(low_part, one_hot)
    small[8:16, lanes:] = jnp.zeros((8, part_width - lanes), jnp.float32)
    for index, mask in enumerate(masks):
        copy = pltpu.make_async_remote_copy(
            src_ref=small,
            dst_ref=pair_box.at[index],
            send_sem=pair_sems.at[0, index],
            recv_sem=pair_sems.at[1, index],
            device_id={"replica": mine ^ mask},
            device_id_type=MESH,
        )
        copy.start()
        pace(1)
        copy.wait()
        small[...] += pair_box[index]
    small_out[...] = small[...]

    @pl.loop(clock["time"], chunks + clock["gaps"][4] + skew * parts.last_phase)
    def _(now):
        tick(now)

    for line in (res_line, first_line, branch_line, small_line):
        line.wait_sends()
    result_copy.wait()
    input_copy.wait()


def backward(count, replicas, length, flat, n2, grad_gate, grad_up, back, res, middle, cot, x, q, k, v, att, lse, n1, wq, wk, wv, wo, gains, bias, ids):
    rows, width = middle.shape
    total = count * rows
    columns = wq.shape[1]
    bf, f32 = jnp.bfloat16, jnp.float32
    shape = jax.ShapeDtypeStruct
    steps = count - 1
    dma = pltpu.SemaphoreType.DMA
    units = grad_up.shape[1]
    chunk = flat.shape[0] // 5
    ffn_rows = 3 * flat.shape[0]
    attn_rows = 4 * columns * width // lanes
    skew, subs = 3, 2
    levels = replicas.bit_length() - 2
    masks = levels + 1
    depth = skew * (levels + 2)
    part_width = width // count
    vmem = pltpu.VMEM
    blocks = lambda kind: vmem((count, rows, width), kind)
    narrow = lambda: vmem((count, rows, columns), bf)
    boxes = lambda: vmem((count + 1, rows, width), bf)
    return pl.pallas_call(
        functools.partial(
            backward_kernel, count, replicas, chunk, ffn_rows // chunk, wo.size // lanes // chunk,
            attn_rows // chunk, skew, subs
        ),
        name="backward",
        out_shape=(
            shape((ffn_rows + attn_rows, lanes), bf),
            shape((2 * flat.shape[0] + attn_rows, lanes), bf),
            shape((rows, width), bf),
            shape((rows, width), bf),
            shape((16, part_width), f32),
        ),
        in_specs=[smem_space] + [any_space] * 19 + [vmem_space] * 3,
        out_specs=[any_space] * 4 + [vmem_space],
        scratch_shapes=[
            blocks(bf), blocks(bf), vmem((rows, width), f32), vmem((rows, width), bf), vmem((rows, width), bf),
            narrow(), narrow(), narrow(), narrow(), vmem((count, rows, lanes), f32), blocks(bf),
            vmem(wq.shape, bf), vmem(wk.shape, bf), vmem(wv.shape, bf), vmem(wo.shape, bf),
            boxes(), boxes(), vmem((rows, width), f32), vmem((rows, width), f32), vmem((rows, width), f32), blocks(bf),
            narrow(),
            vmem((lanes, total), f32), vmem((lanes, total), f32), vmem((total, 3 * columns), bf), vmem((total, units), bf),
            vmem((rows, rows), bf), vmem((8, 2 * total), f32), vmem((256, total), bf),
            vmem((2, width // lanes, 256, lanes), bf), vmem((2, rows, width), bf),
            vmem((16, part_width), f32), vmem((count, 8, part_width), f32), vmem((count + 1, 8, part_width), f32),
            vmem((masks, 16, part_width), f32),
            vmem((depth, chunk // 2, lanes), bf), vmem((2 * skew, chunk // 2, lanes), bf),
            vmem((2 * skew, 2, chunk // 4, lanes), bf),
            dma((18,)), dma((2, 2, steps * subs)), dma((2, 2, steps * subs)), dma((2, 2, steps * subs)),
            dma((2, 2, steps * subs)),
            dma((2, 2, steps)), dma((2, masks)), dma((2, width // lanes)), dma((2,)),
            dma((2, 2 * levels + 3, 3, 2 * skew)),
        ],
        compiler_params=pltpu.CompilerParams(
            collective_id=1, has_side_effects=True, vmem_limit_bytes=61 * 2**20
        ),
    )(length, flat, n2, grad_gate, grad_up, back, res, middle, cot, x, q, k, v, att, lse, n1, wq, wk, wv, wo, gains, bias, ids)


def widen_kernel(plan, slots, sums, result, input_grad, small, *refs):
    targets, (inbox, outbox, in_sems, out_sems, pass_sems) = refs[:-5], refs[-5:]
    passed = [
        pltpu.make_async_copy(source, target, pass_sems.at[index])
        for index, (source, target) in enumerate(zip((result, input_grad), targets))
    ]
    for copy in passed:
        copy.start()
    gain1, gain2, table = targets[2:5]
    for index, gain in enumerate((gain1, gain2)):
        for row in range(gain.shape[0]):
            gain[row : row + 1, :] = small[index : index + 1, row * lanes : (row + 1) * lanes]
    table[...] = small[8:16, 0:lanes].T[: table.shape[0], : table.shape[1]]
    targets = targets[5:]
    tiles = [
        (target, start, height, depth // lanes, size, row)
        for target, (start, height, depth, size) in zip(targets, plan)
        for row in range(0, height, size)
    ]

    def load(number):
        _, start, height, panels, size, row = tiles[number]
        slot = number % slots

        @pl.loop(0, panels)
        def _(panel):
            pltpu.make_async_copy(
                sums.at[pl.ds(start + row + panel * height, size)],
                inbox.at[slot, pl.ds(pl.multiple_of(panel * size, size), size)],
                in_sems.at[slot],
            ).start()

    def store(number):
        target, _, _, panels, size, row = tiles[number]
        return pltpu.make_async_copy(
            outbox.at[number % slots, pl.ds(0, size), pl.ds(0, panels * lanes)],
            target.at[pl.ds(row, size)],
            out_sems.at[number % slots],
        )

    for number in range(min(slots - 1, len(tiles))):
        load(number)
    for number in range(len(tiles)):
        _, _, _, panels, size, _ = tiles[number]
        slot = number % slots
        if number + slots - 1 < len(tiles):
            load(number + slots - 1)
        whole = inbox.at[slot, pl.ds(0, panels * size)]
        pltpu.make_async_copy(whole, whole, in_sems.at[slot]).wait()
        if number >= slots:
            store(number - slots).wait()

        @pl.loop(0, panels)
        def _(panel):
            outbox[slot, pl.ds(0, size), pl.ds(pl.multiple_of(panel * lanes, lanes), lanes)] = inbox[
                slot, pl.ds(pl.multiple_of(panel * size, size), size)
            ].astype(jnp.float32)

        store(number).start()
    for number in range(max(len(tiles) - slots, 0), len(tiles)):
        store(number).wait()
    for copy in passed:
        copy.wait()


def widen(sums, result, input_grad, small, table_shape, shapes):
    slots = 4
    plan, start = [], 0
    for height, depth in shapes:
        size = 512 if depth <= 1024 else 256
        while height % size:
            size //= 2
        plan.append((start, height, depth, size))
        start += height * depth // lanes
    most_in = max(size * depth // lanes for _, _, depth, size in plan)
    most_rows = max(size for _, _, _, size in plan)
    return pl.pallas_call(
        functools.partial(widen_kernel, plan, slots),
        name="widen",
        out_shape=[jax.ShapeDtypeStruct(result.shape, result.dtype)] * 2
        + [jax.ShapeDtypeStruct((small.shape[1] // lanes, lanes), jnp.float32)] * 2
        + [jax.ShapeDtypeStruct(table_shape, jnp.float32)]
        + [jax.ShapeDtypeStruct(shape, jnp.float32) for shape in shapes],
        in_specs=[any_space] * 3 + [vmem_space],
        out_specs=[any_space] * 2 + [vmem_space] * 3 + [any_space] * len(shapes),
        scratch_shapes=[
            pltpu.VMEM((slots, most_in, lanes), jnp.bfloat16),
            pltpu.VMEM((slots, most_rows, max(depth for _, depth in shapes)), jnp.float32),
            pltpu.SemaphoreType.DMA((slots,)),
            pltpu.SemaphoreType.DMA((slots,)),
            pltpu.SemaphoreType.DMA((2,)),
        ],
        compiler_params=pltpu.CompilerParams(vmem_limit_bytes=61 * 2**20),
    )(sums, result, input_grad, small)


def local(
    inputs,
    seq_lengths,
    bucket_ids,
    norm1_gain,
    w_query,
    w_key,
    w_value,
    w_attn_out,
    bias_table,
    norm2_gain,
    w_gate,
    w_up,
    w_ffn_out,
    cotangent,
):
    count = lax.axis_size("group")
    replicas = lax.axis_size("replica")
    longest = max(2 * count * inputs.shape[1], norm1_gain.shape[0])
    longest = -(-longest // 1024) * 1024
    packed = jnp.concatenate(
        [
            jnp.pad(vector.astype(jnp.float32), (0, longest - vector.shape[0]), constant_values=-1)
            for vector in (norm1_gain, norm2_gain, bucket_ids)
        ]
    ).reshape(-1, lanes)
    (
        normed_one, query, key, value, attended, log_totals, middle, flat, back_part, result_part, normed_all,
        grad_gate, grad_up, gains, bias, ids,
    ) = forward(
        count, seq_lengths, inputs[0], cotangent[0], w_query, w_key, w_value, w_attn_out, w_ffn_out, w_gate, w_up,
        packed, bias_table.T,
    )
    sums, _, result, input_grad, small = backward(
        count, replicas, seq_lengths, flat, normed_all, grad_gate, grad_up, back_part, result_part, middle,
        cotangent[0], inputs[0], query, key, value, attended, log_totals, normed_one,
        w_query, w_key, w_value, w_attn_out, gains, bias, ids,
    )
    weights = (w_ffn_out, w_gate, w_up, w_attn_out, w_query, w_key, w_value)
    (
        result, input_grad, gain1_grad, gain2_grad, table_grad,
        ffn_out_grad, gate_grad, up_grad, attn_out_grad, query_grad, key_grad, value_grad,
    ) = widen(sums, result, input_grad, small, bias_table.shape, [weight.shape for weight in weights])
    return (
        result[None],
        input_grad[None],
        gain1_grad.reshape(-1),
        query_grad,
        key_grad,
        value_grad,
        attn_out_grad,
        table_grad,
        gain2_grad.reshape(-1),
        gate_grad,
        up_grad,
        ffn_out_grad,
    )


def solution(mesh):
    placed = (
        P("replica", "group", None),
        P("replica"),
        P(),
        P("group"),
        P(None, "group"),
        P(None, "group"),
        P(None, "group"),
        P("group", None),
        P(None, "group"),
        P("group"),
        P(None, "group"),
        P(None, "group"),
        P("group", None),
        P("replica", "group", None),
    )
    return jax.shard_map(
        local,
        mesh=mesh,
        in_specs=placed,
        out_specs=(
            P("replica", "group", None),
            P("replica", "group", None),
            P("group"),
            P(None, "group"),
            P(None, "group"),
            P(None, "group"),
            P("group", None),
            P(None, "group"),
            P("group"),
            P(None, "group"),
            P(None, "group"),
            P("group", None),
        ),
        check_vma=False,
    )
```

```python
import functools
import jax
import jax.numpy as jnp
from jax import lax
from jax.experimental import pallas as pl
from jax.experimental.pallas import tpu as pltpu
from jax.sharding import PartitionSpec as P

epsilon = 1e-06
negative = -1000000000.0
head_dim = 64
lanes = 128
MESH = pl.DeviceIdType.MESH
any_space = pl.BlockSpec(memory_space=pl.ANY)
vmem_space = pl.BlockSpec(memory_space=pltpu.VMEM)
smem_space = pl.BlockSpec(memory_space=pltpu.SMEM)


def nn_dot(left, right):
    return jnp.dot(left, right, preferred_element_type=jnp.float32)


def nt_dot(left, right):
    return lax.dot_general(
        left, right, (((1,), (1,)), ((), ())), preferred_element_type=jnp.float32
    )


def line_barrier(me, count):
    barrier = pltpu.get_barrier_semaphore()

    @pl.when(me > 0)
    def _():
        pl.semaphore_signal(barrier, inc=1, device_id={"group": me - 1}, device_id_type=MESH)

    @pl.when(me < count - 1)
    def _():
        pl.semaphore_signal(barrier, inc=1, device_id={"group": me + 1}, device_id_type=MESH)

    peers = jnp.where(me > 0, 1, 0) + jnp.where(me < count - 1, 1, 0)
    pl.semaphore_wait(barrier, peers)


class LineGather:
    def __init__(self, me, count, buffer, sems, subs=1, own=None):
        self.me, self.count, self.buffer, self.sems, self.subs = me, count, buffer, sems, subs
        self.own = own
        self.pieces = (count - 1) * subs
        self.size = buffer.shape[1] // subs

    def copy(self, side, piece, hops):
        block = self.me - hops if side == 0 else self.me + hops
        part = pl.ds(piece % self.subs * self.size, self.size)
        here = self.buffer.at[block, part]
        return pltpu.make_async_remote_copy(
            src_ref=here if hops or self.own is None else self.own.at[part],
            dst_ref=here,
            send_sem=self.sems.at[side, 0, piece],
            recv_sem=self.sems.at[side, 1, piece],
            device_id={"group": self.me + (1 if side == 0 else -1)},
            device_id_type=MESH,
        )

    def sends(self, side, piece):
        hops = piece // self.subs
        if side == 0:
            return (self.me - hops >= 0) & (self.me + 1 < self.count)
        return (self.me + hops < self.count) & (self.me >= 1)

    def arrives(self, side, piece):
        hops = piece // self.subs
        if side == 0:
            return self.me - 1 - hops >= 0
        return self.me + 1 + hops < self.count

    def send_side(self, side, piece):
        @pl.when(self.sends(side, piece))
        def _():
            self.copy(side, piece, piece // self.subs).start()

    def send(self, piece):
        for side in range(2):
            self.send_side(side, piece)

    def begin(self):
        for piece in range(self.subs):
            self.send(piece)

    def arrive(self, piece):
        for side in range(2):
            @pl.when(self.arrives(side, piece))
            def _():
                self.copy(side, piece, piece // self.subs + 1).wait_recv()

        if piece + self.subs < self.pieces:
            self.send(piece + self.subs)

    def arrive_block(self, hops, body):
        for piece in range(hops * self.subs, (hops + 1) * self.subs):
            self.arrive(piece)
        self.each_block(hops, body)

    def each_block(self, hops, body):
        @pl.loop(0, 2)
        def _(side):
            block = jnp.where(side == 0, self.me - 1 - hops, self.me + 1 + hops)

            @pl.when((block >= 0) & (block < self.count))
            def _():
                body(block)

    def wait_sends(self):
        for piece in range(self.pieces):
            for side in range(2):
                @pl.when(self.sends(side, piece))
                def _():
                    self.copy(side, piece, piece // self.subs).wait_send()


class LineScatter:
    def __init__(self, me, count, parts, inbox, total, sems, subs=1):
        self.me, self.count, self.parts, self.inbox = me, count, parts, inbox
        self.total, self.sems, self.subs = total, sems, subs
        self.times = (count - 1) * subs + 1
        self.size = parts.shape[1] // subs

    def order(self, index):
        picked = 0
        for device in range(self.count):
            due = [(step * self.subs + self.count - 1 - device, step) for step in range(device)]
            due += [
                (step * self.subs + device, self.count - 1 - step)
                for step in range(self.count - 1 - device)
            ]
            blocks = [block for _, block in sorted(due)] + [device]
            picked = picked + jnp.where(self.me == device, blocks[index], 0)
        return picked

    def copy(self, side, piece):
        step = piece // self.subs
        here = pl.ds(pl.multiple_of(piece % self.subs * self.size, self.size), self.size)
        owner = step if side == 0 else self.count - 1 - step
        return pltpu.make_async_remote_copy(
            src_ref=self.parts.at[owner, here],
            dst_ref=self.inbox.at[self.slot(side, step), here],
            send_sem=self.sems.at[side, 0, piece],
            recv_sem=self.sems.at[side, 1, piece],
            device_id={"group": self.me + (-1 if side == 0 else 1)},
            device_id_type=MESH,
        )

    def slot(self, side, step):
        return step if side == 0 else self.count - step

    def at_time(self, time):
        for side in range(2):
            before = self.count - 1 - self.me if side == 0 else self.me
            after = self.count - 1 - before
            piece = time - before
            step = piece // self.subs

            @pl.when((piece >= 0) & (step < after))
            def _():
                owner = step if side == 0 else self.count - 1 - step
                here = pl.ds(pl.multiple_of(piece % self.subs * self.size, self.size), self.size)

                @pl.when(before > 0)
                def _():
                    self.copy(side, piece).wait_recv()
                    self.parts[owner, here, :] = (
                        self.parts[owner, here, :].astype(jnp.float32)
                        + self.inbox[self.slot(side, step), here, :].astype(jnp.float32)
                    ).astype(self.parts.dtype)

                self.copy(side, piece).start()

            @pl.when((piece >= 0) & (step == after) & (before > 0))
            def _():
                here = pl.ds(pl.multiple_of(piece % self.subs * self.size, self.size), self.size)
                self.copy(side, piece).wait_recv()
                self.total[here, :] += self.inbox[self.slot(side, step), here, :].astype(jnp.float32)

    def wait_sends(self):
        for piece in range((self.count - 1) * self.subs):
            step = piece // self.subs
            for side in range(2):
                after = self.me if side == 0 else self.count - 1 - self.me

                @pl.when(step < after)
                def _():
                    self.copy(side, piece).wait_send()


def head_masks():
    lane = lax.broadcasted_iota(jnp.int32, (1, lanes), 1)
    first = (lane < head_dim).astype(jnp.float32)
    return first.astype(jnp.bfloat16), (1.0 - first).astype(jnp.bfloat16)


def offset_bias(bias_ref, head, row_start, rows, total):
    width = bias_ref.shape[1]
    shift = lax.rem(row_start + (width - (total - 1)), width)
    vector = pltpu.roll(jnp.broadcast_to(bias_ref[pl.ds(head, 1), :], (8, width)), shift, 1)
    vector = jnp.broadcast_to(vector[0:1, :], (rows, width))
    return pltpu.roll(vector, 0, 1, stride=1, stride_axis=0)[:, :total]


def rms_rows(values):
    return lax.rsqrt(jnp.mean(values * values, axis=-1, keepdims=True) + epsilon)


def gelu_parts(gate):
    root = 0.7978845608028654
    inner = root * (gate + 0.044715 * gate * gate * gate)
    tanh = jnp.tanh(inner)
    half = 0.5 * (1.0 + tanh)
    slope = half + 0.5 * gate * (1.0 - tanh * tanh) * root * (1.0 + 3 * 0.044715 * gate * gate)
    return gate * half, slope


def forward_kernel(
    count, tile, subs,
    length_ref,
    x_hbm, cot_hbm, wq_hbm, wk_hbm, wv_hbm, wo_hbm, wf_hbm, wg_hbm, wu_hbm, packed_ref, table_ref,
    n1_out, q_out, k_out, v_out, att_out, lse_out, middle_out, flat_out, back_out, res_out, n2_out, gate_out, up_out,
    gains_out, bias_out, ids_out,
    x_all, g_all, gains_all, wq, wk, wv, wo, wf, wg, wu, back_buf, inbox, n1_buf, q_buf, k_buf, v_buf, att_buf, lse_buf,
    total_buf, hid, grad_gate, grad_up, grad_hidden, res_buf, turned, stage,
    local_sems, x_sems, g_sems, c_sems, s_sems, n_sems, out_sems, stage_sems,
):
    me = lax.axis_index("group")
    rows, width = x_hbm.shape
    total = rows * count
    columns = wq.shape[1]
    units = wg.shape[1]
    local_heads = columns // head_dim
    n2_all, parts = x_all, back_buf
    loads = [
        pltpu.make_async_copy(source, target, local_sems.at[index])
        for index, (source, target) in enumerate(
            [
                (x_hbm, x_all.at[me]),
                (cot_hbm, g_all.at[me]),
                (wq_hbm, wq),
                (wk_hbm, wk),
                (wv_hbm, wv),
                (wo_hbm, wo),
                (wf_hbm, wf),
                (wg_hbm, wg),
                (wu_hbm, wu),
            ]
        )
    ]
    for load in loads:
        load.start()
    line_barrier(me, count)
    x_line = LineGather(me, count, x_all, x_sems, subs, x_hbm)
    g_line = LineGather(me, count, gains_all, g_sems)
    c_line = LineGather(me, count, g_all, c_sems, subs)
    n_line = LineGather(me, count, n2_all, n_sems, subs)

    def packed_row(index, length):
        first = index * (packed_ref.shape[0] // 3)
        return jnp.concatenate(
            [packed_ref[row : row + 1, :] for row in range(first, first + length // lanes)], axis=1
        )

    for index in range(2):
        gains_all[me, index : index + 1, :] = packed_row(index, width // count)
    g_line.begin()
    x_line.begin()
    loads[1].wait()
    position = me * rows + lax.broadcasted_iota(jnp.int32, (rows, 1), 0)
    g_all[me] = g_all[me] * (position < length_ref[0]).astype(jnp.float32).astype(jnp.bfloat16)

    ids = packed_row(2, 2 * total)
    ids_out[...] = jnp.broadcast_to(ids, ids_out.shape)
    bucket = lax.broadcasted_iota(jnp.int32, (table_ref.shape[1], 2 * total), 0).astype(jnp.float32)
    one_hot = (bucket == ids).astype(jnp.float32).astype(jnp.bfloat16)
    bias_out[...] = nn_dot(table_ref[...], one_hot)

    for piece in range(g_line.pieces):
        g_line.arrive(piece)
    for owner in range(count):
        gains_out[:, owner * (width // count) : (owner + 1) * (width // count)] = gains_all[owner]
    for index in (0, 2, 3, 4):
        loads[index].wait()

    def project(block):
        values = x_all[block].astype(jnp.float32)
        normed = (values * rms_rows(values) * gains_out[0:1, :]).astype(jnp.bfloat16)
        n1_buf[block] = normed
        q_buf[block] = nn_dot(normed, wq[...]).astype(jnp.bfloat16)
        k_buf[block] = nn_dot(normed, wk[...]).astype(jnp.bfloat16)
        v_buf[block] = nn_dot(normed, wv[...]).astype(jnp.bfloat16)

    def begin_cotangent(sent):
        for side in range(2):
            last = me if side == 0 else count - 1 - me

            @pl.when(last == sent)
            def _():
                for piece in range(subs):
                    c_line.send_side(side, piece)

    begin_cotangent(0)
    for piece in range(subs):
        x_line.arrive(piece)
    begin_cotangent(1)
    project(me)
    x_line.each_block(0, project)
    for hops in range(1, count - 1):
        for piece in range(hops * subs, (hops + 1) * subs):
            x_line.arrive(piece)
        begin_cotangent(hops + 1)
        x_line.each_block(hops, project)

    loads[5].wait()
    mask_first, mask_second = head_masks()
    key_valid = lax.broadcasted_iota(jnp.int32, (1, total), 1) < length_ref[0]
    lane = lax.broadcasted_iota(jnp.int32, (1, lanes), 1)

    def attend(block):
        lse_buf[block] = jnp.zeros((rows, lanes), jnp.float32)

        @pl.loop(0, local_heads // 2)
        def _(pair):
            cols = pl.ds(pl.multiple_of(pair * lanes, lanes), lanes)
            query = q_buf[block, :, cols]
            key = k_buf[:, :, cols].reshape(total, lanes)
            value = v_buf[:, :, cols].reshape(total, lanes)
            outs = []
            for half, mask in enumerate((mask_first, mask_second)):
                head = pair * 2 + half
                scores = nt_dot(query * mask, key)
                scores = scores + offset_bias(bias_out, head, block * rows, rows, total)
                scores = jnp.where(key_valid, scores, negative)
                top = jnp.max(scores, axis=-1, keepdims=True)
                expd = jnp.exp(scores - top)
                summed = jnp.sum(expd, axis=-1, keepdims=True)
                probs = (expd * (1.0 / summed)).astype(jnp.bfloat16)
                outs.append(nn_dot(probs, value))
                lse_buf[block] = jnp.where(lane == head, top + jnp.log(summed), lse_buf[block])
            att_buf[block, :, cols] = jnp.where(lane < head_dim, outs[0], outs[1]).astype(
                jnp.bfloat16
            )

    scatter = LineScatter(me, count, parts, inbox, total_buf, s_sems, subs)
    arrived = 0
    for index in range(count - 1):
        block = scatter.order(index)
        attend(block)
        parts[block] = nn_dot(att_buf[block], wo[...]).astype(jnp.bfloat16)
        if index == 0:
            x_line.wait_sends()
        scatter.at_time(index)
        if index:
            c_line.arrive(arrived)
            arrived += 1
    attend(me)
    total_buf[...] = x_all[me].astype(jnp.float32) + nn_dot(att_buf[me], wo[...])
    early = [(n1_buf, n1_out), (q_buf, q_out), (k_buf, k_out), (v_buf, v_out), (att_buf, att_out), (lse_buf, lse_out)]
    late = [
        (total_buf, middle_out), (back_buf, back_out), (res_buf, res_out), (n2_all, n2_out), (grad_gate, gate_out),
        (grad_up, up_out),
    ]
    outs = [
        pltpu.make_async_copy(source, target, out_sems.at[index])
        for index, (source, target) in enumerate(early + late)
    ]
    for copy in outs[: len(early)]:
        copy.start()
    for time in range(count - 1, scatter.times):
        scatter.at_time(time)
        if arrived < c_line.pieces:
            c_line.arrive(arrived)
            arrived += 1
    middle = total_buf[...]
    n2_all[me] = (middle * rms_rows(middle) * gains_out[1:2, :]).astype(jnp.bfloat16)
    n_line.begin()
    outs[len(early)].start()
    for piece in range(arrived, c_line.pieces):
        c_line.arrive(piece)

    for load in loads[6:]:
        load.wait()

    @pl.loop(0, units // tile)
    def _(index):
        here = pl.ds(pl.multiple_of(index * tile, tile), tile)
        grad_hidden[:, here] = nt_dot(g_all[...].reshape(total, width), wf[here, :])

    scatter.wait_sends()

    def block_pass(block):
        normed = n2_all[block]
        here = pl.ds(pl.multiple_of(block * rows, rows), rows)
        gate = nn_dot(normed, wg[...])
        up = nn_dot(normed, wu[...])
        act, slope = gelu_parts(gate)
        hid[block] = (act * up).astype(jnp.bfloat16)
        grads = grad_hidden[here, :]
        grad_gate[here, :] = (grads * up * slope).astype(jnp.bfloat16)
        grad_up[here, :] = (grads * act).astype(jnp.bfloat16)
        res_buf[block] = nn_dot(hid[block], wf[...]).astype(jnp.bfloat16)
        half = width // 2
        for cols in (pl.ds(0, half), pl.ds(half, half)):
            back_buf[block, :, cols] = (
                nt_dot(grad_gate[here, :], wg[cols, :]) + nt_dot(grad_up[here, :], wu[cols, :])
            ).astype(jnp.bfloat16)

    for piece in range(subs):
        n_line.arrive(piece)
    block_pass(me)
    n_line.each_block(0, block_pass)
    for hops in range(1, count - 1):
        n_line.arrive_block(hops, block_pass)
    for copy in outs[len(early) + 1 :]:
        copy.start()

    def weight_grad(left, right, base, height):
        depth = right.shape[2]
        panels = depth // lanes
        factor = right[...].reshape(total, depth)

        def store(slot, panel, row):
            return pltpu.make_async_copy(
                stage.at[slot, panel],
                flat_out.at[pl.ds(base + panel * height + row, tile)],
                stage_sems.at[slot, panel],
            )

        @pl.loop(0, height // tile)
        def _(index):
            slot = lax.rem(index, 2)
            row = pl.multiple_of(index * tile, tile)
            turned[...] = left[:, :, pl.ds(row, tile)].reshape(total, tile).T
            product = nn_dot(turned[...], factor).astype(jnp.bfloat16)

            @pl.when(index >= 2)
            def _():
                for panel in range(panels):
                    store(slot, panel, row).wait()

            for panel in range(panels):
                stage[slot, panel] = product[:, panel * lanes : (panel + 1) * lanes]
                store(slot, panel, row).start()

        for slot in range(2):
            for panel in range(panels):
                store(slot, panel, 0).wait()

    weight_grad(hid, g_all, 0, units)
    for line in (g_line, c_line, n_line):
        line.wait_sends()
    for copy in outs:
        copy.wait()


def forward(count, length, x, cot, wq, wk, wv, wo, wf, wg, wu, packed, table):
    rows, width = x.shape
    columns, units = wq.shape[1], wg.shape[1]
    total = count * rows
    tile = 128 if units % 256 else 256
    bf, f32 = jnp.bfloat16, jnp.float32
    shape = jax.ShapeDtypeStruct
    steps = count - 1
    subs = 2
    dma = pltpu.SemaphoreType.DMA
    vmem = pltpu.VMEM
    blocks = (count, rows, width)
    narrow = (count, rows, columns)
    return pl.pallas_call(
        functools.partial(forward_kernel, count, tile, subs),
        name="forward",
        out_shape=(
            shape(blocks, bf), shape(narrow, bf), shape(narrow, bf), shape(narrow, bf), shape(narrow, bf),
            shape((count, rows, lanes), f32), shape((rows, width), f32),
            shape((units * width // lanes, lanes), bf), shape(blocks, bf), shape(blocks, bf), shape(blocks, bf),
            shape((total, units), bf), shape((total, units), bf),
            shape((8, width), f32), shape((columns // head_dim, 2 * total), f32), shape((8, 2 * total), f32),
        ),
        in_specs=[smem_space] + [any_space] * 9 + [vmem_space] * 2,
        out_specs=[any_space] * 13 + [vmem_space] * 3,
        scratch_shapes=[
            vmem(blocks, bf), vmem(blocks, bf), vmem((count, 8, width // count), f32),
            vmem(wq.shape, bf), vmem(wk.shape, bf), vmem(wv.shape, bf), vmem(wo.shape, bf),
            vmem(wf.shape, bf), vmem(wg.shape, bf), vmem(wu.shape, bf),
            vmem(blocks, bf), vmem((count + 1, rows, width), bf), vmem(blocks, bf),
            vmem(narrow, bf), vmem(narrow, bf), vmem(narrow, bf), vmem(narrow, bf), vmem((count, rows, lanes), f32),
            vmem((rows, width), f32), vmem((count, rows, units), bf), vmem((total, units), bf), vmem((total, units), bf),
            vmem((total, units), f32), vmem(blocks, bf), vmem((tile, total), bf),
            vmem((2, width // lanes, tile, lanes), bf),
            dma((9,)), dma((2, 2, steps * subs)), dma((2, 2, steps)), dma((2, 2, steps * subs)),
            dma((2, 2, steps * subs)), dma((2, 2, steps * subs)), dma((12,)), dma((2, width // lanes)),
        ],
        compiler_params=pltpu.CompilerParams(
            collective_id=0, has_side_effects=True, vmem_limit_bytes=61 * 2**20
        ),
    )(length, x, cot, wq, wk, wv, wo, wf, wg, wu, packed, table)


def when(condition, body):
    if isinstance(condition, bool):
        if condition:
            body()
    else:
        pl.when(condition)(body)


class ReplicaSum:
    def __init__(self, replicas, chunk, source, target, work, core_box, path_box, sems):
        self.mine = lax.axis_index("replica")
        self.chunk, self.source, self.target = chunk, source, target
        self.work, self.core_box, self.path_box, self.sems = work, core_box, path_box, sems
        self.depth, self.slots = work.shape[0], core_box.shape[0]
        bits = [1 << index for index in range(1, replicas.bit_length() - 1)]
        self.orders = (bits, bits[::-1])
        self.levels = len(bits)
        self.last_phase = 2 * self.levels + 2
        self.half = chunk // 2

    def bit(self, mask):
        return jnp.where((self.mine & mask) != 0, 1, 0)

    def region(self, path, level):
        size = self.half // 2
        offset = path * size
        for mask in self.orders[path][:level]:
            size //= 2
            offset = offset + self.bit(mask) * size
        return offset, size

    def out_rows(self, chunk, offset, size):
        start = chunk * self.chunk + self.bit(1) * self.half + offset
        return self.target.at[pl.ds(pl.multiple_of(start, 16), size)]

    def sem(self, kind, phase, path, chunk):
        return self.sems.at[kind, phase, path, chunk % self.slots]

    def remote(self, source, target, phase, path, chunk, mask):
        return pltpu.make_async_remote_copy(
            src_ref=source,
            dst_ref=target,
            send_sem=self.sem(0, phase, path, chunk),
            recv_sem=self.sem(1, phase, path, chunk),
            device_id={"replica": self.mine ^ mask},
            device_id_type=MESH,
        )

    def core_copy(self, chunk):
        start = chunk * self.chunk + (1 - self.bit(1)) * self.half
        return self.remote(
            self.source(start, self.half), self.core_box.at[chunk % self.slots], 0, 0, chunk, 1
        )

    def load_copy(self, chunk):
        start = chunk * self.chunk + self.bit(1) * self.half
        return pltpu.make_async_copy(
            self.source(start, self.half), self.work.at[chunk % self.depth], self.sem(0, 0, 1, chunk)
        )

    def reduce_copy(self, chunk, path, level):
        mask = self.orders[path][level - 1]
        offset, size = self.region(path, level - 1)
        size //= 2
        start = pl.multiple_of(offset + (1 - self.bit(mask)) * size, 16)
        return self.remote(
            self.work.at[chunk % self.depth, pl.ds(start, size)],
            self.box(chunk, path, level),
            level, path, chunk, mask,
        )

    def box(self, chunk, path, level):
        size = self.half // 2 >> level
        start = sum(self.half // 2 >> step for step in range(1, level))
        return self.path_box.at[chunk % self.slots, path, pl.ds(start, size)]

    def add_box(self, chunk, path, level):
        offset, size = self.region(path, level)
        here = pl.ds(pl.multiple_of(offset, 16), size)
        slot = chunk % self.depth
        self.work[slot, here, :] = self.work[slot, here, :] + self.box(chunk, path, level)[...]

    def own_copy(self, chunk, path):
        offset, size = self.region(path, self.levels)
        return pltpu.make_async_copy(
            self.work.at[chunk % self.depth, pl.ds(pl.multiple_of(offset, 16), size)],
            self.out_rows(chunk, offset, size),
            self.sems.at[1, 0, 1 + path, chunk % self.slots],
        )

    def spread_copy(self, chunk, path, level):
        offset, size = self.region(path, level)
        if level == self.levels:
            source = self.work.at[chunk % self.depth, pl.ds(pl.multiple_of(offset, 16), size)]
        else:
            source = self.out_rows(chunk, offset, size)
        return self.remote(
            source, self.out_rows(chunk, offset, size),
            2 * self.levels + 1 - level, path, chunk, self.orders[path][level - 1],
        )

    def share_copy(self, chunk):
        rows = self.out_rows(chunk, 0, self.half)
        return self.remote(rows, rows, self.last_phase - 1, 0, chunk, 1)

    def advance(self, phase, chunk):
        levels = self.levels
        if phase == 0:
            self.core_copy(chunk).start()
            self.load_copy(chunk).start()
        elif phase <= levels + 1:
            if phase == 1:
                self.load_copy(chunk).wait()
                self.core_copy(chunk).wait()
                slot = chunk % self.depth
                self.work[slot] = self.work[slot] + self.core_box[chunk % self.slots]
            for path in range(2):
                if phase > 1:
                    self.reduce_copy(chunk, path, phase - 1).wait()
                    self.add_box(chunk, path, phase - 1)
                if phase <= levels:
                    self.reduce_copy(chunk, path, phase).start()
                else:
                    self.own_copy(chunk, path).start()
                    self.spread_copy(chunk, path, levels).start()
        else:
            level = 2 * levels + 1 - phase
            if level >= 0:
                for path in range(2):
                    self.spread_copy(chunk, path, level + 1).wait()
                    if level + 1 == levels:
                        self.own_copy(chunk, path).wait()
                    if level >= 1:
                        self.spread_copy(chunk, path, level).start()
                if level == 0:
                    self.share_copy(chunk).start()


scatter_pace, gather_pace, pair_pace = 1.0, 1.0, 1.0


def rms_backward(values, grads, gain):
    scale = rms_rows(values)
    unit = values * scale
    scaled = grads * gain
    inner = jnp.mean(scaled * unit, axis=-1, keepdims=True)
    return scale * (scaled - unit * inner), jnp.sum(grads * unit, axis=0, keepdims=True)


def backward_kernel(
    count, replicas, chunk, ffn_chunks, out_chunks, attn_chunks, skew, subs,
    length_ref,
    flat_hbm, n2_hbm, gate_hbm, up_hbm, back_hbm, res_hbm, middle_hbm, cot_hbm, x_hbm,
    q_hbm, k_hbm, v_hbm, att_hbm, lse_hbm, n1_hbm,
    wq_hbm, wk_hbm, wv_hbm, wo_hbm, gains_ref, bias_ref, ids_ref,
    sums_out, flat_out, result_out, input_out, small_out,
    back, res, middle, cot, x_own, q_buf, k_buf, v_buf, att_buf, lse_buf, n1_buf, wq, wk, wv, wo,
    back_box, res_box, total_buf, res_total, middle_grad, branch, grad_att, key_acc, value_acc, grad_qkv, grad_up,
    reverse, offsets, turned, stage, out_buf, small, small_parts, small_box, pair_box,
    work, core_box, path_box,
    load_sems, b_sems, r_sems, f_sems, a_sems, p_sems, pair_sems, stage_sems, out_sems, sum_sems,
):
    me = lax.axis_index("group")
    mine = lax.axis_index("replica")
    rows, width = middle.shape
    total = rows * count
    columns = wq.shape[1]
    local_heads = columns // head_dim
    units = grad_up.shape[1]
    sources = [
        back_hbm, n2_hbm, gate_hbm, up_hbm, middle_hbm, cot_hbm, x_hbm, wo_hbm, att_hbm, q_hbm, k_hbm, v_hbm,
        lse_hbm, wq_hbm, wk_hbm, wv_hbm, res_hbm, n1_hbm,
    ]
    targets = [
        back, n1_buf, grad_qkv.at[:, pl.ds(0, units)], grad_up, middle, cot, x_own, wo, att_buf, q_buf, k_buf, v_buf,
        lse_buf, wq, wk, wv, res, n1_buf,
    ]
    loads = [
        pltpu.make_async_copy(source, target, load_sems.at[index])
        for index, (source, target) in enumerate(zip(sources, targets))
    ]
    masks = [1 << index for index in range(replicas.bit_length() - 1)]
    barrier = pltpu.get_barrier_semaphore()

    @pl.when(me > 0)
    def _():
        pl.semaphore_signal(barrier, inc=1, device_id={"group": me - 1}, device_id_type=MESH)

    @pl.when(me < count - 1)
    def _():
        pl.semaphore_signal(barrier, inc=1, device_id={"group": me + 1}, device_id_type=MESH)

    for mask in masks:
        pl.semaphore_signal(barrier, inc=1, device_id={"replica": mine ^ mask}, device_id_type=MESH)
    peers = jnp.where(me > 0, 1, 0) + jnp.where(me < count - 1, 1, 0) + len(masks)
    for load in loads[:7]:
        load.start()
    pl.semaphore_wait(barrier, peers)

    first_rows = flat_hbm.shape[0]
    from_first_chunks = first_rows // chunk
    from_ffn = ffn_chunks
    chunks = from_ffn + attn_chunks

    def make_source(source_ref, base):
        return lambda start, size: source_ref.at[pl.ds(pl.multiple_of(start - base, 16), size)]

    parts = ReplicaSum(replicas, chunk, None, sums_out, work, core_box, path_box, sum_sems)
    from_first, from_second = make_source(flat_hbm, 0), make_source(flat_out, first_rows)
    clock = {"time": 0, "gaps": [0] + [None] * 4, "credit": 0.0}
    each = from_first_chunks
    bounds = [0, each, 2 * each, 3 * each, from_ffn + out_chunks, chunks]

    def start_piece(source, piece):
        parts.source = source
        parts.core_copy(piece).start()
        parts.load_copy(piece).start()

    def tick(time):
        for phase in range(parts.last_phase, -1, -1):
            entry = time - skew * phase
            inside, piece = False, entry
            for gap, low, high in zip(clock["gaps"], bounds, bounds[1:]):
                if gap is None:
                    continue
                if isinstance(entry, int):
                    if low + gap <= entry < high + gap:
                        inside, piece = True, entry - gap
                else:
                    here = (entry >= low + gap) & (entry < high + gap)
                    inside = inside | here
                    piece = jnp.where(here, entry - gap, piece)

            def body(phase=phase, piece=piece):
                if phase == parts.last_phase:
                    parts.share_copy(piece).wait()
                elif phase:
                    parts.source = lambda start, size: flat_hbm.at[pl.ds(0, size)]
                    parts.advance(phase, piece)

            if phase:
                when(inside, body)
            else:
                first, second = piece < from_first_chunks, piece >= from_first_chunks
                if isinstance(entry, int):
                    first, second = first and inside, second and inside
                else:
                    first, second = first & inside, second & inside
                when(first, functools.partial(start_piece, from_first, piece))
                when(second, functools.partial(start_piece, from_second, piece))

    def pace(amount):
        clock["credit"] += amount
        while clock["credit"] >= 1:
            tick(clock["time"])
            clock["time"] += 1
            clock["credit"] -= 1

    back_line = LineScatter(me, count, back, back_box, total_buf, b_sems, subs)
    res_line = LineScatter(me, count, res, res_box, res_total, r_sems, subs)
    first_line = LineScatter(me, count, back, back_box, total_buf, f_sems, subs)
    branch_line = LineGather(me, count, branch, a_sems, subs)
    small_line = LineScatter(me, count, small_parts, small_box, small.at[pl.ds(0, 8)], p_sems)

    tile = 256

    def weight_grad(left, factor, base, height, per_output, splits=1):
        panels = factor.shape[1] // lanes
        tiles = height // tile

        def store(slot, panel, row):
            return pltpu.make_async_copy(
                stage.at[slot, panel],
                flat_out.at[pl.ds(base + panel * height + row, tile)],
                stage_sems.at[slot, panel],
            )

        def run(first, last):
            @pl.loop(first, last)
            def _(index):
                slot = lax.rem(index, 2)
                row = pl.multiple_of(index * tile, tile)
                turned[...] = left[:, :, pl.ds(row, tile)].reshape(total, tile).T
                product = nn_dot(turned[...], factor).astype(jnp.bfloat16)

                @pl.when(index >= 2)
                def _():
                    for panel in range(panels):
                        store(slot, panel, row).wait()

                for panel in range(panels):
                    stage[slot, panel] = product[:, panel * lanes : (panel + 1) * lanes]
                    store(slot, panel, row).start()

        for split in range(splits):
            if split:
                pace(1)
            run(tiles * split // splits, tiles * (split + 1) // splits)
        for slot in range(min(2, tiles)):
            for panel in range(panels):
                store(slot, panel, 0).wait()

    def enter(group):
        before = clock["gaps"][group - 1]
        clock["gaps"][group] = max(clock["time"] - bounds[group], before)

    tick(0)
    for load in loads[7:17]:
        load.start()
    loads[0].wait()
    total_buf[...] = back[me].astype(jnp.float32)
    back_line.at_time(0)
    clock["time"] = 1
    pace(2 * skew - 1)
    for load in loads[1:3]:
        load.wait()
    gate_base, attn_base = 0, 2 * units * width // lanes
    weight_grad(n1_buf, grad_qkv[:, 0:units], gate_base, width, units, 2)
    enter(1)
    pace(1)
    back_line.at_time(1)
    pace(1)
    back_line.at_time(2)
    pace(1)
    loads[3].wait()
    weight_grad(n1_buf, grad_up[...], gate_base + units * width // lanes, width, units, 2)
    enter(2)
    loads[17].start()
    anti = lax.broadcasted_iota(jnp.int32, (rows, rows), 0) + lax.broadcasted_iota(
        jnp.int32, (rows, rows), 1
    )
    reverse[...] = (anti == rows - 1).astype(jnp.float32).astype(jnp.bfloat16)
    for now in range(3, back_line.times):
        back_line.at_time(now)
        pace(scatter_pace)
    for load in loads[4:7]:
        load.wait()
    position = me * rows + lax.broadcasted_iota(jnp.int32, (rows, 1), 0)
    valid = (position < length_ref[0]).astype(jnp.float32)
    grad_mid, gain_grad = rms_backward(middle[...], total_buf[...], gains_ref[1:2, :])
    middle_grad[...] = cot[...].astype(jnp.float32) * valid + grad_mid
    branch[me] = middle_grad[...].astype(jnp.bfloat16)
    branch_line.begin()
    small_parts[...] = jnp.zeros_like(small_parts)
    part_width = width // count
    for owner in range(count):
        small_parts[owner, 1:2, :] = gain_grad[:, owner * part_width : (owner + 1) * part_width]
    for load in loads[7:18]:
        load.wait()
    res_total[...] = middle[...] + res[me].astype(jnp.float32)

    def attended_grad(block):
        grad_att[block] = nt_dot(branch[block], wo[...]).astype(jnp.bfloat16)

    attended_grad(me)
    for piece in range(branch_line.pieces):
        branch_line.arrive(piece)
        pace(gather_pace)
        if piece % subs == subs - 1:
            branch_line.each_block(piece // subs, attended_grad)

    weight_grad(att_buf, branch[...].reshape(total, width), attn_base, columns, width)
    enter(3)
    pace(1)
    mask_first, mask_second = head_masks()
    key_valid = lax.broadcasted_iota(jnp.int32, (1, total), 1) < length_ref[0]
    lane = lax.broadcasted_iota(jnp.int32, (1, lanes), 1)
    offsets[...] = jnp.zeros_like(offsets)

    def head_pair(pair):
        cols = pl.ds(pl.multiple_of(pair * lanes, lanes), lanes)
        key = k_buf[:, :, cols].reshape(total, lanes)
        value = v_buf[:, :, cols].reshape(total, lanes)
        key_acc[...] = jnp.zeros_like(key_acc)
        value_acc[...] = jnp.zeros_like(value_acc)

        @pl.loop(0, count)
        def _(block):
            query = q_buf[block, :, cols]
            grads = grad_att[block, :, cols]
            logs = lse_buf[block]
            query_parts = []
            for half, mask in enumerate((mask_first, mask_second)):
                head = pair * 2 + half
                query_half, grads_half = query * mask, grads * mask
                scores = nt_dot(query_half, key)
                scores = scores + offset_bias(bias_ref, head, block * rows, rows, total)
                scores = jnp.where(key_valid, scores, negative)
                log_total = jnp.sum(jnp.where(lane == head, logs, 0.0), axis=-1, keepdims=True)
                probs = jnp.exp(scores - log_total)
                grad_probs = nt_dot(grads_half, value)
                inner = jnp.sum(probs * grad_probs, axis=-1, keepdims=True)
                grad_scores = (probs * (grad_probs - inner)).astype(jnp.bfloat16)
                query_parts.append(nn_dot(grad_scores, key))
                key_acc[...] += nn_dot(query_half.astype(jnp.float32).T.astype(jnp.bfloat16), grad_scores)
                value_acc[...] += nn_dot(
                    grads_half.astype(jnp.float32).T.astype(jnp.bfloat16), probs.astype(jnp.bfloat16)
                )
                turned_scores = nn_dot(reverse[...], grad_scores)
                padded = jnp.concatenate([turned_scores, jnp.zeros_like(turned_scores)], axis=1)
                sheared = pltpu.roll(padded, 0, 1, stride=1, stride_axis=0)
                sums = jnp.broadcast_to(jnp.sum(sheared, axis=0, keepdims=True), (8, 2 * total))
                sums = pltpu.roll(sums, total - rows - block * rows, 1)
                offsets[pl.ds(head, 1), :] += sums[0:1, :]
            grad_qkv[pl.ds(pl.multiple_of(block * rows, rows), rows), cols] = jnp.where(
                lane < head_dim, query_parts[0], query_parts[1]
            ).astype(jnp.bfloat16)

        grad_qkv[:, pl.ds(pl.multiple_of(columns + pair * lanes, lanes), lanes)] = key_acc[
            ...
        ].T.astype(jnp.bfloat16)
        grad_qkv[:, pl.ds(pl.multiple_of(2 * columns + pair * lanes, lanes), lanes)] = value_acc[
            ...
        ].T.astype(jnp.bfloat16)

    res_time = 0
    for pair in range(local_heads // 2):
        if res_time < 3:
            res_line.at_time(res_time)
            res_time += 1
        head_pair(pair)
        pace(pair_pace)

    back_line.wait_sends()

    quarter = width // 4
    for start in range(0, width, quarter):
        cols = pl.ds(start, quarter)
        back[:, :, cols] = (
            (
                nt_dot(grad_qkv[:, 0:columns], wq[cols, :])
                + nt_dot(grad_qkv[:, columns : 2 * columns], wk[cols, :])
                + nt_dot(grad_qkv[:, 2 * columns : 3 * columns], wv[cols, :])
            )
            .astype(jnp.bfloat16)
            .reshape(count, rows, quarter)
        )
        if start == quarter:
            pace(1)
    for now in range(count - 1):
        first_line.at_time(now)
    pace(1)
    total_buf[...] = back[me].astype(jnp.float32)
    weight_grad(n1_buf, grad_qkv[...], attn_base + columns * width // lanes, width, columns, 2)
    enter(4)
    pace(skew)
    for now in range(count - 1, first_line.times):
        first_line.at_time(now)
        pace(1)
    grad_in, gain_grad = rms_backward(
        x_own[...].astype(jnp.float32), total_buf[...], gains_ref[0:1, :]
    )
    out_buf[1] = (middle_grad[...] + grad_in).astype(jnp.bfloat16)
    input_copy = pltpu.make_async_copy(out_buf.at[1], input_out, out_sems.at[1])
    input_copy.start()
    for owner in range(count):
        small_parts[owner, 0:1, :] = gain_grad[:, owner * part_width : (owner + 1) * part_width]
    small[0:8, :] = small_parts[me]
    for now in range(max(small_line.times, res_line.times - res_time)):
        if now < small_line.times:
            small_line.at_time(now)
        if res_time < res_line.times:
            res_line.at_time(res_time)
            res_time += 1
        pace(1)
    out_buf[0] = res_total[...].astype(jnp.bfloat16)
    result_copy = pltpu.make_async_copy(out_buf.at[0], result_out, out_sems.at[0])
    result_copy.start()
    bucket = lax.broadcasted_iota(jnp.int32, (lanes, ids_ref.shape[1]), 0).astype(jnp.float32)
    one_hot = (bucket == ids_ref[0:1, :]).astype(jnp.float32).astype(jnp.bfloat16)
    high = offsets[...].astype(jnp.bfloat16)
    rest = offsets[...] - high.astype(jnp.float32)
    middle_part = rest.astype(jnp.bfloat16)
    low_part = (rest - middle_part.astype(jnp.float32)).astype(jnp.bfloat16)
    small[8:16, 0:lanes] = nt_dot(high, one_hot) + nt_dot(middle_part, one_hot) + nt_dot(low_part, one_hot)
    small[8:16, lanes:] = jnp.zeros((8, part_width - lanes), jnp.float32)
    for index, mask in enumerate(masks):
        copy = pltpu.make_async_remote_copy(
            src_ref=small,
            dst_ref=pair_box.at[index],
            send_sem=pair_sems.at[0, index],
            recv_sem=pair_sems.at[1, index],
            device_id={"replica": mine ^ mask},
            device_id_type=MESH,
        )
        copy.start()
        pace(1)
        copy.wait()
        small[...] += pair_box[index]
    small_out[...] = small[...]

    @pl.loop(clock["time"], chunks + clock["gaps"][4] + skew * parts.last_phase)
    def _(now):
        tick(now)

    for line in (res_line, first_line, branch_line, small_line):
        line.wait_sends()
    result_copy.wait()
    input_copy.wait()


def backward(count, replicas, length, flat, n2, grad_gate, grad_up, back, res, middle, cot, x, q, k, v, att, lse, n1, wq, wk, wv, wo, gains, bias, ids):
    rows, width = middle.shape
    total = count * rows
    columns = wq.shape[1]
    bf, f32 = jnp.bfloat16, jnp.float32
    shape = jax.ShapeDtypeStruct
    steps = count - 1
    dma = pltpu.SemaphoreType.DMA
    units = grad_up.shape[1]
    chunk = flat.shape[0] // 5
    ffn_rows = 3 * flat.shape[0]
    attn_rows = 4 * columns * width // lanes
    skew, subs = 3, 2
    levels = replicas.bit_length() - 2
    masks = levels + 1
    depth = skew * (levels + 2)
    part_width = width // count
    vmem = pltpu.VMEM
    blocks = lambda kind: vmem((count, rows, width), kind)
    narrow = lambda: vmem((count, rows, columns), bf)
    boxes = lambda: vmem((count + 1, rows, width), bf)
    return pl.pallas_call(
        functools.partial(
            backward_kernel, count, replicas, chunk, ffn_rows // chunk, wo.size // lanes // chunk,
            attn_rows // chunk, skew, subs
        ),
        name="backward",
        out_shape=(
            shape((ffn_rows + attn_rows, lanes), bf),
            shape((2 * flat.shape[0] + attn_rows, lanes), bf),
            shape((rows, width), bf),
            shape((rows, width), bf),
            shape((16, part_width), f32),
        ),
        in_specs=[smem_space] + [any_space] * 19 + [vmem_space] * 3,
        out_specs=[any_space] * 4 + [vmem_space],
        scratch_shapes=[
            blocks(bf), blocks(bf), vmem((rows, width), f32), vmem((rows, width), bf), vmem((rows, width), bf),
            narrow(), narrow(), narrow(), narrow(), vmem((count, rows, lanes), f32), blocks(bf),
            vmem(wq.shape, bf), vmem(wk.shape, bf), vmem(wv.shape, bf), vmem(wo.shape, bf),
            boxes(), boxes(), vmem((rows, width), f32), vmem((rows, width), f32), vmem((rows, width), f32), blocks(bf),
            narrow(),
            vmem((lanes, total), f32), vmem((lanes, total), f32), vmem((total, 3 * columns), bf), vmem((total, units), bf),
            vmem((rows, rows), bf), vmem((8, 2 * total), f32), vmem((256, total), bf),
            vmem((2, width // lanes, 256, lanes), bf), vmem((2, rows, width), bf),
            vmem((16, part_width), f32), vmem((count, 8, part_width), f32), vmem((count + 1, 8, part_width), f32),
            vmem((masks, 16, part_width), f32),
            vmem((depth, chunk // 2, lanes), bf), vmem((2 * skew, chunk // 2, lanes), bf),
            vmem((2 * skew, 2, chunk // 4, lanes), bf),
            dma((18,)), dma((2, 2, steps * subs)), dma((2, 2, steps * subs)), dma((2, 2, steps * subs)),
            dma((2, 2, steps * subs)),
            dma((2, 2, steps)), dma((2, masks)), dma((2, width // lanes)), dma((2,)),
            dma((2, 2 * levels + 3, 3, 2 * skew)),
        ],
        compiler_params=pltpu.CompilerParams(
            collective_id=1, has_side_effects=True, vmem_limit_bytes=61 * 2**20
        ),
    )(length, flat, n2, grad_gate, grad_up, back, res, middle, cot, x, q, k, v, att, lse, n1, wq, wk, wv, wo, gains, bias, ids)


def widen_kernel(plan, slots, sums, result, input_grad, small, *refs):
    targets, (inbox, outbox, passed, in_sems, out_sems, pass_sems) = refs[:-6], refs[-6:]
    held = [
        pltpu.make_async_copy(source, passed.at[index], pass_sems.at[0, index])
        for index, source in enumerate((result, input_grad))
    ]
    given = [
        pltpu.make_async_copy(passed.at[index], target, pass_sems.at[1, index])
        for index, target in enumerate(targets[:2])
    ]
    for copy in held:
        copy.start()
    gain1, gain2, table = targets[2:5]
    for index, gain in enumerate((gain1, gain2)):
        for row in range(gain.shape[0]):
            gain[row : row + 1, :] = small[index : index + 1, row * lanes : (row + 1) * lanes]
    table[...] = small[8 : 8 + table.shape[0], 0 : table.shape[1]]
    targets = targets[5:]
    tiles = [
        (target, start, height, depth // lanes, size, row)
        for target, (start, height, depth, size) in zip(targets, plan)
        for row in range(0, height, size)
    ]

    def load(number):
        _, start, height, panels, size, row = tiles[number]
        slot = number % slots

        @pl.loop(0, panels)
        def _(panel):
            pltpu.make_async_copy(
                sums.at[pl.ds(start + row + panel * height, size)],
                inbox.at[slot, pl.ds(pl.multiple_of(panel * size, size), size)],
                in_sems.at[slot],
            ).start()

    def store(number):
        target, _, _, panels, size, row = tiles[number]
        return pltpu.make_async_copy(
            outbox.at[number % slots, pl.ds(0, size), pl.ds(0, panels * lanes)],
            target.at[pl.ds(row, size)],
            out_sems.at[number % slots],
        )

    for number in range(min(slots - 1, len(tiles))):
        load(number)
    for number in range(len(tiles)):
        _, _, _, panels, size, _ = tiles[number]
        slot = number % slots
        if number + slots - 1 < len(tiles):
            load(number + slots - 1)
        whole = inbox.at[slot, pl.ds(0, panels * size)]
        pltpu.make_async_copy(whole, whole, in_sems.at[slot]).wait()
        if number >= slots:
            store(number - slots).wait()

        @pl.loop(0, panels)
        def _(panel):
            outbox[slot, pl.ds(0, size), pl.ds(pl.multiple_of(panel * lanes, lanes), lanes)] = inbox[
                slot, pl.ds(pl.multiple_of(panel * size, size), size)
            ].astype(jnp.float32)

        store(number).start()
        if number == slots:
            for first, second in zip(held, given):
                first.wait()
                second.start()
    for number in range(max(len(tiles) - slots, 0), len(tiles)):
        store(number).wait()
    for copy in given:
        copy.wait()


def widen(sums, result, input_grad, small, table_shape, shapes):
    slots = 4
    plan, start = [], 0
    for height, depth in shapes:
        size = 512 if depth <= 1024 else 256
        while height % size:
            size //= 2
        plan.append((start, height, depth, size))
        start += height * depth // lanes
    most_in = max(size * depth // lanes for _, _, depth, size in plan)
    most_rows = max(size for _, _, _, size in plan)
    return pl.pallas_call(
        functools.partial(widen_kernel, plan, slots),
        name="widen",
        out_shape=[jax.ShapeDtypeStruct(result.shape, result.dtype)] * 2
        + [jax.ShapeDtypeStruct((small.shape[1] // lanes, lanes), jnp.float32)] * 2
        + [jax.ShapeDtypeStruct(table_shape, jnp.float32)]
        + [jax.ShapeDtypeStruct(shape, jnp.float32) for shape in shapes],
        in_specs=[any_space] * 3 + [vmem_space],
        out_specs=[any_space] * 2 + [vmem_space] * 3 + [any_space] * len(shapes),
        scratch_shapes=[
            pltpu.VMEM((slots, most_in, lanes), jnp.bfloat16),
            pltpu.VMEM((slots, most_rows, max(depth for _, depth in shapes)), jnp.float32),
            pltpu.VMEM((2,) + result.shape, result.dtype),
            pltpu.SemaphoreType.DMA((slots,)),
            pltpu.SemaphoreType.DMA((slots,)),
            pltpu.SemaphoreType.DMA((2, 2)),
        ],
        compiler_params=pltpu.CompilerParams(vmem_limit_bytes=61 * 2**20),
    )(sums, result, input_grad, small)


def local(
    inputs,
    seq_lengths,
    bucket_ids,
    norm1_gain,
    w_query,
    w_key,
    w_value,
    w_attn_out,
    bias_table,
    norm2_gain,
    w_gate,
    w_up,
    w_ffn_out,
    cotangent,
):
    count = lax.axis_size("group")
    replicas = lax.axis_size("replica")
    longest = max(2 * count * inputs.shape[1], norm1_gain.shape[0])
    longest = -(-longest // 1024) * 1024
    packed = jnp.concatenate(
        [
            jnp.pad(vector.astype(jnp.float32), (0, longest - vector.shape[0]), constant_values=-1)
            for vector in (norm1_gain, norm2_gain, bucket_ids)
        ]
    ).reshape(-1, lanes)
    (
        normed_one, query, key, value, attended, log_totals, middle, flat, back_part, result_part, normed_all,
        grad_gate, grad_up, gains, bias, ids,
    ) = forward(
        count, seq_lengths, inputs[0], cotangent[0], w_query, w_key, w_value, w_attn_out, w_ffn_out, w_gate, w_up,
        packed, bias_table.T,
    )
    sums, _, result, input_grad, small = backward(
        count, replicas, seq_lengths, flat, normed_all, grad_gate, grad_up, back_part, result_part, middle,
        cotangent[0], inputs[0], query, key, value, attended, log_totals, normed_one,
        w_query, w_key, w_value, w_attn_out, gains, bias, ids,
    )
    weights = (w_ffn_out, w_gate, w_up, w_attn_out, w_query, w_key, w_value)
    (
        result, input_grad, gain1_grad, gain2_grad, table_grad,
        ffn_out_grad, gate_grad, up_grad, attn_out_grad, query_grad, key_grad, value_grad,
    ) = widen(
        sums, result, input_grad, small, bias_table.shape[::-1], [weight.shape for weight in weights]
    )
    return (
        result[None],
        input_grad[None],
        gain1_grad.reshape(-1),
        query_grad,
        key_grad,
        value_grad,
        attn_out_grad,
        table_grad.T,
        gain2_grad.reshape(-1),
        gate_grad,
        up_grad,
        ffn_out_grad,
    )


def solution(mesh):
    placed = (
        P("replica", "group", None),
        P("replica"),
        P(),
        P("group"),
        P(None, "group"),
        P(None, "group"),
        P(None, "group"),
        P("group", None),
        P(None, "group"),
        P("group"),
        P(None, "group"),
        P(None, "group"),
        P("group", None),
        P("replica", "group", None),
    )
    return jax.shard_map(
        local,
        mesh=mesh,
        in_specs=placed,
        out_specs=(
            P("replica", "group", None),
            P("replica", "group", None),
            P("group"),
            P(None, "group"),
            P(None, "group"),
            P(None, "group"),
            P("group", None),
            P(None, "group"),
            P("group"),
            P(None, "group"),
            P(None, "group"),
            P("group", None),
        ),
        check_vma=False,
    )
```

```python
import functools
import jax
import jax.numpy as jnp
from jax import lax
from jax.experimental import pallas as pl
from jax.experimental.pallas import tpu as pltpu
from jax.sharding import PartitionSpec as P

epsilon = 1e-06
negative = -1000000000.0
head_dim = 64
lanes = 128
MESH = pl.DeviceIdType.MESH
any_space = pl.BlockSpec(memory_space=pl.ANY)
vmem_space = pl.BlockSpec(memory_space=pltpu.VMEM)
smem_space = pl.BlockSpec(memory_space=pltpu.SMEM)


def nn_dot(left, right):
    return jnp.dot(left, right, preferred_element_type=jnp.float32)


def nt_dot(left, right):
    return lax.dot_general(
        left, right, (((1,), (1,)), ((), ())), preferred_element_type=jnp.float32
    )


def line_barrier(me, count):
    barrier = pltpu.get_barrier_semaphore()

    @pl.when(me > 0)
    def _():
        pl.semaphore_signal(barrier, inc=1, device_id={"group": me - 1}, device_id_type=MESH)

    @pl.when(me < count - 1)
    def _():
        pl.semaphore_signal(barrier, inc=1, device_id={"group": me + 1}, device_id_type=MESH)

    peers = jnp.where(me > 0, 1, 0) + jnp.where(me < count - 1, 1, 0)
    pl.semaphore_wait(barrier, peers)


class LineGather:
    def __init__(self, me, count, buffer, sems, subs=1, own=None):
        self.me, self.count, self.buffer, self.sems, self.subs = me, count, buffer, sems, subs
        self.own = own
        self.pieces = (count - 1) * subs
        self.size = buffer.shape[1] // subs

    def copy(self, side, piece, hops):
        block = self.me - hops if side == 0 else self.me + hops
        part = pl.ds(piece % self.subs * self.size, self.size)
        here = self.buffer.at[block, part]
        return pltpu.make_async_remote_copy(
            src_ref=here if hops or self.own is None else self.own.at[part],
            dst_ref=here,
            send_sem=self.sems.at[side, 0, piece],
            recv_sem=self.sems.at[side, 1, piece],
            device_id={"group": self.me + (1 if side == 0 else -1)},
            device_id_type=MESH,
        )

    def sends(self, side, piece):
        hops = piece // self.subs
        if side == 0:
            return (self.me - hops >= 0) & (self.me + 1 < self.count)
        return (self.me + hops < self.count) & (self.me >= 1)

    def arrives(self, side, piece):
        hops = piece // self.subs
        if side == 0:
            return self.me - 1 - hops >= 0
        return self.me + 1 + hops < self.count

    def send_side(self, side, piece):
        @pl.when(self.sends(side, piece))
        def _():
            self.copy(side, piece, piece // self.subs).start()

    def send(self, piece):
        for side in range(2):
            self.send_side(side, piece)

    def begin(self):
        for piece in range(self.subs):
            self.send(piece)

    def arrive(self, piece):
        for side in range(2):
            @pl.when(self.arrives(side, piece))
            def _():
                self.copy(side, piece, piece // self.subs + 1).wait_recv()

        if piece + self.subs < self.pieces:
            self.send(piece + self.subs)

    def arrive_block(self, hops, body):
        for piece in range(hops * self.subs, (hops + 1) * self.subs):
            self.arrive(piece)
        self.each_block(hops, body)

    def each_block(self, hops, body):
        @pl.loop(0, 2)
        def _(side):
            block = jnp.where(side == 0, self.me - 1 - hops, self.me + 1 + hops)

            @pl.when((block >= 0) & (block < self.count))
            def _():
                body(block)

    def wait_sends(self):
        for piece in range(self.pieces):
            for side in range(2):
                @pl.when(self.sends(side, piece))
                def _():
                    self.copy(side, piece, piece // self.subs).wait_send()


class LineScatter:
    def __init__(self, me, count, parts, inbox, total, sems, subs=1):
        self.me, self.count, self.parts, self.inbox = me, count, parts, inbox
        self.total, self.sems, self.subs = total, sems, subs
        self.steps = count - 1
        self.times = self.steps * subs + 1
        self.size = parts.shape[1] // subs

    def order(self, index):
        picked = 0
        for device in range(self.count):
            due = [(step + self.count - 1 - device, step) for step in range(device)]
            due += [
                (step + device, self.count - 1 - step) for step in range(self.count - 1 - device)
            ]
            blocks = [block for _, block in sorted(due)] + [device]
            picked = picked + jnp.where(self.me == device, blocks[index], 0)
        return picked

    def copy(self, side, piece):
        step = piece % self.steps
        here = pl.ds(pl.multiple_of(piece // self.steps * self.size, self.size), self.size)
        owner = step if side == 0 else self.count - 1 - step
        return pltpu.make_async_remote_copy(
            src_ref=self.parts.at[owner, here],
            dst_ref=self.inbox.at[self.slot(side, step), here],
            send_sem=self.sems.at[side, 0, piece],
            recv_sem=self.sems.at[side, 1, piece],
            device_id={"group": self.me + (-1 if side == 0 else 1)},
            device_id_type=MESH,
        )

    def slot(self, side, step):
        return step if side == 0 else self.count - step

    def at_time(self, time):
        for side in range(2):
            before = self.count - 1 - self.me if side == 0 else self.me
            after = self.count - 1 - before
            piece = time - before
            inside = (piece >= 0) & (piece < self.subs * self.steps)
            piece = jnp.where(inside, piece, 0)
            step = piece % self.steps

            @pl.when(inside & (step < after))
            def _():
                owner = step if side == 0 else self.count - 1 - step
                here = pl.ds(pl.multiple_of(piece // self.steps * self.size, self.size), self.size)

                @pl.when(before > 0)
                def _():
                    self.copy(side, piece).wait_recv()
                    self.parts[owner, here, :] = (
                        self.parts[owner, here, :].astype(jnp.float32)
                        + self.inbox[self.slot(side, step), here, :].astype(jnp.float32)
                    ).astype(self.parts.dtype)

                self.copy(side, piece).start()

            @pl.when(inside & (step == after) & (before > 0))
            def _():
                here = pl.ds(pl.multiple_of(piece // self.steps * self.size, self.size), self.size)
                self.copy(side, piece).wait_recv()
                self.total[here, :] += self.inbox[self.slot(side, step), here, :].astype(jnp.float32)

    def wait_sends(self):
        for piece in range(self.steps * self.subs):
            step = piece % self.steps
            for side in range(2):
                after = self.me if side == 0 else self.count - 1 - self.me

                @pl.when(step < after)
                def _():
                    self.copy(side, piece).wait_send()


def head_masks():
    lane = lax.broadcasted_iota(jnp.int32, (1, lanes), 1)
    first = (lane < head_dim).astype(jnp.float32)
    return first.astype(jnp.bfloat16), (1.0 - first).astype(jnp.bfloat16)


def offset_bias(bias_ref, head, row_start, rows, total):
    width = bias_ref.shape[1]
    shift = lax.rem(row_start + (width - (total - 1)), width)
    vector = pltpu.roll(jnp.broadcast_to(bias_ref[pl.ds(head, 1), :], (8, width)), shift, 1)
    vector = jnp.broadcast_to(vector[0:1, :], (rows, width))
    return pltpu.roll(vector, 0, 1, stride=1, stride_axis=0)[:, :total]


def rms_rows(values):
    return lax.rsqrt(jnp.mean(values * values, axis=-1, keepdims=True) + epsilon)


def gelu_parts(gate):
    root = 0.7978845608028654
    inner = root * (gate + 0.044715 * gate * gate * gate)
    tanh = jnp.tanh(inner)
    half = 0.5 * (1.0 + tanh)
    slope = half + 0.5 * gate * (1.0 - tanh * tanh) * root * (1.0 + 3 * 0.044715 * gate * gate)
    return gate * half, slope


def forward_kernel(
    count, tile, subs,
    length_ref,
    x_hbm, cot_hbm, wq_hbm, wk_hbm, wv_hbm, wo_hbm, wf_hbm, wg_hbm, wu_hbm, packed_ref, table_ref,
    n1_out, q_out, k_out, v_out, att_out, lse_out, middle_out, flat_out, back_out, res_out, n2_out, gate_out, up_out,
    gains_out, bias_out, ids_out,
    x_all, g_all, gains_all, wq, wk, wv, wo, wf, wg, wu, back_buf, inbox, n1_buf, q_buf, k_buf, v_buf, att_buf, lse_buf,
    total_buf, hid, grad_gate, grad_up, grad_hidden, res_buf, turned, stage,
    local_sems, x_sems, g_sems, c_sems, s_sems, n_sems, out_sems, stage_sems,
):
    me = lax.axis_index("group")
    rows, width = x_hbm.shape
    total = rows * count
    columns = wq.shape[1]
    units = wg.shape[1]
    local_heads = columns // head_dim
    n2_all, parts = x_all, back_buf
    loads = [
        pltpu.make_async_copy(source, target, local_sems.at[index])
        for index, (source, target) in enumerate(
            [
                (x_hbm, x_all.at[me]),
                (cot_hbm, g_all.at[me]),
                (wq_hbm, wq),
                (wk_hbm, wk),
                (wv_hbm, wv),
                (wo_hbm, wo),
                (wf_hbm, wf),
                (wg_hbm, wg),
                (wu_hbm, wu),
            ]
        )
    ]
    for load in loads:
        load.start()
    line_barrier(me, count)
    x_line = LineGather(me, count, x_all, x_sems, subs, x_hbm)
    g_line = LineGather(me, count, gains_all, g_sems)
    c_line = LineGather(me, count, g_all, c_sems, subs)
    n_line = LineGather(me, count, n2_all, n_sems, subs)

    def packed_row(index, length):
        first = index * (packed_ref.shape[0] // 3)
        return jnp.concatenate(
            [packed_ref[row : row + 1, :] for row in range(first, first + length // lanes)], axis=1
        )

    for index in range(2):
        gains_all[me, index : index + 1, :] = packed_row(index, width // count)
    g_line.begin()
    x_line.begin()
    loads[1].wait()
    position = me * rows + lax.broadcasted_iota(jnp.int32, (rows, 1), 0)
    g_all[me] = g_all[me] * (position < length_ref[0]).astype(jnp.float32).astype(jnp.bfloat16)

    ids = packed_row(2, 2 * total)
    ids_out[...] = jnp.broadcast_to(ids, ids_out.shape)
    bucket = lax.broadcasted_iota(jnp.int32, (table_ref.shape[1], 2 * total), 0).astype(jnp.float32)
    one_hot = (bucket == ids).astype(jnp.float32).astype(jnp.bfloat16)
    bias_out[...] = nn_dot(table_ref[...], one_hot)

    for piece in range(g_line.pieces):
        g_line.arrive(piece)
    for owner in range(count):
        gains_out[:, owner * (width // count) : (owner + 1) * (width // count)] = gains_all[owner]
    for index in (0, 2, 3, 4):
        loads[index].wait()

    def project(block):
        values = x_all[block].astype(jnp.float32)
        normed = (values * rms_rows(values) * gains_out[0:1, :]).astype(jnp.bfloat16)
        n1_buf[block] = normed
        q_buf[block] = nn_dot(normed, wq[...]).astype(jnp.bfloat16)
        k_buf[block] = nn_dot(normed, wk[...]).astype(jnp.bfloat16)
        v_buf[block] = nn_dot(normed, wv[...]).astype(jnp.bfloat16)

    def begin_cotangent(sent):
        for side in range(2):
            last = me if side == 0 else count - 1 - me

            @pl.when(last == sent)
            def _():
                for piece in range(subs):
                    c_line.send_side(side, piece)

    begin_cotangent(0)
    for piece in range(subs):
        x_line.arrive(piece)
    begin_cotangent(1)
    project(me)
    x_line.each_block(0, project)
    for hops in range(1, count - 1):
        for piece in range(hops * subs, (hops + 1) * subs):
            x_line.arrive(piece)
        begin_cotangent(hops + 1)
        x_line.each_block(hops, project)

    loads[5].wait()
    mask_first, mask_second = head_masks()
    key_valid = lax.broadcasted_iota(jnp.int32, (1, total), 1) < length_ref[0]
    lane = lax.broadcasted_iota(jnp.int32, (1, lanes), 1)

    def attend(block):
        lse_buf[block] = jnp.zeros((rows, lanes), jnp.float32)

        @pl.loop(0, local_heads // 2)
        def _(pair):
            cols = pl.ds(pl.multiple_of(pair * lanes, lanes), lanes)
            query = q_buf[block, :, cols]
            key = k_buf[:, :, cols].reshape(total, lanes)
            value = v_buf[:, :, cols].reshape(total, lanes)
            outs = []
            for half, mask in enumerate((mask_first, mask_second)):
                head = pair * 2 + half
                scores = nt_dot(query * mask, key)
                scores = scores + offset_bias(bias_out, head, block * rows, rows, total)
                scores = jnp.where(key_valid, scores, negative)
                top = jnp.max(scores, axis=-1, keepdims=True)
                expd = jnp.exp(scores - top)
                summed = jnp.sum(expd, axis=-1, keepdims=True)
                probs = (expd * (1.0 / summed)).astype(jnp.bfloat16)
                outs.append(nn_dot(probs, value))
                lse_buf[block] = jnp.where(lane == head, top + jnp.log(summed), lse_buf[block])
            att_buf[block, :, cols] = jnp.where(lane < head_dim, outs[0], outs[1]).astype(
                jnp.bfloat16
            )

    scatter = LineScatter(me, count, parts, inbox, total_buf, s_sems, subs)
    arrived = 0
    for index in range(count - 1):
        block = scatter.order(index)
        attend(block)
        parts[block] = nn_dot(att_buf[block], wo[...]).astype(jnp.bfloat16)
        if index == 0:
            x_line.wait_sends()
        scatter.at_time(index)
        if index:
            c_line.arrive(arrived)
            arrived += 1
    attend(me)
    total_buf[...] = x_all[me].astype(jnp.float32) + nn_dot(att_buf[me], wo[...])
    early = [(n1_buf, n1_out), (q_buf, q_out), (k_buf, k_out), (v_buf, v_out), (att_buf, att_out), (lse_buf, lse_out)]
    late = [
        (total_buf, middle_out), (back_buf, back_out), (res_buf, res_out), (n2_all, n2_out), (grad_gate, gate_out),
        (grad_up, up_out),
    ]
    outs = [
        pltpu.make_async_copy(source, target, out_sems.at[index])
        for index, (source, target) in enumerate(early + late)
    ]
    for copy in outs[: len(early)]:
        copy.start()
    size = rows // subs
    steps = count - 1

    def second_norm(sub):
        here = pl.ds(sub * size, size)
        middle = total_buf[here, :]
        n2_all[me, here, :] = (middle * rms_rows(middle) * gains_out[1:2, :]).astype(jnp.bfloat16)
        n_line.send(sub)

    came = 0
    for time in range(steps, scatter.times):
        scatter.at_time(time)
        if time % steps == 0:
            second_norm(time // steps - 1)
        if time > steps and came < steps - 1:
            n_line.arrive(came * subs)
            came += 1
        if arrived < c_line.pieces:
            c_line.arrive(arrived)
            arrived += 1
    outs[len(early)].start()
    for piece in range(arrived, c_line.pieces):
        c_line.arrive(piece)

    for load in loads[6:]:
        load.wait()

    @pl.loop(0, units // tile)
    def _(index):
        here = pl.ds(pl.multiple_of(index * tile, tile), tile)
        grad_hidden[:, :, here] = nt_dot(g_all[...].reshape(total, width), wf[here, :]).reshape(
            count, rows, tile
        )

    scatter.wait_sends()

    def hidden_pass(sub):
        here = pl.ds(sub * size, size)
        normed = n2_all[:, here, :].reshape(count * size, width)
        part = units // 2 if units % 256 == 0 else units
        for start in range(0, units, part):
            cols = pl.ds(start, part)
            gate = nn_dot(normed, wg[:, cols])
            up = nn_dot(normed, wu[:, cols])
            act, slope = gelu_parts(gate)
            grads = grad_hidden[:, here, cols].reshape(count * size, part)
            for target, values in (
                (hid, act * up),
                (grad_gate, grads * up * slope),
                (grad_up, grads * act),
            ):
                target[:, here, cols] = values.astype(jnp.bfloat16).reshape(count, size, part)

    def out_pass(sub):
        here = pl.ds(sub * size, size)
        left = [buffer[:, here, :].reshape(count * size, units) for buffer in (grad_gate, grad_up, hid)]
        half = width // 2
        for cols in (pl.ds(0, half), pl.ds(half, half)):
            back_buf[:, here, cols] = (
                (nt_dot(left[0], wg[cols, :]) + nt_dot(left[1], wu[cols, :]))
                .astype(jnp.bfloat16)
                .reshape(count, size, half)
            )
            res_buf[:, here, cols] = nn_dot(left[2], wf[:, cols]).astype(jnp.bfloat16).reshape(count, size, half)

    for sub in range(subs):
        if sub:
            hops = 0
            for compute in (hidden_pass, out_pass):
                n_line.arrive(hops * subs + sub)
                hops += 1
                compute(sub - 1)
            for hops in range(hops, steps):
                n_line.arrive(hops * subs + sub)
        else:
            for hops in range(came, steps):
                n_line.arrive(hops * subs)
    hidden_pass(subs - 1)
    out_pass(subs - 1)
    for copy in outs[len(early) + 1 :]:
        copy.start()

    def weight_grad(left, right, base, height):
        depth = right.shape[2]
        panels = depth // lanes
        factor = right[...].reshape(total, depth)

        def store(slot, panel, row):
            return pltpu.make_async_copy(
                stage.at[slot, panel],
                flat_out.at[pl.ds(base + panel * height + row, tile)],
                stage_sems.at[slot, panel],
            )

        @pl.loop(0, height // tile)
        def _(index):
            slot = lax.rem(index, 2)
            row = pl.multiple_of(index * tile, tile)
            turned[...] = left[:, :, pl.ds(row, tile)].reshape(total, tile).T
            product = nn_dot(turned[...], factor).astype(jnp.bfloat16)

            @pl.when(index >= 2)
            def _():
                for panel in range(panels):
                    store(slot, panel, row).wait()

            for panel in range(panels):
                stage[slot, panel] = product[:, panel * lanes : (panel + 1) * lanes]
                store(slot, panel, row).start()

        for slot in range(2):
            for panel in range(panels):
                store(slot, panel, 0).wait()

    weight_grad(hid, g_all, 0, units)
    for line in (g_line, c_line, n_line):
        line.wait_sends()
    for copy in outs:
        copy.wait()


def forward(count, length, x, cot, wq, wk, wv, wo, wf, wg, wu, packed, table):
    rows, width = x.shape
    columns, units = wq.shape[1], wg.shape[1]
    total = count * rows
    tile = 128 if units % 256 else 256
    bf, f32 = jnp.bfloat16, jnp.float32
    shape = jax.ShapeDtypeStruct
    steps = count - 1
    subs = 2
    dma = pltpu.SemaphoreType.DMA
    vmem = pltpu.VMEM
    blocks = (count, rows, width)
    narrow = (count, rows, columns)
    return pl.pallas_call(
        functools.partial(forward_kernel, count, tile, subs),
        name="forward",
        out_shape=(
            shape(blocks, bf), shape(narrow, bf), shape(narrow, bf), shape(narrow, bf), shape(narrow, bf),
            shape((count, rows, lanes), f32), shape((rows, width), f32),
            shape((units * width // lanes, lanes), bf), shape(blocks, bf), shape(blocks, bf), shape(blocks, bf),
            shape((count, rows, units), bf), shape((count, rows, units), bf),
            shape((8, width), f32), shape((columns // head_dim, 2 * total), f32), shape((8, 2 * total), f32),
        ),
        in_specs=[smem_space] + [any_space] * 9 + [vmem_space] * 2,
        out_specs=[any_space] * 13 + [vmem_space] * 3,
        scratch_shapes=[
            vmem(blocks, bf), vmem(blocks, bf), vmem((count, 8, width // count), f32),
            vmem(wq.shape, bf), vmem(wk.shape, bf), vmem(wv.shape, bf), vmem(wo.shape, bf),
            vmem(wf.shape, bf), vmem(wg.shape, bf), vmem(wu.shape, bf),
            vmem(blocks, bf), vmem((count + 1, rows, width), bf), vmem(blocks, bf),
            vmem(narrow, bf), vmem(narrow, bf), vmem(narrow, bf), vmem(narrow, bf), vmem((count, rows, lanes), f32),
            vmem((rows, width), f32), vmem((count, rows, units), bf), vmem((count, rows, units), bf),
            vmem((count, rows, units), bf), vmem((count, rows, units), f32), vmem(blocks, bf), vmem((tile, total), bf),
            vmem((2, width // lanes, tile, lanes), bf),
            dma((9,)), dma((2, 2, steps * subs)), dma((2, 2, steps)), dma((2, 2, steps * subs)),
            dma((2, 2, steps * subs)), dma((2, 2, steps * subs)), dma((12,)), dma((2, width // lanes)),
        ],
        compiler_params=pltpu.CompilerParams(
            collective_id=0, has_side_effects=True, vmem_limit_bytes=61 * 2**20
        ),
    )(length, x, cot, wq, wk, wv, wo, wf, wg, wu, packed, table)


def when(condition, body):
    if isinstance(condition, bool):
        if condition:
            body()
    else:
        pl.when(condition)(body)


class ReplicaSum:
    def __init__(self, replicas, chunk, source, target, work, core_box, path_box, sems):
        self.mine = lax.axis_index("replica")
        self.chunk, self.source, self.target = chunk, source, target
        self.work, self.core_box, self.path_box, self.sems = work, core_box, path_box, sems
        self.depth, self.slots = work.shape[0], core_box.shape[0]
        bits = [1 << index for index in range(1, replicas.bit_length() - 1)]
        self.orders = (bits, bits[::-1])
        self.levels = len(bits)
        self.last_phase = 2 * self.levels + 2
        self.half = chunk // 2

    def bit(self, mask):
        return jnp.where((self.mine & mask) != 0, 1, 0)

    def region(self, path, level):
        size = self.half // 2
        offset = path * size
        for mask in self.orders[path][:level]:
            size //= 2
            offset = offset + self.bit(mask) * size
        return offset, size

    def out_rows(self, chunk, offset, size):
        start = chunk * self.chunk + self.bit(1) * self.half + offset
        return self.target.at[pl.ds(pl.multiple_of(start, 16), size)]

    def sem(self, kind, phase, path, chunk):
        return self.sems.at[kind, phase, path, chunk % self.slots]

    def remote(self, source, target, phase, path, chunk, mask):
        return pltpu.make_async_remote_copy(
            src_ref=source,
            dst_ref=target,
            send_sem=self.sem(0, phase, path, chunk),
            recv_sem=self.sem(1, phase, path, chunk),
            device_id={"replica": self.mine ^ mask},
            device_id_type=MESH,
        )

    def core_copy(self, chunk):
        start = chunk * self.chunk + (1 - self.bit(1)) * self.half
        return self.remote(
            self.source(start, self.half), self.core_box.at[chunk % self.slots], 0, 0, chunk, 1
        )

    def load_copy(self, chunk):
        start = chunk * self.chunk + self.bit(1) * self.half
        return pltpu.make_async_copy(
            self.source(start, self.half), self.work.at[chunk % self.depth], self.sem(0, 0, 1, chunk)
        )

    def reduce_copy(self, chunk, path, level):
        mask = self.orders[path][level - 1]
        offset, size = self.region(path, level - 1)
        size //= 2
        start = pl.multiple_of(offset + (1 - self.bit(mask)) * size, 16)
        return self.remote(
            self.work.at[chunk % self.depth, pl.ds(start, size)],
            self.box(chunk, path, level),
            level, path, chunk, mask,
        )

    def box(self, chunk, path, level):
        size = self.half // 2 >> level
        start = sum(self.half // 2 >> step for step in range(1, level))
        return self.path_box.at[chunk % self.slots, path, pl.ds(start, size)]

    def add_box(self, chunk, path, level):
        offset, size = self.region(path, level)
        here = pl.ds(pl.multiple_of(offset, 16), size)
        slot = chunk % self.depth
        self.work[slot, here, :] = self.work[slot, here, :] + self.box(chunk, path, level)[...]

    def own_copy(self, chunk, path):
        offset, size = self.region(path, self.levels)
        return pltpu.make_async_copy(
            self.work.at[chunk % self.depth, pl.ds(pl.multiple_of(offset, 16), size)],
            self.out_rows(chunk, offset, size),
            self.sems.at[1, 0, 1 + path, chunk % self.slots],
        )

    def spread_copy(self, chunk, path, level):
        offset, size = self.region(path, level)
        if level == self.levels:
            source = self.work.at[chunk % self.depth, pl.ds(pl.multiple_of(offset, 16), size)]
        else:
            source = self.out_rows(chunk, offset, size)
        return self.remote(
            source, self.out_rows(chunk, offset, size),
            2 * self.levels + 1 - level, path, chunk, self.orders[path][level - 1],
        )

    def share_copy(self, chunk):
        rows = self.out_rows(chunk, 0, self.half)
        return self.remote(rows, rows, self.last_phase - 1, 0, chunk, 1)

    def advance(self, phase, chunk):
        levels = self.levels
        if phase == 0:
            self.core_copy(chunk).start()
            self.load_copy(chunk).start()
        elif phase <= levels + 1:
            if phase == 1:
                self.load_copy(chunk).wait()
                self.core_copy(chunk).wait()
                slot = chunk % self.depth
                self.work[slot] = self.work[slot] + self.core_box[chunk % self.slots]
            for path in range(2):
                if phase > 1:
                    self.reduce_copy(chunk, path, phase - 1).wait()
                    self.add_box(chunk, path, phase - 1)
                if phase <= levels:
                    self.reduce_copy(chunk, path, phase).start()
                else:
                    self.own_copy(chunk, path).start()
                    self.spread_copy(chunk, path, levels).start()
        else:
            level = 2 * levels + 1 - phase
            if level >= 0:
                for path in range(2):
                    self.spread_copy(chunk, path, level + 1).wait()
                    if level + 1 == levels:
                        self.own_copy(chunk, path).wait()
                    if level >= 1:
                        self.spread_copy(chunk, path, level).start()
                if level == 0:
                    self.share_copy(chunk).start()


scatter_pace, gather_pace, pair_pace = 1.0, 0.7, 1.0


def rms_backward(values, grads, gain):
    scale = rms_rows(values)
    unit = values * scale
    scaled = grads * gain
    inner = jnp.mean(scaled * unit, axis=-1, keepdims=True)
    return scale * (scaled - unit * inner), jnp.sum(grads * unit, axis=0, keepdims=True)


def backward_kernel(
    count, replicas, chunk, ffn_chunks, out_chunks, attn_chunks, skew, subs,
    length_ref,
    flat_hbm, n2_hbm, gate_hbm, up_hbm, back_hbm, res_hbm, middle_hbm, cot_hbm, x_hbm,
    q_hbm, k_hbm, v_hbm, att_hbm, lse_hbm, n1_hbm,
    wq_hbm, wk_hbm, wv_hbm, wo_hbm, gains_ref, bias_ref, ids_ref,
    sums_out, flat_out, result_out, input_out, small_out,
    back, res, middle, cot, x_own, q_buf, k_buf, v_buf, att_buf, lse_buf, n1_buf, wq, wk, wv, wo,
    back_box, res_box, total_buf, res_total, middle_grad, branch, grad_att, key_acc, value_acc, grad_qkv, grad_up,
    reverse, offsets, turned, stage, out_buf, small, small_parts, small_box, pair_box,
    work, core_box, path_box,
    load_sems, b_sems, r_sems, f_sems, a_sems, p_sems, pair_sems, stage_sems, out_sems, sum_sems,
):
    me = lax.axis_index("group")
    mine = lax.axis_index("replica")
    rows, width = middle.shape
    total = rows * count
    columns = wq.shape[1]
    local_heads = columns // head_dim
    units = grad_up.shape[1]
    sources = [
        back_hbm, n2_hbm, gate_hbm, up_hbm, middle_hbm, cot_hbm, x_hbm, wo_hbm, att_hbm, q_hbm, k_hbm, v_hbm,
        lse_hbm, wq_hbm, wk_hbm, wv_hbm, res_hbm, n1_hbm,
    ]
    targets = [
        back, n1_buf, grad_qkv.at[:, pl.ds(0, units)], grad_up, middle, cot, x_own, wo, att_buf, q_buf, k_buf, v_buf,
        lse_buf, wq, wk, wv, res, n1_buf,
    ]
    loads = [
        pltpu.make_async_copy(source, target, load_sems.at[index])
        for index, (source, target) in enumerate(zip(sources, targets))
    ]
    masks = [1 << index for index in range(replicas.bit_length() - 1)]
    barrier = pltpu.get_barrier_semaphore()

    @pl.when(me > 0)
    def _():
        pl.semaphore_signal(barrier, inc=1, device_id={"group": me - 1}, device_id_type=MESH)

    @pl.when(me < count - 1)
    def _():
        pl.semaphore_signal(barrier, inc=1, device_id={"group": me + 1}, device_id_type=MESH)

    for mask in masks:
        pl.semaphore_signal(barrier, inc=1, device_id={"replica": mine ^ mask}, device_id_type=MESH)
    peers = jnp.where(me > 0, 1, 0) + jnp.where(me < count - 1, 1, 0) + len(masks)
    for load in loads[:7]:
        load.start()
    pl.semaphore_wait(barrier, peers)

    first_rows = flat_hbm.shape[0]
    from_first_chunks = first_rows // chunk
    from_ffn = ffn_chunks
    chunks = from_ffn + attn_chunks

    def make_source(source_ref, base):
        return lambda start, size: source_ref.at[pl.ds(pl.multiple_of(start - base, 16), size)]

    parts = ReplicaSum(replicas, chunk, None, sums_out, work, core_box, path_box, sum_sems)
    from_first, from_second = make_source(flat_hbm, 0), make_source(flat_out, first_rows)
    clock = {"time": 0, "gaps": [0] + [None] * 4, "credit": 0.0}
    each = from_first_chunks
    bounds = [0, each, 2 * each, 3 * each, from_ffn + out_chunks, chunks]

    def start_piece(source, piece):
        parts.source = source
        parts.core_copy(piece).start()
        parts.load_copy(piece).start()

    def tick(time):
        for phase in range(parts.last_phase, -1, -1):
            entry = time - skew * phase
            inside, piece = False, entry
            for gap, low, high in zip(clock["gaps"], bounds, bounds[1:]):
                if gap is None:
                    continue
                if isinstance(entry, int):
                    if low + gap <= entry < high + gap:
                        inside, piece = True, entry - gap
                else:
                    here = (entry >= low + gap) & (entry < high + gap)
                    inside = inside | here
                    piece = jnp.where(here, entry - gap, piece)

            def body(phase=phase, piece=piece):
                if phase == parts.last_phase:
                    parts.share_copy(piece).wait()
                elif phase:
                    parts.source = lambda start, size: flat_hbm.at[pl.ds(0, size)]
                    parts.advance(phase, piece)

            if phase:
                when(inside, body)
            else:
                first, second = piece < from_first_chunks, piece >= from_first_chunks
                if isinstance(entry, int):
                    first, second = first and inside, second and inside
                else:
                    first, second = first & inside, second & inside
                when(first, functools.partial(start_piece, from_first, piece))
                when(second, functools.partial(start_piece, from_second, piece))

    def pace(amount):
        clock["credit"] += amount
        while clock["credit"] >= 1:
            tick(clock["time"])
            clock["time"] += 1
            clock["credit"] -= 1

    back_line = LineScatter(me, count, back, back_box, total_buf, b_sems, subs)
    res_line = LineScatter(me, count, res, res_box, res_total, r_sems, subs)
    first_line = LineScatter(me, count, back, back_box, total_buf, f_sems, subs)
    branch_line = LineGather(me, count, branch, a_sems, subs)
    small_line = LineScatter(me, count, small_parts, small_box, small.at[pl.ds(0, 8)], p_sems)

    tile = 256

    def weight_grad(left, factor, base, height, per_output, splits=1):
        panels = factor.shape[1] // lanes
        tiles = height // tile

        def store(slot, panel, row):
            return pltpu.make_async_copy(
                stage.at[slot, panel],
                flat_out.at[pl.ds(base + panel * height + row, tile)],
                stage_sems.at[slot, panel],
            )

        def run(first, last):
            @pl.loop(first, last)
            def _(index):
                slot = lax.rem(index, 2)
                row = pl.multiple_of(index * tile, tile)
                turned[...] = left[:, :, pl.ds(row, tile)].reshape(total, tile).T
                product = nn_dot(turned[...], factor).astype(jnp.bfloat16)

                @pl.when(index >= 2)
                def _():
                    for panel in range(panels):
                        store(slot, panel, row).wait()

                for panel in range(panels):
                    stage[slot, panel] = product[:, panel * lanes : (panel + 1) * lanes]
                    store(slot, panel, row).start()

        for split in range(splits):
            if split:
                pace(1)
            run(tiles * split // splits, tiles * (split + 1) // splits)
        for slot in range(min(2, tiles)):
            for panel in range(panels):
                store(slot, panel, 0).wait()

    def enter(group):
        before = clock["gaps"][group - 1]
        clock["gaps"][group] = max(clock["time"] - bounds[group], before)

    tick(0)
    for load in loads[7:17]:
        load.start()
    loads[0].wait()
    total_buf[...] = back[me].astype(jnp.float32)
    back_line.at_time(0)
    clock["time"] = 1
    pace(2 * skew - 1)
    for load in loads[1:3]:
        load.wait()
    gate_base, attn_base = 0, 2 * units * width // lanes
    weight_grad(n1_buf, grad_qkv[:, 0:units], gate_base, width, units, 2)
    enter(1)
    pace(1)
    back_line.at_time(1)
    pace(1)
    back_line.at_time(2)
    pace(1)
    loads[3].wait()
    weight_grad(n1_buf, grad_up[...], gate_base + units * width // lanes, width, units, 2)
    enter(2)
    loads[17].start()
    anti = lax.broadcasted_iota(jnp.int32, (rows, rows), 0) + lax.broadcasted_iota(
        jnp.int32, (rows, rows), 1
    )
    reverse[...] = (anti == rows - 1).astype(jnp.float32).astype(jnp.bfloat16)
    part_width = width // count
    size, steps = rows // subs, count - 1
    small_parts[...] = jnp.zeros_like(small_parts)
    for load in loads[4:7]:
        load.wait()

    def second_norm_back(sub):
        here = pl.ds(sub * size, size)
        position = me * rows + sub * size + lax.broadcasted_iota(jnp.int32, (size, 1), 0)
        valid = (position < length_ref[0]).astype(jnp.float32)
        grad_mid, gain_grad = rms_backward(middle[here, :], total_buf[here, :], gains_ref[1:2, :])
        grad_mid = cot[here, :].astype(jnp.float32) * valid + grad_mid
        middle_grad[here, :] = grad_mid
        branch[me, here, :] = grad_mid.astype(jnp.bfloat16)
        branch_line.send(sub)
        for owner in range(count):
            small_parts[owner, 1:2, :] += gain_grad[:, owner * part_width : (owner + 1) * part_width]

    came = 0
    for now in range(3, back_line.times):
        back_line.at_time(now)
        if now % steps == 0:
            second_norm_back(now // steps - 1)
        if now > steps and came < steps - 1:
            branch_line.arrive(came * subs)
            came += 1
        pace(scatter_pace)
    for load in loads[7:18]:
        load.wait()
    res_total[...] = middle[...] + res[me].astype(jnp.float32)

    def attended_grad(block):
        grad_att[block] = nt_dot(branch[block], wo[...]).astype(jnp.bfloat16)

    attended_grad(me)
    for sub in range(subs):
        for hops in range(came if sub == 0 else 0, steps):
            branch_line.arrive(hops * subs + sub)
            pace(gather_pace)
            if sub == subs - 1:
                branch_line.each_block(hops, attended_grad)

    weight_grad(att_buf, branch[...].reshape(total, width), attn_base, columns, width)
    enter(3)
    pace(1)
    mask_first, mask_second = head_masks()
    key_valid = lax.broadcasted_iota(jnp.int32, (1, total), 1) < length_ref[0]
    lane = lax.broadcasted_iota(jnp.int32, (1, lanes), 1)
    offsets[...] = jnp.zeros_like(offsets)

    def head_pair(pair):
        cols = pl.ds(pl.multiple_of(pair * lanes, lanes), lanes)
        key = k_buf[:, :, cols].reshape(total, lanes)
        value = v_buf[:, :, cols].reshape(total, lanes)
        key_acc[...] = jnp.zeros_like(key_acc)
        value_acc[...] = jnp.zeros_like(value_acc)

        @pl.loop(0, count)
        def _(block):
            query = q_buf[block, :, cols]
            grads = grad_att[block, :, cols]
            logs = lse_buf[block]
            query_parts = []
            for half, mask in enumerate((mask_first, mask_second)):
                head = pair * 2 + half
                query_half, grads_half = query * mask, grads * mask
                scores = nt_dot(query_half, key)
                scores = scores + offset_bias(bias_ref, head, block * rows, rows, total)
                scores = jnp.where(key_valid, scores, negative)
                log_total = jnp.sum(jnp.where(lane == head, logs, 0.0), axis=-1, keepdims=True)
                probs = jnp.exp(scores - log_total)
                grad_probs = nt_dot(grads_half, value)
                inner = jnp.sum(probs * grad_probs, axis=-1, keepdims=True)
                grad_scores = (probs * (grad_probs - inner)).astype(jnp.bfloat16)
                query_parts.append(nn_dot(grad_scores, key))
                key_acc[...] += nn_dot(query_half.astype(jnp.float32).T.astype(jnp.bfloat16), grad_scores)
                value_acc[...] += nn_dot(
                    grads_half.astype(jnp.float32).T.astype(jnp.bfloat16), probs.astype(jnp.bfloat16)
                )
                turned_scores = nn_dot(reverse[...], grad_scores)
                padded = jnp.concatenate([turned_scores, jnp.zeros_like(turned_scores)], axis=1)
                sheared = pltpu.roll(padded, 0, 1, stride=1, stride_axis=0)
                sums = jnp.broadcast_to(jnp.sum(sheared, axis=0, keepdims=True), (8, 2 * total))
                sums = pltpu.roll(sums, total - rows - block * rows, 1)
                offsets[pl.ds(head, 1), :] += sums[0:1, :]
            grad_qkv[pl.ds(pl.multiple_of(block * rows, rows), rows), cols] = jnp.where(
                lane < head_dim, query_parts[0], query_parts[1]
            ).astype(jnp.bfloat16)

        grad_qkv[:, pl.ds(pl.multiple_of(columns + pair * lanes, lanes), lanes)] = key_acc[
            ...
        ].T.astype(jnp.bfloat16)
        grad_qkv[:, pl.ds(pl.multiple_of(2 * columns + pair * lanes, lanes), lanes)] = value_acc[
            ...
        ].T.astype(jnp.bfloat16)

    res_time = 0
    for pair in range(local_heads // 2):
        if res_time < 3:
            res_line.at_time(res_time)
            res_time += 1
        head_pair(pair)
        pace(pair_pace)

    back_line.wait_sends()

    quarter = width // 4
    for start in range(0, width, quarter):
        cols = pl.ds(start, quarter)
        back[:, :, cols] = (
            (
                nt_dot(grad_qkv[:, 0:columns], wq[cols, :])
                + nt_dot(grad_qkv[:, columns : 2 * columns], wk[cols, :])
                + nt_dot(grad_qkv[:, 2 * columns : 3 * columns], wv[cols, :])
            )
            .astype(jnp.bfloat16)
            .reshape(count, rows, quarter)
        )
        if start == quarter:
            pace(1)
    for now in range(count - 1):
        first_line.at_time(now)
    pace(1)
    total_buf[...] = back[me].astype(jnp.float32)
    weight_grad(n1_buf, grad_qkv[...], attn_base + columns * width // lanes, width, columns, 2)
    enter(4)
    pace(skew)
    for now in range(count - 1, first_line.times):
        first_line.at_time(now)
        pace(1)
    grad_in, gain_grad = rms_backward(
        x_own[...].astype(jnp.float32), total_buf[...], gains_ref[0:1, :]
    )
    out_buf[1] = (middle_grad[...] + grad_in).astype(jnp.bfloat16)
    input_copy = pltpu.make_async_copy(out_buf.at[1], input_out, out_sems.at[1])
    input_copy.start()
    for owner in range(count):
        small_parts[owner, 0:1, :] = gain_grad[:, owner * part_width : (owner + 1) * part_width]
    small[0:8, :] = small_parts[me]
    for now in range(max(small_line.times, res_line.times - res_time)):
        if now < small_line.times:
            small_line.at_time(now)
        if res_time < res_line.times:
            res_line.at_time(res_time)
            res_time += 1
        pace(1)
    out_buf[0] = res_total[...].astype(jnp.bfloat16)
    result_copy = pltpu.make_async_copy(out_buf.at[0], result_out, out_sems.at[0])
    result_copy.start()
    bucket = lax.broadcasted_iota(jnp.int32, (lanes, ids_ref.shape[1]), 0).astype(jnp.float32)
    one_hot = (bucket == ids_ref[0:1, :]).astype(jnp.float32).astype(jnp.bfloat16)
    high = offsets[...].astype(jnp.bfloat16)
    rest = offsets[...] - high.astype(jnp.float32)
    middle_part = rest.astype(jnp.bfloat16)
    low_part = (rest - middle_part.astype(jnp.float32)).astype(jnp.bfloat16)
    small[8:16, 0:lanes] = nt_dot(high, one_hot) + nt_dot(middle_part, one_hot) + nt_dot(low_part, one_hot)
    small[8:16, lanes:] = jnp.zeros((8, part_width - lanes), jnp.float32)
    for index, mask in enumerate(masks):
        copy = pltpu.make_async_remote_copy(
            src_ref=small,
            dst_ref=pair_box.at[index],
            send_sem=pair_sems.at[0, index],
            recv_sem=pair_sems.at[1, index],
            device_id={"replica": mine ^ mask},
            device_id_type=MESH,
        )
        copy.start()
        pace(1)
        copy.wait()
        small[...] += pair_box[index]
    small_out[...] = small[...]

    @pl.loop(clock["time"], chunks + clock["gaps"][4] + skew * parts.last_phase)
    def _(now):
        tick(now)

    for line in (res_line, first_line, branch_line, small_line):
        line.wait_sends()
    result_copy.wait()
    input_copy.wait()


def backward(count, replicas, length, flat, n2, grad_gate, grad_up, back, res, middle, cot, x, q, k, v, att, lse, n1, wq, wk, wv, wo, gains, bias, ids):
    rows, width = middle.shape
    total = count * rows
    columns = wq.shape[1]
    bf, f32 = jnp.bfloat16, jnp.float32
    shape = jax.ShapeDtypeStruct
    steps = count - 1
    dma = pltpu.SemaphoreType.DMA
    units = grad_up.shape[1]
    chunk = flat.shape[0] // 5
    ffn_rows = 3 * flat.shape[0]
    attn_rows = 4 * columns * width // lanes
    skew, subs = 3, 2
    levels = replicas.bit_length() - 2
    masks = levels + 1
    depth = skew * (levels + 2)
    part_width = width // count
    vmem = pltpu.VMEM
    blocks = lambda kind: vmem((count, rows, width), kind)
    narrow = lambda: vmem((count, rows, columns), bf)
    boxes = lambda: vmem((count + 1, rows, width), bf)
    return pl.pallas_call(
        functools.partial(
            backward_kernel, count, replicas, chunk, ffn_rows // chunk, wo.size // lanes // chunk,
            attn_rows // chunk, skew, subs
        ),
        name="backward",
        out_shape=(
            shape((ffn_rows + attn_rows, lanes), bf),
            shape((2 * flat.shape[0] + attn_rows, lanes), bf),
            shape((rows, width), bf),
            shape((rows, width), bf),
            shape((16, part_width), f32),
        ),
        in_specs=[smem_space] + [any_space] * 19 + [vmem_space] * 3,
        out_specs=[any_space] * 4 + [vmem_space],
        scratch_shapes=[
            blocks(bf), blocks(bf), vmem((rows, width), f32), vmem((rows, width), bf), vmem((rows, width), bf),
            narrow(), narrow(), narrow(), narrow(), vmem((count, rows, lanes), f32), blocks(bf),
            vmem(wq.shape, bf), vmem(wk.shape, bf), vmem(wv.shape, bf), vmem(wo.shape, bf),
            boxes(), boxes(), vmem((rows, width), f32), vmem((rows, width), f32), vmem((rows, width), f32), blocks(bf),
            narrow(),
            vmem((lanes, total), f32), vmem((lanes, total), f32), vmem((total, 3 * columns), bf), vmem((total, units), bf),
            vmem((rows, rows), bf), vmem((8, 2 * total), f32), vmem((256, total), bf),
            vmem((2, width // lanes, 256, lanes), bf), vmem((2, rows, width), bf),
            vmem((16, part_width), f32), vmem((count, 8, part_width), f32), vmem((count + 1, 8, part_width), f32),
            vmem((masks, 16, part_width), f32),
            vmem((depth, chunk // 2, lanes), bf), vmem((2 * skew, chunk // 2, lanes), bf),
            vmem((2 * skew, 2, chunk // 4, lanes), bf),
            dma((18,)), dma((2, 2, steps * subs)), dma((2, 2, steps * subs)), dma((2, 2, steps * subs)),
            dma((2, 2, steps * subs)),
            dma((2, 2, steps)), dma((2, masks)), dma((2, width // lanes)), dma((2,)),
            dma((2, 2 * levels + 3, 3, 2 * skew)),
        ],
        compiler_params=pltpu.CompilerParams(
            collective_id=1, has_side_effects=True, vmem_limit_bytes=61 * 2**20
        ),
    )(length, flat, n2, grad_gate, grad_up, back, res, middle, cot, x, q, k, v, att, lse, n1, wq, wk, wv, wo, gains, bias, ids)


def widen_kernel(plan, slots, sums, result, input_grad, small, *refs):
    targets, (inbox, outbox, passed, in_sems, out_sems, pass_sems) = refs[:-6], refs[-6:]
    held = [
        pltpu.make_async_copy(source, passed.at[index], pass_sems.at[0, index])
        for index, source in enumerate((result, input_grad))
    ]
    given = [
        pltpu.make_async_copy(passed.at[index], target, pass_sems.at[1, index])
        for index, target in enumerate(targets[:2])
    ]
    for copy in held:
        copy.start()
    gain1, gain2, table = targets[2:5]
    for index, gain in enumerate((gain1, gain2)):
        for row in range(gain.shape[0]):
            gain[row : row + 1, :] = small[index : index + 1, row * lanes : (row + 1) * lanes]
    table[...] = small[8 : 8 + table.shape[0], 0 : table.shape[1]]
    targets = targets[5:]
    tiles = [
        (target, start, height, depth // lanes, size, row)
        for target, (start, height, depth, size) in zip(targets, plan)
        for row in range(0, height, size)
    ]

    def load(number):
        _, start, height, panels, size, row = tiles[number]
        slot = number % slots

        @pl.loop(0, panels)
        def _(panel):
            pltpu.make_async_copy(
                sums.at[pl.ds(start + row + panel * height, size)],
                inbox.at[slot, pl.ds(pl.multiple_of(panel * size, size), size)],
                in_sems.at[slot],
            ).start()

    def store(number):
        target, _, _, panels, size, row = tiles[number]
        return pltpu.make_async_copy(
            outbox.at[number % slots, pl.ds(0, size), pl.ds(0, panels * lanes)],
            target.at[pl.ds(row, size)],
            out_sems.at[number % slots],
        )

    for number in range(min(slots - 1, len(tiles))):
        load(number)
    for number in range(len(tiles)):
        _, _, _, panels, size, _ = tiles[number]
        slot = number % slots
        if number + slots - 1 < len(tiles):
            load(number + slots - 1)
        whole = inbox.at[slot, pl.ds(0, panels * size)]
        pltpu.make_async_copy(whole, whole, in_sems.at[slot]).wait()
        if number >= slots:
            store(number - slots).wait()

        @pl.loop(0, panels)
        def _(panel):
            outbox[slot, pl.ds(0, size), pl.ds(pl.multiple_of(panel * lanes, lanes), lanes)] = inbox[
                slot, pl.ds(pl.multiple_of(panel * size, size), size)
            ].astype(jnp.float32)

        store(number).start()
        if number == slots:
            for first, second in zip(held, given):
                first.wait()
                second.start()
    for number in range(max(len(tiles) - slots, 0), len(tiles)):
        store(number).wait()
    for copy in given:
        copy.wait()


def widen(sums, result, input_grad, small, table_shape, shapes):
    slots = 4
    plan, start = [], 0
    for height, depth in shapes:
        size = 512 if depth <= 1024 else 256
        while height % size:
            size //= 2
        plan.append((start, height, depth, size))
        start += height * depth // lanes
    most_in = max(size * depth // lanes for _, _, depth, size in plan)
    most_rows = max(size for _, _, _, size in plan)
    return pl.pallas_call(
        functools.partial(widen_kernel, plan, slots),
        name="widen",
        out_shape=[jax.ShapeDtypeStruct(result.shape, result.dtype)] * 2
        + [jax.ShapeDtypeStruct((small.shape[1] // lanes, lanes), jnp.float32)] * 2
        + [jax.ShapeDtypeStruct(table_shape, jnp.float32)]
        + [jax.ShapeDtypeStruct(shape, jnp.float32) for shape in shapes],
        in_specs=[any_space] * 3 + [vmem_space],
        out_specs=[any_space] * 2 + [vmem_space] * 3 + [any_space] * len(shapes),
        scratch_shapes=[
            pltpu.VMEM((slots, most_in, lanes), jnp.bfloat16),
            pltpu.VMEM((slots, most_rows, max(depth for _, depth in shapes)), jnp.float32),
            pltpu.VMEM((2,) + result.shape, result.dtype),
            pltpu.SemaphoreType.DMA((slots,)),
            pltpu.SemaphoreType.DMA((slots,)),
            pltpu.SemaphoreType.DMA((2, 2)),
        ],
        compiler_params=pltpu.CompilerParams(vmem_limit_bytes=61 * 2**20),
    )(sums, result, input_grad, small)


def local(
    inputs,
    seq_lengths,
    bucket_ids,
    norm1_gain,
    w_query,
    w_key,
    w_value,
    w_attn_out,
    bias_table,
    norm2_gain,
    w_gate,
    w_up,
    w_ffn_out,
    cotangent,
):
    count = lax.axis_size("group")
    replicas = lax.axis_size("replica")
    longest = max(2 * count * inputs.shape[1], norm1_gain.shape[0])
    longest = -(-longest // 1024) * 1024
    packed = jnp.concatenate(
        [
            jnp.pad(vector.astype(jnp.float32), (0, longest - vector.shape[0]), constant_values=-1)
            for vector in (norm1_gain, norm2_gain, bucket_ids)
        ]
    ).reshape(-1, lanes)
    (
        normed_one, query, key, value, attended, log_totals, middle, flat, back_part, result_part, normed_all,
        grad_gate, grad_up, gains, bias, ids,
    ) = forward(
        count, seq_lengths, inputs[0], cotangent[0], w_query, w_key, w_value, w_attn_out, w_ffn_out, w_gate, w_up,
        packed, bias_table.T,
    )
    grad_gate, grad_up = (array.reshape(-1, array.shape[2]) for array in (grad_gate, grad_up))
    sums, _, result, input_grad, small = backward(
        count, replicas, seq_lengths, flat, normed_all, grad_gate, grad_up, back_part, result_part, middle,
        cotangent[0], inputs[0], query, key, value, attended, log_totals, normed_one,
        w_query, w_key, w_value, w_attn_out, gains, bias, ids,
    )
    weights = (w_ffn_out, w_gate, w_up, w_attn_out, w_query, w_key, w_value)
    (
        result, input_grad, gain1_grad, gain2_grad, table_grad,
        ffn_out_grad, gate_grad, up_grad, attn_out_grad, query_grad, key_grad, value_grad,
    ) = widen(
        sums, result, input_grad, small, bias_table.shape[::-1], [weight.shape for weight in weights]
    )
    return (
        result[None],
        input_grad[None],
        gain1_grad.reshape(-1),
        query_grad,
        key_grad,
        value_grad,
        attn_out_grad,
        table_grad.T,
        gain2_grad.reshape(-1),
        gate_grad,
        up_grad,
        ffn_out_grad,
    )


def solution(mesh):
    placed = (
        P("replica", "group", None),
        P("replica"),
        P(),
        P("group"),
        P(None, "group"),
        P(None, "group"),
        P(None, "group"),
        P("group", None),
        P(None, "group"),
        P("group"),
        P(None, "group"),
        P(None, "group"),
        P("group", None),
        P("replica", "group", None),
    )
    return jax.shard_map(
        local,
        mesh=mesh,
        in_specs=placed,
        out_specs=(
            P("replica", "group", None),
            P("replica", "group", None),
            P("group"),
            P(None, "group"),
            P(None, "group"),
            P(None, "group"),
            P("group", None),
            P(None, "group"),
            P("group"),
            P(None, "group"),
            P(None, "group"),
            P("group", None),
        ),
        check_vma=False,
    )
```

```python
import functools
import jax
import jax.numpy as jnp
from jax import lax
from jax.experimental import pallas as pl
from jax.experimental.pallas import tpu as pltpu
from jax.sharding import PartitionSpec as P

epsilon = 1e-06
negative = -1000000000.0
head_dim = 64
lanes = 128
MESH = pl.DeviceIdType.MESH
any_space = pl.BlockSpec(memory_space=pl.ANY)
vmem_space = pl.BlockSpec(memory_space=pltpu.VMEM)
smem_space = pl.BlockSpec(memory_space=pltpu.SMEM)


def nn_dot(left, right):
    return jnp.dot(left, right, preferred_element_type=jnp.float32)


def nt_dot(left, right):
    return lax.dot_general(
        left, right, (((1,), (1,)), ((), ())), preferred_element_type=jnp.float32
    )


def line_barrier(me, count):
    barrier = pltpu.get_barrier_semaphore()

    @pl.when(me > 0)
    def _():
        pl.semaphore_signal(barrier, inc=1, device_id={"group": me - 1}, device_id_type=MESH)

    @pl.when(me < count - 1)
    def _():
        pl.semaphore_signal(barrier, inc=1, device_id={"group": me + 1}, device_id_type=MESH)

    peers = jnp.where(me > 0, 1, 0) + jnp.where(me < count - 1, 1, 0)
    pl.semaphore_wait(barrier, peers)


class LineGather:
    def __init__(self, me, count, buffer, sems, subs=1, own=None):
        self.me, self.count, self.buffer, self.sems, self.subs = me, count, buffer, sems, subs
        self.own = own
        self.pieces = (count - 1) * subs
        self.size = buffer.shape[1] // subs

    def copy(self, side, piece, hops):
        block = self.me - hops if side == 0 else self.me + hops
        part = pl.ds(piece % self.subs * self.size, self.size)
        here = self.buffer.at[block, part]
        return pltpu.make_async_remote_copy(
            src_ref=here if hops or self.own is None else self.own.at[part],
            dst_ref=here,
            send_sem=self.sems.at[side, 0, piece],
            recv_sem=self.sems.at[side, 1, piece],
            device_id={"group": self.me + (1 if side == 0 else -1)},
            device_id_type=MESH,
        )

    def sends(self, side, piece):
        hops = piece // self.subs
        if side == 0:
            return (self.me - hops >= 0) & (self.me + 1 < self.count)
        return (self.me + hops < self.count) & (self.me >= 1)

    def arrives(self, side, piece):
        hops = piece // self.subs
        if side == 0:
            return self.me - 1 - hops >= 0
        return self.me + 1 + hops < self.count

    def send_side(self, side, piece):
        @pl.when(self.sends(side, piece))
        def _():
            self.copy(side, piece, piece // self.subs).start()

    def send(self, piece):
        for side in range(2):
            self.send_side(side, piece)

    def begin(self):
        for piece in range(self.subs):
            self.send(piece)

    def arrive(self, piece):
        for side in range(2):
            @pl.when(self.arrives(side, piece))
            def _():
                self.copy(side, piece, piece // self.subs + 1).wait_recv()

        if piece + self.subs < self.pieces:
            self.send(piece + self.subs)

    def arrive_block(self, hops, body):
        for piece in range(hops * self.subs, (hops + 1) * self.subs):
            self.arrive(piece)
        self.each_block(hops, body)

    def each_block(self, hops, body):
        @pl.loop(0, 2)
        def _(side):
            block = jnp.where(side == 0, self.me - 1 - hops, self.me + 1 + hops)

            @pl.when((block >= 0) & (block < self.count))
            def _():
                body(block)

    def wait_sends(self):
        for piece in range(self.pieces):
            for side in range(2):
                @pl.when(self.sends(side, piece))
                def _():
                    self.copy(side, piece, piece // self.subs).wait_send()


class LineScatter:
    def __init__(self, me, count, parts, inbox, total, sems, subs=1):
        self.me, self.count, self.parts, self.inbox = me, count, parts, inbox
        self.total, self.sems, self.subs = total, sems, subs
        self.times = (count - 1) * subs + 1
        self.size = parts.shape[1] // subs

    def order(self, index):
        picked = 0
        for device in range(self.count):
            due = [(step * self.subs + self.count - 1 - device, step) for step in range(device)]
            due += [
                (step * self.subs + device, self.count - 1 - step)
                for step in range(self.count - 1 - device)
            ]
            blocks = [block for _, block in sorted(due)] + [device]
            picked = picked + jnp.where(self.me == device, blocks[index], 0)
        return picked

    def copy(self, side, piece):
        step = piece // self.subs
        here = pl.ds(pl.multiple_of(piece % self.subs * self.size, self.size), self.size)
        owner = step if side == 0 else self.count - 1 - step
        return pltpu.make_async_remote_copy(
            src_ref=self.parts.at[owner, here],
            dst_ref=self.inbox.at[self.slot(side, step), here],
            send_sem=self.sems.at[side, 0, piece],
            recv_sem=self.sems.at[side, 1, piece],
            device_id={"group": self.me + (-1 if side == 0 else 1)},
            device_id_type=MESH,
        )

    def slot(self, side, step):
        return step if side == 0 else self.count - step

    def at_time(self, time):
        for side in range(2):
            before = self.count - 1 - self.me if side == 0 else self.me
            after = self.count - 1 - before
            piece = time - before
            step = piece // self.subs

            @pl.when((piece >= 0) & (step < after))
            def _():
                owner = step if side == 0 else self.count - 1 - step
                here = pl.ds(pl.multiple_of(piece % self.subs * self.size, self.size), self.size)

                @pl.when(before > 0)
                def _():
                    self.copy(side, piece).wait_recv()
                    self.parts[owner, here, :] = (
                        self.parts[owner, here, :].astype(jnp.float32)
                        + self.inbox[self.slot(side, step), here, :].astype(jnp.float32)
                    ).astype(self.parts.dtype)

                self.copy(side, piece).start()

            @pl.when((piece >= 0) & (step == after) & (before > 0))
            def _():
                here = pl.ds(pl.multiple_of(piece % self.subs * self.size, self.size), self.size)
                self.copy(side, piece).wait_recv()
                self.total[here, :] += self.inbox[self.slot(side, step), here, :].astype(jnp.float32)

    def wait_sends(self):
        for piece in range((self.count - 1) * self.subs):
            step = piece // self.subs
            for side in range(2):
                after = self.me if side == 0 else self.count - 1 - self.me

                @pl.when(step < after)
                def _():
                    self.copy(side, piece).wait_send()


def head_masks():
    lane = lax.broadcasted_iota(jnp.int32, (1, lanes), 1)
    first = (lane < head_dim).astype(jnp.float32)
    return first.astype(jnp.bfloat16), (1.0 - first).astype(jnp.bfloat16)


def offset_bias(bias_ref, head, row_start, rows, total):
    width = bias_ref.shape[1]
    shift = lax.rem(row_start + (width - (total - 1)), width)
    vector = pltpu.roll(jnp.broadcast_to(bias_ref[pl.ds(head, 1), :], (8, width)), shift, 1)
    vector = jnp.broadcast_to(vector[0:1, :], (rows, width))
    return pltpu.roll(vector, 0, 1, stride=1, stride_axis=0)[:, :total]


def rms_rows(values):
    return lax.rsqrt(jnp.mean(values * values, axis=-1, keepdims=True) + epsilon)


def gelu_parts(gate):
    root = 0.7978845608028654
    inner = root * (gate + 0.044715 * gate * gate * gate)
    tanh = jnp.tanh(inner)
    half = 0.5 * (1.0 + tanh)
    slope = half + 0.5 * gate * (1.0 - tanh * tanh) * root * (1.0 + 3 * 0.044715 * gate * gate)
    return gate * half, slope


def forward_kernel(
    count, tile, subs,
    length_ref,
    x_hbm, cot_hbm, wq_hbm, wk_hbm, wv_hbm, wo_hbm, wf_hbm, wg_hbm, wu_hbm, packed_ref, table_ref,
    n1_out, q_out, k_out, v_out, att_out, lse_out, middle_out, flat_out, back_out, res_out, n2_out, gate_out, up_out,
    gains_out, bias_out, ids_out,
    x_all, g_all, gains_all, wq, wk, wv, wo, wf, wg, wu, back_buf, inbox, n1_buf, q_buf, k_buf, v_buf, att_buf, lse_buf,
    total_buf, hid, grad_gate, grad_up, grad_hidden, res_buf, turned, stage,
    local_sems, x_sems, g_sems, c_sems, s_sems, n_sems, out_sems, stage_sems,
):
    me = lax.axis_index("group")
    rows, width = x_hbm.shape
    total = rows * count
    columns = wq.shape[1]
    units = wg.shape[1]
    local_heads = columns // head_dim
    n2_all, parts = x_all, back_buf
    loads = [
        pltpu.make_async_copy(source, target, local_sems.at[index])
        for index, (source, target) in enumerate(
            [
                (x_hbm, x_all.at[me]),
                (cot_hbm, g_all.at[me]),
                (wq_hbm, wq),
                (wk_hbm, wk),
                (wv_hbm, wv),
                (wo_hbm, wo),
                (wf_hbm, wf),
                (wg_hbm, wg),
                (wu_hbm, wu),
            ]
        )
    ]
    for load in loads[:2]:
        load.start()
    line_barrier(me, count)
    x_line = LineGather(me, count, x_all, x_sems, subs, x_hbm)
    g_line = LineGather(me, count, gains_all, g_sems)
    c_line = LineGather(me, count, g_all, c_sems, subs)
    n_line = LineGather(me, count, n2_all, n_sems, subs)

    def packed_row(index, length):
        first = index * (packed_ref.shape[0] // 3)
        return jnp.concatenate(
            [packed_ref[row : row + 1, :] for row in range(first, first + length // lanes)], axis=1
        )

    for index in range(2):
        gains_all[me, index : index + 1, :] = packed_row(index, width // count)
    g_line.begin()
    x_line.begin()
    for load in loads[2:6]:
        load.start()
    loads[1].wait()
    position = me * rows + lax.broadcasted_iota(jnp.int32, (rows, 1), 0)
    g_all[me] = g_all[me] * (position < length_ref[0]).astype(jnp.float32).astype(jnp.bfloat16)

    ids = packed_row(2, 2 * total)
    ids_out[...] = jnp.broadcast_to(ids, ids_out.shape)
    bucket = lax.broadcasted_iota(jnp.int32, (table_ref.shape[1], 2 * total), 0).astype(jnp.float32)
    one_hot = (bucket == ids).astype(jnp.float32).astype(jnp.bfloat16)
    bias_out[...] = nn_dot(table_ref[...], one_hot)

    for piece in range(g_line.pieces):
        g_line.arrive(piece)
    for owner in range(count):
        gains_out[:, owner * (width // count) : (owner + 1) * (width // count)] = gains_all[owner]
    for index in (0, 2, 3, 4):
        loads[index].wait()

    def project(block):
        values = x_all[block].astype(jnp.float32)
        normed = (values * rms_rows(values) * gains_out[0:1, :]).astype(jnp.bfloat16)
        n1_buf[block] = normed
        q_buf[block] = nn_dot(normed, wq[...]).astype(jnp.bfloat16)
        k_buf[block] = nn_dot(normed, wk[...]).astype(jnp.bfloat16)
        v_buf[block] = nn_dot(normed, wv[...]).astype(jnp.bfloat16)

    def begin_cotangent(sent):
        for side in range(2):
            last = me if side == 0 else count - 1 - me

            @pl.when(last == sent)
            def _():
                for piece in range(subs):
                    c_line.send_side(side, piece)

    begin_cotangent(0)
    for piece in range(subs):
        x_line.arrive(piece)
    begin_cotangent(1)
    project(me)
    x_line.each_block(0, project)
    for hops in range(1, count - 1):
        for piece in range(hops * subs, (hops + 1) * subs):
            x_line.arrive(piece)
        begin_cotangent(hops + 1)
        if hops == 1:
            for load in loads[6:]:
                load.start()
        x_line.each_block(hops, project)

    loads[5].wait()
    mask_first, mask_second = head_masks()
    key_valid = lax.broadcasted_iota(jnp.int32, (1, total), 1) < length_ref[0]
    lane = lax.broadcasted_iota(jnp.int32, (1, lanes), 1)

    def attend(block):
        lse_buf[block] = jnp.zeros((rows, lanes), jnp.float32)

        @pl.loop(0, local_heads // 2)
        def _(pair):
            cols = pl.ds(pl.multiple_of(pair * lanes, lanes), lanes)
            query = q_buf[block, :, cols]
            key = k_buf[:, :, cols].reshape(total, lanes)
            value = v_buf[:, :, cols].reshape(total, lanes)
            outs = []
            for half, mask in enumerate((mask_first, mask_second)):
                head = pair * 2 + half
                scores = nt_dot(query * mask, key)
                scores = scores + offset_bias(bias_out, head, block * rows, rows, total)
                scores = jnp.where(key_valid, scores, negative)
                top = jnp.max(scores, axis=-1, keepdims=True)
                expd = jnp.exp(scores - top)
                summed = jnp.sum(expd, axis=-1, keepdims=True)
                probs = (expd * (1.0 / summed)).astype(jnp.bfloat16)
                outs.append(nn_dot(probs, value))
                lse_buf[block] = jnp.where(lane == head, top + jnp.log(summed), lse_buf[block])
            att_buf[block, :, cols] = jnp.where(lane < head_dim, outs[0], outs[1]).astype(
                jnp.bfloat16
            )

    scatter = LineScatter(me, count, parts, inbox, total_buf, s_sems, subs)
    arrived = 0
    for index in range(count - 1):
        block = scatter.order(index)
        attend(block)
        parts[block] = nn_dot(att_buf[block], wo[...]).astype(jnp.bfloat16)
        if index == 0:
            x_line.wait_sends()
        scatter.at_time(index)
        if index:
            c_line.arrive(arrived)
            arrived += 1
    attend(me)
    total_buf[...] = x_all[me].astype(jnp.float32) + nn_dot(att_buf[me], wo[...])
    early = [(n1_buf, n1_out), (q_buf, q_out), (k_buf, k_out), (v_buf, v_out), (att_buf, att_out), (lse_buf, lse_out)]
    late = [
        (total_buf, middle_out), (back_buf, back_out), (res_buf, res_out), (n2_all, n2_out), (grad_gate, gate_out),
        (grad_up, up_out),
    ]
    outs = [
        pltpu.make_async_copy(source, target, out_sems.at[index])
        for index, (source, target) in enumerate(early + late)
    ]
    for copy in outs[: len(early)]:
        copy.start()
    for time in range(count - 1, scatter.times):
        scatter.at_time(time)
        if arrived < c_line.pieces:
            c_line.arrive(arrived)
            arrived += 1
    middle = total_buf[...]
    n2_all[me] = (middle * rms_rows(middle) * gains_out[1:2, :]).astype(jnp.bfloat16)
    n_line.begin()
    outs[len(early)].start()
    for piece in range(arrived, c_line.pieces):
        c_line.arrive(piece)

    for load in loads[6:]:
        load.wait()

    @pl.loop(0, units // tile)
    def _(index):
        here = pl.ds(pl.multiple_of(index * tile, tile), tile)
        grad_hidden[:, here] = nt_dot(g_all[...].reshape(total, width), wf[here, :])

    scatter.wait_sends()

    def block_pass(block):
        normed = n2_all[block]
        here = pl.ds(pl.multiple_of(block * rows, rows), rows)
        gate = nn_dot(normed, wg[...])
        up = nn_dot(normed, wu[...])
        act, slope = gelu_parts(gate)
        hid[block] = (act * up).astype(jnp.bfloat16)
        grads = grad_hidden[here, :]
        grad_gate[here, :] = (grads * up * slope).astype(jnp.bfloat16)
        grad_up[here, :] = (grads * act).astype(jnp.bfloat16)
        res_buf[block] = nn_dot(hid[block], wf[...]).astype(jnp.bfloat16)
        half = width // 2
        for cols in (pl.ds(0, half), pl.ds(half, half)):
            back_buf[block, :, cols] = (
                nt_dot(grad_gate[here, :], wg[cols, :]) + nt_dot(grad_up[here, :], wu[cols, :])
            ).astype(jnp.bfloat16)

    for piece in range(subs):
        n_line.arrive(piece)
    block_pass(me)
    n_line.each_block(0, block_pass)
    for hops in range(1, count - 1):
        n_line.arrive_block(hops, block_pass)
    for copy in outs[len(early) + 1 :]:
        copy.start()

    def weight_grad(left, right, base, height):
        depth = right.shape[2]
        panels = depth // lanes
        factor = right[...].reshape(total, depth)

        def store(slot, panel, row):
            return pltpu.make_async_copy(
                stage.at[slot, panel],
                flat_out.at[pl.ds(base + panel * height + row, tile)],
                stage_sems.at[slot, panel],
            )

        @pl.loop(0, height // tile)
        def _(index):
            slot = lax.rem(index, 2)
            row = pl.multiple_of(index * tile, tile)
            turned[...] = left[:, :, pl.ds(row, tile)].reshape(total, tile).T
            product = nn_dot(turned[...], factor).astype(jnp.bfloat16)

            @pl.when(index >= 2)
            def _():
                for panel in range(panels):
                    store(slot, panel, row).wait()

            for panel in range(panels):
                stage[slot, panel] = product[:, panel * lanes : (panel + 1) * lanes]
                store(slot, panel, row).start()

        for slot in range(2):
            for panel in range(panels):
                store(slot, panel, 0).wait()

    weight_grad(hid, g_all, 0, units)
    for line in (g_line, c_line, n_line):
        line.wait_sends()
    for copy in outs:
        copy.wait()


def forward(count, length, x, cot, wq, wk, wv, wo, wf, wg, wu, packed, table):
    rows, width = x.shape
    columns, units = wq.shape[1], wg.shape[1]
    total = count * rows
    tile = 128 if units % 256 else 256
    bf, f32 = jnp.bfloat16, jnp.float32
    shape = jax.ShapeDtypeStruct
    steps = count - 1
    subs = 2
    dma = pltpu.SemaphoreType.DMA
    vmem = pltpu.VMEM
    blocks = (count, rows, width)
    narrow = (count, rows, columns)
    return pl.pallas_call(
        functools.partial(forward_kernel, count, tile, subs),
        name="forward",
        out_shape=(
            shape(blocks, bf), shape(narrow, bf), shape(narrow, bf), shape(narrow, bf), shape(narrow, bf),
            shape((count, rows, lanes), f32), shape((rows, width), f32),
            shape((units * width // lanes, lanes), bf), shape(blocks, bf), shape(blocks, bf), shape(blocks, bf),
            shape((total, units), bf), shape((total, units), bf),
            shape((8, width), f32), shape((columns // head_dim, 2 * total), f32), shape((8, 2 * total), f32),
        ),
        in_specs=[smem_space] + [any_space] * 9 + [vmem_space] * 2,
        out_specs=[any_space] * 13 + [vmem_space] * 3,
        scratch_shapes=[
            vmem(blocks, bf), vmem(blocks, bf), vmem((count, 8, width // count), f32),
            vmem(wq.shape, bf), vmem(wk.shape, bf), vmem(wv.shape, bf), vmem(wo.shape, bf),
            vmem(wf.shape, bf), vmem(wg.shape, bf), vmem(wu.shape, bf),
            vmem(blocks, bf), vmem((count + 1, rows, width), bf), vmem(blocks, bf),
            vmem(narrow, bf), vmem(narrow, bf), vmem(narrow, bf), vmem(narrow, bf), vmem((count, rows, lanes), f32),
            vmem((rows, width), f32), vmem((count, rows, units), bf), vmem((total, units), bf), vmem((total, units), bf),
            vmem((total, units), f32), vmem(blocks, bf), vmem((tile, total), bf),
            vmem((2, width // lanes, tile, lanes), bf),
            dma((9,)), dma((2, 2, steps * subs)), dma((2, 2, steps)), dma((2, 2, steps * subs)),
            dma((2, 2, steps * subs)), dma((2, 2, steps * subs)), dma((12,)), dma((2, width // lanes)),
        ],
        compiler_params=pltpu.CompilerParams(
            collective_id=0, has_side_effects=True, vmem_limit_bytes=61 * 2**20
        ),
    )(length, x, cot, wq, wk, wv, wo, wf, wg, wu, packed, table)


def when(condition, body):
    if isinstance(condition, bool):
        if condition:
            body()
    else:
        pl.when(condition)(body)


class ReplicaSum:
    def __init__(self, replicas, chunk, source, target, work, core_box, path_box, sems):
        self.mine = lax.axis_index("replica")
        self.chunk, self.source, self.target = chunk, source, target
        self.work, self.core_box, self.path_box, self.sems = work, core_box, path_box, sems
        self.depth, self.slots = work.shape[0], core_box.shape[0]
        bits = [1 << index for index in range(1, replicas.bit_length() - 1)]
        self.orders = (bits, bits[::-1])
        self.levels = len(bits)
        self.last_phase = 2 * self.levels + 2
        self.half = chunk // 2

    def bit(self, mask):
        return jnp.where((self.mine & mask) != 0, 1, 0)

    def region(self, path, level):
        size = self.half // 2
        offset = path * size
        for mask in self.orders[path][:level]:
            size //= 2
            offset = offset + self.bit(mask) * size
        return offset, size

    def out_rows(self, chunk, offset, size):
        start = chunk * self.chunk + self.bit(1) * self.half + offset
        return self.target.at[pl.ds(pl.multiple_of(start, 16), size)]

    def sem(self, kind, phase, path, chunk):
        return self.sems.at[kind, phase, path, chunk % self.slots]

    def remote(self, source, target, phase, path, chunk, mask):
        return pltpu.make_async_remote_copy(
            src_ref=source,
            dst_ref=target,
            send_sem=self.sem(0, phase, path, chunk),
            recv_sem=self.sem(1, phase, path, chunk),
            device_id={"replica": self.mine ^ mask},
            device_id_type=MESH,
        )

    def core_copy(self, chunk):
        start = chunk * self.chunk + (1 - self.bit(1)) * self.half
        return self.remote(
            self.source(start, self.half), self.core_box.at[chunk % self.slots], 0, 0, chunk, 1
        )

    def load_copy(self, chunk):
        start = chunk * self.chunk + self.bit(1) * self.half
        return pltpu.make_async_copy(
            self.source(start, self.half), self.work.at[chunk % self.depth], self.sem(0, 0, 1, chunk)
        )

    def reduce_copy(self, chunk, path, level):
        mask = self.orders[path][level - 1]
        offset, size = self.region(path, level - 1)
        size //= 2
        start = pl.multiple_of(offset + (1 - self.bit(mask)) * size, 16)
        return self.remote(
            self.work.at[chunk % self.depth, pl.ds(start, size)],
            self.box(chunk, path, level),
            level, path, chunk, mask,
        )

    def box(self, chunk, path, level):
        size = self.half // 2 >> level
        start = sum(self.half // 2 >> step for step in range(1, level))
        return self.path_box.at[chunk % self.slots, path, pl.ds(start, size)]

    def add_box(self, chunk, path, level):
        offset, size = self.region(path, level)
        here = pl.ds(pl.multiple_of(offset, 16), size)
        slot = chunk % self.depth
        self.work[slot, here, :] = self.work[slot, here, :] + self.box(chunk, path, level)[...]

    def own_copy(self, chunk, path):
        offset, size = self.region(path, self.levels)
        return pltpu.make_async_copy(
            self.work.at[chunk % self.depth, pl.ds(pl.multiple_of(offset, 16), size)],
            self.out_rows(chunk, offset, size),
            self.sems.at[1, 0, 1 + path, chunk % self.slots],
        )

    def spread_copy(self, chunk, path, level):
        offset, size = self.region(path, level)
        if level == self.levels:
            source = self.work.at[chunk % self.depth, pl.ds(pl.multiple_of(offset, 16), size)]
        else:
            source = self.out_rows(chunk, offset, size)
        return self.remote(
            source, self.out_rows(chunk, offset, size),
            2 * self.levels + 1 - level, path, chunk, self.orders[path][level - 1],
        )

    def share_copy(self, chunk):
        rows = self.out_rows(chunk, 0, self.half)
        return self.remote(rows, rows, self.last_phase - 1, 0, chunk, 1)

    def advance(self, phase, chunk):
        levels = self.levels
        if phase == 0:
            self.core_copy(chunk).start()
            self.load_copy(chunk).start()
        elif phase <= levels + 1:
            if phase == 1:
                self.load_copy(chunk).wait()
                self.core_copy(chunk).wait()
                slot = chunk % self.depth
                self.work[slot] = self.work[slot] + self.core_box[chunk % self.slots]
            for path in range(2):
                if phase > 1:
                    self.reduce_copy(chunk, path, phase - 1).wait()
                    self.add_box(chunk, path, phase - 1)
                if phase <= levels:
                    self.reduce_copy(chunk, path, phase).start()
                else:
                    self.own_copy(chunk, path).start()
                    self.spread_copy(chunk, path, levels).start()
        else:
            level = 2 * levels + 1 - phase
            if level >= 0:
                for path in range(2):
                    self.spread_copy(chunk, path, level + 1).wait()
                    if level + 1 == levels:
                        self.own_copy(chunk, path).wait()
                    if level >= 1:
                        self.spread_copy(chunk, path, level).start()
                if level == 0:
                    self.share_copy(chunk).start()


scatter_pace, gather_pace, pair_pace = 1.0, 1.0, 1.0


def rms_backward(values, grads, gain):
    scale = rms_rows(values)
    unit = values * scale
    scaled = grads * gain
    inner = jnp.mean(scaled * unit, axis=-1, keepdims=True)
    return scale * (scaled - unit * inner), jnp.sum(grads * unit, axis=0, keepdims=True)


def backward_kernel(
    count, replicas, chunk, ffn_chunks, out_chunks, attn_chunks, skew, subs,
    length_ref,
    flat_hbm, n2_hbm, gate_hbm, up_hbm, back_hbm, res_hbm, middle_hbm, cot_hbm, x_hbm,
    q_hbm, k_hbm, v_hbm, att_hbm, lse_hbm, n1_hbm,
    wq_hbm, wk_hbm, wv_hbm, wo_hbm, gains_ref, bias_ref, ids_ref,
    sums_out, flat_out, result_out, input_out, small_out,
    back, res, middle, cot, x_own, q_buf, k_buf, v_buf, att_buf, lse_buf, n1_buf, wq, wk, wv, wo,
    back_box, res_box, total_buf, res_total, middle_grad, branch, grad_att, key_acc, value_acc, grad_qkv, grad_up,
    reverse, offsets, turned, stage, out_buf, small, small_parts, small_box, pair_box,
    work, core_box, path_box,
    load_sems, b_sems, r_sems, f_sems, a_sems, p_sems, pair_sems, stage_sems, out_sems, sum_sems,
):
    me = lax.axis_index("group")
    mine = lax.axis_index("replica")
    rows, width = middle.shape
    total = rows * count
    columns = wq.shape[1]
    local_heads = columns // head_dim
    units = grad_up.shape[1]
    sources = [
        back_hbm, n2_hbm, gate_hbm, up_hbm, middle_hbm, cot_hbm, x_hbm, wo_hbm, att_hbm, q_hbm, k_hbm, v_hbm,
        lse_hbm, wq_hbm, wk_hbm, wv_hbm, res_hbm, n1_hbm,
    ]
    targets = [
        back, n1_buf, grad_qkv.at[:, pl.ds(0, units)], grad_up, middle, cot, x_own, wo, att_buf, q_buf, k_buf, v_buf,
        lse_buf, wq, wk, wv, res, n1_buf,
    ]
    loads = [
        pltpu.make_async_copy(source, target, load_sems.at[index])
        for index, (source, target) in enumerate(zip(sources, targets))
    ]
    masks = [1 << index for index in range(replicas.bit_length() - 1)]
    barrier = pltpu.get_barrier_semaphore()

    @pl.when(me > 0)
    def _():
        pl.semaphore_signal(barrier, inc=1, device_id={"group": me - 1}, device_id_type=MESH)

    @pl.when(me < count - 1)
    def _():
        pl.semaphore_signal(barrier, inc=1, device_id={"group": me + 1}, device_id_type=MESH)

    for mask in masks:
        pl.semaphore_signal(barrier, inc=1, device_id={"replica": mine ^ mask}, device_id_type=MESH)
    peers = jnp.where(me > 0, 1, 0) + jnp.where(me < count - 1, 1, 0) + len(masks)
    pl.semaphore_wait(barrier, peers)

    first_rows = flat_hbm.shape[0]
    from_first_chunks = first_rows // chunk
    from_ffn = ffn_chunks
    chunks = from_ffn + attn_chunks

    def make_source(source_ref, base):
        return lambda start, size: source_ref.at[pl.ds(pl.multiple_of(start - base, 16), size)]

    parts = ReplicaSum(replicas, chunk, None, sums_out, work, core_box, path_box, sum_sems)
    from_first, from_second = make_source(flat_hbm, 0), make_source(flat_out, first_rows)
    clock = {"time": 0, "gaps": [0] + [None] * 4, "credit": 0.0}
    each = from_first_chunks
    bounds = [0, each, 2 * each, 3 * each, from_ffn + out_chunks, chunks]

    def start_piece(source, piece):
        parts.source = source
        parts.core_copy(piece).start()
        parts.load_copy(piece).start()

    def tick(time):
        for phase in range(parts.last_phase, -1, -1):
            entry = time - skew * phase
            inside, piece = False, entry
            for gap, low, high in zip(clock["gaps"], bounds, bounds[1:]):
                if gap is None:
                    continue
                if isinstance(entry, int):
                    if low + gap <= entry < high + gap:
                        inside, piece = True, entry - gap
                else:
                    here = (entry >= low + gap) & (entry < high + gap)
                    inside = inside | here
                    piece = jnp.where(here, entry - gap, piece)

            def body(phase=phase, piece=piece):
                if phase == parts.last_phase:
                    parts.share_copy(piece).wait()
                elif phase:
                    parts.source = lambda start, size: flat_hbm.at[pl.ds(0, size)]
                    parts.advance(phase, piece)

            if phase:
                when(inside, body)
            else:
                first, second = piece < from_first_chunks, piece >= from_first_chunks
                if isinstance(entry, int):
                    first, second = first and inside, second and inside
                else:
                    first, second = first & inside, second & inside
                when(first, functools.partial(start_piece, from_first, piece))
                when(second, functools.partial(start_piece, from_second, piece))

    def pace(amount):
        clock["credit"] += amount
        while clock["credit"] >= 1:
            tick(clock["time"])
            clock["time"] += 1
            clock["credit"] -= 1

    back_line = LineScatter(me, count, back, back_box, total_buf, b_sems, subs)
    res_line = LineScatter(me, count, res, res_box, res_total, r_sems, subs)
    first_line = LineScatter(me, count, back, back_box, total_buf, f_sems, subs)
    branch_line = LineGather(me, count, branch, a_sems, subs)
    small_line = LineScatter(me, count, small_parts, small_box, small.at[pl.ds(0, 8)], p_sems)

    tile = 256

    def weight_grad(left, factor, base, height, per_output, splits=1):
        panels = factor.shape[1] // lanes
        tiles = height // tile

        def store(slot, panel, row):
            return pltpu.make_async_copy(
                stage.at[slot, panel],
                flat_out.at[pl.ds(base + panel * height + row, tile)],
                stage_sems.at[slot, panel],
            )

        def run(first, last):
            @pl.loop(first, last)
            def _(index):
                slot = lax.rem(index, 2)
                row = pl.multiple_of(index * tile, tile)
                turned[...] = left[:, :, pl.ds(row, tile)].reshape(total, tile).T
                product = nn_dot(turned[...], factor).astype(jnp.bfloat16)

                @pl.when(index >= 2)
                def _():
                    for panel in range(panels):
                        store(slot, panel, row).wait()

                for panel in range(panels):
                    stage[slot, panel] = product[:, panel * lanes : (panel + 1) * lanes]
                    store(slot, panel, row).start()

        for split in range(splits):
            if split:
                pace(1)
            run(tiles * split // splits, tiles * (split + 1) // splits)
        for slot in range(min(2, tiles)):
            for panel in range(panels):
                store(slot, panel, 0).wait()

    def enter(group):
        before = clock["gaps"][group - 1]
        clock["gaps"][group] = max(clock["time"] - bounds[group], before)

    for now in range(skew):
        tick(now)
    for load in loads[:17]:
        load.start()
    loads[0].wait()
    total_buf[...] = back[me].astype(jnp.float32)
    back_line.at_time(0)
    clock["time"] = skew
    pace(skew)
    for load in loads[1:3]:
        load.wait()
    gate_base, attn_base = 0, 2 * units * width // lanes
    weight_grad(n1_buf, grad_qkv[:, 0:units], gate_base, width, units, 2)
    enter(1)
    pace(1)
    back_line.at_time(1)
    pace(1)
    back_line.at_time(2)
    pace(1)
    loads[3].wait()
    weight_grad(n1_buf, grad_up[...], gate_base + units * width // lanes, width, units, 2)
    enter(2)
    loads[17].start()
    anti = lax.broadcasted_iota(jnp.int32, (rows, rows), 0) + lax.broadcasted_iota(
        jnp.int32, (rows, rows), 1
    )
    reverse[...] = (anti == rows - 1).astype(jnp.float32).astype(jnp.bfloat16)
    for now in range(3, back_line.times):
        back_line.at_time(now)
        pace(scatter_pace)
    for load in loads[4:7]:
        load.wait()
    position = me * rows + lax.broadcasted_iota(jnp.int32, (rows, 1), 0)
    valid = (position < length_ref[0]).astype(jnp.float32)
    grad_mid, gain_grad = rms_backward(middle[...], total_buf[...], gains_ref[1:2, :])
    middle_grad[...] = cot[...].astype(jnp.float32) * valid + grad_mid
    branch[me] = middle_grad[...].astype(jnp.bfloat16)
    branch_line.begin()
    small_parts[...] = jnp.zeros_like(small_parts)
    part_width = width // count
    for owner in range(count):
        small_parts[owner, 1:2, :] = gain_grad[:, owner * part_width : (owner + 1) * part_width]
    for load in loads[7:18]:
        load.wait()
    res_total[...] = middle[...] + res[me].astype(jnp.float32)

    def attended_grad(block):
        grad_att[block] = nt_dot(branch[block], wo[...]).astype(jnp.bfloat16)

    attended_grad(me)
    for piece in range(branch_line.pieces):
        branch_line.arrive(piece)
        pace(gather_pace)
        if piece % subs == subs - 1:
            branch_line.each_block(piece // subs, attended_grad)

    weight_grad(att_buf, branch[...].reshape(total, width), attn_base, columns, width)
    enter(3)
    pace(1)
    mask_first, mask_second = head_masks()
    key_valid = lax.broadcasted_iota(jnp.int32, (1, total), 1) < length_ref[0]
    lane = lax.broadcasted_iota(jnp.int32, (1, lanes), 1)
    offsets[...] = jnp.zeros_like(offsets)

    def head_pair(pair):
        cols = pl.ds(pl.multiple_of(pair * lanes, lanes), lanes)
        key = k_buf[:, :, cols].reshape(total, lanes)
        value = v_buf[:, :, cols].reshape(total, lanes)
        key_acc[...] = jnp.zeros_like(key_acc)
        value_acc[...] = jnp.zeros_like(value_acc)

        @pl.loop(0, count)
        def _(block):
            query = q_buf[block, :, cols]
            grads = grad_att[block, :, cols]
            logs = lse_buf[block]
            query_parts = []
            for half, mask in enumerate((mask_first, mask_second)):
                head = pair * 2 + half
                query_half, grads_half = query * mask, grads * mask
                scores = nt_dot(query_half, key)
                scores = scores + offset_bias(bias_ref, head, block * rows, rows, total)
                scores = jnp.where(key_valid, scores, negative)
                log_total = jnp.sum(jnp.where(lane == head, logs, 0.0), axis=-1, keepdims=True)
                probs = jnp.exp(scores - log_total)
                grad_probs = nt_dot(grads_half, value)
                inner = jnp.sum(probs * grad_probs, axis=-1, keepdims=True)
                grad_scores = (probs * (grad_probs - inner)).astype(jnp.bfloat16)
                query_parts.append(nn_dot(grad_scores, key))
                key_acc[...] += nn_dot(query_half.astype(jnp.float32).T.astype(jnp.bfloat16), grad_scores)
                value_acc[...] += nn_dot(
                    grads_half.astype(jnp.float32).T.astype(jnp.bfloat16), probs.astype(jnp.bfloat16)
                )
                turned_scores = nn_dot(reverse[...], grad_scores)
                padded = jnp.concatenate([turned_scores, jnp.zeros_like(turned_scores)], axis=1)
                sheared = pltpu.roll(padded, 0, 1, stride=1, stride_axis=0)
                sums = jnp.broadcast_to(jnp.sum(sheared, axis=0, keepdims=True), (8, 2 * total))
                sums = pltpu.roll(sums, total - rows - block * rows, 1)
                offsets[pl.ds(head, 1), :] += sums[0:1, :]
            grad_qkv[pl.ds(pl.multiple_of(block * rows, rows), rows), cols] = jnp.where(
                lane < head_dim, query_parts[0], query_parts[1]
            ).astype(jnp.bfloat16)

        grad_qkv[:, pl.ds(pl.multiple_of(columns + pair * lanes, lanes), lanes)] = key_acc[
            ...
        ].T.astype(jnp.bfloat16)
        grad_qkv[:, pl.ds(pl.multiple_of(2 * columns + pair * lanes, lanes), lanes)] = value_acc[
            ...
        ].T.astype(jnp.bfloat16)

    res_time = 0
    for pair in range(local_heads // 2):
        if res_time < 3:
            res_line.at_time(res_time)
            res_time += 1
        head_pair(pair)
        pace(pair_pace)

    back_line.wait_sends()

    quarter = width // 4
    for start in range(0, width, quarter):
        cols = pl.ds(start, quarter)
        back[:, :, cols] = (
            (
                nt_dot(grad_qkv[:, 0:columns], wq[cols, :])
                + nt_dot(grad_qkv[:, columns : 2 * columns], wk[cols, :])
                + nt_dot(grad_qkv[:, 2 * columns : 3 * columns], wv[cols, :])
            )
            .astype(jnp.bfloat16)
            .reshape(count, rows, quarter)
        )
        if start == quarter:
            pace(1)
    for now in range(count - 1):
        first_line.at_time(now)
    pace(1)
    total_buf[...] = back[me].astype(jnp.float32)
    weight_grad(n1_buf, grad_qkv[...], attn_base + columns * width // lanes, width, columns, 2)
    enter(4)
    pace(skew)
    for now in range(count - 1, first_line.times):
        first_line.at_time(now)
        pace(1)
    grad_in, gain_grad = rms_backward(
        x_own[...].astype(jnp.float32), total_buf[...], gains_ref[0:1, :]
    )
    out_buf[1] = (middle_grad[...] + grad_in).astype(jnp.bfloat16)
    input_copy = pltpu.make_async_copy(out_buf.at[1], input_out, out_sems.at[1])
    input_copy.start()
    for owner in range(count):
        small_parts[owner, 0:1, :] = gain_grad[:, owner * part_width : (owner + 1) * part_width]
    small[0:8, :] = small_parts[me]
    for now in range(max(small_line.times, res_line.times - res_time)):
        if now < small_line.times:
            small_line.at_time(now)
        if res_time < res_line.times:
            res_line.at_time(res_time)
            res_time += 1
        pace(1)
    out_buf[0] = res_total[...].astype(jnp.bfloat16)
    result_copy = pltpu.make_async_copy(out_buf.at[0], result_out, out_sems.at[0])
    result_copy.start()
    bucket = lax.broadcasted_iota(jnp.int32, (lanes, ids_ref.shape[1]), 0).astype(jnp.float32)
    one_hot = (bucket == ids_ref[0:1, :]).astype(jnp.float32).astype(jnp.bfloat16)
    high = offsets[...].astype(jnp.bfloat16)
    rest = offsets[...] - high.astype(jnp.float32)
    middle_part = rest.astype(jnp.bfloat16)
    low_part = (rest - middle_part.astype(jnp.float32)).astype(jnp.bfloat16)
    small[8:16, 0:lanes] = nt_dot(high, one_hot) + nt_dot(middle_part, one_hot) + nt_dot(low_part, one_hot)
    small[8:16, lanes:] = jnp.zeros((8, part_width - lanes), jnp.float32)
    for index, mask in enumerate(masks):
        copy = pltpu.make_async_remote_copy(
            src_ref=small,
            dst_ref=pair_box.at[index],
            send_sem=pair_sems.at[0, index],
            recv_sem=pair_sems.at[1, index],
            device_id={"replica": mine ^ mask},
            device_id_type=MESH,
        )
        copy.start()
        pace(1)
        copy.wait()
        small[...] += pair_box[index]
    small_out[...] = small[...]

    @pl.loop(clock["time"], chunks + clock["gaps"][4] + skew * parts.last_phase)
    def _(now):
        tick(now)

    for line in (res_line, first_line, branch_line, small_line):
        line.wait_sends()
    result_copy.wait()
    input_copy.wait()


def backward(count, replicas, length, flat, n2, grad_gate, grad_up, back, res, middle, cot, x, q, k, v, att, lse, n1, wq, wk, wv, wo, gains, bias, ids):
    rows, width = middle.shape
    total = count * rows
    columns = wq.shape[1]
    bf, f32 = jnp.bfloat16, jnp.float32
    shape = jax.ShapeDtypeStruct
    steps = count - 1
    dma = pltpu.SemaphoreType.DMA
    units = grad_up.shape[1]
    chunk = flat.shape[0] // 5
    ffn_rows = 3 * flat.shape[0]
    attn_rows = 4 * columns * width // lanes
    skew, subs = 3, 2
    levels = replicas.bit_length() - 2
    masks = levels + 1
    depth = skew * (levels + 2)
    part_width = width // count
    vmem = pltpu.VMEM
    blocks = lambda kind: vmem((count, rows, width), kind)
    narrow = lambda: vmem((count, rows, columns), bf)
    boxes = lambda: vmem((count + 1, rows, width), bf)
    return pl.pallas_call(
        functools.partial(
            backward_kernel, count, replicas, chunk, ffn_rows // chunk, wo.size // lanes // chunk,
            attn_rows // chunk, skew, subs
        ),
        name="backward",
        out_shape=(
            shape((ffn_rows + attn_rows, lanes), bf),
            shape((2 * flat.shape[0] + attn_rows, lanes), bf),
            shape((rows, width), bf),
            shape((rows, width), bf),
            shape((16, part_width), f32),
        ),
        in_specs=[smem_space] + [any_space] * 19 + [vmem_space] * 3,
        out_specs=[any_space] * 4 + [vmem_space],
        scratch_shapes=[
            blocks(bf), blocks(bf), vmem((rows, width), f32), vmem((rows, width), bf), vmem((rows, width), bf),
            narrow(), narrow(), narrow(), narrow(), vmem((count, rows, lanes), f32), blocks(bf),
            vmem(wq.shape, bf), vmem(wk.shape, bf), vmem(wv.shape, bf), vmem(wo.shape, bf),
            boxes(), boxes(), vmem((rows, width), f32), vmem((rows, width), f32), vmem((rows, width), f32), blocks(bf),
            narrow(),
            vmem((lanes, total), f32), vmem((lanes, total), f32), vmem((total, 3 * columns), bf), vmem((total, units), bf),
            vmem((rows, rows), bf), vmem((8, 2 * total), f32), vmem((256, total), bf),
            vmem((2, width // lanes, 256, lanes), bf), vmem((2, rows, width), bf),
            vmem((16, part_width), f32), vmem((count, 8, part_width), f32), vmem((count + 1, 8, part_width), f32),
            vmem((masks, 16, part_width), f32),
            vmem((depth, chunk // 2, lanes), bf), vmem((2 * skew, chunk // 2, lanes), bf),
            vmem((2 * skew, 2, chunk // 4, lanes), bf),
            dma((18,)), dma((2, 2, steps * subs)), dma((2, 2, steps * subs)), dma((2, 2, steps * subs)),
            dma((2, 2, steps * subs)),
            dma((2, 2, steps)), dma((2, masks)), dma((2, width // lanes)), dma((2,)),
            dma((2, 2 * levels + 3, 3, 2 * skew)),
        ],
        compiler_params=pltpu.CompilerParams(
            collective_id=1, has_side_effects=True, vmem_limit_bytes=61 * 2**20
        ),
    )(length, flat, n2, grad_gate, grad_up, back, res, middle, cot, x, q, k, v, att, lse, n1, wq, wk, wv, wo, gains, bias, ids)


def widen_kernel(plan, slots, sums, result, input_grad, small, *refs):
    targets, (inbox, outbox, passed, in_sems, out_sems, pass_sems) = refs[:-6], refs[-6:]
    held = [
        pltpu.make_async_copy(source, passed.at[index], pass_sems.at[0, index])
        for index, source in enumerate((result, input_grad))
    ]
    given = [
        pltpu.make_async_copy(passed.at[index], target, pass_sems.at[1, index])
        for index, target in enumerate(targets[:2])
    ]
    for copy in held:
        copy.start()
    gain1, gain2, table = targets[2:5]
    for index, gain in enumerate((gain1, gain2)):
        for row in range(gain.shape[0]):
            gain[row : row + 1, :] = small[index : index + 1, row * lanes : (row + 1) * lanes]
    table[...] = small[8 : 8 + table.shape[0], 0 : table.shape[1]]
    targets = targets[5:]
    tiles = [
        (target, start, height, depth // lanes, size, row)
        for target, (start, height, depth, size) in zip(targets, plan)
        for row in range(0, height, size)
    ]

    def load(number):
        _, start, height, panels, size, row = tiles[number]
        slot = number % slots

        @pl.loop(0, panels)
        def _(panel):
            pltpu.make_async_copy(
                sums.at[pl.ds(start + row + panel * height, size)],
                inbox.at[slot, pl.ds(pl.multiple_of(panel * size, size), size)],
                in_sems.at[slot],
            ).start()

    def store(number):
        target, _, _, panels, size, row = tiles[number]
        return pltpu.make_async_copy(
            outbox.at[number % slots, pl.ds(0, size), pl.ds(0, panels * lanes)],
            target.at[pl.ds(row, size)],
            out_sems.at[number % slots],
        )

    for number in range(min(slots - 1, len(tiles))):
        load(number)
    for number in range(len(tiles)):
        _, _, _, panels, size, _ = tiles[number]
        slot = number % slots
        if number + slots - 1 < len(tiles):
            load(number + slots - 1)
        whole = inbox.at[slot, pl.ds(0, panels * size)]
        pltpu.make_async_copy(whole, whole, in_sems.at[slot]).wait()
        if number >= slots:
            store(number - slots).wait()

        @pl.loop(0, panels)
        def _(panel):
            outbox[slot, pl.ds(0, size), pl.ds(pl.multiple_of(panel * lanes, lanes), lanes)] = inbox[
                slot, pl.ds(pl.multiple_of(panel * size, size), size)
            ].astype(jnp.float32)

        store(number).start()
        if number == slots:
            for first, second in zip(held, given):
                first.wait()
                second.start()
    for number in range(max(len(tiles) - slots, 0), len(tiles)):
        store(number).wait()
    for copy in given:
        copy.wait()


def widen(sums, result, input_grad, small, table_shape, shapes):
    slots = 4
    plan, start = [], 0
    for height, depth in shapes:
        size = 512 if depth <= 1024 else 256
        while height % size:
            size //= 2
        plan.append((start, height, depth, size))
        start += height * depth // lanes
    most_in = max(size * depth // lanes for _, _, depth, size in plan)
    most_rows = max(size for _, _, _, size in plan)
    return pl.pallas_call(
        functools.partial(widen_kernel, plan, slots),
        name="widen",
        out_shape=[jax.ShapeDtypeStruct(result.shape, result.dtype)] * 2
        + [jax.ShapeDtypeStruct((small.shape[1] // lanes, lanes), jnp.float32)] * 2
        + [jax.ShapeDtypeStruct(table_shape, jnp.float32)]
        + [jax.ShapeDtypeStruct(shape, jnp.float32) for shape in shapes],
        in_specs=[any_space] * 3 + [vmem_space],
        out_specs=[any_space] * 2 + [vmem_space] * 3 + [any_space] * len(shapes),
        scratch_shapes=[
            pltpu.VMEM((slots, most_in, lanes), jnp.bfloat16),
            pltpu.VMEM((slots, most_rows, max(depth for _, depth in shapes)), jnp.float32),
            pltpu.VMEM((2,) + result.shape, result.dtype),
            pltpu.SemaphoreType.DMA((slots,)),
            pltpu.SemaphoreType.DMA((slots,)),
            pltpu.SemaphoreType.DMA((2, 2)),
        ],
        compiler_params=pltpu.CompilerParams(vmem_limit_bytes=61 * 2**20),
    )(sums, result, input_grad, small)


def local(
    inputs,
    seq_lengths,
    bucket_ids,
    norm1_gain,
    w_query,
    w_key,
    w_value,
    w_attn_out,
    bias_table,
    norm2_gain,
    w_gate,
    w_up,
    w_ffn_out,
    cotangent,
):
    count = lax.axis_size("group")
    replicas = lax.axis_size("replica")
    longest = max(2 * count * inputs.shape[1], norm1_gain.shape[0])
    longest = -(-longest // 1024) * 1024
    packed = jnp.concatenate(
        [
            jnp.pad(vector.astype(jnp.float32), (0, longest - vector.shape[0]), constant_values=-1)
            for vector in (norm1_gain, norm2_gain, bucket_ids)
        ]
    ).reshape(-1, lanes)
    (
        normed_one, query, key, value, attended, log_totals, middle, flat, back_part, result_part, normed_all,
        grad_gate, grad_up, gains, bias, ids,
    ) = forward(
        count, seq_lengths, inputs[0], cotangent[0], w_query, w_key, w_value, w_attn_out, w_ffn_out, w_gate, w_up,
        packed, bias_table.T,
    )
    sums, _, result, input_grad, small = backward(
        count, replicas, seq_lengths, flat, normed_all, grad_gate, grad_up, back_part, result_part, middle,
        cotangent[0], inputs[0], query, key, value, attended, log_totals, normed_one,
        w_query, w_key, w_value, w_attn_out, gains, bias, ids,
    )
    weights = (w_ffn_out, w_gate, w_up, w_attn_out, w_query, w_key, w_value)
    (
        result, input_grad, gain1_grad, gain2_grad, table_grad,
        ffn_out_grad, gate_grad, up_grad, attn_out_grad, query_grad, key_grad, value_grad,
    ) = widen(
        sums, result, input_grad, small, bias_table.shape[::-1], [weight.shape for weight in weights]
    )
    return (
        result[None],
        input_grad[None],
        gain1_grad.reshape(-1),
        query_grad,
        key_grad,
        value_grad,
        attn_out_grad,
        table_grad.T,
        gain2_grad.reshape(-1),
        gate_grad,
        up_grad,
        ffn_out_grad,
    )


def solution(mesh):
    placed = (
        P("replica", "group", None),
        P("replica"),
        P(),
        P("group"),
        P(None, "group"),
        P(None, "group"),
        P(None, "group"),
        P("group", None),
        P(None, "group"),
        P("group"),
        P(None, "group"),
        P(None, "group"),
        P("group", None),
        P("replica", "group", None),
    )
    return jax.shard_map(
        local,
        mesh=mesh,
        in_specs=placed,
        out_specs=(
            P("replica", "group", None),
            P("replica", "group", None),
            P("group"),
            P(None, "group"),
            P(None, "group"),
            P(None, "group"),
            P("group", None),
            P(None, "group"),
            P("group"),
            P(None, "group"),
            P(None, "group"),
            P("group", None),
        ),
        check_vma=False,
    )
```

```python
import functools
import jax
import jax.numpy as jnp
from jax import lax
from jax.experimental import pallas as pl
from jax.experimental.pallas import tpu as pltpu
from jax.sharding import PartitionSpec as P

epsilon = 1e-06
negative = -1000000000.0
head_dim = 64
lanes = 128
MESH = pl.DeviceIdType.MESH
any_space = pl.BlockSpec(memory_space=pl.ANY)
vmem_space = pl.BlockSpec(memory_space=pltpu.VMEM)
smem_space = pl.BlockSpec(memory_space=pltpu.SMEM)


def nn_dot(left, right):
    return jnp.dot(left, right, preferred_element_type=jnp.float32)


def nt_dot(left, right):
    return lax.dot_general(
        left, right, (((1,), (1,)), ((), ())), preferred_element_type=jnp.float32
    )


def line_barrier(me, count):
    barrier = pltpu.get_barrier_semaphore()

    @pl.when(me > 0)
    def _():
        pl.semaphore_signal(barrier, inc=1, device_id={"group": me - 1}, device_id_type=MESH)

    @pl.when(me < count - 1)
    def _():
        pl.semaphore_signal(barrier, inc=1, device_id={"group": me + 1}, device_id_type=MESH)

    peers = jnp.where(me > 0, 1, 0) + jnp.where(me < count - 1, 1, 0)
    pl.semaphore_wait(barrier, peers)


class LineGather:
    def __init__(self, me, count, buffer, sems, subs=1, own=None):
        self.me, self.count, self.buffer, self.sems, self.subs = me, count, buffer, sems, subs
        self.own = own
        self.pieces = (count - 1) * subs
        self.size = buffer.shape[1] // subs

    def copy(self, side, piece, hops):
        block = self.me - hops if side == 0 else self.me + hops
        part = pl.ds(piece % self.subs * self.size, self.size)
        here = self.buffer.at[block, part]
        return pltpu.make_async_remote_copy(
            src_ref=here if hops or self.own is None else self.own.at[part],
            dst_ref=here,
            send_sem=self.sems.at[side, 0, piece],
            recv_sem=self.sems.at[side, 1, piece],
            device_id={"group": self.me + (1 if side == 0 else -1)},
            device_id_type=MESH,
        )

    def sends(self, side, piece):
        hops = piece // self.subs
        if side == 0:
            return (self.me - hops >= 0) & (self.me + 1 < self.count)
        return (self.me + hops < self.count) & (self.me >= 1)

    def arrives(self, side, piece):
        hops = piece // self.subs
        if side == 0:
            return self.me - 1 - hops >= 0
        return self.me + 1 + hops < self.count

    def send_side(self, side, piece):
        @pl.when(self.sends(side, piece))
        def _():
            self.copy(side, piece, piece // self.subs).start()

    def send(self, piece):
        for side in range(2):
            self.send_side(side, piece)

    def begin(self):
        for piece in range(self.subs):
            self.send(piece)

    def arrive(self, piece):
        for side in range(2):
            @pl.when(self.arrives(side, piece))
            def _():
                self.copy(side, piece, piece // self.subs + 1).wait_recv()

        if piece + self.subs < self.pieces:
            self.send(piece + self.subs)

    def arrive_block(self, hops, body):
        for piece in range(hops * self.subs, (hops + 1) * self.subs):
            self.arrive(piece)
        self.each_block(hops, body)

    def each_block(self, hops, body):
        @pl.loop(0, 2)
        def _(side):
            block = jnp.where(side == 0, self.me - 1 - hops, self.me + 1 + hops)

            @pl.when((block >= 0) & (block < self.count))
            def _():
                body(block)

    def wait_sends(self):
        for piece in range(self.pieces):
            for side in range(2):
                @pl.when(self.sends(side, piece))
                def _():
                    self.copy(side, piece, piece // self.subs).wait_send()


class LineScatter:
    def __init__(self, me, count, parts, inbox, total, sems, subs=1):
        self.me, self.count, self.parts, self.inbox = me, count, parts, inbox
        self.total, self.sems, self.subs = total, sems, subs
        self.steps = count - 1
        self.times = self.steps * subs + 1
        self.size = parts.shape[1] // subs

    def order(self, index):
        picked = 0
        for device in range(self.count):
            due = [(step + self.count - 1 - device, step) for step in range(device)]
            due += [
                (step + device, self.count - 1 - step) for step in range(self.count - 1 - device)
            ]
            blocks = [block for _, block in sorted(due)] + [device]
            picked = picked + jnp.where(self.me == device, blocks[index], 0)
        return picked

    def copy(self, side, piece):
        step = piece % self.steps
        here = pl.ds(pl.multiple_of(piece // self.steps * self.size, self.size), self.size)
        owner = step if side == 0 else self.count - 1 - step
        return pltpu.make_async_remote_copy(
            src_ref=self.parts.at[owner, here],
            dst_ref=self.inbox.at[self.slot(side, step), here],
            send_sem=self.sems.at[side, 0, piece],
            recv_sem=self.sems.at[side, 1, piece],
            device_id={"group": self.me + (-1 if side == 0 else 1)},
            device_id_type=MESH,
        )

    def slot(self, side, step):
        return step if side == 0 else self.count - step

    def at_time(self, time):
        for side in range(2):
            before = self.count - 1 - self.me if side == 0 else self.me
            after = self.count - 1 - before
            piece = time - before
            inside = (piece >= 0) & (piece < self.subs * self.steps)
            piece = jnp.where(inside, piece, 0)
            step = piece % self.steps

            @pl.when(inside & (step < after))
            def _():
                owner = step if side == 0 else self.count - 1 - step
                here = pl.ds(pl.multiple_of(piece // self.steps * self.size, self.size), self.size)

                @pl.when(before > 0)
                def _():
                    self.copy(side, piece).wait_recv()
                    self.parts[owner, here, :] = (
                        self.parts[owner, here, :].astype(jnp.float32)
                        + self.inbox[self.slot(side, step), here, :].astype(jnp.float32)
                    ).astype(self.parts.dtype)

                self.copy(side, piece).start()

            @pl.when(inside & (step == after) & (before > 0))
            def _():
                here = pl.ds(pl.multiple_of(piece // self.steps * self.size, self.size), self.size)
                self.copy(side, piece).wait_recv()
                self.total[here, :] += self.inbox[self.slot(side, step), here, :].astype(jnp.float32)

    def wait_sends(self):
        for piece in range(self.steps * self.subs):
            step = piece % self.steps
            for side in range(2):
                after = self.me if side == 0 else self.count - 1 - self.me

                @pl.when(step < after)
                def _():
                    self.copy(side, piece).wait_send()


def head_masks():
    lane = lax.broadcasted_iota(jnp.int32, (1, lanes), 1)
    first = (lane < head_dim).astype(jnp.float32)
    return first.astype(jnp.bfloat16), (1.0 - first).astype(jnp.bfloat16)


def offset_bias(bias_ref, head, row_start, rows, total):
    width = bias_ref.shape[1]
    shift = lax.rem(row_start + (width - (total - 1)), width)
    vector = pltpu.roll(jnp.broadcast_to(bias_ref[pl.ds(head, 1), :], (8, width)), shift, 1)
    vector = jnp.broadcast_to(vector[0:1, :], (rows, width))
    return pltpu.roll(vector, 0, 1, stride=1, stride_axis=0)[:, :total]


def rms_rows(values):
    return lax.rsqrt(jnp.mean(values * values, axis=-1, keepdims=True) + epsilon)


def gelu_parts(gate):
    root = 0.7978845608028654
    inner = root * (gate + 0.044715 * gate * gate * gate)
    tanh = jnp.tanh(inner)
    half = 0.5 * (1.0 + tanh)
    slope = half + 0.5 * gate * (1.0 - tanh * tanh) * root * (1.0 + 3 * 0.044715 * gate * gate)
    return gate * half, slope


def forward_kernel(
    count, tile, subs,
    length_ref,
    x_hbm, cot_hbm, wq_hbm, wk_hbm, wv_hbm, wo_hbm, wf_hbm, wg_hbm, wu_hbm, packed_ref, table_ref,
    n1_out, q_out, k_out, v_out, att_out, lse_out, middle_out, flat_out, back_out, res_out, n2_out, gate_out, up_out,
    gains_out, bias_out, ids_out,
    x_all, g_all, gains_all, wq, wk, wv, wo, wf, wg, wu, back_buf, inbox, n1_buf, q_buf, k_buf, v_buf, att_buf, lse_buf,
    total_buf, hid, grad_gate, grad_up, grad_hidden, res_buf, turned, stage,
    local_sems, x_sems, g_sems, c_sems, s_sems, n_sems, out_sems, stage_sems,
):
    me = lax.axis_index("group")
    rows, width = x_hbm.shape
    total = rows * count
    columns = wq.shape[1]
    units = wg.shape[1]
    local_heads = columns // head_dim
    n2_all, parts = x_all, back_buf
    loads = [
        pltpu.make_async_copy(source, target, local_sems.at[index])
        for index, (source, target) in enumerate(
            [
                (x_hbm, x_all.at[me]),
                (cot_hbm, g_all.at[me]),
                (wq_hbm, wq),
                (wk_hbm, wk),
                (wv_hbm, wv),
                (wo_hbm, wo),
                (wf_hbm, wf),
                (wg_hbm, wg),
                (wu_hbm, wu),
            ]
        )
    ]
    for load in loads[:2]:
        load.start()
    line_barrier(me, count)
    x_line = LineGather(me, count, x_all, x_sems, subs, x_hbm)
    g_line = LineGather(me, count, gains_all, g_sems)
    c_line = LineGather(me, count, g_all, c_sems, subs)
    n_line = LineGather(me, count, n2_all, n_sems, subs)

    def packed_row(index, length):
        first = index * (packed_ref.shape[0] // 3)
        return jnp.concatenate(
            [packed_ref[row : row + 1, :] for row in range(first, first + length // lanes)], axis=1
        )

    for index in range(2):
        gains_all[me, index : index + 1, :] = packed_row(index, width // count)
    g_line.begin()
    x_line.begin()
    for load in loads[2:6]:
        load.start()
    loads[1].wait()
    position = me * rows + lax.broadcasted_iota(jnp.int32, (rows, 1), 0)
    g_all[me] = g_all[me] * (position < length_ref[0]).astype(jnp.float32).astype(jnp.bfloat16)

    ids = packed_row(2, 2 * total)
    ids_out[...] = jnp.broadcast_to(ids, ids_out.shape)
    bucket = lax.broadcasted_iota(jnp.int32, (table_ref.shape[1], 2 * total), 0).astype(jnp.float32)
    one_hot = (bucket == ids).astype(jnp.float32).astype(jnp.bfloat16)
    bias_out[...] = nn_dot(table_ref[...], one_hot)

    for piece in range(g_line.pieces):
        g_line.arrive(piece)
    for owner in range(count):
        gains_out[:, owner * (width // count) : (owner + 1) * (width // count)] = gains_all[owner]
    for index in (0, 2, 3, 4):
        loads[index].wait()

    def project(block):
        values = x_all[block].astype(jnp.float32)
        normed = (values * rms_rows(values) * gains_out[0:1, :]).astype(jnp.bfloat16)
        n1_buf[block] = normed
        q_buf[block] = nn_dot(normed, wq[...]).astype(jnp.bfloat16)
        k_buf[block] = nn_dot(normed, wk[...]).astype(jnp.bfloat16)
        v_buf[block] = nn_dot(normed, wv[...]).astype(jnp.bfloat16)

    def begin_cotangent(sent):
        for side in range(2):
            last = me if side == 0 else count - 1 - me

            @pl.when(last == sent)
            def _():
                for piece in range(subs):
                    c_line.send_side(side, piece)

    begin_cotangent(0)
    for piece in range(subs):
        x_line.arrive(piece)
    begin_cotangent(1)
    project(me)
    x_line.each_block(0, project)
    for hops in range(1, count - 1):
        for piece in range(hops * subs, (hops + 1) * subs):
            x_line.arrive(piece)
        begin_cotangent(hops + 1)
        if hops == 1:
            for load in loads[6:]:
                load.start()
        x_line.each_block(hops, project)

    loads[5].wait()
    mask_first, mask_second = head_masks()
    key_valid = lax.broadcasted_iota(jnp.int32, (1, total), 1) < length_ref[0]
    lane = lax.broadcasted_iota(jnp.int32, (1, lanes), 1)

    def attend(block):
        lse_buf[block] = jnp.zeros((rows, lanes), jnp.float32)

        @pl.loop(0, local_heads // 2)
        def _(pair):
            cols = pl.ds(pl.multiple_of(pair * lanes, lanes), lanes)
            query = q_buf[block, :, cols]
            key = k_buf[:, :, cols].reshape(total, lanes)
            value = v_buf[:, :, cols].reshape(total, lanes)
            outs = []
            for half, mask in enumerate((mask_first, mask_second)):
                head = pair * 2 + half
                scores = nt_dot(query * mask, key)
                scores = scores + offset_bias(bias_out, head, block * rows, rows, total)
                scores = jnp.where(key_valid, scores, negative)
                top = jnp.max(scores, axis=-1, keepdims=True)
                expd = jnp.exp(scores - top)
                summed = jnp.sum(expd, axis=-1, keepdims=True)
                probs = (expd * (1.0 / summed)).astype(jnp.bfloat16)
                outs.append(nn_dot(probs, value))
                lse_buf[block] = jnp.where(lane == head, top + jnp.log(summed), lse_buf[block])
            att_buf[block, :, cols] = jnp.where(lane < head_dim, outs[0], outs[1]).astype(
                jnp.bfloat16
            )

    scatter = LineScatter(me, count, parts, inbox, total_buf, s_sems, subs)
    arrived = 0
    for index in range(count - 1):
        block = scatter.order(index)
        attend(block)
        parts[block] = nn_dot(att_buf[block], wo[...]).astype(jnp.bfloat16)
        if index == 0:
            x_line.wait_sends()
        scatter.at_time(index)
        if index:
            c_line.arrive(arrived)
            arrived += 1
    attend(me)
    total_buf[...] = x_all[me].astype(jnp.float32) + nn_dot(att_buf[me], wo[...])
    early = [(n1_buf, n1_out), (q_buf, q_out), (k_buf, k_out), (v_buf, v_out), (att_buf, att_out), (lse_buf, lse_out)]
    late = [
        (total_buf, middle_out), (back_buf, back_out), (res_buf, res_out), (n2_all, n2_out), (grad_gate, gate_out),
        (grad_up, up_out),
    ]
    outs = [
        pltpu.make_async_copy(source, target, out_sems.at[index])
        for index, (source, target) in enumerate(early + late)
    ]
    for copy in outs[: len(early)]:
        copy.start()
    for time in range(count - 1, scatter.times):
        scatter.at_time(time)
        if arrived < c_line.pieces:
            c_line.arrive(arrived)
            arrived += 1
    middle = total_buf[...]
    n2_all[me] = (middle * rms_rows(middle) * gains_out[1:2, :]).astype(jnp.bfloat16)
    n_line.begin()
    outs[len(early)].start()
    for piece in range(arrived, c_line.pieces):
        c_line.arrive(piece)

    for load in loads[6:]:
        load.wait()

    @pl.loop(0, units // tile)
    def _(index):
        here = pl.ds(pl.multiple_of(index * tile, tile), tile)
        grad_hidden[:, here] = nt_dot(g_all[...].reshape(total, width), wf[here, :])

    scatter.wait_sends()

    def block_pass(block):
        normed = n2_all[block]
        here = pl.ds(pl.multiple_of(block * rows, rows), rows)
        gate = nn_dot(normed, wg[...])
        up = nn_dot(normed, wu[...])
        act, slope = gelu_parts(gate)
        hid[block] = (act * up).astype(jnp.bfloat16)
        grads = grad_hidden[here, :]
        grad_gate[here, :] = (grads * up * slope).astype(jnp.bfloat16)
        grad_up[here, :] = (grads * act).astype(jnp.bfloat16)
        res_buf[block] = nn_dot(hid[block], wf[...]).astype(jnp.bfloat16)
        half = width // 2
        for cols in (pl.ds(0, half), pl.ds(half, half)):
            back_buf[block, :, cols] = (
                nt_dot(grad_gate[here, :], wg[cols, :]) + nt_dot(grad_up[here, :], wu[cols, :])
            ).astype(jnp.bfloat16)

    for piece in range(subs):
        n_line.arrive(piece)
    block_pass(me)
    n_line.each_block(0, block_pass)
    for hops in range(1, count - 1):
        n_line.arrive_block(hops, block_pass)
    for copy in outs[len(early) + 1 :]:
        copy.start()

    def weight_grad(left, right, base, height):
        depth = right.shape[2]
        panels = depth // lanes
        factor = right[...].reshape(total, depth)

        def store(slot, panel, row):
            return pltpu.make_async_copy(
                stage.at[slot, panel],
                flat_out.at[pl.ds(base + panel * height + row, tile)],
                stage_sems.at[slot, panel],
            )

        @pl.loop(0, height // tile)
        def _(index):
            slot = lax.rem(index, 2)
            row = pl.multiple_of(index * tile, tile)
            turned[...] = left[:, :, pl.ds(row, tile)].reshape(total, tile).T
            product = nn_dot(turned[...], factor).astype(jnp.bfloat16)

            @pl.when(index >= 2)
            def _():
                for panel in range(panels):
                    store(slot, panel, row).wait()

            for panel in range(panels):
                stage[slot, panel] = product[:, panel * lanes : (panel + 1) * lanes]
                store(slot, panel, row).start()

        for slot in range(2):
            for panel in range(panels):
                store(slot, panel, 0).wait()

    weight_grad(hid, g_all, 0, units)
    for line in (g_line, c_line, n_line):
        line.wait_sends()
    for copy in outs:
        copy.wait()


def forward(count, length, x, cot, wq, wk, wv, wo, wf, wg, wu, packed, table):
    rows, width = x.shape
    columns, units = wq.shape[1], wg.shape[1]
    total = count * rows
    tile = 128 if units % 256 else 256
    bf, f32 = jnp.bfloat16, jnp.float32
    shape = jax.ShapeDtypeStruct
    steps = count - 1
    subs = 2
    dma = pltpu.SemaphoreType.DMA
    vmem = pltpu.VMEM
    blocks = (count, rows, width)
    narrow = (count, rows, columns)
    return pl.pallas_call(
        functools.partial(forward_kernel, count, tile, subs),
        name="forward",
        out_shape=(
            shape(blocks, bf), shape(narrow, bf), shape(narrow, bf), shape(narrow, bf), shape(narrow, bf),
            shape((count, rows, lanes), f32), shape((rows, width), f32),
            shape((units * width // lanes, lanes), bf), shape(blocks, bf), shape(blocks, bf), shape(blocks, bf),
            shape((total, units), bf), shape((total, units), bf),
            shape((8, width), f32), shape((columns // head_dim, 2 * total), f32), shape((8, 2 * total), f32),
        ),
        in_specs=[smem_space] + [any_space] * 9 + [vmem_space] * 2,
        out_specs=[any_space] * 13 + [vmem_space] * 3,
        scratch_shapes=[
            vmem(blocks, bf), vmem(blocks, bf), vmem((count, 8, width // count), f32),
            vmem(wq.shape, bf), vmem(wk.shape, bf), vmem(wv.shape, bf), vmem(wo.shape, bf),
            vmem(wf.shape, bf), vmem(wg.shape, bf), vmem(wu.shape, bf),
            vmem(blocks, bf), vmem((count + 1, rows, width), bf), vmem(blocks, bf),
            vmem(narrow, bf), vmem(narrow, bf), vmem(narrow, bf), vmem(narrow, bf), vmem((count, rows, lanes), f32),
            vmem((rows, width), f32), vmem((count, rows, units), bf), vmem((total, units), bf), vmem((total, units), bf),
            vmem((total, units), f32), vmem(blocks, bf), vmem((tile, total), bf),
            vmem((2, width // lanes, tile, lanes), bf),
            dma((9,)), dma((2, 2, steps * subs)), dma((2, 2, steps)), dma((2, 2, steps * subs)),
            dma((2, 2, steps * subs)), dma((2, 2, steps * subs)), dma((12,)), dma((2, width // lanes)),
        ],
        compiler_params=pltpu.CompilerParams(
            collective_id=0, has_side_effects=True, vmem_limit_bytes=61 * 2**20
        ),
    )(length, x, cot, wq, wk, wv, wo, wf, wg, wu, packed, table)


def when(condition, body):
    if isinstance(condition, bool):
        if condition:
            body()
    else:
        pl.when(condition)(body)


class ReplicaSum:
    def __init__(self, replicas, chunk, source, target, work, core_box, path_box, sems):
        self.mine = lax.axis_index("replica")
        self.chunk, self.source, self.target = chunk, source, target
        self.work, self.core_box, self.path_box, self.sems = work, core_box, path_box, sems
        self.depth, self.slots = work.shape[0], core_box.shape[0]
        bits = [1 << index for index in range(1, replicas.bit_length() - 1)]
        self.orders = (bits, bits[::-1])
        self.levels = len(bits)
        self.last_phase = 2 * self.levels + 2
        self.half = chunk // 2

    def bit(self, mask):
        return jnp.where((self.mine & mask) != 0, 1, 0)

    def region(self, path, level):
        size = self.half // 2
        offset = path * size
        for mask in self.orders[path][:level]:
            size //= 2
            offset = offset + self.bit(mask) * size
        return offset, size

    def out_rows(self, chunk, offset, size):
        start = chunk * self.chunk + self.bit(1) * self.half + offset
        return self.target.at[pl.ds(pl.multiple_of(start, 16), size)]

    def sem(self, kind, phase, path, chunk):
        return self.sems.at[kind, phase, path, chunk % self.slots]

    def remote(self, source, target, phase, path, chunk, mask):
        return pltpu.make_async_remote_copy(
            src_ref=source,
            dst_ref=target,
            send_sem=self.sem(0, phase, path, chunk),
            recv_sem=self.sem(1, phase, path, chunk),
            device_id={"replica": self.mine ^ mask},
            device_id_type=MESH,
        )

    def core_copy(self, chunk):
        start = chunk * self.chunk + (1 - self.bit(1)) * self.half
        return self.remote(
            self.source(start, self.half), self.core_box.at[chunk % self.slots], 0, 0, chunk, 1
        )

    def load_copy(self, chunk):
        start = chunk * self.chunk + self.bit(1) * self.half
        return pltpu.make_async_copy(
            self.source(start, self.half), self.work.at[chunk % self.depth], self.sem(0, 0, 1, chunk)
        )

    def reduce_copy(self, chunk, path, level):
        mask = self.orders[path][level - 1]
        offset, size = self.region(path, level - 1)
        size //= 2
        start = pl.multiple_of(offset + (1 - self.bit(mask)) * size, 16)
        return self.remote(
            self.work.at[chunk % self.depth, pl.ds(start, size)],
            self.box(chunk, path, level),
            level, path, chunk, mask,
        )

    def box(self, chunk, path, level):
        size = self.half // 2 >> level
        start = sum(self.half // 2 >> step for step in range(1, level))
        return self.path_box.at[chunk % self.slots, path, pl.ds(start, size)]

    def add_box(self, chunk, path, level):
        offset, size = self.region(path, level)
        here = pl.ds(pl.multiple_of(offset, 16), size)
        slot = chunk % self.depth
        self.work[slot, here, :] = self.work[slot, here, :] + self.box(chunk, path, level)[...]

    def own_copy(self, chunk, path):
        offset, size = self.region(path, self.levels)
        return pltpu.make_async_copy(
            self.work.at[chunk % self.depth, pl.ds(pl.multiple_of(offset, 16), size)],
            self.out_rows(chunk, offset, size),
            self.sems.at[1, 0, 1 + path, chunk % self.slots],
        )

    def spread_copy(self, chunk, path, level):
        offset, size = self.region(path, level)
        if level == self.levels:
            source = self.work.at[chunk % self.depth, pl.ds(pl.multiple_of(offset, 16), size)]
        else:
            source = self.out_rows(chunk, offset, size)
        return self.remote(
            source, self.out_rows(chunk, offset, size),
            2 * self.levels + 1 - level, path, chunk, self.orders[path][level - 1],
        )

    def share_copy(self, chunk):
        rows = self.out_rows(chunk, 0, self.half)
        return self.remote(rows, rows, self.last_phase - 1, 0, chunk, 1)

    def advance(self, phase, chunk):
        levels = self.levels
        if phase == 0:
            self.core_copy(chunk).start()
            self.load_copy(chunk).start()
        elif phase <= levels + 1:
            if phase == 1:
                self.load_copy(chunk).wait()
                self.core_copy(chunk).wait()
                slot = chunk % self.depth
                self.work[slot] = self.work[slot] + self.core_box[chunk % self.slots]
            for path in range(2):
                if phase > 1:
                    self.reduce_copy(chunk, path, phase - 1).wait()
                    self.add_box(chunk, path, phase - 1)
                if phase <= levels:
                    self.reduce_copy(chunk, path, phase).start()
                else:
                    self.own_copy(chunk, path).start()
                    self.spread_copy(chunk, path, levels).start()
        else:
            level = 2 * levels + 1 - phase
            if level >= 0:
                for path in range(2):
                    self.spread_copy(chunk, path, level + 1).wait()
                    if level + 1 == levels:
                        self.own_copy(chunk, path).wait()
                    if level >= 1:
                        self.spread_copy(chunk, path, level).start()
                if level == 0:
                    self.share_copy(chunk).start()


scatter_pace, gather_pace, pair_pace = 1.0, 0.7, 1.0


def rms_backward(values, grads, gain):
    scale = rms_rows(values)
    unit = values * scale
    scaled = grads * gain
    inner = jnp.mean(scaled * unit, axis=-1, keepdims=True)
    return scale * (scaled - unit * inner), jnp.sum(grads * unit, axis=0, keepdims=True)


def backward_kernel(
    count, replicas, chunk, ffn_chunks, out_chunks, attn_chunks, skew, subs,
    length_ref,
    flat_hbm, n2_hbm, gate_hbm, up_hbm, back_hbm, res_hbm, middle_hbm, cot_hbm, x_hbm,
    q_hbm, k_hbm, v_hbm, att_hbm, lse_hbm, n1_hbm,
    wq_hbm, wk_hbm, wv_hbm, wo_hbm, gains_ref, bias_ref, ids_ref,
    sums_out, flat_out, result_out, input_out, small_out,
    back, res, middle, cot, x_own, q_buf, k_buf, v_buf, att_buf, lse_buf, n1_buf, wq, wk, wv, wo,
    back_box, res_box, total_buf, res_total, middle_grad, branch, grad_att, key_acc, value_acc, grad_qkv, grad_up,
    reverse, offsets, turned, stage, out_buf, small, small_parts, small_box, pair_box,
    work, core_box, path_box,
    load_sems, b_sems, r_sems, f_sems, a_sems, p_sems, pair_sems, stage_sems, out_sems, sum_sems,
):
    me = lax.axis_index("group")
    mine = lax.axis_index("replica")
    rows, width = middle.shape
    total = rows * count
    columns = wq.shape[1]
    local_heads = columns // head_dim
    units = grad_up.shape[1]
    sources = [
        back_hbm, n2_hbm, gate_hbm, up_hbm, middle_hbm, cot_hbm, x_hbm, wo_hbm, att_hbm, q_hbm, k_hbm, v_hbm,
        lse_hbm, wq_hbm, wk_hbm, wv_hbm, res_hbm, n1_hbm,
    ]
    targets = [
        back, n1_buf, grad_qkv.at[:, pl.ds(0, units)], grad_up, middle, cot, x_own, wo, att_buf, q_buf, k_buf, v_buf,
        lse_buf, wq, wk, wv, res, n1_buf,
    ]
    loads = [
        pltpu.make_async_copy(source, target, load_sems.at[index])
        for index, (source, target) in enumerate(zip(sources, targets))
    ]
    masks = [1 << index for index in range(replicas.bit_length() - 1)]
    barrier = pltpu.get_barrier_semaphore()

    @pl.when(me > 0)
    def _():
        pl.semaphore_signal(barrier, inc=1, device_id={"group": me - 1}, device_id_type=MESH)

    @pl.when(me < count - 1)
    def _():
        pl.semaphore_signal(barrier, inc=1, device_id={"group": me + 1}, device_id_type=MESH)

    for mask in masks:
        pl.semaphore_signal(barrier, inc=1, device_id={"replica": mine ^ mask}, device_id_type=MESH)
    peers = jnp.where(me > 0, 1, 0) + jnp.where(me < count - 1, 1, 0) + len(masks)
    pl.semaphore_wait(barrier, peers)

    first_rows = flat_hbm.shape[0]
    from_first_chunks = first_rows // chunk
    from_ffn = ffn_chunks
    chunks = from_ffn + attn_chunks

    def make_source(source_ref, base):
        return lambda start, size: source_ref.at[pl.ds(pl.multiple_of(start - base, 16), size)]

    parts = ReplicaSum(replicas, chunk, None, sums_out, work, core_box, path_box, sum_sems)
    from_first, from_second = make_source(flat_hbm, 0), make_source(flat_out, first_rows)
    clock = {"time": 0, "gaps": [0] + [None] * 4, "credit": 0.0}
    each = from_first_chunks
    bounds = [0, each, 2 * each, 3 * each, from_ffn + out_chunks, chunks]

    def start_piece(source, piece):
        parts.source = source
        parts.core_copy(piece).start()
        parts.load_copy(piece).start()

    def tick(time):
        for phase in range(parts.last_phase, -1, -1):
            entry = time - skew * phase
            inside, piece = False, entry
            for gap, low, high in zip(clock["gaps"], bounds, bounds[1:]):
                if gap is None:
                    continue
                if isinstance(entry, int):
                    if low + gap <= entry < high + gap:
                        inside, piece = True, entry - gap
                else:
                    here = (entry >= low + gap) & (entry < high + gap)
                    inside = inside | here
                    piece = jnp.where(here, entry - gap, piece)

            def body(phase=phase, piece=piece):
                if phase == parts.last_phase:
                    parts.share_copy(piece).wait()
                elif phase:
                    parts.source = lambda start, size: flat_hbm.at[pl.ds(0, size)]
                    parts.advance(phase, piece)

            if phase:
                when(inside, body)
            else:
                first, second = piece < from_first_chunks, piece >= from_first_chunks
                if isinstance(entry, int):
                    first, second = first and inside, second and inside
                else:
                    first, second = first & inside, second & inside
                when(first, functools.partial(start_piece, from_first, piece))
                when(second, functools.partial(start_piece, from_second, piece))

    def pace(amount):
        clock["credit"] += amount
        while clock["credit"] >= 1:
            tick(clock["time"])
            clock["time"] += 1
            clock["credit"] -= 1

    back_line = LineScatter(me, count, back, back_box, total_buf, b_sems, subs)
    res_line = LineScatter(me, count, res, res_box, res_total, r_sems, subs)
    first_line = LineScatter(me, count, back, back_box, total_buf, f_sems, subs)
    branch_line = LineGather(me, count, branch, a_sems, subs)
    small_line = LineScatter(me, count, small_parts, small_box, small.at[pl.ds(0, 8)], p_sems)

    tile = 256

    def weight_grad(left, factor, base, height, per_output, splits=1):
        panels = factor.shape[1] // lanes
        tiles = height // tile

        def store(slot, panel, row):
            return pltpu.make_async_copy(
                stage.at[slot, panel],
                flat_out.at[pl.ds(base + panel * height + row, tile)],
                stage_sems.at[slot, panel],
            )

        def run(first, last):
            @pl.loop(first, last)
            def _(index):
                slot = lax.rem(index, 2)
                row = pl.multiple_of(index * tile, tile)
                turned[...] = left[:, :, pl.ds(row, tile)].reshape(total, tile).T
                product = nn_dot(turned[...], factor).astype(jnp.bfloat16)

                @pl.when(index >= 2)
                def _():
                    for panel in range(panels):
                        store(slot, panel, row).wait()

                for panel in range(panels):
                    stage[slot, panel] = product[:, panel * lanes : (panel + 1) * lanes]
                    store(slot, panel, row).start()

        for split in range(splits):
            if split:
                pace(1)
            run(tiles * split // splits, tiles * (split + 1) // splits)
        for slot in range(min(2, tiles)):
            for panel in range(panels):
                store(slot, panel, 0).wait()

    def enter(group):
        before = clock["gaps"][group - 1]
        clock["gaps"][group] = max(clock["time"] - bounds[group], before)

    for now in range(skew):
        tick(now)
    for load in loads[:17]:
        load.start()
    loads[0].wait()
    total_buf[...] = back[me].astype(jnp.float32)
    back_line.at_time(0)
    clock["time"] = skew
    pace(skew)
    for load in loads[1:3]:
        load.wait()
    gate_base, attn_base = 0, 2 * units * width // lanes
    weight_grad(n1_buf, grad_qkv[:, 0:units], gate_base, width, units, 2)
    enter(1)
    pace(1)
    back_line.at_time(1)
    pace(1)
    back_line.at_time(2)
    pace(1)
    loads[3].wait()
    weight_grad(n1_buf, grad_up[...], gate_base + units * width // lanes, width, units, 2)
    enter(2)
    loads[17].start()
    anti = lax.broadcasted_iota(jnp.int32, (rows, rows), 0) + lax.broadcasted_iota(
        jnp.int32, (rows, rows), 1
    )
    reverse[...] = (anti == rows - 1).astype(jnp.float32).astype(jnp.bfloat16)
    part_width = width // count
    size, steps = rows // subs, count - 1
    small_parts[...] = jnp.zeros_like(small_parts)
    for load in loads[4:7]:
        load.wait()

    def second_norm_back(sub):
        here = pl.ds(sub * size, size)
        position = me * rows + sub * size + lax.broadcasted_iota(jnp.int32, (size, 1), 0)
        valid = (position < length_ref[0]).astype(jnp.float32)
        grad_mid, gain_grad = rms_backward(middle[here, :], total_buf[here, :], gains_ref[1:2, :])
        grad_mid = cot[here, :].astype(jnp.float32) * valid + grad_mid
        middle_grad[here, :] = grad_mid
        branch[me, here, :] = grad_mid.astype(jnp.bfloat16)
        branch_line.send(sub)
        for owner in range(count):
            small_parts[owner, 1:2, :] += gain_grad[:, owner * part_width : (owner + 1) * part_width]

    came = 0
    for now in range(3, back_line.times):
        back_line.at_time(now)
        if now % steps == 0:
            second_norm_back(now // steps - 1)
        if now > steps and came < steps - 1:
            branch_line.arrive(came * subs)
            came += 1
        pace(scatter_pace)
    for load in loads[7:18]:
        load.wait()
    res_total[...] = middle[...] + res[me].astype(jnp.float32)

    def attended_grad(block):
        grad_att[block] = nt_dot(branch[block], wo[...]).astype(jnp.bfloat16)

    attended_grad(me)
    for sub in range(subs):
        for hops in range(came if sub == 0 else 0, steps):
            branch_line.arrive(hops * subs + sub)
            pace(gather_pace)
            if sub == subs - 1:
                branch_line.each_block(hops, attended_grad)

    weight_grad(att_buf, branch[...].reshape(total, width), attn_base, columns, width)
    enter(3)
    pace(1)
    mask_first, mask_second = head_masks()
    key_valid = lax.broadcasted_iota(jnp.int32, (1, total), 1) < length_ref[0]
    lane = lax.broadcasted_iota(jnp.int32, (1, lanes), 1)
    offsets[...] = jnp.zeros_like(offsets)

    def head_pair(pair):
        cols = pl.ds(pl.multiple_of(pair * lanes, lanes), lanes)
        key = k_buf[:, :, cols].reshape(total, lanes)
        value = v_buf[:, :, cols].reshape(total, lanes)
        key_acc[...] = jnp.zeros_like(key_acc)
        value_acc[...] = jnp.zeros_like(value_acc)

        @pl.loop(0, count)
        def _(block):
            query = q_buf[block, :, cols]
            grads = grad_att[block, :, cols]
            logs = lse_buf[block]
            query_parts = []
            for half, mask in enumerate((mask_first, mask_second)):
                head = pair * 2 + half
                query_half, grads_half = query * mask, grads * mask
                scores = nt_dot(query_half, key)
                scores = scores + offset_bias(bias_ref, head, block * rows, rows, total)
                scores = jnp.where(key_valid, scores, negative)
                log_total = jnp.sum(jnp.where(lane == head, logs, 0.0), axis=-1, keepdims=True)
                probs = jnp.exp(scores - log_total)
                grad_probs = nt_dot(grads_half, value)
                inner = jnp.sum(probs * grad_probs, axis=-1, keepdims=True)
                grad_scores = (probs * (grad_probs - inner)).astype(jnp.bfloat16)
                query_parts.append(nn_dot(grad_scores, key))
                key_acc[...] += nn_dot(query_half.astype(jnp.float32).T.astype(jnp.bfloat16), grad_scores)
                value_acc[...] += nn_dot(
                    grads_half.astype(jnp.float32).T.astype(jnp.bfloat16), probs.astype(jnp.bfloat16)
                )
                turned_scores = nn_dot(reverse[...], grad_scores)
                padded = jnp.concatenate([turned_scores, jnp.zeros_like(turned_scores)], axis=1)
                sheared = pltpu.roll(padded, 0, 1, stride=1, stride_axis=0)
                sums = jnp.broadcast_to(jnp.sum(sheared, axis=0, keepdims=True), (8, 2 * total))
                sums = pltpu.roll(sums, total - rows - block * rows, 1)
                offsets[pl.ds(head, 1), :] += sums[0:1, :]
            grad_qkv[pl.ds(pl.multiple_of(block * rows, rows), rows), cols] = jnp.where(
                lane < head_dim, query_parts[0], query_parts[1]
            ).astype(jnp.bfloat16)

        grad_qkv[:, pl.ds(pl.multiple_of(columns + pair * lanes, lanes), lanes)] = key_acc[
            ...
        ].T.astype(jnp.bfloat16)
        grad_qkv[:, pl.ds(pl.multiple_of(2 * columns + pair * lanes, lanes), lanes)] = value_acc[
            ...
        ].T.astype(jnp.bfloat16)

    res_time = 0
    for pair in range(local_heads // 2):
        if res_time < 3:
            res_line.at_time(res_time)
            res_time += 1
        head_pair(pair)
        pace(pair_pace)

    back_line.wait_sends()

    quarter = width // 4
    for start in range(0, width, quarter):
        cols = pl.ds(start, quarter)
        back[:, :, cols] = (
            (
                nt_dot(grad_qkv[:, 0:columns], wq[cols, :])
                + nt_dot(grad_qkv[:, columns : 2 * columns], wk[cols, :])
                + nt_dot(grad_qkv[:, 2 * columns : 3 * columns], wv[cols, :])
            )
            .astype(jnp.bfloat16)
            .reshape(count, rows, quarter)
        )
        if start == quarter:
            pace(1)
    for now in range(count - 1):
        first_line.at_time(now)
    pace(1)
    total_buf[...] = back[me].astype(jnp.float32)
    weight_grad(n1_buf, grad_qkv[...], attn_base + columns * width // lanes, width, columns, 2)
    enter(4)
    pace(skew)
    for now in range(count - 1, first_line.times):
        first_line.at_time(now)
        pace(1)
    grad_in, gain_grad = rms_backward(
        x_own[...].astype(jnp.float32), total_buf[...], gains_ref[0:1, :]
    )
    out_buf[1] = (middle_grad[...] + grad_in).astype(jnp.bfloat16)
    input_copy = pltpu.make_async_copy(out_buf.at[1], input_out, out_sems.at[1])
    input_copy.start()
    for owner in range(count):
        small_parts[owner, 0:1, :] = gain_grad[:, owner * part_width : (owner + 1) * part_width]
    small[0:8, :] = small_parts[me]
    for now in range(max(small_line.times, res_line.times - res_time)):
        if now < small_line.times:
            small_line.at_time(now)
        if res_time < res_line.times:
            res_line.at_time(res_time)
            res_time += 1
        pace(1)
    out_buf[0] = res_total[...].astype(jnp.bfloat16)
    result_copy = pltpu.make_async_copy(out_buf.at[0], result_out, out_sems.at[0])
    result_copy.start()
    bucket = lax.broadcasted_iota(jnp.int32, (lanes, ids_ref.shape[1]), 0).astype(jnp.float32)
    one_hot = (bucket == ids_ref[0:1, :]).astype(jnp.float32).astype(jnp.bfloat16)
    high = offsets[...].astype(jnp.bfloat16)
    rest = offsets[...] - high.astype(jnp.float32)
    middle_part = rest.astype(jnp.bfloat16)
    low_part = (rest - middle_part.astype(jnp.float32)).astype(jnp.bfloat16)
    small[8:16, 0:lanes] = nt_dot(high, one_hot) + nt_dot(middle_part, one_hot) + nt_dot(low_part, one_hot)
    small[8:16, lanes:] = jnp.zeros((8, part_width - lanes), jnp.float32)
    for index, mask in enumerate(masks):
        copy = pltpu.make_async_remote_copy(
            src_ref=small,
            dst_ref=pair_box.at[index],
            send_sem=pair_sems.at[0, index],
            recv_sem=pair_sems.at[1, index],
            device_id={"replica": mine ^ mask},
            device_id_type=MESH,
        )
        copy.start()
        pace(1)
        copy.wait()
        small[...] += pair_box[index]
    small_out[...] = small[...]

    @pl.loop(clock["time"], chunks + clock["gaps"][4] + skew * parts.last_phase)
    def _(now):
        tick(now)

    for line in (res_line, first_line, branch_line, small_line):
        line.wait_sends()
    result_copy.wait()
    input_copy.wait()


def backward(count, replicas, length, flat, n2, grad_gate, grad_up, back, res, middle, cot, x, q, k, v, att, lse, n1, wq, wk, wv, wo, gains, bias, ids):
    rows, width = middle.shape
    total = count * rows
    columns = wq.shape[1]
    bf, f32 = jnp.bfloat16, jnp.float32
    shape = jax.ShapeDtypeStruct
    steps = count - 1
    dma = pltpu.SemaphoreType.DMA
    units = grad_up.shape[1]
    chunk = flat.shape[0] // 5
    ffn_rows = 3 * flat.shape[0]
    attn_rows = 4 * columns * width // lanes
    skew, subs = 3, 2
    levels = replicas.bit_length() - 2
    masks = levels + 1
    depth = skew * (levels + 2)
    part_width = width // count
    vmem = pltpu.VMEM
    blocks = lambda kind: vmem((count, rows, width), kind)
    narrow = lambda: vmem((count, rows, columns), bf)
    boxes = lambda: vmem((count + 1, rows, width), bf)
    return pl.pallas_call(
        functools.partial(
            backward_kernel, count, replicas, chunk, ffn_rows // chunk, wo.size // lanes // chunk,
            attn_rows // chunk, skew, subs
        ),
        name="backward",
        out_shape=(
            shape((ffn_rows + attn_rows, lanes), bf),
            shape((2 * flat.shape[0] + attn_rows, lanes), bf),
            shape((rows, width), bf),
            shape((rows, width), bf),
            shape((16, part_width), f32),
        ),
        in_specs=[smem_space] + [any_space] * 19 + [vmem_space] * 3,
        out_specs=[any_space] * 4 + [vmem_space],
        scratch_shapes=[
            blocks(bf), blocks(bf), vmem((rows, width), f32), vmem((rows, width), bf), vmem((rows, width), bf),
            narrow(), narrow(), narrow(), narrow(), vmem((count, rows, lanes), f32), blocks(bf),
            vmem(wq.shape, bf), vmem(wk.shape, bf), vmem(wv.shape, bf), vmem(wo.shape, bf),
            boxes(), boxes(), vmem((rows, width), f32), vmem((rows, width), f32), vmem((rows, width), f32), blocks(bf),
            narrow(),
            vmem((lanes, total), f32), vmem((lanes, total), f32), vmem((total, 3 * columns), bf), vmem((total, units), bf),
            vmem((rows, rows), bf), vmem((8, 2 * total), f32), vmem((256, total), bf),
            vmem((2, width // lanes, 256, lanes), bf), vmem((2, rows, width), bf),
            vmem((16, part_width), f32), vmem((count, 8, part_width), f32), vmem((count + 1, 8, part_width), f32),
            vmem((masks, 16, part_width), f32),
            vmem((depth, chunk // 2, lanes), bf), vmem((2 * skew, chunk // 2, lanes), bf),
            vmem((2 * skew, 2, chunk // 4, lanes), bf),
            dma((18,)), dma((2, 2, steps * subs)), dma((2, 2, steps * subs)), dma((2, 2, steps * subs)),
            dma((2, 2, steps * subs)),
            dma((2, 2, steps)), dma((2, masks)), dma((2, width // lanes)), dma((2,)),
            dma((2, 2 * levels + 3, 3, 2 * skew)),
        ],
        compiler_params=pltpu.CompilerParams(
            collective_id=1, has_side_effects=True, vmem_limit_bytes=61 * 2**20
        ),
    )(length, flat, n2, grad_gate, grad_up, back, res, middle, cot, x, q, k, v, att, lse, n1, wq, wk, wv, wo, gains, bias, ids)


def widen_kernel(plan, slots, sums, result, input_grad, small, *refs):
    targets, (inbox, outbox, passed, in_sems, out_sems, pass_sems) = refs[:-6], refs[-6:]
    held = [
        pltpu.make_async_copy(source, passed.at[index], pass_sems.at[0, index])
        for index, source in enumerate((result, input_grad))
    ]
    given = [
        pltpu.make_async_copy(passed.at[index], target, pass_sems.at[1, index])
        for index, target in enumerate(targets[:2])
    ]
    for copy in held:
        copy.start()
    gain1, gain2, table = targets[2:5]
    for index, gain in enumerate((gain1, gain2)):
        for row in range(gain.shape[0]):
            gain[row : row + 1, :] = small[index : index + 1, row * lanes : (row + 1) * lanes]
    table[...] = small[8 : 8 + table.shape[0], 0 : table.shape[1]]
    targets = targets[5:]
    tiles = [
        (target, start, height, depth // lanes, size, row)
        for target, (start, height, depth, size) in zip(targets, plan)
        for row in range(0, height, size)
    ]

    def load(number):
        _, start, height, panels, size, row = tiles[number]
        slot = number % slots

        @pl.loop(0, panels)
        def _(panel):
            pltpu.make_async_copy(
                sums.at[pl.ds(start + row + panel * height, size)],
                inbox.at[slot, pl.ds(pl.multiple_of(panel * size, size), size)],
                in_sems.at[slot],
            ).start()

    def store(number):
        target, _, _, panels, size, row = tiles[number]
        return pltpu.make_async_copy(
            outbox.at[number % slots, pl.ds(0, size), pl.ds(0, panels * lanes)],
            target.at[pl.ds(row, size)],
            out_sems.at[number % slots],
        )

    for number in range(min(slots - 1, len(tiles))):
        load(number)
    for number in range(len(tiles)):
        _, _, _, panels, size, _ = tiles[number]
        slot = number % slots
        if number + slots - 1 < len(tiles):
            load(number + slots - 1)
        whole = inbox.at[slot, pl.ds(0, panels * size)]
        pltpu.make_async_copy(whole, whole, in_sems.at[slot]).wait()
        if number >= slots:
            store(number - slots).wait()

        @pl.loop(0, panels)
        def _(panel):
            outbox[slot, pl.ds(0, size), pl.ds(pl.multiple_of(panel * lanes, lanes), lanes)] = inbox[
                slot, pl.ds(pl.multiple_of(panel * size, size), size)
            ].astype(jnp.float32)

        store(number).start()
        if number == slots:
            for first, second in zip(held, given):
                first.wait()
                second.start()
    for number in range(max(len(tiles) - slots, 0), len(tiles)):
        store(number).wait()
    for copy in given:
        copy.wait()


def widen(sums, result, input_grad, small, table_shape, shapes):
    slots = 4
    plan, start = [], 0
    for height, depth in shapes:
        size = 512 if depth <= 1024 else 256
        while height % size:
            size //= 2
        plan.append((start, height, depth, size))
        start += height * depth // lanes
    most_in = max(size * depth // lanes for _, _, depth, size in plan)
    most_rows = max(size for _, _, _, size in plan)
    return pl.pallas_call(
        functools.partial(widen_kernel, plan, slots),
        name="widen",
        out_shape=[jax.ShapeDtypeStruct(result.shape, result.dtype)] * 2
        + [jax.ShapeDtypeStruct((small.shape[1] // lanes, lanes), jnp.float32)] * 2
        + [jax.ShapeDtypeStruct(table_shape, jnp.float32)]
        + [jax.ShapeDtypeStruct(shape, jnp.float32) for shape in shapes],
        in_specs=[any_space] * 3 + [vmem_space],
        out_specs=[any_space] * 2 + [vmem_space] * 3 + [any_space] * len(shapes),
        scratch_shapes=[
            pltpu.VMEM((slots, most_in, lanes), jnp.bfloat16),
            pltpu.VMEM((slots, most_rows, max(depth for _, depth in shapes)), jnp.float32),
            pltpu.VMEM((2,) + result.shape, result.dtype),
            pltpu.SemaphoreType.DMA((slots,)),
            pltpu.SemaphoreType.DMA((slots,)),
            pltpu.SemaphoreType.DMA((2, 2)),
        ],
        compiler_params=pltpu.CompilerParams(vmem_limit_bytes=61 * 2**20),
    )(sums, result, input_grad, small)


def local(
    inputs,
    seq_lengths,
    bucket_ids,
    norm1_gain,
    w_query,
    w_key,
    w_value,
    w_attn_out,
    bias_table,
    norm2_gain,
    w_gate,
    w_up,
    w_ffn_out,
    cotangent,
):
    count = lax.axis_size("group")
    replicas = lax.axis_size("replica")
    longest = max(2 * count * inputs.shape[1], norm1_gain.shape[0])
    longest = -(-longest // 1024) * 1024
    packed = jnp.concatenate(
        [
            jnp.pad(vector.astype(jnp.float32), (0, longest - vector.shape[0]), constant_values=-1)
            for vector in (norm1_gain, norm2_gain, bucket_ids)
        ]
    ).reshape(-1, lanes)
    (
        normed_one, query, key, value, attended, log_totals, middle, flat, back_part, result_part, normed_all,
        grad_gate, grad_up, gains, bias, ids,
    ) = forward(
        count, seq_lengths, inputs[0], cotangent[0], w_query, w_key, w_value, w_attn_out, w_ffn_out, w_gate, w_up,
        packed, bias_table.T,
    )
    sums, _, result, input_grad, small = backward(
        count, replicas, seq_lengths, flat, normed_all, grad_gate, grad_up, back_part, result_part, middle,
        cotangent[0], inputs[0], query, key, value, attended, log_totals, normed_one,
        w_query, w_key, w_value, w_attn_out, gains, bias, ids,
    )
    weights = (w_ffn_out, w_gate, w_up, w_attn_out, w_query, w_key, w_value)
    (
        result, input_grad, gain1_grad, gain2_grad, table_grad,
        ffn_out_grad, gate_grad, up_grad, attn_out_grad, query_grad, key_grad, value_grad,
    ) = widen(
        sums, result, input_grad, small, bias_table.shape[::-1], [weight.shape for weight in weights]
    )
    return (
        result[None],
        input_grad[None],
        gain1_grad.reshape(-1),
        query_grad,
        key_grad,
        value_grad,
        attn_out_grad,
        table_grad.T,
        gain2_grad.reshape(-1),
        gate_grad,
        up_grad,
        ffn_out_grad,
    )


def solution(mesh):
    placed = (
        P("replica", "group", None),
        P("replica"),
        P(),
        P("group"),
        P(None, "group"),
        P(None, "group"),
        P(None, "group"),
        P("group", None),
        P(None, "group"),
        P("group"),
        P(None, "group"),
        P(None, "group"),
        P("group", None),
        P("replica", "group", None),
    )
    return jax.shard_map(
        local,
        mesh=mesh,
        in_specs=placed,
        out_specs=(
            P("replica", "group", None),
            P("replica", "group", None),
            P("group"),
            P(None, "group"),
            P(None, "group"),
            P(None, "group"),
            P("group", None),
            P(None, "group"),
            P("group"),
            P(None, "group"),
            P(None, "group"),
            P("group", None),
        ),
        check_vma=False,
    )
```

```python
import functools
import jax
import jax.numpy as jnp
from jax import lax
from jax.experimental import pallas as pl
from jax.experimental.pallas import tpu as pltpu
from jax.sharding import PartitionSpec as P

epsilon = 1e-06
negative = -1000000000.0
head_dim = 64
lanes = 128
MESH = pl.DeviceIdType.MESH
any_space = pl.BlockSpec(memory_space=pl.ANY)
vmem_space = pl.BlockSpec(memory_space=pltpu.VMEM)
smem_space = pl.BlockSpec(memory_space=pltpu.SMEM)


def nn_dot(left, right):
    return jnp.dot(left, right, preferred_element_type=jnp.float32)


def nt_dot(left, right):
    return lax.dot_general(
        left, right, (((1,), (1,)), ((), ())), preferred_element_type=jnp.float32
    )


def line_barrier(me, count):
    barrier = pltpu.get_barrier_semaphore()

    @pl.when(me > 0)
    def _():
        pl.semaphore_signal(barrier, inc=1, device_id={"group": me - 1}, device_id_type=MESH)

    @pl.when(me < count - 1)
    def _():
        pl.semaphore_signal(barrier, inc=1, device_id={"group": me + 1}, device_id_type=MESH)

    peers = jnp.where(me > 0, 1, 0) + jnp.where(me < count - 1, 1, 0)
    pl.semaphore_wait(barrier, peers)


class LineGather:
    def __init__(self, me, count, buffer, sems, subs=1, own=None):
        self.me, self.count, self.buffer, self.sems, self.subs = me, count, buffer, sems, subs
        self.own = own
        self.pieces = (count - 1) * subs
        self.size = buffer.shape[1] // subs

    def copy(self, side, piece, hops):
        block = self.me - hops if side == 0 else self.me + hops
        part = pl.ds(piece % self.subs * self.size, self.size)
        here = self.buffer.at[block, part]
        return pltpu.make_async_remote_copy(
            src_ref=here if hops or self.own is None else self.own.at[part],
            dst_ref=here,
            send_sem=self.sems.at[side, 0, piece],
            recv_sem=self.sems.at[side, 1, piece],
            device_id={"group": self.me + (1 if side == 0 else -1)},
            device_id_type=MESH,
        )

    def sends(self, side, piece):
        hops = piece // self.subs
        if side == 0:
            return (self.me - hops >= 0) & (self.me + 1 < self.count)
        return (self.me + hops < self.count) & (self.me >= 1)

    def arrives(self, side, piece):
        hops = piece // self.subs
        if side == 0:
            return self.me - 1 - hops >= 0
        return self.me + 1 + hops < self.count

    def send_side(self, side, piece):
        @pl.when(self.sends(side, piece))
        def _():
            self.copy(side, piece, piece // self.subs).start()

    def send(self, piece):
        for side in range(2):
            self.send_side(side, piece)

    def begin(self):
        for piece in range(self.subs):
            self.send(piece)

    def arrive(self, piece):
        for side in range(2):
            @pl.when(self.arrives(side, piece))
            def _():
                self.copy(side, piece, piece // self.subs + 1).wait_recv()

        if piece + self.subs < self.pieces:
            self.send(piece + self.subs)

    def arrive_block(self, hops, body):
        for piece in range(hops * self.subs, (hops + 1) * self.subs):
            self.arrive(piece)
        self.each_block(hops, body)

    def each_block(self, hops, body):
        @pl.loop(0, 2)
        def _(side):
            block = jnp.where(side == 0, self.me - 1 - hops, self.me + 1 + hops)

            @pl.when((block >= 0) & (block < self.count))
            def _():
                body(block)

    def wait_sends(self):
        for piece in range(self.pieces):
            for side in range(2):
                @pl.when(self.sends(side, piece))
                def _():
                    self.copy(side, piece, piece // self.subs).wait_send()


class LineScatter:
    def __init__(self, me, count, parts, inbox, total, sems, subs=1):
        self.me, self.count, self.parts, self.inbox = me, count, parts, inbox
        self.total, self.sems, self.subs = total, sems, subs
        self.times = (count - 1) * subs + 1
        self.size = parts.shape[1] // subs

    def order(self, index):
        picked = 0
        for device in range(self.count):
            due = [(step * self.subs + self.count - 1 - device, step) for step in range(device)]
            due += [
                (step * self.subs + device, self.count - 1 - step)
                for step in range(self.count - 1 - device)
            ]
            blocks = [block for _, block in sorted(due)] + [device]
            picked = picked + jnp.where(self.me == device, blocks[index], 0)
        return picked

    def copy(self, side, piece):
        step = piece // self.subs
        here = pl.ds(pl.multiple_of(piece % self.subs * self.size, self.size), self.size)
        owner = step if side == 0 else self.count - 1 - step
        return pltpu.make_async_remote_copy(
            src_ref=self.parts.at[owner, here],
            dst_ref=self.inbox.at[self.slot(side, step), here],
            send_sem=self.sems.at[side, 0, piece],
            recv_sem=self.sems.at[side, 1, piece],
            device_id={"group": self.me + (-1 if side == 0 else 1)},
            device_id_type=MESH,
        )

    def slot(self, side, step):
        return step if side == 0 else self.count - step

    def at_time(self, time):
        for side in range(2):
            before = self.count - 1 - self.me if side == 0 else self.me
            after = self.count - 1 - before
            piece = time - before
            step = piece // self.subs

            @pl.when((piece >= 0) & (step < after))
            def _():
                owner = step if side == 0 else self.count - 1 - step
                here = pl.ds(pl.multiple_of(piece % self.subs * self.size, self.size), self.size)

                @pl.when(before > 0)
                def _():
                    self.copy(side, piece).wait_recv()
                    self.parts[owner, here, :] = (
                        self.parts[owner, here, :].astype(jnp.float32)
                        + self.inbox[self.slot(side, step), here, :].astype(jnp.float32)
                    ).astype(self.parts.dtype)

                self.copy(side, piece).start()

            @pl.when((piece >= 0) & (step == after) & (before > 0))
            def _():
                here = pl.ds(pl.multiple_of(piece % self.subs * self.size, self.size), self.size)
                self.copy(side, piece).wait_recv()
                self.total[here, :] += self.inbox[self.slot(side, step), here, :].astype(jnp.float32)

    def wait_sends(self):
        for piece in range((self.count - 1) * self.subs):
            step = piece // self.subs
            for side in range(2):
                after = self.me if side == 0 else self.count - 1 - self.me

                @pl.when(step < after)
                def _():
                    self.copy(side, piece).wait_send()


def head_masks():
    lane = lax.broadcasted_iota(jnp.int32, (1, lanes), 1)
    first = (lane < head_dim).astype(jnp.float32)
    return first.astype(jnp.bfloat16), (1.0 - first).astype(jnp.bfloat16)


def offset_bias(bias_ref, head, row_start, rows, total):
    width = bias_ref.shape[1]
    shift = lax.rem(row_start + (width - (total - 1)), width)
    vector = pltpu.roll(jnp.broadcast_to(bias_ref[pl.ds(head, 1), :], (8, width)), shift, 1)
    vector = jnp.broadcast_to(vector[0:1, :], (rows, width))
    return pltpu.roll(vector, 0, 1, stride=1, stride_axis=0)[:, :total]


def rms_rows(values):
    return lax.rsqrt(jnp.mean(values * values, axis=-1, keepdims=True) + epsilon)


def gelu_parts(gate):
    root = 0.7978845608028654
    inner = root * (gate + 0.044715 * gate * gate * gate)
    tanh = jnp.tanh(inner)
    half = 0.5 * (1.0 + tanh)
    slope = half + 0.5 * gate * (1.0 - tanh * tanh) * root * (1.0 + 3 * 0.044715 * gate * gate)
    return gate * half, slope


def forward_kernel(
    count, tile, subs,
    length_ref,
    x_hbm, cot_hbm, wq_hbm, wk_hbm, wv_hbm, wo_hbm, wf_hbm, wg_hbm, wu_hbm, packed_ref, table_ref,
    n1_out, q_out, k_out, v_out, att_out, lse_out, middle_out, flat_out, back_out, res_out, n2_out, gate_out, up_out,
    gains_out, bias_out, ids_out,
    x_all, g_all, gains_all, wq, wk, wv, wo, wf, wg, wu, back_buf, inbox, n1_buf, q_buf, k_buf, v_buf, att_buf, lse_buf,
    total_buf, hid, grad_gate, grad_up, grad_hidden, res_buf, turned, stage,
    local_sems, x_sems, g_sems, c_sems, s_sems, n_sems, out_sems, stage_sems,
):
    me = lax.axis_index("group")
    rows, width = x_hbm.shape
    total = rows * count
    columns = wq.shape[1]
    units = wg.shape[1]
    local_heads = columns // head_dim
    n2_all, parts = x_all, back_buf
    loads = [
        pltpu.make_async_copy(source, target, local_sems.at[index])
        for index, (source, target) in enumerate(
            [
                (x_hbm, x_all.at[me]),
                (cot_hbm, g_all.at[me]),
                (wq_hbm, wq),
                (wk_hbm, wk),
                (wv_hbm, wv),
                (wo_hbm, wo),
                (wf_hbm, wf),
                (wg_hbm, wg),
                (wu_hbm, wu),
            ]
        )
    ]
    for load in loads[:2]:
        load.start()
    line_barrier(me, count)
    x_line = LineGather(me, count, x_all, x_sems, subs, x_hbm)
    g_line = LineGather(me, count, gains_all, g_sems)
    c_line = LineGather(me, count, g_all, c_sems, subs)
    n_line = LineGather(me, count, n2_all, n_sems, subs)

    def packed_row(index, length):
        first = index * (packed_ref.shape[0] // 3)
        return jnp.concatenate(
            [packed_ref[row : row + 1, :] for row in range(first, first + length // lanes)], axis=1
        )

    for index in range(2):
        gains_all[me, index : index + 1, :] = packed_row(index, width // count)
    g_line.begin()
    x_line.begin()
    for load in loads[2:6]:
        load.start()
    loads[1].wait()
    position = me * rows + lax.broadcasted_iota(jnp.int32, (rows, 1), 0)
    g_all[me] = g_all[me] * (position < length_ref[0]).astype(jnp.float32).astype(jnp.bfloat16)

    ids = packed_row(2, 2 * total)
    ids_out[...] = jnp.broadcast_to(ids, ids_out.shape)
    bucket = lax.broadcasted_iota(jnp.int32, (table_ref.shape[1], 2 * total), 0).astype(jnp.float32)
    one_hot = (bucket == ids).astype(jnp.float32).astype(jnp.bfloat16)
    bias_out[...] = nn_dot(table_ref[...], one_hot)

    for piece in range(g_line.pieces):
        g_line.arrive(piece)
    for owner in range(count):
        gains_out[:, owner * (width // count) : (owner + 1) * (width // count)] = gains_all[owner]
    for index in (0, 2, 3, 4):
        loads[index].wait()

    def project(block):
        values = x_all[block].astype(jnp.float32)
        normed = (values * rms_rows(values) * gains_out[0:1, :]).astype(jnp.bfloat16)
        n1_buf[block] = normed
        q_buf[block] = nn_dot(normed, wq[...]).astype(jnp.bfloat16)
        k_buf[block] = nn_dot(normed, wk[...]).astype(jnp.bfloat16)
        v_buf[block] = nn_dot(normed, wv[...]).astype(jnp.bfloat16)

    def begin_cotangent(sent):
        for side in range(2):
            last = me if side == 0 else count - 1 - me

            @pl.when(last == sent)
            def _():
                for piece in range(subs):
                    c_line.send_side(side, piece)

    begin_cotangent(0)
    for piece in range(subs):
        x_line.arrive(piece)
    begin_cotangent(1)
    project(me)
    x_line.each_block(0, project)
    for hops in range(1, count - 1):
        for piece in range(hops * subs, (hops + 1) * subs):
            x_line.arrive(piece)
        begin_cotangent(hops + 1)
        if hops == 1:
            for load in loads[6:]:
                load.start()
        x_line.each_block(hops, project)

    loads[5].wait()
    mask_first, mask_second = head_masks()
    key_valid = lax.broadcasted_iota(jnp.int32, (1, total), 1) < length_ref[0]
    lane = lax.broadcasted_iota(jnp.int32, (1, lanes), 1)

    def attend(block):
        lse_buf[block] = jnp.zeros((rows, lanes), jnp.float32)

        @pl.loop(0, local_heads // 2)
        def _(pair):
            cols = pl.ds(pl.multiple_of(pair * lanes, lanes), lanes)
            query = q_buf[block, :, cols]
            key = k_buf[:, :, cols].reshape(total, lanes)
            value = v_buf[:, :, cols].reshape(total, lanes)
            outs = []
            for half, mask in enumerate((mask_first, mask_second)):
                head = pair * 2 + half
                scores = nt_dot(query * mask, key)
                scores = scores + offset_bias(bias_out, head, block * rows, rows, total)
                scores = jnp.where(key_valid, scores, negative)
                top = jnp.max(scores, axis=-1, keepdims=True)
                expd = jnp.exp(scores - top)
                summed = jnp.sum(expd, axis=-1, keepdims=True)
                probs = (expd * (1.0 / summed)).astype(jnp.bfloat16)
                outs.append(nn_dot(probs, value))
                lse_buf[block] = jnp.where(lane == head, top + jnp.log(summed), lse_buf[block])
            att_buf[block, :, cols] = jnp.where(lane < head_dim, outs[0], outs[1]).astype(
                jnp.bfloat16
            )

    scatter = LineScatter(me, count, parts, inbox, total_buf, s_sems, subs)
    arrived = 0
    for index in range(count - 1):
        block = scatter.order(index)
        attend(block)
        parts[block] = nn_dot(att_buf[block], wo[...]).astype(jnp.bfloat16)
        if index == 0:
            x_line.wait_sends()
        scatter.at_time(index)
        if index:
            c_line.arrive(arrived)
            arrived += 1
    attend(me)
    total_buf[...] = x_all[me].astype(jnp.float32) + nn_dot(att_buf[me], wo[...])
    early = [(n1_buf, n1_out), (q_buf, q_out), (k_buf, k_out), (v_buf, v_out), (att_buf, att_out), (lse_buf, lse_out)]
    late = [
        (total_buf, middle_out), (back_buf, back_out), (res_buf, res_out), (n2_all, n2_out), (grad_gate, gate_out),
        (grad_up, up_out),
    ]
    outs = [
        pltpu.make_async_copy(source, target, out_sems.at[index])
        for index, (source, target) in enumerate(early + late)
    ]
    for copy in outs[: len(early)]:
        copy.start()
    for time in range(count - 1, scatter.times):
        scatter.at_time(time)
        if arrived < c_line.pieces:
            c_line.arrive(arrived)
            arrived += 1
    middle = total_buf[...]
    n2_all[me] = (middle * rms_rows(middle) * gains_out[1:2, :]).astype(jnp.bfloat16)
    n_line.begin()
    outs[len(early)].start()
    for piece in range(arrived, c_line.pieces):
        c_line.arrive(piece)

    for load in loads[6:]:
        load.wait()

    @pl.loop(0, units // tile)
    def _(index):
        here = pl.ds(pl.multiple_of(index * tile, tile), tile)
        grad_hidden[:, here] = nt_dot(g_all[...].reshape(total, width), wf[here, :])

    scatter.wait_sends()

    def block_pass(block):
        normed = n2_all[block]
        here = pl.ds(pl.multiple_of(block * rows, rows), rows)
        gate = nn_dot(normed, wg[...])
        up = nn_dot(normed, wu[...])
        act, slope = gelu_parts(gate)
        hid[block] = (act * up).astype(jnp.bfloat16)
        grads = grad_hidden[here, :]
        grad_gate[here, :] = (grads * up * slope).astype(jnp.bfloat16)
        grad_up[here, :] = (grads * act).astype(jnp.bfloat16)
        res_buf[block] = nn_dot(hid[block], wf[...]).astype(jnp.bfloat16)
        half = width // 2
        for cols in (pl.ds(0, half), pl.ds(half, half)):
            back_buf[block, :, cols] = (
                nt_dot(grad_gate[here, :], wg[cols, :]) + nt_dot(grad_up[here, :], wu[cols, :])
            ).astype(jnp.bfloat16)

    for piece in range(subs):
        n_line.arrive(piece)
    block_pass(me)
    n_line.each_block(0, block_pass)
    for hops in range(1, count - 1):
        n_line.arrive_block(hops, block_pass)
    for copy in outs[len(early) + 1 :]:
        copy.start()

    def weight_grad(left, right, base, height):
        depth = right.shape[2]
        panels = depth // lanes
        factor = right[...].reshape(total, depth)

        def store(slot, panel, row):
            return pltpu.make_async_copy(
                stage.at[slot, panel],
                flat_out.at[pl.ds(base + panel * height + row, tile)],
                stage_sems.at[slot, panel],
            )

        @pl.loop(0, height // tile)
        def _(index):
            slot = lax.rem(index, 2)
            row = pl.multiple_of(index * tile, tile)
            turned[...] = left[:, :, pl.ds(row, tile)].reshape(total, tile).T
            product = nn_dot(turned[...], factor).astype(jnp.bfloat16)

            @pl.when(index >= 2)
            def _():
                for panel in range(panels):
                    store(slot, panel, row).wait()

            for panel in range(panels):
                stage[slot, panel] = product[:, panel * lanes : (panel + 1) * lanes]
                store(slot, panel, row).start()

        for slot in range(2):
            for panel in range(panels):
                store(slot, panel, 0).wait()

    weight_grad(hid, g_all, 0, units)
    for line in (g_line, c_line, n_line):
        line.wait_sends()
    for copy in outs:
        copy.wait()


def forward(count, length, x, cot, wq, wk, wv, wo, wf, wg, wu, packed, table):
    rows, width = x.shape
    columns, units = wq.shape[1], wg.shape[1]
    total = count * rows
    tile = 128 if units % 256 else 256
    bf, f32 = jnp.bfloat16, jnp.float32
    shape = jax.ShapeDtypeStruct
    steps = count - 1
    subs = 2
    dma = pltpu.SemaphoreType.DMA
    vmem = pltpu.VMEM
    blocks = (count, rows, width)
    narrow = (count, rows, columns)
    return pl.pallas_call(
        functools.partial(forward_kernel, count, tile, subs),
        name="forward",
        out_shape=(
            shape(blocks, bf), shape(narrow, bf), shape(narrow, bf), shape(narrow, bf), shape(narrow, bf),
            shape((count, rows, lanes), f32), shape((rows, width), f32),
            shape((units * width // lanes, lanes), bf), shape(blocks, bf), shape(blocks, bf), shape(blocks, bf),
            shape((total, units), bf), shape((total, units), bf),
            shape((8, width), f32), shape((columns // head_dim, 2 * total), f32), shape((8, 2 * total), f32),
        ),
        in_specs=[smem_space] + [any_space] * 9 + [vmem_space] * 2,
        out_specs=[any_space] * 13 + [vmem_space] * 3,
        scratch_shapes=[
            vmem(blocks, bf), vmem(blocks, bf), vmem((count, 8, width // count), f32),
            vmem(wq.shape, bf), vmem(wk.shape, bf), vmem(wv.shape, bf), vmem(wo.shape, bf),
            vmem(wf.shape, bf), vmem(wg.shape, bf), vmem(wu.shape, bf),
            vmem(blocks, bf), vmem((count + 1, rows, width), bf), vmem(blocks, bf),
            vmem(narrow, bf), vmem(narrow, bf), vmem(narrow, bf), vmem(narrow, bf), vmem((count, rows, lanes), f32),
            vmem((rows, width), f32), vmem((count, rows, units), bf), vmem((total, units), bf), vmem((total, units), bf),
            vmem((total, units), f32), vmem(blocks, bf), vmem((tile, total), bf),
            vmem((2, width // lanes, tile, lanes), bf),
            dma((9,)), dma((2, 2, steps * subs)), dma((2, 2, steps)), dma((2, 2, steps * subs)),
            dma((2, 2, steps * subs)), dma((2, 2, steps * subs)), dma((12,)), dma((2, width // lanes)),
        ],
        compiler_params=pltpu.CompilerParams(
            collective_id=0, has_side_effects=True, vmem_limit_bytes=61 * 2**20
        ),
    )(length, x, cot, wq, wk, wv, wo, wf, wg, wu, packed, table)


def when(condition, body):
    if isinstance(condition, bool):
        if condition:
            body()
    else:
        pl.when(condition)(body)


class ReplicaSum:
    def __init__(self, replicas, chunk, source, target, work, core_box, path_box, sems):
        self.mine = lax.axis_index("replica")
        self.chunk, self.source, self.target = chunk, source, target
        self.work, self.core_box, self.path_box, self.sems = work, core_box, path_box, sems
        self.depth, self.slots = work.shape[0], core_box.shape[0]
        bits = [1 << index for index in range(1, replicas.bit_length() - 1)]
        self.orders = (bits, bits[::-1])
        self.levels = len(bits)
        self.last_phase = 2 * self.levels + 2
        self.half = chunk // 2

    def bit(self, mask):
        return jnp.where((self.mine & mask) != 0, 1, 0)

    def region(self, path, level):
        size = self.half // 2
        offset = path * size
        for mask in self.orders[path][:level]:
            size //= 2
            offset = offset + self.bit(mask) * size
        return offset, size

    def out_rows(self, chunk, offset, size):
        start = chunk * self.chunk + self.bit(1) * self.half + offset
        return self.target.at[pl.ds(pl.multiple_of(start, 16), size)]

    def sem(self, kind, phase, path, chunk):
        return self.sems.at[kind, phase, path, chunk % self.slots]

    def remote(self, source, target, phase, path, chunk, mask):
        return pltpu.make_async_remote_copy(
            src_ref=source,
            dst_ref=target,
            send_sem=self.sem(0, phase, path, chunk),
            recv_sem=self.sem(1, phase, path, chunk),
            device_id={"replica": self.mine ^ mask},
            device_id_type=MESH,
        )

    def core_copy(self, chunk):
        start = chunk * self.chunk + (1 - self.bit(1)) * self.half
        return self.remote(
            self.source(start, self.half), self.core_box.at[chunk % self.slots], 0, 0, chunk, 1
        )

    def load_copy(self, chunk):
        start = chunk * self.chunk + self.bit(1) * self.half
        return pltpu.make_async_copy(
            self.source(start, self.half), self.work.at[chunk % self.depth], self.sem(0, 0, 1, chunk)
        )

    def reduce_copy(self, chunk, path, level):
        mask = self.orders[path][level - 1]
        offset, size = self.region(path, level - 1)
        size //= 2
        start = pl.multiple_of(offset + (1 - self.bit(mask)) * size, 16)
        return self.remote(
            self.work.at[chunk % self.depth, pl.ds(start, size)],
            self.box(chunk, path, level),
            level, path, chunk, mask,
        )

    def box(self, chunk, path, level):
        size = self.half // 2 >> level
        start = sum(self.half // 2 >> step for step in range(1, level))
        return self.path_box.at[chunk % self.slots, path, pl.ds(start, size)]

    def add_box(self, chunk, path, level):
        offset, size = self.region(path, level)
        here = pl.ds(pl.multiple_of(offset, 16), size)
        slot = chunk % self.depth
        self.work[slot, here, :] = self.work[slot, here, :] + self.box(chunk, path, level)[...]

    def own_copy(self, chunk, path):
        offset, size = self.region(path, self.levels)
        return pltpu.make_async_copy(
            self.work.at[chunk % self.depth, pl.ds(pl.multiple_of(offset, 16), size)],
            self.out_rows(chunk, offset, size),
            self.sems.at[1, 0, 1 + path, chunk % self.slots],
        )

    def spread_copy(self, chunk, path, level):
        offset, size = self.region(path, level)
        if level == self.levels:
            source = self.work.at[chunk % self.depth, pl.ds(pl.multiple_of(offset, 16), size)]
        else:
            source = self.out_rows(chunk, offset, size)
        return self.remote(
            source, self.out_rows(chunk, offset, size),
            2 * self.levels + 1 - level, path, chunk, self.orders[path][level - 1],
        )

    def share_copy(self, chunk):
        rows = self.out_rows(chunk, 0, self.half)
        return self.remote(rows, rows, self.last_phase - 1, 0, chunk, 1)

    def advance(self, phase, chunk):
        levels = self.levels
        if phase == 0:
            self.core_copy(chunk).start()
            self.load_copy(chunk).start()
        elif phase <= levels + 1:
            if phase == 1:
                self.load_copy(chunk).wait()
                self.core_copy(chunk).wait()
                slot = chunk % self.depth
                self.work[slot] = self.work[slot] + self.core_box[chunk % self.slots]
            for path in range(2):
                if phase > 1:
                    self.reduce_copy(chunk, path, phase - 1).wait()
                    self.add_box(chunk, path, phase - 1)
                if phase <= levels:
                    self.reduce_copy(chunk, path, phase).start()
                else:
                    self.own_copy(chunk, path).start()
                    self.spread_copy(chunk, path, levels).start()
        else:
            level = 2 * levels + 1 - phase
            if level >= 0:
                for path in range(2):
                    self.spread_copy(chunk, path, level + 1).wait()
                    if level + 1 == levels:
                        self.own_copy(chunk, path).wait()
                    if level >= 1:
                        self.spread_copy(chunk, path, level).start()
                if level == 0:
                    self.share_copy(chunk).start()


scatter_pace, gather_pace, pair_pace = 1.0, 0.85, 1.0


def rms_backward(values, grads, gain):
    scale = rms_rows(values)
    unit = values * scale
    scaled = grads * gain
    inner = jnp.mean(scaled * unit, axis=-1, keepdims=True)
    return scale * (scaled - unit * inner), jnp.sum(grads * unit, axis=0, keepdims=True)


def backward_kernel(
    count, replicas, chunk, ffn_chunks, out_chunks, attn_chunks, skew, subs,
    length_ref,
    flat_hbm, n2_hbm, gate_hbm, up_hbm, back_hbm, res_hbm, middle_hbm, cot_hbm, x_hbm,
    q_hbm, k_hbm, v_hbm, att_hbm, lse_hbm, n1_hbm,
    wq_hbm, wk_hbm, wv_hbm, wo_hbm, gains_ref, bias_ref, ids_ref,
    sums_out, flat_out, result_out, input_out, small_out,
    back, res, middle, cot, x_own, q_buf, k_buf, v_buf, att_buf, lse_buf, n1_buf, wq, wk, wv, wo,
    back_box, res_box, total_buf, res_total, middle_grad, branch, grad_att, key_acc, value_acc, grad_qkv, grad_up,
    reverse, offsets, turned, stage, out_buf, small, small_parts, small_box, pair_box,
    work, core_box, path_box,
    load_sems, b_sems, r_sems, f_sems, a_sems, p_sems, pair_sems, stage_sems, out_sems, sum_sems,
):
    me = lax.axis_index("group")
    mine = lax.axis_index("replica")
    rows, width = middle.shape
    total = rows * count
    columns = wq.shape[1]
    local_heads = columns // head_dim
    units = grad_up.shape[1]
    sources = [
        back_hbm, n2_hbm, gate_hbm, up_hbm, middle_hbm, cot_hbm, x_hbm, wo_hbm, att_hbm, q_hbm, k_hbm, v_hbm,
        lse_hbm, wq_hbm, wk_hbm, wv_hbm, res_hbm, n1_hbm,
    ]
    targets = [
        back, n1_buf, grad_qkv.at[:, pl.ds(0, units)], grad_up, middle, cot, x_own, wo, att_buf, q_buf, k_buf, v_buf,
        lse_buf, wq, wk, wv, res, n1_buf,
    ]
    loads = [
        pltpu.make_async_copy(source, target, load_sems.at[index])
        for index, (source, target) in enumerate(zip(sources, targets))
    ]
    masks = [1 << index for index in range(replicas.bit_length() - 1)]
    barrier = pltpu.get_barrier_semaphore()

    @pl.when(me > 0)
    def _():
        pl.semaphore_signal(barrier, inc=1, device_id={"group": me - 1}, device_id_type=MESH)

    @pl.when(me < count - 1)
    def _():
        pl.semaphore_signal(barrier, inc=1, device_id={"group": me + 1}, device_id_type=MESH)

    for mask in masks:
        pl.semaphore_signal(barrier, inc=1, device_id={"replica": mine ^ mask}, device_id_type=MESH)
    peers = jnp.where(me > 0, 1, 0) + jnp.where(me < count - 1, 1, 0) + len(masks)
    pl.semaphore_wait(barrier, peers)

    first_rows = flat_hbm.shape[0]
    from_first_chunks = first_rows // chunk
    from_ffn = ffn_chunks
    chunks = from_ffn + attn_chunks

    def make_source(source_ref, base):
        return lambda start, size: source_ref.at[pl.ds(pl.multiple_of(start - base, 16), size)]

    parts = ReplicaSum(replicas, chunk, None, sums_out, work, core_box, path_box, sum_sems)
    from_first, from_second = make_source(flat_hbm, 0), make_source(flat_out, first_rows)
    clock = {"time": 0, "gaps": [0] + [None] * 4, "credit": 0.0}
    each = from_first_chunks
    bounds = [0, each, 2 * each, 3 * each, from_ffn + out_chunks, chunks]

    def start_piece(source, piece):
        parts.source = source
        parts.core_copy(piece).start()
        parts.load_copy(piece).start()

    def tick(time):
        for phase in range(parts.last_phase, -1, -1):
            entry = time - skew * phase
            inside, piece = False, entry
            for gap, low, high in zip(clock["gaps"], bounds, bounds[1:]):
                if gap is None:
                    continue
                if isinstance(entry, int):
                    if low + gap <= entry < high + gap:
                        inside, piece = True, entry - gap
                else:
                    here = (entry >= low + gap) & (entry < high + gap)
                    inside = inside | here
                    piece = jnp.where(here, entry - gap, piece)

            def body(phase=phase, piece=piece):
                if phase == parts.last_phase:
                    parts.share_copy(piece).wait()
                elif phase:
                    parts.source = lambda start, size: flat_hbm.at[pl.ds(0, size)]
                    parts.advance(phase, piece)

            if phase:
                when(inside, body)
            else:
                first, second = piece < from_first_chunks, piece >= from_first_chunks
                if isinstance(entry, int):
                    first, second = first and inside, second and inside
                else:
                    first, second = first & inside, second & inside
                when(first, functools.partial(start_piece, from_first, piece))
                when(second, functools.partial(start_piece, from_second, piece))

    def pace(amount):
        clock["credit"] += amount
        while clock["credit"] >= 1:
            tick(clock["time"])
            clock["time"] += 1
            clock["credit"] -= 1

    back_line = LineScatter(me, count, back, back_box, total_buf, b_sems, subs)
    res_line = LineScatter(me, count, res, res_box, res_total, r_sems, subs)
    first_line = LineScatter(me, count, back, back_box, total_buf, f_sems, subs)
    branch_line = LineGather(me, count, branch, a_sems, subs)
    small_line = LineScatter(me, count, small_parts, small_box, small.at[pl.ds(0, 8)], p_sems)

    tile = 256

    def weight_grad(left, factor, base, height, per_output, splits=1):
        panels = factor.shape[1] // lanes
        tiles = height // tile

        def store(slot, panel, row):
            return pltpu.make_async_copy(
                stage.at[slot, panel],
                flat_out.at[pl.ds(base + panel * height + row, tile)],
                stage_sems.at[slot, panel],
            )

        def run(first, last):
            @pl.loop(first, last)
            def _(index):
                slot = lax.rem(index, 2)
                row = pl.multiple_of(index * tile, tile)
                turned[...] = left[:, :, pl.ds(row, tile)].reshape(total, tile).T
                product = nn_dot(turned[...], factor).astype(jnp.bfloat16)

                @pl.when(index >= 2)
                def _():
                    for panel in range(panels):
                        store(slot, panel, row).wait()

                for panel in range(panels):
                    stage[slot, panel] = product[:, panel * lanes : (panel + 1) * lanes]
                    store(slot, panel, row).start()

        for split in range(splits):
            if split:
                pace(1)
            run(tiles * split // splits, tiles * (split + 1) // splits)
        for slot in range(min(2, tiles)):
            for panel in range(panels):
                store(slot, panel, 0).wait()

    def enter(group):
        before = clock["gaps"][group - 1]
        clock["gaps"][group] = max(clock["time"] - bounds[group], before)

    for now in range(skew):
        tick(now)
    for load in loads[:17]:
        load.start()
    loads[0].wait()
    total_buf[...] = back[me].astype(jnp.float32)
    back_line.at_time(0)
    clock["time"] = skew
    pace(skew)
    for load in loads[1:3]:
        load.wait()
    gate_base, attn_base = 0, 2 * units * width // lanes
    weight_grad(n1_buf, grad_qkv[:, 0:units], gate_base, width, units, 2)
    enter(1)
    pace(1)
    back_line.at_time(1)
    pace(1)
    back_line.at_time(2)
    pace(1)
    loads[3].wait()
    weight_grad(n1_buf, grad_up[...], gate_base + units * width // lanes, width, units, 2)
    enter(2)
    loads[17].start()
    anti = lax.broadcasted_iota(jnp.int32, (rows, rows), 0) + lax.broadcasted_iota(
        jnp.int32, (rows, rows), 1
    )
    reverse[...] = (anti == rows - 1).astype(jnp.float32).astype(jnp.bfloat16)
    for now in range(3, back_line.times):
        back_line.at_time(now)
        pace(scatter_pace)
    for load in loads[4:7]:
        load.wait()
    position = me * rows + lax.broadcasted_iota(jnp.int32, (rows, 1), 0)
    valid = (position < length_ref[0]).astype(jnp.float32)
    grad_mid, gain_grad = rms_backward(middle[...], total_buf[...], gains_ref[1:2, :])
    middle_grad[...] = cot[...].astype(jnp.float32) * valid + grad_mid
    branch[me] = middle_grad[...].astype(jnp.bfloat16)
    branch_line.begin()
    small_parts[...] = jnp.zeros_like(small_parts)
    part_width = width // count
    for owner in range(count):
        small_parts[owner, 1:2, :] = gain_grad[:, owner * part_width : (owner + 1) * part_width]
    for load in loads[7:18]:
        load.wait()
    res_total[...] = middle[...] + res[me].astype(jnp.float32)

    def attended_grad(block):
        grad_att[block] = nt_dot(branch[block], wo[...]).astype(jnp.bfloat16)

    attended_grad(me)
    for piece in range(branch_line.pieces):
        branch_line.arrive(piece)
        pace(gather_pace)
        if piece % subs == subs - 1:
            branch_line.each_block(piece // subs, attended_grad)

    weight_grad(att_buf, branch[...].reshape(total, width), attn_base, columns, width)
    enter(3)
    pace(1)
    mask_first, mask_second = head_masks()
    key_valid = lax.broadcasted_iota(jnp.int32, (1, total), 1) < length_ref[0]
    lane = lax.broadcasted_iota(jnp.int32, (1, lanes), 1)
    offsets[...] = jnp.zeros_like(offsets)

    def head_pair(pair):
        cols = pl.ds(pl.multiple_of(pair * lanes, lanes), lanes)
        key = k_buf[:, :, cols].reshape(total, lanes)
        value = v_buf[:, :, cols].reshape(total, lanes)
        key_acc[...] = jnp.zeros_like(key_acc)
        value_acc[...] = jnp.zeros_like(value_acc)

        @pl.loop(0, count)
        def _(block):
            query = q_buf[block, :, cols]
            grads = grad_att[block, :, cols]
            logs = lse_buf[block]
            query_parts = []
            for half, mask in enumerate((mask_first, mask_second)):
                head = pair * 2 + half
                query_half, grads_half = query * mask, grads * mask
                scores = nt_dot(query_half, key)
                scores = scores + offset_bias(bias_ref, head, block * rows, rows, total)
                scores = jnp.where(key_valid, scores, negative)
                log_total = jnp.sum(jnp.where(lane == head, logs, 0.0), axis=-1, keepdims=True)
                probs = jnp.exp(scores - log_total)
                grad_probs = nt_dot(grads_half, value)
                inner = jnp.sum(probs * grad_probs, axis=-1, keepdims=True)
                grad_scores = (probs * (grad_probs - inner)).astype(jnp.bfloat16)
                query_parts.append(nn_dot(grad_scores, key))
                key_acc[...] += nn_dot(query_half.astype(jnp.float32).T.astype(jnp.bfloat16), grad_scores)
                value_acc[...] += nn_dot(
                    grads_half.astype(jnp.float32).T.astype(jnp.bfloat16), probs.astype(jnp.bfloat16)
                )
                turned_scores = nn_dot(reverse[...], grad_scores)
                padded = jnp.concatenate([turned_scores, jnp.zeros_like(turned_scores)], axis=1)
                sheared = pltpu.roll(padded, 0, 1, stride=1, stride_axis=0)
                sums = jnp.broadcast_to(jnp.sum(sheared, axis=0, keepdims=True), (8, 2 * total))
                sums = pltpu.roll(sums, total - rows - block * rows, 1)
                offsets[pl.ds(head, 1), :] += sums[0:1, :]
            grad_qkv[pl.ds(pl.multiple_of(block * rows, rows), rows), cols] = jnp.where(
                lane < head_dim, query_parts[0], query_parts[1]
            ).astype(jnp.bfloat16)

        grad_qkv[:, pl.ds(pl.multiple_of(columns + pair * lanes, lanes), lanes)] = key_acc[
            ...
        ].T.astype(jnp.bfloat16)
        grad_qkv[:, pl.ds(pl.multiple_of(2 * columns + pair * lanes, lanes), lanes)] = value_acc[
            ...
        ].T.astype(jnp.bfloat16)

    res_time = 0
    for pair in range(local_heads // 2):
        if res_time < 3:
            res_line.at_time(res_time)
            res_time += 1
        head_pair(pair)
        pace(pair_pace)

    back_line.wait_sends()

    quarter = width // 4
    for start in range(0, width, quarter):
        cols = pl.ds(start, quarter)
        back[:, :, cols] = (
            (
                nt_dot(grad_qkv[:, 0:columns], wq[cols, :])
                + nt_dot(grad_qkv[:, columns : 2 * columns], wk[cols, :])
                + nt_dot(grad_qkv[:, 2 * columns : 3 * columns], wv[cols, :])
            )
            .astype(jnp.bfloat16)
            .reshape(count, rows, quarter)
        )
        if start == quarter:
            pace(1)
    for now in range(count - 1):
        first_line.at_time(now)
    pace(1)
    total_buf[...] = back[me].astype(jnp.float32)
    weight_grad(n1_buf, grad_qkv[...], attn_base + columns * width // lanes, width, columns, 2)
    enter(4)
    pace(skew)
    for now in range(count - 1, first_line.times):
        first_line.at_time(now)
        pace(1)
    grad_in, gain_grad = rms_backward(
        x_own[...].astype(jnp.float32), total_buf[...], gains_ref[0:1, :]
    )
    out_buf[1] = (middle_grad[...] + grad_in).astype(jnp.bfloat16)
    input_copy = pltpu.make_async_copy(out_buf.at[1], input_out, out_sems.at[1])
    input_copy.start()
    for owner in range(count):
        small_parts[owner, 0:1, :] = gain_grad[:, owner * part_width : (owner + 1) * part_width]
    small[0:8, :] = small_parts[me]
    for now in range(max(small_line.times, res_line.times - res_time)):
        if now < small_line.times:
            small_line.at_time(now)
        if res_time < res_line.times:
            res_line.at_time(res_time)
            res_time += 1
        pace(1)
    out_buf[0] = res_total[...].astype(jnp.bfloat16)
    result_copy = pltpu.make_async_copy(out_buf.at[0], result_out, out_sems.at[0])
    result_copy.start()
    bucket = lax.broadcasted_iota(jnp.int32, (lanes, ids_ref.shape[1]), 0).astype(jnp.float32)
    one_hot = (bucket == ids_ref[0:1, :]).astype(jnp.float32).astype(jnp.bfloat16)
    high = offsets[...].astype(jnp.bfloat16)
    rest = offsets[...] - high.astype(jnp.float32)
    middle_part = rest.astype(jnp.bfloat16)
    low_part = (rest - middle_part.astype(jnp.float32)).astype(jnp.bfloat16)
    small[8:16, 0:lanes] = nt_dot(high, one_hot) + nt_dot(middle_part, one_hot) + nt_dot(low_part, one_hot)
    small[8:16, lanes:] = jnp.zeros((8, part_width - lanes), jnp.float32)
    for index, mask in enumerate(masks):
        copy = pltpu.make_async_remote_copy(
            src_ref=small,
            dst_ref=pair_box.at[index],
            send_sem=pair_sems.at[0, index],
            recv_sem=pair_sems.at[1, index],
            device_id={"replica": mine ^ mask},
            device_id_type=MESH,
        )
        copy.start()
        pace(1)
        copy.wait()
        small[...] += pair_box[index]
    small_out[...] = small[...]

    @pl.loop(clock["time"], chunks + clock["gaps"][4] + skew * parts.last_phase)
    def _(now):
        tick(now)

    for line in (res_line, first_line, branch_line, small_line):
        line.wait_sends()
    result_copy.wait()
    input_copy.wait()


def backward(count, replicas, length, flat, n2, grad_gate, grad_up, back, res, middle, cot, x, q, k, v, att, lse, n1, wq, wk, wv, wo, gains, bias, ids):
    rows, width = middle.shape
    total = count * rows
    columns = wq.shape[1]
    bf, f32 = jnp.bfloat16, jnp.float32
    shape = jax.ShapeDtypeStruct
    steps = count - 1
    dma = pltpu.SemaphoreType.DMA
    units = grad_up.shape[1]
    chunk = flat.shape[0] // 5
    ffn_rows = 3 * flat.shape[0]
    attn_rows = 4 * columns * width // lanes
    skew, subs = 3, 2
    levels = replicas.bit_length() - 2
    masks = levels + 1
    depth = skew * (levels + 2)
    part_width = width // count
    vmem = pltpu.VMEM
    blocks = lambda kind: vmem((count, rows, width), kind)
    narrow = lambda: vmem((count, rows, columns), bf)
    boxes = lambda: vmem((count + 1, rows, width), bf)
    return pl.pallas_call(
        functools.partial(
            backward_kernel, count, replicas, chunk, ffn_rows // chunk, wo.size // lanes // chunk,
            attn_rows // chunk, skew, subs
        ),
        name="backward",
        out_shape=(
            shape((ffn_rows + attn_rows, lanes), bf),
            shape((2 * flat.shape[0] + attn_rows, lanes), bf),
            shape((rows, width), bf),
            shape((rows, width), bf),
            shape((16, part_width), f32),
        ),
        in_specs=[smem_space] + [any_space] * 19 + [vmem_space] * 3,
        out_specs=[any_space] * 4 + [vmem_space],
        scratch_shapes=[
            blocks(bf), blocks(bf), vmem((rows, width), f32), vmem((rows, width), bf), vmem((rows, width), bf),
            narrow(), narrow(), narrow(), narrow(), vmem((count, rows, lanes), f32), blocks(bf),
            vmem(wq.shape, bf), vmem(wk.shape, bf), vmem(wv.shape, bf), vmem(wo.shape, bf),
            boxes(), boxes(), vmem((rows, width), f32), vmem((rows, width), f32), vmem((rows, width), f32), blocks(bf),
            narrow(),
            vmem((lanes, total), f32), vmem((lanes, total), f32), vmem((total, 3 * columns), bf), vmem((total, units), bf),
            vmem((rows, rows), bf), vmem((8, 2 * total), f32), vmem((256, total), bf),
            vmem((2, width // lanes, 256, lanes), bf), vmem((2, rows, width), bf),
            vmem((16, part_width), f32), vmem((count, 8, part_width), f32), vmem((count + 1, 8, part_width), f32),
            vmem((masks, 16, part_width), f32),
            vmem((depth, chunk // 2, lanes), bf), vmem((2 * skew, chunk // 2, lanes), bf),
            vmem((2 * skew, 2, chunk // 4, lanes), bf),
            dma((18,)), dma((2, 2, steps * subs)), dma((2, 2, steps * subs)), dma((2, 2, steps * subs)),
            dma((2, 2, steps * subs)),
            dma((2, 2, steps)), dma((2, masks)), dma((2, width // lanes)), dma((2,)),
            dma((2, 2 * levels + 3, 3, 2 * skew)),
        ],
        compiler_params=pltpu.CompilerParams(
            collective_id=1, has_side_effects=True, vmem_limit_bytes=61 * 2**20
        ),
    )(length, flat, n2, grad_gate, grad_up, back, res, middle, cot, x, q, k, v, att, lse, n1, wq, wk, wv, wo, gains, bias, ids)


def widen_kernel(plan, slots, sums, result, input_grad, small, *refs):
    targets, (inbox, outbox, passed, in_sems, out_sems, pass_sems) = refs[:-6], refs[-6:]
    held = [
        pltpu.make_async_copy(source, passed.at[index], pass_sems.at[0, index])
        for index, source in enumerate((result, input_grad))
    ]
    given = [
        pltpu.make_async_copy(passed.at[index], target, pass_sems.at[1, index])
        for index, target in enumerate(targets[:2])
    ]
    for copy in held:
        copy.start()
    gain1, gain2, table = targets[2:5]
    for index, gain in enumerate((gain1, gain2)):
        for row in range(gain.shape[0]):
            gain[row : row + 1, :] = small[index : index + 1, row * lanes : (row + 1) * lanes]
    table[...] = small[8 : 8 + table.shape[0], 0 : table.shape[1]]
    targets = targets[5:]
    tiles = [
        (target, start, height, depth // lanes, size, row)
        for target, (start, height, depth, size) in zip(targets, plan)
        for row in range(0, height, size)
    ]

    def load(number):
        _, start, height, panels, size, row = tiles[number]
        slot = number % slots

        @pl.loop(0, panels)
        def _(panel):
            pltpu.make_async_copy(
                sums.at[pl.ds(start + row + panel * height, size)],
                inbox.at[slot, pl.ds(pl.multiple_of(panel * size, size), size)],
                in_sems.at[slot],
            ).start()

    def store(number):
        target, _, _, panels, size, row = tiles[number]
        return pltpu.make_async_copy(
            outbox.at[number % slots, pl.ds(0, size), pl.ds(0, panels * lanes)],
            target.at[pl.ds(row, size)],
            out_sems.at[number % slots],
        )

    for number in range(min(slots - 1, len(tiles))):
        load(number)
    for number in range(len(tiles)):
        _, _, _, panels, size, _ = tiles[number]
        slot = number % slots
        if number + slots - 1 < len(tiles):
            load(number + slots - 1)
        whole = inbox.at[slot, pl.ds(0, panels * size)]
        pltpu.make_async_copy(whole, whole, in_sems.at[slot]).wait()
        if number >= slots:
            store(number - slots).wait()

        @pl.loop(0, panels)
        def _(panel):
            outbox[slot, pl.ds(0, size), pl.ds(pl.multiple_of(panel * lanes, lanes), lanes)] = inbox[
                slot, pl.ds(pl.multiple_of(panel * size, size), size)
            ].astype(jnp.float32)

        store(number).start()
        if number == slots:
            for first, second in zip(held, given):
                first.wait()
                second.start()
    for number in range(max(len(tiles) - slots, 0), len(tiles)):
        store(number).wait()
    for copy in given:
        copy.wait()


def widen(sums, result, input_grad, small, table_shape, shapes):
    slots = 4
    plan, start = [], 0
    for height, depth in shapes:
        size = 512 if depth <= 1024 else 256
        while height % size:
            size //= 2
        plan.append((start, height, depth, size))
        start += height * depth // lanes
    most_in = max(size * depth // lanes for _, _, depth, size in plan)
    most_rows = max(size for _, _, _, size in plan)
    return pl.pallas_call(
        functools.partial(widen_kernel, plan, slots),
        name="widen",
        out_shape=[jax.ShapeDtypeStruct(result.shape, result.dtype)] * 2
        + [jax.ShapeDtypeStruct((small.shape[1] // lanes, lanes), jnp.float32)] * 2
        + [jax.ShapeDtypeStruct(table_shape, jnp.float32)]
        + [jax.ShapeDtypeStruct(shape, jnp.float32) for shape in shapes],
        in_specs=[any_space] * 3 + [vmem_space],
        out_specs=[any_space] * 2 + [vmem_space] * 3 + [any_space] * len(shapes),
        scratch_shapes=[
            pltpu.VMEM((slots, most_in, lanes), jnp.bfloat16),
            pltpu.VMEM((slots, most_rows, max(depth for _, depth in shapes)), jnp.float32),
            pltpu.VMEM((2,) + result.shape, result.dtype),
            pltpu.SemaphoreType.DMA((slots,)),
            pltpu.SemaphoreType.DMA((slots,)),
            pltpu.SemaphoreType.DMA((2, 2)),
        ],
        compiler_params=pltpu.CompilerParams(vmem_limit_bytes=61 * 2**20),
    )(sums, result, input_grad, small)


def local(
    inputs,
    seq_lengths,
    bucket_ids,
    norm1_gain,
    w_query,
    w_key,
    w_value,
    w_attn_out,
    bias_table,
    norm2_gain,
    w_gate,
    w_up,
    w_ffn_out,
    cotangent,
):
    count = lax.axis_size("group")
    replicas = lax.axis_size("replica")
    longest = max(2 * count * inputs.shape[1], norm1_gain.shape[0])
    longest = -(-longest // 1024) * 1024
    packed = jnp.concatenate(
        [
            jnp.pad(vector.astype(jnp.float32), (0, longest - vector.shape[0]), constant_values=-1)
            for vector in (norm1_gain, norm2_gain, bucket_ids)
        ]
    ).reshape(-1, lanes)
    (
        normed_one, query, key, value, attended, log_totals, middle, flat, back_part, result_part, normed_all,
        grad_gate, grad_up, gains, bias, ids,
    ) = forward(
        count, seq_lengths, inputs[0], cotangent[0], w_query, w_key, w_value, w_attn_out, w_ffn_out, w_gate, w_up,
        packed, bias_table.T,
    )
    sums, _, result, input_grad, small = backward(
        count, replicas, seq_lengths, flat, normed_all, grad_gate, grad_up, back_part, result_part, middle,
        cotangent[0], inputs[0], query, key, value, attended, log_totals, normed_one,
        w_query, w_key, w_value, w_attn_out, gains, bias, ids,
    )
    weights = (w_ffn_out, w_gate, w_up, w_attn_out, w_query, w_key, w_value)
    (
        result, input_grad, gain1_grad, gain2_grad, table_grad,
        ffn_out_grad, gate_grad, up_grad, attn_out_grad, query_grad, key_grad, value_grad,
    ) = widen(
        sums, result, input_grad, small, bias_table.shape[::-1], [weight.shape for weight in weights]
    )
    return (
        result[None],
        input_grad[None],
        gain1_grad.reshape(-1),
        query_grad,
        key_grad,
        value_grad,
        attn_out_grad,
        table_grad.T,
        gain2_grad.reshape(-1),
        gate_grad,
        up_grad,
        ffn_out_grad,
    )


def solution(mesh):
    placed = (
        P("replica", "group", None),
        P("replica"),
        P(),
        P("group"),
        P(None, "group"),
        P(None, "group"),
        P(None, "group"),
        P("group", None),
        P(None, "group"),
        P("group"),
        P(None, "group"),
        P(None, "group"),
        P("group", None),
        P("replica", "group", None),
    )
    return jax.shard_map(
        local,
        mesh=mesh,
        in_specs=placed,
        out_specs=(
            P("replica", "group", None),
            P("replica", "group", None),
            P("group"),
            P(None, "group"),
            P(None, "group"),
            P(None, "group"),
            P("group", None),
            P(None, "group"),
            P("group"),
            P(None, "group"),
            P(None, "group"),
            P("group", None),
        ),
        check_vma=False,
    )
```
